32 devices in a mesh: fsdp: 8 (over z, y), tp: 4 (over x, core).
Axes of the slice: x: 2, y: 2, z: 4, core: 2. Of those that a mesh axis runs over, the one named last changes fastest.
Arguments:
- latents: float32 [16, 256, 16], P('fsdp', 'tp'), may hold values from -6 to 6
- noise: float32 [16, 256, 16], P('fsdp', 'tp'), may hold values from -6 to 6
- timesteps: int32 [16], replicated, may hold values from 0 to 999
- labels: int32 [16], replicated, may hold values from 0 to 999
- step_count: int32 [1], replicated, may hold values from 1 to 20
- tables: float32 [1288, 768], P(None, 'fsdp'), may hold values from -0.75 to 0.75
- time_weight: float32 [768, 768], P('fsdp'), may hold values from -0.21875 to 0.21875
- cond_weight: float32 [10752, 768], P('fsdp'), may hold values from -0.108253175 to 0.108253175
- cond_bias: float32 [10752], P('fsdp'), may hold values from -1 to 1
- attn_weight: float32 [2, 4, 768, 768], P(None, None, 'fsdp', 'tp'), may hold values from -0.649519 to 0.649519
- mlp_weight: float32 [2, 2, 768, 3072], P(None, None, 'fsdp', 'tp'), may hold values from -0.21875 to 0.21875
- tables_first: float32 [1288, 768], P(None, 'fsdp'), may hold values from -5.340576e-05 to 5.340576e-05
- tables_second: float32 [1288, 768], P(None, 'fsdp'), may hold values from 9.765625e-13 to 3.94113e-10
- time_first: float32 [768, 768], P('fsdp'), may hold values from -5.340576e-05 to 5.340576e-05
- time_second: float32 [768, 768], P('fsdp'), may hold values from 9.765625e-13 to 3.90625e-12
- cond_first: float32 [10752, 768], P('fsdp'), may hold values from -5.340576e-05 to 5.340576e-05
- cond_second: float32 [10752, 768], P('fsdp'), may hold values from 9.765625e-13 to 3.90625e-12
- bias_first: float32 [10752], P('fsdp'), may hold values from -5.340576e-05 to 5.340576e-05
- bias_second: float32 [10752], P('fsdp'), may hold values from 9.765625e-13 to 3.90625e-12
- attn_first: float32 [2, 4, 768, 768], P(None, None, 'fsdp', 'tp'), may hold values from -5.340576e-05 to 5.340576e-05
- attn_second: float32 [2, 4, 768, 768], P(None, None, 'fsdp', 'tp'), may hold values from 9.765625e-13 to 3.90625e-12
- mlp_first: float32 [2, 2, 768, 3072], P(None, None, 'fsdp', 'tp'), may hold values from -5.340576e-05 to 5.340576e-05
- mlp_second: float32 [2, 2, 768, 3072], P(None, None, 'fsdp', 'tp'), may hold values from 9.765625e-13 to 3.90625e-12
Outputs:
- loss: float32 [], replicated
- grad_norm: float32 [], replicated
- tables_new: float32 [1288, 768], P(None, 'fsdp')
- tables_first_new: float32 [1288, 768], P(None, 'fsdp')
- tables_second_new: float32 [1288, 768], P(None, 'fsdp')
- time_new: float32 [768, 768], P('fsdp')
- time_first_new: float32 [768, 768], P('fsdp')
- time_second_new: float32 [768, 768], P('fsdp')
- cond_new: float32 [10752, 768], P('fsdp')
- cond_first_new: float32 [10752, 768], P('fsdp')
- cond_second_new: float32 [10752, 768], P('fsdp')
- bias_new: float32 [10752], P('fsdp')
- bias_first_new: float32 [10752], P('fsdp')
- bias_second_new: float32 [10752], P('fsdp')
- attn_new: float32 [2, 4, 768, 768], P(None, None, 'fsdp', 'tp')
- attn_first_new: float32 [2, 4, 768, 768], P(None, None, 'fsdp', 'tp')
- attn_second_new: float32 [2, 4, 768, 768], P(None, None, 'fsdp', 'tp')
- mlp_new: float32 [2, 2, 768, 3072], P(None, None, 'fsdp', 'tp')
- mlp_first_new: float32 [2, 2, 768, 3072], P(None, None, 'fsdp', 'tp')
- mlp_second_new: float32 [2, 2, 768, 3072], P(None, None, 'fsdp', 'tp')
The draws below stay inside these ranges and needn't reach their ends.
All inputs are finite; a program needn't handle non-finite values.
Results may differ from the reference program's by a relative error of at most 0.018.
Values may be sent and summed in bfloat16 or wider, within the bound.
A program may use at most 192 MiB of HBM per device.

```python
import math
import jax
import jax.numpy as jnp
from jax import lax

D = 768
HEADS = 12
HEAD_DIM = 64
FF = 3072
NCLASS = 1000
FREQ = 256
PATCH_DIM = 16
GRID = 16
LAYERS = 2
SEQ = 256
BATCH = 16
TOKENS = 4096
NCOND = 10752
NTAB = 1288


def clipped_normal(key, shape, scale):
    return jnp.clip(jax.random.normal(key, shape, jnp.float32), -3.0, 3.0) * scale


def draw_tables(key, part):
    subkeys = jax.random.split(key, 4)
    patch_rows = clipped_normal(subkeys[0], (PATCH_DIM, D), 0.25)
    output_rows = clipped_normal(subkeys[1], (PATCH_DIM, D), D ** (-0.5))
    time_rows = clipped_normal(subkeys[2], (FREQ, D), FREQ ** (-0.5))
    label_rows = clipped_normal(subkeys[3], (NCLASS, D), 0.2)
    return jnp.concatenate([patch_rows, output_rows, time_rows, label_rows], axis=0).astype(jnp.float32)


def draw_cond_weight(key, part):
    return clipped_normal(key, (NCOND, D), D ** (-0.5)).astype(jnp.float32)


def draw_attn_weight(key, part):
    subkeys = jax.random.split(key, 2)
    inputs_side = clipped_normal(subkeys[0], (LAYERS, 3, D, D), D ** (-0.5))
    output_side = clipped_normal(subkeys[1], (LAYERS, 1, D, D), 6.0 * D ** (-0.5))
    return jnp.concatenate([inputs_side, output_side], axis=1).astype(jnp.float32)


def draw_tables_second(key, part):
    entries = NTAB * D + D * D + (D + 1) * NCOND + LAYERS * (4 * D * D + 2 * D * FF)
    head_factor = 1.0 + TOKENS * entries / ((TOKENS + 76000.0) * PATCH_DIM * D)
    logs = jax.random.uniform(key, (NTAB, D), jnp.float32, 0.0, math.log(4.0))
    row_ids = jnp.arange(NTAB, dtype=jnp.int32)[:, None]
    factor = jnp.where(row_ids < 2 * PATCH_DIM, head_factor, 1.0)
    return (4e-09 / TOKENS * factor * jnp.exp(logs)).astype(jnp.float32)


def touch_ends(drawn, own_key, low, high):
    longest = drawn.shape.index(max(drawn.shape))
    spots = []
    for shift in (0, 1):
        where = [jax.random.randint(jax.random.fold_in(own_key, axis), (), 0, length) for axis, length in enumerate(drawn.shape)]
        where[longest] = (where[longest] + shift) % drawn.shape[longest]
        spots.append(tuple(where))
    return drawn.at[spots[0]].set(low).at[spots[1]].set(high)


def block_scale(key, extent, cuts, low, largest):
    factor_of = 1.0
    for dim, shards_of in cuts:
        steps = jax.random.uniform(jax.random.fold_in(jax.random.fold_in(key, 6), dim), (shards_of,), jnp.float32, low / len(cuts), largest / len(cuts))
        factor_of = factor_of * jnp.repeat(jnp.exp(steps), extent[dim] // shards_of).reshape((-1,) + (1,) * (len(extent) - 1 - dim))
    return factor_of


def bell_draw(own_key, shape, deviation, most, cuts=(), kind=jnp.bfloat16):
    result = deviation * jax.random.normal(own_key, shape, jnp.float32)
    if cuts:
        result = result * block_scale(own_key, shape, cuts, -0.22, 0.18)
    return jnp.clip(result, -most, most).astype(kind)


def setup_inputs(seed: int = 0) -> dict:
    key_of = jax.random.split(jax.random.key(seed), 24)
    latents = bell_draw(key_of[0], (BATCH, SEQ, PATCH_DIM), 1.0, 6.0, ((0, 8), (1, 4)), jnp.float32)
    noise = bell_draw(key_of[1], (BATCH, SEQ, PATCH_DIM), 1.0, 6.0, ((0, 8), (1, 4)), jnp.float32)
    timesteps = touch_ends(jax.random.randint(key_of[2], (BATCH,), 0, 1000), jax.random.fold_in(key_of[2], 1), 0, 999).astype(jnp.int32)
    labels = touch_ends(jax.random.randint(key_of[3], (BATCH,), 0, NCLASS), jax.random.fold_in(key_of[3], 1), 0, NCLASS - 1).astype(jnp.int32)
    step_count = jax.random.randint(key_of[4], (1,), 1, 21).astype(jnp.int32)
    tables = draw_tables(jax.random.fold_in(key_of[23], 71), 0)
    time_weight = bell_draw(key_of[6], (D, D), D ** -0.5, 0.21875, ((0, 8),), jnp.float32)
    cond_weight = draw_cond_weight(jax.random.fold_in(key_of[23], 71), 0)
    cond_bias = bell_draw(key_of[8], (NCOND,), 0.3, 1.0, ((0, 8),), jnp.float32)
    attn_weight = draw_attn_weight(jax.random.fold_in(key_of[23], 71), 0)
    mlp_weight = bell_draw(key_of[10], (LAYERS, 2, D, FF), D ** -0.5, 0.21875, ((2, 8), (3, 4)), jnp.float32)
    tables_first = bell_draw(key_of[11], (NTAB, D), (0.00022 * TOKENS ** -0.5), 5.340576171875e-05, ((1, 8),), jnp.float32)
    tables_second = draw_tables_second(jax.random.fold_in(key_of[23], 71), 0)
    time_first = bell_draw(key_of[13], (D, D), (0.00022 * TOKENS ** -0.5), 5.340576171875e-05, ((0, 8),), jnp.float32)
    time_second = jnp.clip(jnp.exp(math.log(3.906249889523705e-12) - 1.3862944 * jax.random.uniform(key_of[14], (D, D), jnp.float32) ** block_scale(key_of[14], (D, D), ((0, 8),), -0.2, 0.2)), 9.765624723809263e-13, 3.906249889523705e-12)
    cond_first = bell_draw(key_of[15], (NCOND, D), (0.00022 * TOKENS ** -0.5), 5.340576171875e-05, ((0, 8),), jnp.float32)
    cond_second = jnp.clip(jnp.exp(math.log(3.906249889523705e-12) - 1.3862944 * jax.random.uniform(key_of[16], (NCOND, D), jnp.float32) ** block_scale(key_of[16], (NCOND, D), ((0, 8),), -0.2, 0.2)), 9.765624723809263e-13, 3.906249889523705e-12)
    bias_first = bell_draw(key_of[17], (NCOND,), (0.00022 * TOKENS ** -0.5), 5.340576171875e-05, ((0, 8),), jnp.float32)
    bias_second = jnp.clip(jnp.exp(math.log(3.906249889523705e-12) - 1.3862944 * jax.random.uniform(key_of[18], (NCOND,), jnp.float32) ** block_scale(key_of[18], (NCOND,), ((0, 8),), -0.2, 0.2)), 9.765624723809263e-13, 3.906249889523705e-12)
    attn_first = bell_draw(key_of[19], (LAYERS, 4, D, D), (0.00022 * TOKENS ** -0.5), 5.340576171875e-05, ((2, 8), (3, 4)), jnp.float32)
    attn_second = jnp.clip(jnp.exp(math.log(3.906249889523705e-12) - 1.3862944 * jax.random.uniform(key_of[20], (LAYERS, 4, D, D), jnp.float32) ** block_scale(key_of[20], (LAYERS, 4, D, D), ((2, 8), (3, 4)), -0.2, 0.2)), 9.765624723809263e-13, 3.906249889523705e-12)
    mlp_first = bell_draw(key_of[21], (LAYERS, 2, D, FF), (0.00022 * TOKENS ** -0.5), 5.340576171875e-05, ((2, 8), (3, 4)), jnp.float32)
    mlp_second = jnp.clip(jnp.exp(math.log(3.906249889523705e-12) - 1.3862944 * jax.random.uniform(key_of[22], (LAYERS, 2, D, FF), jnp.float32) ** block_scale(key_of[22], (LAYERS, 2, D, FF), ((2, 8), (3, 4)), -0.2, 0.2)), 9.765624723809263e-13, 3.906249889523705e-12)
    return {"latents": latents, "noise": noise, "timesteps": timesteps, "labels": labels, "step_count": step_count, "tables": tables, "time_weight": time_weight, "cond_weight": cond_weight, "cond_bias": cond_bias, "attn_weight": attn_weight, "mlp_weight": mlp_weight, "tables_first": tables_first, "tables_second": tables_second, "time_first": time_first, "time_second": time_second, "cond_first": cond_first, "cond_second": cond_second, "bias_first": bias_first, "bias_second": bias_second, "attn_first": attn_first, "attn_second": attn_second, "mlp_first": mlp_first, "mlp_second": mlp_second}


@jax.custom_vjp
def low(v):
    return lax.optimization_barrier(v.astype(jnp.bfloat16)).astype(jnp.float32)

@jax.custom_vjp
def low_back(v):
    return v

def low_keep(v):
    return (low(v), None)

def low_pass(kept, grad):
    return (grad,)

def back_keep(v):
    return (v, None)

def back_low(kept, grad):
    return (low(grad),)
low.defvjp(low_keep, low_pass)
low_back.defvjp(back_keep, back_low)
highest = lax.Precision.HIGHEST
norm_eps = 1e-06
beta_first = 0.9
beta_second = 0.999
adam_eps = 1e-08
learn_rate = 0.2
weight_decay = 0.01
clip_scale = 0.002
diffusion_steps = 1000.0

def round_both(value):
    return low(low_back(value))

def timestep_features(timesteps):
    half_width = FREQ // 2
    omegas = jnp.exp(-math.log(10000.0) * jnp.arange(half_width, dtype=jnp.float32) / half_width)
    angles = timesteps.astype(jnp.float32)[:, None] * omegas[None, :]
    return jnp.concatenate([jnp.cos(angles), jnp.sin(angles)], axis=1)

def position_table(start_at, number):
    quarter = D // 4
    omegas = 1.0 / jnp.power(10000.0, jnp.arange(quarter, dtype=jnp.float32) / quarter)
    token_ids = start_at + jnp.arange(number, dtype=jnp.int32)
    row_angles = (token_ids // GRID).astype(jnp.float32)[:, None] * omegas[None, :]
    col_angles = (token_ids % GRID).astype(jnp.float32)[:, None] * omegas[None, :]
    return jnp.concatenate([jnp.sin(row_angles), jnp.cos(row_angles), jnp.sin(col_angles), jnp.cos(col_angles)], axis=1)

def signal_share(timesteps):
    phase = (timesteps.astype(jnp.float32) / diffusion_steps + 0.008) / 1.008 * (math.pi / 2)
    return jnp.cos(phase) ** 2

def layer_norm(values):
    centred = values - lax.optimization_barrier(jnp.mean(values, axis=-1, keepdims=True))
    return centred * lax.rsqrt(lax.optimization_barrier(jnp.mean(centred * centred, axis=-1, keepdims=True)) + norm_eps)

def modulate(values, shift, scale):
    return layer_norm(values) * (1.0 + scale[:, None, :]) + shift[:, None, :]

def group_loss(low_weights, inputs):
    low_tables, low_attn, low_mlp = low_weights
    clean, noise, timesteps, modul = inputs
    batch_size = clean.shape[0]
    share = signal_share(timesteps)[:, None, None]
    noisy = low(jnp.sqrt(share) * clean + jnp.sqrt(1.0 - share) * noise)
    resid = low_back(jnp.einsum('bsp,pd->bsd', noisy, low_tables[:PATCH_DIM], precision=highest)) + position_table(0, SEQ)[None]
    for layer in range(LAYERS):
        base = layer * 6 * D
        pieces = [modul[:, base + piece_index * D:base + (piece_index + 1) * D] for piece_index in range(6)]
        weights = low_attn[layer]
        hidden = low(modulate(resid, pieces[0], pieces[1]))
        projected = round_both(jnp.einsum('bsd,kde->kbse', hidden, weights[:3], precision=highest))
        per_head = projected.reshape(3, batch_size, SEQ, HEADS, HEAD_DIM)
        scores = low_back(jnp.einsum('bqhe,bkhe->bhqk', per_head[0], per_head[1], precision=highest) * HEAD_DIM ** (-0.5))
        attn_probs = jax.nn.softmax(scores, axis=-1)
        attended = round_both(jnp.einsum('bhqk,bkhe->bqhe', low(attn_probs), per_head[2], precision=highest)).reshape(batch_size, SEQ, D)
        branch = low_back(jnp.einsum('bse,fe->bsf', attended, weights[3], precision=highest))
        resid = resid + pieces[2][:, None, :] * branch
        hidden = low(modulate(resid, pieces[3], pieces[4]))
        upward = low_back(jnp.einsum('bsd,df->bsf', hidden, low_mlp[layer, 0], precision=highest))
        active = low(jax.nn.gelu(upward, approximate=True))
        branch = low_back(jnp.einsum('bsf,df->bsd', active, low_mlp[layer, 1], precision=highest))
        resid = resid + pieces[5][:, None, :] * branch
    final_base = 6 * LAYERS * D
    final = low(modulate(resid, modul[:, final_base:final_base + D], modul[:, final_base + D:final_base + 2 * D]))
    predicted = low_back(jnp.einsum('bsd,pd->bsp', final, low_tables[PATCH_DIM:2 * PATCH_DIM], precision=highest))
    difference = predicted - noise
    return jnp.sum(difference * difference)

def total_loss(tables, time_weight, cond_weight, cond_bias, attn_weight, mlp_weight, latents, noise, timesteps, labels):
    low_tables = low(tables)
    features = low(timestep_features(timesteps))
    time_pre = low_back(jnp.dot(features, low_tables[2 * PATCH_DIM:2 * PATCH_DIM + FREQ], precision=highest))
    time_hidden = low(jax.nn.silu(time_pre))
    label_rows = low_tables[2 * PATCH_DIM + FREQ:]
    cond = low_back(jnp.dot(time_hidden, low(time_weight), precision=highest) + label_rows[labels])
    cond_act = low(jax.nn.silu(cond))
    modul = low_back(jnp.dot(cond_act, low(cond_weight).T, precision=highest) + low(cond_bias)[None, :])
    low_weights = (low_tables, low(attn_weight), low(mlp_weight))
    group = math.gcd(BATCH, max(1, 4096 // SEQ))
    groups = BATCH // group

    def reshaped(value):
        return value.reshape((groups, group) + value.shape[1:])

    def group_step(carry, inputs):
        return (carry + group_loss(low_weights, inputs), None)
    total, unused = lax.scan(jax.checkpoint(group_step), jnp.zeros((), jnp.float32), (reshaped(latents), reshaped(noise), reshaped(timesteps), reshaped(modul)))
    return total / (BATCH * SEQ * PATCH_DIM)

def adam_update(weight, grad, first, second, count):
    first_new = beta_first * first + (1.0 - beta_first) * grad
    second_new = beta_second * second + (1.0 - beta_second) * grad * grad
    first_hat = first_new / (1.0 - jnp.power(beta_first, count))
    second_hat = second_new / (1.0 - jnp.power(beta_second, count))
    weight_new = weight - learn_rate * (first_hat / (jnp.sqrt(second_hat) + adam_eps) + weight_decay * weight)
    return [weight_new, first_new, second_new]

def reference(latents, noise, timesteps, labels, step_count, tables, time_weight, cond_weight, cond_bias, attn_weight, mlp_weight, tables_first, tables_second, time_first, time_second, cond_first, cond_second, bias_first, bias_second, attn_first, attn_second, mlp_first, mlp_second):
    weights = (tables, time_weight, cond_weight, cond_bias, attn_weight, mlp_weight)

    def loss_of(tab, tim, con, bia, att, mlw):
        return total_loss(tab, tim, con, bia, att, mlw, latents, noise, timesteps, labels)
    loss, backward = jax.vjp(loss_of, *weights)
    grads = backward(jnp.ones((), jnp.float32))
    norm = jnp.sqrt(sum((jnp.sum(grad * grad) for grad in grads)))
    entries = NTAB * D + D * D + (D + 1) * NCOND + LAYERS * (4 * D * D + 2 * D * FF)
    limit = clip_scale * math.sqrt(entries / (BATCH * SEQ))
    factor = jnp.minimum(1.0, limit / norm)
    count = step_count[0].astype(jnp.float32)
    states = ((tables_first, tables_second), (time_first, time_second), (cond_first, cond_second), (bias_first, bias_second), (attn_first, attn_second), (mlp_first, mlp_second))
    results = []
    for weight, grad, state in zip(weights, grads, states):
        results.extend(adam_update(weight, grad * factor, state[0], state[1], count))
    return (loss, norm, results[0], results[1], results[2], results[3], results[4], results[5], results[6], results[7], results[8], results[9], results[10], results[11], results[12], results[13], results[14], results[15], results[16], results[17])
```

```python
from functools import partial
import math

import jax
import jax.numpy as jnp
from jax import lax
from jax.sharding import PartitionSpec as P

D = 768
HEAD_DIM = 64
FF = 3072
NCLASS = 1000
FREQ = 256
PATCH_DIM = 16
GRID = 16
LAYERS = 2
SEQ = 256
NCOND = 10752
NTAB = 1288


norm_eps = 1e-06
beta_first = 0.9
beta_second = 0.999
adam_eps = 1e-08
learn_rate = 0.2
weight_decay = 0.01
clip_scale = 0.002
diffusion_steps = 1000.0


def timestep_features(timesteps):
    half_width = FREQ // 2
    omegas = jnp.exp(-math.log(10000.0) * jnp.arange(half_width, dtype=jnp.float32) / half_width)
    angles = timesteps.astype(jnp.float32)[:, None] * omegas[None, :]
    return jnp.concatenate([jnp.cos(angles), jnp.sin(angles)], axis=1)


def signal_share(timesteps):
    phase = (timesteps.astype(jnp.float32) / diffusion_steps + 0.008) / 1.008 * (math.pi / 2)
    return jnp.cos(phase) ** 2


def butterfly_bits(number):
    bits = []
    bit = 1
    while bit < number:
        bits.append(bit)
        bit *= 2
    return bits


def split_radices(number):
    radices = []
    while number > 1:
        radix = 4 if number % 4 == 0 else 2
        radices.append(radix)
        number //= radix
    return radices


class Routes:
    def __init__(self, mesh):
        self.num_fsdp = mesh.shape["fsdp"]
        self.num_tp = mesh.shape["tp"]
        self.outer = split_radices(self.num_fsdp // 2)

    def core(self, value):
        return lax.ppermute(value, "tp", [(t, t ^ 1) for t in range(self.num_tp)])

    def across(self, value):
        return lax.ppermute(value, "tp", [(t, t ^ 2) for t in range(self.num_tp)])

    def pair(self, value):
        return lax.ppermute(value, "fsdp", [(f, f ^ 1) for f in range(self.num_fsdp)])

    def shift(self, value, stride, radix, amount):
        pairs = []
        for f in range(self.num_fsdp):
            digit = (f // stride) % radix
            pairs.append((f, f + ((digit + amount) % radix - digit) * stride))
        return lax.ppermute(value, "fsdp", pairs)

    def slot_owner(self, fsdp_index, slots):
        per_pair = self.num_fsdp // 2
        pair_part = (slots // per_pair + fsdp_index) % 2
        rest = slots % per_pair
        owner = pair_part
        stride = 2
        for radix in self.outer:
            digit = (rest + fsdp_index // stride) % radix
            owner = owner + digit * stride
            rest = rest // radix
            stride *= radix
        return owner

    def gather_outer(self, block):
        stride = 2
        for radix in self.outer:
            block = jnp.concatenate(
                [block] + [self.shift(block, stride, radix, -k) for k in range(1, radix)], axis=0
            )
            stride *= radix
        return block

    def gather_rows(self, block):
        held = self.gather_outer(block)
        return jnp.concatenate([held, self.pair(held)], axis=0)

    def gather_both(self, block, across_last):
        held = self.gather_outer(block)
        if across_last:
            own = jnp.concatenate([held, self.pair(held)], axis=0)
            return (own, self.across(own))
        other = self.across(held)
        return (
            jnp.concatenate([held, self.pair(held)], axis=0),
            jnp.concatenate([other, self.pair(other)], axis=0),
        )

    def scatter_rows(self, total, dtype=jnp.bfloat16):
        half = total.shape[0] // 2
        received = self.pair(total[half:].astype(dtype))
        held = total[:half] + received.astype(jnp.float32)
        strides = []
        stride = 2
        for radix in self.outer:
            strides.append(stride)
            stride *= radix
        for radix, stride in reversed(list(zip(self.outer, strides))):
            size = held.shape[0] // radix
            parts = [
                self.shift(held[k * size : (k + 1) * size].astype(dtype), stride, radix, k)
                for k in range(1, radix)
            ]
            held = held[:size]
            for part in parts:
                held = held + part.astype(jnp.float32)
        return held

    def scatter_both(self, own, other):
        received = self.across(other.astype(jnp.bfloat16))
        return self.scatter_rows(own + received.astype(jnp.float32))

    def sum_fsdp(self, value):
        for bit in butterfly_bits(self.num_fsdp):
            value = value + lax.ppermute(
                value, "fsdp", [(f, f ^ bit) for f in range(self.num_fsdp)]
            )
        return value

    def sum_all(self, value):
        value = value + self.core(value)
        value = value + self.across(value)
        return self.sum_fsdp(value)


def after(value, *earlier):
    return lax.optimization_barrier((value,) + earlier)[0]


def dot_f32(left, right, left_dim, right_dim):
    return lax.dot_general(
        left, right, (((left_dim,), (right_dim,)), ((), ())), preferred_element_type=jnp.float32
    )


def layer_norm(values):
    centred = values - jnp.mean(values, axis=-1, keepdims=True)
    inverse = lax.rsqrt(jnp.mean(centred * centred, axis=-1, keepdims=True) + norm_eps)
    return (centred * inverse, inverse)


def modulate(values, shift, scale):
    normed, inverse = layer_norm(values)
    return ((normed * (1.0 + scale) + shift).astype(jnp.bfloat16), normed, inverse)


def norm_backward(grad_mixed, normed, inverse, scale, counted):
    grad_shift = jnp.sum(grad_mixed[:counted], axis=0)
    grad_scale = jnp.sum(grad_mixed[:counted] * normed[:counted], axis=0)
    grad_normed = grad_mixed * (1.0 + scale)
    centred = grad_normed - jnp.mean(grad_normed, axis=-1, keepdims=True)
    grad_input = (
        centred - normed * jnp.mean(grad_normed * normed, axis=-1, keepdims=True)
    ) * inverse
    return (grad_input, grad_shift, grad_scale)


def core_sum(routes, partial):
    low = partial.astype(jnp.bfloat16)
    far = routes.core(low)
    half = far.shape[0] // 2
    swapped = jnp.concatenate([far[half:], far[:half]], axis=0)
    return low.astype(jnp.float32) + swapped.astype(jnp.float32)


def attend(routes, hidden, weights):
    seq_len = hidden.shape[0]
    query_key = jnp.stack([dot_f32(hidden, w, 1, 0) for w in weights[0]]).astype(jnp.bfloat16)
    value_out = jnp.stack([dot_f32(hidden, w, 1, 0) for w in weights[1]]).astype(jnp.bfloat16)
    width = query_key.shape[2] // 2
    local_heads = width // HEAD_DIM
    query_key = query_key.reshape(2, seq_len, 2 * local_heads, HEAD_DIM)
    query, key = (query_key[:, :, :local_heads], query_key[:, :, local_heads:])
    value = value_out[:, :, :width].reshape(2, seq_len, local_heads, HEAD_DIM)
    scores = jnp.einsum(
        "xqhe,xkhe->xhqk", query, key, preferred_element_type=jnp.float32
    ) * HEAD_DIM ** (-0.5)
    exped = jnp.exp(scores - jnp.max(scores, axis=-1, keepdims=True))
    probs = exped / jnp.sum(exped, axis=-1, keepdims=True)
    attended = jnp.einsum(
        "xhqk,xkhe->xqhe", probs.astype(jnp.bfloat16), value, preferred_element_type=jnp.float32
    )
    attended = attended.astype(jnp.bfloat16).reshape(2, seq_len, width)
    padded = jnp.concatenate([jnp.zeros_like(attended), attended], axis=2)
    partial_out = dot_f32(padded[0], weights[1][0], 1, 1) + dot_f32(padded[1], weights[1][1], 1, 1)
    return (core_sum(routes, partial_out), (hidden, query, key, value, probs, padded))


def attend_backward(routes, grad_full, kept, weights):
    hidden, query, key, value, probs, padded = kept
    seq_len = hidden.shape[0]
    scale = HEAD_DIM ** (-0.5)
    width = padded.shape[2] // 2
    local_heads = width // HEAD_DIM
    grad_attended = jnp.stack([dot_f32(grad_full, w, 1, 0) for w in weights[1]])
    grad_attended = grad_attended[:, :, width:].astype(jnp.bfloat16)
    grad_attended = grad_attended.reshape(2, seq_len, local_heads, HEAD_DIM)
    grad_probs = jnp.einsum(
        "xqhe,xkhe->xhqk", grad_attended, value, preferred_element_type=jnp.float32
    )
    grad_value = jnp.einsum(
        "xhqk,xqhe->xkhe",
        probs.astype(jnp.bfloat16),
        grad_attended,
        preferred_element_type=jnp.float32,
    )
    inner = jnp.sum(probs * grad_probs, axis=-1, keepdims=True)
    grad_scores = (probs * (grad_probs - inner)).astype(jnp.bfloat16)
    grad_query = (
        jnp.einsum("xhqk,xkhe->xqhe", grad_scores, key, preferred_element_type=jnp.float32) * scale
    )
    grad_key = (
        jnp.einsum("xhqk,xqhe->xkhe", grad_scores, query, preferred_element_type=jnp.float32) * scale
    )
    grad_qk = jnp.concatenate([grad_query, grad_key], axis=2).astype(jnp.bfloat16)
    grad_qk = grad_qk.reshape(2, seq_len, 2 * width)
    grad_v = grad_value.astype(jnp.bfloat16).reshape(2, seq_len, width)
    grad_v = jnp.concatenate([grad_v, jnp.zeros_like(grad_v)], axis=2)
    grad_hidden = jnp.zeros(hidden.shape, jnp.float32)
    for k in range(2):
        grad_hidden = grad_hidden + dot_f32(grad_qk[k], weights[0][k], 1, 1)
        grad_hidden = grad_hidden + dot_f32(grad_v[k], weights[1][k], 1, 1)
    grad_hidden = core_sum(routes, grad_hidden)
    qk_own, qk_other = [dot_f32(hidden, grad_qk[k], 0, 0) for k in range(2)]
    both = jnp.concatenate([hidden, grad_full], axis=0)
    vo_own, vo_other = [
        dot_f32(both, jnp.concatenate([grad_v[k], padded[k]], axis=0), 0, 0) for k in range(2)
    ]
    grads = (routes.scatter_both(qk_own, qk_other), routes.scatter_both(vo_own, vo_other))
    return (grad_hidden, grads)


def share_rows(routes, rows):
    half = rows.shape[0] // 2
    far = routes.across(rows[:half])
    return jnp.concatenate([rows, far, routes.core(far)], axis=0)


def sum_rows(routes, partial):
    half = partial.shape[0] // 4
    low = partial.astype(jnp.bfloat16)
    received = routes.core(jnp.concatenate([low[3 * half :], low[half : 2 * half]], axis=0))
    received = received.astype(jnp.float32)
    far_sum = (partial[2 * half : 3 * half] + received[:half]).astype(jnp.bfloat16)
    own_sum = partial[:half] + received[half:]
    own_total = (own_sum + routes.across(far_sum).astype(jnp.float32)).astype(jnp.bfloat16)
    return jnp.concatenate([own_total, routes.core(own_total)], axis=0).astype(jnp.float32)


def feed_forward(routes, hidden, weights):
    rows = share_rows(routes, hidden)
    upward = dot_f32(rows, weights[0], 1, 0)
    active = jax.nn.gelu(upward, approximate=True).astype(jnp.bfloat16)
    output = sum_rows(routes, dot_f32(active, weights[1], 1, 1))
    return (output, (rows, upward, active))


def feed_backward(routes, grad_full, kept, weights):
    rows, upward, active = kept
    grad_rows = share_rows(routes, grad_full)
    grad_active = dot_f32(grad_rows, weights[1], 1, 0)
    slope = jax.vjp(partial(jax.nn.gelu, approximate=True), upward)[1]
    grad_up = slope(grad_active)[0].astype(jnp.bfloat16)
    grad_hidden = sum_rows(routes, dot_f32(grad_up, weights[0], 1, 1))
    grad_down_w = routes.scatter_rows(dot_f32(grad_rows, active, 0, 0))
    grad_up_w = routes.scatter_rows(dot_f32(rows, grad_up, 0, 0))
    return (grad_hidden, (grad_up_w, grad_down_w))


def branch_forward(routes, resid, pieces, inner_fn, weights):
    shift, scale, gate = pieces
    hidden, normed, inverse = modulate(resid, shift, scale)
    output, kept = inner_fn(routes, hidden, weights)
    return (resid + gate * output, (normed, inverse, output, kept))


def branch_backward(routes, grad_resid, pieces, saved, inner_back, weights):
    shift, scale, gate = pieces
    normed, inverse, output, kept = saved
    counted = grad_resid.shape[0] // 2
    grad_gate = jnp.sum(grad_resid[:counted] * output[:counted], axis=0)
    grad_output = (gate * grad_resid).astype(jnp.bfloat16)
    grad_mixed, grads = inner_back(routes, grad_output, kept, weights)
    grad_input, grad_shift, grad_scale = norm_backward(grad_mixed, normed, inverse, scale, counted)
    return (grad_resid + grad_input, [grad_shift, grad_scale, grad_gate], grads)


def gather_weights(routes, attn_weight, mlp_weight):
    shards = []
    for layer in range(LAYERS):
        attn = attn_weight[layer].astype(jnp.bfloat16)
        mlp = mlp_weight[layer].astype(jnp.bfloat16)
        shards.append(
            (
                jnp.concatenate([attn[0], attn[1]], axis=1),
                jnp.concatenate([attn[2], attn[3]], axis=1),
                mlp[0],
                mlp[1],
            )
        )
    gathered = []
    earlier = []

    def in_turn(block):
        return after(block, earlier[-2]) if len(earlier) >= 2 else block

    for layer in range(LAYERS):
        query_key, value_out, up, down = shards[layer]
        pairs = []
        for block, across_last in ((query_key, True), (value_out, layer > 0)):
            both = routes.gather_both(in_turn(block), across_last)
            pairs.append(both)
            earlier.append(both[0])
        rows = []
        for block in (up, down):
            rows.append(routes.gather_rows(in_turn(block)))
            earlier.append(rows[-1])
        gathered.append((tuple(pairs), tuple(rows)))
    return gathered


def adam_update(weight, grad, first, second, count):
    first_new = beta_first * first + (1.0 - beta_first) * grad
    second_new = beta_second * second + (1.0 - beta_second) * grad * grad
    first_hat = first_new / (1.0 - jnp.power(beta_first, count))
    second_hat = second_new / (1.0 - jnp.power(beta_second, count))
    weight_new = weight - learn_rate * (
        first_hat / (jnp.sqrt(second_hat) + adam_eps) + weight_decay * weight
    )
    return [weight_new, first_new, second_new]


def body(
    routes,
    latents,
    noise,
    timesteps,
    labels,
    step_count,
    tables,
    time_weight,
    cond_weight,
    cond_bias,
    attn_weight,
    mlp_weight,
    tables_first,
    tables_second,
    time_first,
    time_second,
    cond_first,
    cond_second,
    bias_first,
    bias_second,
    attn_first,
    attn_second,
    mlp_first,
    mlp_second,
):
    fsdp_index = lax.axis_index("fsdp")
    tp_index = lax.axis_index("tp")
    across_index = tp_index // 2
    num_fsdp = routes.num_fsdp
    local_seq = latents.shape[1]
    col_share = tables.shape[1]
    all_latents = timesteps.shape[0]
    total_entries = all_latents * SEQ * PATCH_DIM
    col_start = fsdp_index * col_share
    low_tables = tables.astype(jnp.bfloat16)

    gathered = gather_weights(routes, attn_weight, mlp_weight)
    head = routes.gather_rows(low_tables[: 2 * PATCH_DIM].T)

    features = timestep_features(timesteps).astype(jnp.bfloat16)
    time_pre = jnp.dot(
        features,
        low_tables[2 * PATCH_DIM : 2 * PATCH_DIM + FREQ],
        preferred_element_type=jnp.float32,
    )
    time_hidden = jax.nn.silu(time_pre).astype(jnp.bfloat16)
    label_hot = (labels[:, None] == jnp.arange(NCLASS, dtype=jnp.int32)[None, :]).astype(
        jnp.bfloat16
    )
    label_part = jnp.dot(
        label_hot, low_tables[2 * PATCH_DIM + FREQ :], preferred_element_type=jnp.float32
    )
    low_time = time_weight.astype(jnp.bfloat16)
    cond_part = jnp.dot(time_hidden, low_time, preferred_element_type=jnp.float32)
    placed = lax.dynamic_update_slice(
        jnp.zeros((all_latents, D), jnp.float32), label_part, (0, col_start)
    )
    cond = routes.sum_fsdp(cond_part + placed)
    cond_act = jax.nn.silu(cond).astype(jnp.bfloat16)
    low_cond = cond_weight.astype(jnp.bfloat16)
    low_bias = cond_bias.astype(jnp.bfloat16).astype(jnp.float32)
    mod_part = dot_f32(cond_act, low_cond, 1, 1) + low_bias[None, :]
    modul = lax.all_to_all(
        mod_part.astype(jnp.bfloat16), "fsdp", split_axis=0, concat_axis=1, tiled=True
    )
    modul = lax.dynamic_slice_in_dim(modul, across_index, 1, 0)

    slots = jnp.arange(num_fsdp, dtype=jnp.int32)
    owners = routes.slot_owner(fsdp_index, slots)
    slot_hot = (owners[:, None] == slots[None, :]).astype(jnp.bfloat16)
    pieces_all = jnp.einsum(
        "pfr,sf->psr",
        modul.reshape(-1, num_fsdp, col_share),
        slot_hot,
        preferred_element_type=jnp.float32,
    ).reshape(-1, D)

    data = jnp.stack([latents, noise], axis=1)
    own_data = lax.dynamic_index_in_dim(data, across_index, 0, keepdims=False)
    far_data = lax.dynamic_index_in_dim(data, 1 - across_index, 0, keepdims=False)
    first_data = jnp.concatenate([own_data, routes.across(far_data)], axis=1)
    chip_data = jnp.concatenate([first_data, routes.core(first_data)], axis=1)
    clean, noise_part = (chip_data[0], chip_data[1])
    chunks = jnp.stack([tp_index, tp_index ^ 2, tp_index ^ 1, tp_index ^ 3])
    token_ids = (
        chunks[:, None] * local_seq + jnp.arange(local_seq, dtype=jnp.int32)[None, :]
    ).reshape(-1)
    counted = token_ids.shape[0] // 2

    quarter = D // 4
    col_ids = (
        owners[:, None] * col_share + jnp.arange(col_share, dtype=jnp.int32)[None, :]
    ).reshape(-1)
    omegas = 1.0 / jnp.power(10000.0, (col_ids % quarter).astype(jnp.float32) / quarter)
    angles = jnp.arange(GRID, dtype=jnp.float32)[:, None] * omegas[None, :]
    kinds = (col_ids // quarter)[None, :]
    waves = jnp.where(kinds % 2 == 0, jnp.sin(angles), jnp.cos(angles))
    row_waves = jnp.where(kinds < 2, waves, 0.0)
    col_waves = jnp.where(kinds >= 2, waves, 0.0)
    grid_ids = jnp.arange(GRID, dtype=jnp.int32)[None, :]
    row_hot = (token_ids[:, None] // GRID == grid_ids).astype(jnp.float32)
    col_hot = (token_ids[:, None] % GRID == grid_ids).astype(jnp.float32)
    positions = jnp.dot(
        jnp.concatenate([row_hot, col_hot], axis=1),
        jnp.concatenate([row_waves, col_waves], axis=0),
        precision=lax.Precision.HIGHEST,
    )

    latent_id = fsdp_index * latents.shape[0] + across_index
    share = signal_share(lax.dynamic_slice_in_dim(timesteps, latent_id, 1))[:, None]
    noisy = (jnp.sqrt(share) * clean + jnp.sqrt(1.0 - share) * noise_part).astype(jnp.bfloat16)
    resid = dot_f32(noisy, head[:, :PATCH_DIM], 1, 1) + positions

    saved = []
    for layer in range(LAYERS):
        pieces = [pieces_all[6 * layer + k][None, :] for k in range(6)]
        attn_w, mlp_w = gathered[layer]
        resid, attn_saved = branch_forward(routes, resid, pieces[:3], attend, attn_w)
        resid, mlp_saved = branch_forward(routes, resid, pieces[3:], feed_forward, mlp_w)
        saved.append((attn_saved, mlp_saved))
    final_shift = pieces_all[6 * LAYERS][None, :]
    final_scale = pieces_all[6 * LAYERS + 1][None, :]
    final_low, final_normed, final_inverse = modulate(resid, final_shift, final_scale)
    predicted = dot_f32(final_low, head[:, PATCH_DIM:], 1, 0)
    difference = predicted - noise_part
    loss_part = jnp.sum(difference[:counted] * difference[:counted])
    grad_pred = (difference * (2.0 / total_entries)).astype(jnp.bfloat16)
    output_grad = dot_f32(final_low[:counted], grad_pred[:counted], 0, 0)
    grad_final = dot_f32(grad_pred, head[:, PATCH_DIM:], 1, 1)
    grad_resid, grad_fshift, grad_fscale = norm_backward(
        grad_final, final_normed, final_inverse, final_scale, counted
    )
    layer_mods = [None] * LAYERS
    layer_grads = [None] * LAYERS
    for layer in reversed(range(LAYERS)):
        pieces = [pieces_all[6 * layer + k][None, :] for k in range(6)]
        attn_w, mlp_w = gathered[layer]
        grad_resid, mlp_mods, mlp_grads = branch_backward(
            routes, grad_resid, pieces[3:], saved[layer][1], feed_backward, mlp_w
        )
        grad_resid, attn_mods, attn_grads = branch_backward(
            routes, grad_resid, pieces[:3], saved[layer][0], attend_backward, attn_w
        )
        layer_mods[layer] = attn_mods + mlp_mods
        layer_grads[layer] = attn_grads + mlp_grads
    grad_embed = grad_resid.astype(jnp.bfloat16)
    patch_grad = dot_f32(grad_embed[:counted], noisy[:counted], 0, 0)

    head_grad = jnp.concatenate([patch_grad, output_grad], axis=1)
    head_grad = head_grad + routes.core(head_grad)
    head_grad = head_grad + routes.across(head_grad)
    head_cols = routes.scatter_rows(head_grad, jnp.float32).T

    modul_grad = jnp.stack(layer_mods[0] + layer_mods[1] + [grad_fshift, grad_fscale])
    modul_grad = (modul_grad + routes.core(modul_grad)).astype(jnp.bfloat16)
    modul_grad = jnp.einsum(
        "psr,sf->pfr",
        modul_grad.reshape(-1, num_fsdp, col_share),
        slot_hot,
        preferred_element_type=jnp.float32,
    ).astype(jnp.bfloat16)
    modul_back = lax.all_to_all(
        modul_grad.reshape(num_fsdp, -1), "fsdp", split_axis=0, concat_axis=0, tiled=True
    )
    far_back = routes.across(modul_back)
    is_first = across_index == 0
    modul_back = jnp.stack(
        [jnp.where(is_first, modul_back, far_back), jnp.where(is_first, far_back, modul_back)],
        axis=1,
    ).reshape(all_latents, -1)
    cond_grad_w = dot_f32(modul_back, cond_act, 0, 0)
    bias_grad = jnp.sum(modul_back.astype(jnp.float32), axis=0)
    grad_cond_act = routes.sum_fsdp(dot_f32(modul_back, low_cond, 1, 0))
    silu_slope = jax.vjp(jax.nn.silu, cond)[1]
    grad_cond = silu_slope(grad_cond_act)[0].astype(jnp.bfloat16)
    time_grad = dot_f32(time_hidden, grad_cond, 0, 0)
    grad_hidden = dot_f32(grad_cond, low_time, 1, 1)
    time_slope = jax.vjp(jax.nn.silu, time_pre)[1]
    grad_pre = time_slope(grad_hidden)[0].astype(jnp.bfloat16)
    first_layer_grad = dot_f32(features, grad_pre, 0, 0)
    cond_cols = lax.dynamic_slice_in_dim(grad_cond, col_start, col_share, 1)
    label_grad = dot_f32(label_hot, cond_cols, 0, 0)
    tables_grad = jnp.concatenate([head_cols, first_layer_grad, label_grad], axis=0)

    squares = sum(jnp.sum(part * part) for parts in layer_grads for part in parts)
    owner = (tp_index == 0).astype(jnp.float32)
    squares = squares + owner * sum(
        jnp.sum(part * part) for part in (tables_grad, time_grad, cond_grad_w, bias_grad)
    )
    totals = routes.sum_all(jnp.stack([loss_part, squares]))
    loss = totals[0] / total_entries
    norm = jnp.sqrt(totals[1])
    entries = NTAB * D + D * D + (D + 1) * NCOND + LAYERS * (4 * D * D + 2 * D * FF)
    limit = clip_scale * math.sqrt(entries / (all_latents * SEQ))
    factor = jnp.minimum(1.0, limit / norm)
    count = step_count[0].astype(jnp.float32)
    width = attn_weight.shape[3]
    attn_grad = jnp.stack(
        [
            jnp.stack([qk[:, :width], qk[:, width:], vo[:, :width], vo[:, width:]])
            for qk, vo, _, _ in layer_grads
        ]
    )
    mlp_grad = jnp.stack([jnp.stack([up, down]) for _, _, up, down in layer_grads])
    weights_all = (tables, time_weight, cond_weight, cond_bias, attn_weight, mlp_weight)
    grads_all = (tables_grad, time_grad, cond_grad_w, bias_grad, attn_grad, mlp_grad)
    states = (
        (tables_first, tables_second),
        (time_first, time_second),
        (cond_first, cond_second),
        (bias_first, bias_second),
        (attn_first, attn_second),
        (mlp_first, mlp_second),
    )
    results = [loss, norm]
    for weight, grad, state in zip(weights_all, grads_all, states):
        results.extend(adam_update(weight, grad * factor, state[0], state[1], count))
    return tuple(results)


def solution(mesh):
    vectors = P("fsdp")
    columns = P(None, "fsdp")
    rows = P("fsdp", None)
    blocks = P(None, None, "fsdp", "tp")
    data = P("fsdp", "tp", None)
    weights = (columns, rows, rows, vectors, blocks, blocks)
    states = tuple(spec for spec in weights for _ in range(2))
    updated = tuple(spec for spec in weights for _ in range(3))
    return jax.shard_map(
        partial(body, Routes(mesh)),
        mesh=mesh,
        in_specs=(data, data, P(), P(), P()) + weights + states,
        out_specs=(P(), P()) + updated,
        check_vma=False,
    )
```

```python
from functools import partial
import math

import jax
import jax.numpy as jnp
from jax import lax
import numpy as np
from jax.experimental import pallas as pl
from jax.experimental.pallas import tpu as pltpu
from jax.sharding import PartitionSpec as P

D = 768
HEAD_DIM = 64
FF = 3072
NCLASS = 1000
FREQ = 256
PATCH_DIM = 16
GRID = 16
LAYERS = 2
SEQ = 256
NCOND = 10752
NTAB = 1288


norm_eps = 1e-06
beta_first = 0.9
beta_second = 0.999
adam_eps = 1e-08
learn_rate = 0.2
weight_decay = 0.01
clip_scale = 0.002
diffusion_steps = 1000.0


def timestep_features(timesteps):
    half_width = FREQ // 2
    omegas = jnp.exp(-math.log(10000.0) * jnp.arange(half_width, dtype=jnp.float32) / half_width)
    angles = timesteps.astype(jnp.float32)[:, None] * omegas[None, :]
    return jnp.concatenate([jnp.cos(angles), jnp.sin(angles)], axis=1)


def signal_share(timesteps):
    phase = (timesteps.astype(jnp.float32) / diffusion_steps + 0.008) / 1.008 * (math.pi / 2)
    return jnp.cos(phase) ** 2


def butterfly_bits(number):
    bits = []
    bit = 1
    while bit < number:
        bits.append(bit)
        bit *= 2
    return bits


def split_radices(number):
    radices = []
    while number > 1:
        radix = 4 if number % 4 == 0 else 2
        radices.append(radix)
        number //= radix
    return radices


class Routes:
    def __init__(self, mesh):
        self.num_fsdp = mesh.shape["fsdp"]
        self.num_tp = mesh.shape["tp"]
        self.outer = split_radices(self.num_fsdp // 2)

    def core(self, value):
        return lax.ppermute(value, "tp", [(t, t ^ 1) for t in range(self.num_tp)])

    def across(self, value):
        return lax.ppermute(value, "tp", [(t, t ^ 2) for t in range(self.num_tp)])

    def pair(self, value):
        return lax.ppermute(value, "fsdp", [(f, f ^ 1) for f in range(self.num_fsdp)])

    def shift(self, value, stride, radix, amount):
        pairs = []
        for f in range(self.num_fsdp):
            digit = (f // stride) % radix
            pairs.append((f, f + ((digit + amount) % radix - digit) * stride))
        return lax.ppermute(value, "fsdp", pairs)

    def slot_owner(self, fsdp_index, slots):
        per_pair = self.num_fsdp // 2
        pair_part = (slots // per_pair + fsdp_index) % 2
        rest = slots % per_pair
        owner = pair_part
        stride = 2
        for radix in self.outer:
            digit = (rest + fsdp_index // stride) % radix
            owner = owner + digit * stride
            rest = rest // radix
            stride *= radix
        return owner

    def gather_outer(self, block):
        stride = 2
        for radix in self.outer:
            block = jnp.concatenate(
                [block] + [self.shift(block, stride, radix, -k) for k in range(1, radix)], axis=0
            )
            stride *= radix
        return block

    def gather_rows(self, block):
        held = self.gather_outer(block)
        return jnp.concatenate([held, self.pair(held)], axis=0)

    def gather_both(self, block, across_last):
        held = self.gather_outer(block)
        if across_last:
            own = jnp.concatenate([held, self.pair(held)], axis=0)
            return (own, self.across(own))
        other = self.across(held)
        return (
            jnp.concatenate([held, self.pair(held)], axis=0),
            jnp.concatenate([other, self.pair(other)], axis=0),
        )

    def scatter_rows(self, total, dtype=jnp.bfloat16):
        half = total.shape[0] // 2
        received = self.pair(total[half:].astype(dtype))
        held = total[:half] + received.astype(jnp.float32)
        strides = []
        stride = 2
        for radix in self.outer:
            strides.append(stride)
            stride *= radix
        for radix, stride in reversed(list(zip(self.outer, strides))):
            size = held.shape[0] // radix
            parts = [
                self.shift(held[k * size : (k + 1) * size].astype(dtype), stride, radix, k)
                for k in range(1, radix)
            ]
            held = held[:size]
            for part in parts:
                held = held + part.astype(jnp.float32)
        return held

    def scatter_both(self, own, other):
        received = self.across(other.astype(jnp.bfloat16))
        return self.scatter_rows(own + received.astype(jnp.float32))

    def sum_fsdp(self, value):
        for bit in butterfly_bits(self.num_fsdp):
            value = value + lax.ppermute(
                value, "fsdp", [(f, f ^ bit) for f in range(self.num_fsdp)]
            )
        return value

    def sum_all(self, value):
        value = value + self.core(value)
        value = value + self.across(value)
        return self.sum_fsdp(value)


def after(value, *earlier):
    return lax.optimization_barrier((value,) + earlier)[0]


def dot_f32(left, right, left_dim, right_dim):
    return lax.dot_general(
        left, right, (((left_dim,), (right_dim,)), ((), ())), preferred_element_type=jnp.float32
    )


def layer_norm(values):
    centred = values - jnp.mean(values, axis=-1, keepdims=True)
    inverse = lax.rsqrt(jnp.mean(centred * centred, axis=-1, keepdims=True) + norm_eps)
    return (centred * inverse, inverse)


def modulate(values, shift, scale):
    normed, inverse = layer_norm(values)
    return ((normed * (1.0 + scale) + shift).astype(jnp.bfloat16), normed, inverse)


def norm_backward(grad_mixed, normed, inverse, scale, counted):
    grad_shift = jnp.sum(grad_mixed[:counted], axis=0)
    grad_scale = jnp.sum(grad_mixed[:counted] * normed[:counted], axis=0)
    grad_normed = grad_mixed * (1.0 + scale)
    centred = grad_normed - jnp.mean(grad_normed, axis=-1, keepdims=True)
    grad_input = (
        centred - normed * jnp.mean(grad_normed * normed, axis=-1, keepdims=True)
    ) * inverse
    return (grad_input, grad_shift, grad_scale)


def core_sum(routes, partial):
    low = partial.astype(jnp.bfloat16)
    far = routes.core(low)
    half = far.shape[0] // 2
    swapped = jnp.concatenate([far[half:], far[:half]], axis=0)
    return low.astype(jnp.float32) + swapped.astype(jnp.float32)


def attend(routes, hidden, weights):
    seq_len = hidden.shape[0]
    query_key = jnp.stack([dot_f32(hidden, w, 1, 0) for w in weights[0]]).astype(jnp.bfloat16)
    value_out = jnp.stack([dot_f32(hidden, w, 1, 0) for w in weights[1]]).astype(jnp.bfloat16)
    width = query_key.shape[2] // 2
    local_heads = width // HEAD_DIM
    query_key = query_key.reshape(2, seq_len, 2 * local_heads, HEAD_DIM)
    query, key = (query_key[:, :, :local_heads], query_key[:, :, local_heads:])
    value = value_out[:, :, :width].reshape(2, seq_len, local_heads, HEAD_DIM)
    scores = jnp.einsum(
        "xqhe,xkhe->xhqk", query, key, preferred_element_type=jnp.float32
    ) * HEAD_DIM ** (-0.5)
    exped = jnp.exp(scores - jnp.max(scores, axis=-1, keepdims=True))
    probs = exped / jnp.sum(exped, axis=-1, keepdims=True)
    attended = jnp.einsum(
        "xhqk,xkhe->xqhe", probs.astype(jnp.bfloat16), value, preferred_element_type=jnp.float32
    )
    attended = attended.astype(jnp.bfloat16).reshape(2, seq_len, width)
    padded = jnp.concatenate([jnp.zeros_like(attended), attended], axis=2)
    partial_out = dot_f32(padded[0], weights[1][0], 1, 1) + dot_f32(padded[1], weights[1][1], 1, 1)
    return (core_sum(routes, partial_out), (hidden, query, key, value, probs, padded))


def attend_backward(routes, grad_full, kept, weights):
    hidden, query, key, value, probs, padded = kept
    seq_len = hidden.shape[0]
    scale = HEAD_DIM ** (-0.5)
    width = padded.shape[2] // 2
    local_heads = width // HEAD_DIM
    grad_attended = jnp.stack([dot_f32(grad_full, w, 1, 0) for w in weights[1]])
    grad_attended = grad_attended[:, :, width:].astype(jnp.bfloat16)
    grad_attended = grad_attended.reshape(2, seq_len, local_heads, HEAD_DIM)
    grad_probs = jnp.einsum(
        "xqhe,xkhe->xhqk", grad_attended, value, preferred_element_type=jnp.float32
    )
    grad_value = jnp.einsum(
        "xhqk,xqhe->xkhe",
        probs.astype(jnp.bfloat16),
        grad_attended,
        preferred_element_type=jnp.float32,
    )
    inner = jnp.sum(probs * grad_probs, axis=-1, keepdims=True)
    grad_scores = (probs * (grad_probs - inner)).astype(jnp.bfloat16)
    grad_query = (
        jnp.einsum("xhqk,xkhe->xqhe", grad_scores, key, preferred_element_type=jnp.float32) * scale
    )
    grad_key = (
        jnp.einsum("xhqk,xqhe->xkhe", grad_scores, query, preferred_element_type=jnp.float32) * scale
    )
    grad_qk = jnp.concatenate([grad_query, grad_key], axis=2).astype(jnp.bfloat16)
    grad_qk = grad_qk.reshape(2, seq_len, 2 * width)
    grad_v = grad_value.astype(jnp.bfloat16).reshape(2, seq_len, width)
    grad_v = jnp.concatenate([grad_v, jnp.zeros_like(grad_v)], axis=2)
    grad_hidden = jnp.zeros(hidden.shape, jnp.float32)
    for k in range(2):
        grad_hidden = grad_hidden + dot_f32(grad_qk[k], weights[0][k], 1, 1)
        grad_hidden = grad_hidden + dot_f32(grad_v[k], weights[1][k], 1, 1)
    grad_hidden = core_sum(routes, grad_hidden)
    qk_own, qk_other = [dot_f32(hidden, grad_qk[k], 0, 0) for k in range(2)]
    both = jnp.concatenate([hidden, grad_full], axis=0)
    vo_own, vo_other = [
        dot_f32(both, jnp.concatenate([grad_v[k], padded[k]], axis=0), 0, 0) for k in range(2)
    ]
    grads = (routes.scatter_both(qk_own, qk_other), routes.scatter_both(vo_own, vo_other))
    return (grad_hidden, grads)


def share_rows(routes, rows):
    half = rows.shape[0] // 2
    far = routes.across(rows[:half])
    return jnp.concatenate([rows, far, routes.core(far)], axis=0)


def sum_rows(routes, partial):
    half = partial.shape[0] // 4
    low = partial.astype(jnp.bfloat16)
    received = routes.core(jnp.concatenate([low[3 * half :], low[half : 2 * half]], axis=0))
    received = received.astype(jnp.float32)
    far_sum = (partial[2 * half : 3 * half] + received[:half]).astype(jnp.bfloat16)
    own_sum = partial[:half] + received[half:]
    own_total = (own_sum + routes.across(far_sum).astype(jnp.float32)).astype(jnp.bfloat16)
    return jnp.concatenate([own_total, routes.core(own_total)], axis=0).astype(jnp.float32)


def feed_forward(routes, hidden, weights):
    rows = share_rows(routes, hidden)
    upward = dot_f32(rows, weights[0], 1, 0)
    active = jax.nn.gelu(upward, approximate=True).astype(jnp.bfloat16)
    output = sum_rows(routes, dot_f32(active, weights[1], 1, 1))
    return (output, (rows, upward, active))


def feed_backward(routes, grad_full, kept, weights):
    rows, upward, active = kept
    grad_rows = share_rows(routes, grad_full)
    grad_active = dot_f32(grad_rows, weights[1], 1, 0)
    slope = jax.vjp(partial(jax.nn.gelu, approximate=True), upward)[1]
    grad_up = slope(grad_active)[0].astype(jnp.bfloat16)
    grad_hidden = sum_rows(routes, dot_f32(grad_up, weights[0], 1, 1))
    grad_down_w = routes.scatter_rows(dot_f32(grad_rows, active, 0, 0))
    grad_up_w = routes.scatter_rows(dot_f32(rows, grad_up, 0, 0))
    return (grad_hidden, (grad_up_w, grad_down_w))


def branch_forward(routes, resid, pieces, inner_fn, weights):
    shift, scale, gate = pieces
    hidden, normed, inverse = modulate(resid, shift, scale)
    output, kept = inner_fn(routes, hidden, weights)
    return (resid + gate * output, (normed, inverse, output, kept))


def branch_backward(routes, grad_resid, pieces, saved, inner_back, weights):
    shift, scale, gate = pieces
    normed, inverse, output, kept = saved
    counted = grad_resid.shape[0] // 2
    grad_gate = jnp.sum(grad_resid[:counted] * output[:counted], axis=0)
    grad_output = (gate * grad_resid).astype(jnp.bfloat16)
    grad_mixed, grads = inner_back(routes, grad_output, kept, weights)
    grad_input, grad_shift, grad_scale = norm_backward(grad_mixed, normed, inverse, scale, counted)
    return (grad_resid + grad_input, [grad_shift, grad_scale, grad_gate], grads)


def gather_weights(routes, attn_weight, mlp_weight):
    shards = []
    for layer in range(LAYERS):
        attn = attn_weight[layer].astype(jnp.bfloat16)
        mlp = mlp_weight[layer].astype(jnp.bfloat16)
        shards.append(
            (
                jnp.concatenate([attn[0], attn[1]], axis=1),
                jnp.concatenate([attn[2], attn[3]], axis=1),
                mlp[0],
                mlp[1],
            )
        )
    gathered = []
    earlier = []

    def in_turn(block):
        return after(block, earlier[-2]) if len(earlier) >= 2 else block

    for layer in range(LAYERS):
        query_key, value_out, up, down = shards[layer]
        pairs = []
        for block, across_last in ((query_key, True), (value_out, layer > 0)):
            both = routes.gather_both(in_turn(block), across_last)
            pairs.append(both)
            earlier.append(both[0])
        rows = []
        for block in (up, down):
            rows.append(routes.gather_rows(in_turn(block)))
            earlier.append(rows[-1])
        gathered.append((tuple(pairs), tuple(rows)))
    return gathered


def adam_update(weight, grad, first, second, count):
    first_new = beta_first * first + (1.0 - beta_first) * grad
    second_new = beta_second * second + (1.0 - beta_second) * grad * grad
    first_hat = first_new / (1.0 - jnp.power(beta_first, count))
    second_hat = second_new / (1.0 - jnp.power(beta_second, count))
    weight_new = weight - learn_rate * (
        first_hat / (jnp.sqrt(second_hat) + adam_eps) + weight_decay * weight
    )
    return [weight_new, first_new, second_new]


def body_steps(
    routes,
    latents,
    noise,
    timesteps,
    labels,
    step_count,
    tables,
    time_weight,
    cond_weight,
    cond_bias,
    attn_weight,
    mlp_weight,
    tables_first,
    tables_second,
    time_first,
    time_second,
    cond_first,
    cond_second,
    bias_first,
    bias_second,
    attn_first,
    attn_second,
    mlp_first,
    mlp_second,
):
    fsdp_index = lax.axis_index("fsdp")
    tp_index = lax.axis_index("tp")
    across_index = tp_index // 2
    num_fsdp = routes.num_fsdp
    local_seq = latents.shape[1]
    col_share = tables.shape[1]
    all_latents = timesteps.shape[0]
    total_entries = all_latents * SEQ * PATCH_DIM
    col_start = fsdp_index * col_share
    low_tables = tables.astype(jnp.bfloat16)

    gathered = gather_weights(routes, attn_weight, mlp_weight)
    head = routes.gather_rows(low_tables[: 2 * PATCH_DIM].T)

    features = timestep_features(timesteps).astype(jnp.bfloat16)
    time_pre = jnp.dot(
        features,
        low_tables[2 * PATCH_DIM : 2 * PATCH_DIM + FREQ],
        preferred_element_type=jnp.float32,
    )
    time_hidden = jax.nn.silu(time_pre).astype(jnp.bfloat16)
    label_hot = (labels[:, None] == jnp.arange(NCLASS, dtype=jnp.int32)[None, :]).astype(
        jnp.bfloat16
    )
    label_part = jnp.dot(
        label_hot, low_tables[2 * PATCH_DIM + FREQ :], preferred_element_type=jnp.float32
    )
    low_time = time_weight.astype(jnp.bfloat16)
    cond_part = jnp.dot(time_hidden, low_time, preferred_element_type=jnp.float32)
    placed = lax.dynamic_update_slice(
        jnp.zeros((all_latents, D), jnp.float32), label_part, (0, col_start)
    )
    cond = routes.sum_fsdp(cond_part + placed)
    cond_act = jax.nn.silu(cond).astype(jnp.bfloat16)
    low_cond = cond_weight.astype(jnp.bfloat16)
    low_bias = cond_bias.astype(jnp.bfloat16).astype(jnp.float32)
    mod_part = dot_f32(cond_act, low_cond, 1, 1) + low_bias[None, :]
    modul = lax.all_to_all(
        mod_part.astype(jnp.bfloat16), "fsdp", split_axis=0, concat_axis=1, tiled=True
    )
    modul = lax.dynamic_slice_in_dim(modul, across_index, 1, 0)

    slots = jnp.arange(num_fsdp, dtype=jnp.int32)
    owners = routes.slot_owner(fsdp_index, slots)
    slot_hot = (owners[:, None] == slots[None, :]).astype(jnp.bfloat16)
    pieces_all = jnp.einsum(
        "pfr,sf->psr",
        modul.reshape(-1, num_fsdp, col_share),
        slot_hot,
        preferred_element_type=jnp.float32,
    ).reshape(-1, D)

    data = jnp.stack([latents, noise], axis=1)
    own_data = lax.dynamic_index_in_dim(data, across_index, 0, keepdims=False)
    far_data = lax.dynamic_index_in_dim(data, 1 - across_index, 0, keepdims=False)
    first_data = jnp.concatenate([own_data, routes.across(far_data)], axis=1)
    chip_data = jnp.concatenate([first_data, routes.core(first_data)], axis=1)
    clean, noise_part = (chip_data[0], chip_data[1])
    chunks = jnp.stack([tp_index, tp_index ^ 2, tp_index ^ 1, tp_index ^ 3])
    token_ids = (
        chunks[:, None] * local_seq + jnp.arange(local_seq, dtype=jnp.int32)[None, :]
    ).reshape(-1)
    counted = token_ids.shape[0] // 2

    quarter = D // 4
    col_ids = (
        owners[:, None] * col_share + jnp.arange(col_share, dtype=jnp.int32)[None, :]
    ).reshape(-1)
    omegas = 1.0 / jnp.power(10000.0, (col_ids % quarter).astype(jnp.float32) / quarter)
    angles = jnp.arange(GRID, dtype=jnp.float32)[:, None] * omegas[None, :]
    kinds = (col_ids // quarter)[None, :]
    waves = jnp.where(kinds % 2 == 0, jnp.sin(angles), jnp.cos(angles))
    row_waves = jnp.where(kinds < 2, waves, 0.0)
    col_waves = jnp.where(kinds >= 2, waves, 0.0)
    grid_ids = jnp.arange(GRID, dtype=jnp.int32)[None, :]
    row_hot = (token_ids[:, None] // GRID == grid_ids).astype(jnp.float32)
    col_hot = (token_ids[:, None] % GRID == grid_ids).astype(jnp.float32)
    positions = jnp.dot(
        jnp.concatenate([row_hot, col_hot], axis=1),
        jnp.concatenate([row_waves, col_waves], axis=0),
        precision=lax.Precision.HIGHEST,
    )

    latent_id = fsdp_index * latents.shape[0] + across_index
    share = signal_share(lax.dynamic_slice_in_dim(timesteps, latent_id, 1))[:, None]
    noisy = (jnp.sqrt(share) * clean + jnp.sqrt(1.0 - share) * noise_part).astype(jnp.bfloat16)
    resid = dot_f32(noisy, head[:, :PATCH_DIM], 1, 1) + positions

    saved = []
    for layer in range(LAYERS):
        pieces = [pieces_all[6 * layer + k][None, :] for k in range(6)]
        attn_w, mlp_w = gathered[layer]
        resid, attn_saved = branch_forward(routes, resid, pieces[:3], attend, attn_w)
        resid, mlp_saved = branch_forward(routes, resid, pieces[3:], feed_forward, mlp_w)
        saved.append((attn_saved, mlp_saved))
    final_shift = pieces_all[6 * LAYERS][None, :]
    final_scale = pieces_all[6 * LAYERS + 1][None, :]
    final_low, final_normed, final_inverse = modulate(resid, final_shift, final_scale)
    predicted = dot_f32(final_low, head[:, PATCH_DIM:], 1, 0)
    difference = predicted - noise_part
    loss_part = jnp.sum(difference[:counted] * difference[:counted])
    grad_pred = (difference * (2.0 / total_entries)).astype(jnp.bfloat16)
    output_grad = dot_f32(final_low[:counted], grad_pred[:counted], 0, 0)
    grad_final = dot_f32(grad_pred, head[:, PATCH_DIM:], 1, 1)
    grad_resid, grad_fshift, grad_fscale = norm_backward(
        grad_final, final_normed, final_inverse, final_scale, counted
    )
    layer_mods = [None] * LAYERS
    layer_grads = [None] * LAYERS
    for layer in reversed(range(LAYERS)):
        pieces = [pieces_all[6 * layer + k][None, :] for k in range(6)]
        attn_w, mlp_w = gathered[layer]
        grad_resid, mlp_mods, mlp_grads = branch_backward(
            routes, grad_resid, pieces[3:], saved[layer][1], feed_backward, mlp_w
        )
        grad_resid, attn_mods, attn_grads = branch_backward(
            routes, grad_resid, pieces[:3], saved[layer][0], attend_backward, attn_w
        )
        layer_mods[layer] = attn_mods + mlp_mods
        layer_grads[layer] = attn_grads + mlp_grads
    grad_embed = grad_resid.astype(jnp.bfloat16)
    patch_grad = dot_f32(grad_embed[:counted], noisy[:counted], 0, 0)

    head_grad = jnp.concatenate([patch_grad, output_grad], axis=1)
    head_grad = head_grad + routes.core(head_grad)
    head_grad = head_grad + routes.across(head_grad)
    head_cols = routes.scatter_rows(head_grad, jnp.float32).T

    modul_grad = jnp.stack(layer_mods[0] + layer_mods[1] + [grad_fshift, grad_fscale])
    modul_grad = (modul_grad + routes.core(modul_grad)).astype(jnp.bfloat16)
    modul_grad = jnp.einsum(
        "psr,sf->pfr",
        modul_grad.reshape(-1, num_fsdp, col_share),
        slot_hot,
        preferred_element_type=jnp.float32,
    ).astype(jnp.bfloat16)
    modul_back = lax.all_to_all(
        modul_grad.reshape(num_fsdp, -1), "fsdp", split_axis=0, concat_axis=0, tiled=True
    )
    far_back = routes.across(modul_back)
    is_first = across_index == 0
    modul_back = jnp.stack(
        [jnp.where(is_first, modul_back, far_back), jnp.where(is_first, far_back, modul_back)],
        axis=1,
    ).reshape(all_latents, -1)
    cond_grad_w = dot_f32(modul_back, cond_act, 0, 0)
    bias_grad = jnp.sum(modul_back.astype(jnp.float32), axis=0)
    grad_cond_act = routes.sum_fsdp(dot_f32(modul_back, low_cond, 1, 0))
    silu_slope = jax.vjp(jax.nn.silu, cond)[1]
    grad_cond = silu_slope(grad_cond_act)[0].astype(jnp.bfloat16)
    time_grad = dot_f32(time_hidden, grad_cond, 0, 0)
    grad_hidden = dot_f32(grad_cond, low_time, 1, 1)
    time_slope = jax.vjp(jax.nn.silu, time_pre)[1]
    grad_pre = time_slope(grad_hidden)[0].astype(jnp.bfloat16)
    first_layer_grad = dot_f32(features, grad_pre, 0, 0)
    cond_cols = lax.dynamic_slice_in_dim(grad_cond, col_start, col_share, 1)
    label_grad = dot_f32(label_hot, cond_cols, 0, 0)
    tables_grad = jnp.concatenate([head_cols, first_layer_grad, label_grad], axis=0)

    squares = sum(jnp.sum(part * part) for parts in layer_grads for part in parts)
    owner = (tp_index == 0).astype(jnp.float32)
    squares = squares + owner * sum(
        jnp.sum(part * part) for part in (tables_grad, time_grad, cond_grad_w, bias_grad)
    )
    totals = routes.sum_all(jnp.stack([loss_part, squares]))
    loss = totals[0] / total_entries
    norm = jnp.sqrt(totals[1])
    entries = NTAB * D + D * D + (D + 1) * NCOND + LAYERS * (4 * D * D + 2 * D * FF)
    limit = clip_scale * math.sqrt(entries / (all_latents * SEQ))
    factor = jnp.minimum(1.0, limit / norm)
    count = step_count[0].astype(jnp.float32)
    width = attn_weight.shape[3]
    attn_grad = jnp.stack(
        [
            jnp.stack([qk[:, :width], qk[:, width:], vo[:, :width], vo[:, width:]])
            for qk, vo, _, _ in layer_grads
        ]
    )
    mlp_grad = jnp.stack([jnp.stack([up, down]) for _, _, up, down in layer_grads])
    weights_all = (tables, time_weight, cond_weight, cond_bias, attn_weight, mlp_weight)
    grads_all = (tables_grad, time_grad, cond_grad_w, bias_grad, attn_grad, mlp_grad)
    states = (
        (tables_first, tables_second),
        (time_first, time_second),
        (cond_first, cond_second),
        (bias_first, bias_second),
        (attn_first, attn_second),
        (mlp_first, mlp_second),
    )
    results = [loss, norm]
    for weight, grad, state in zip(weights_all, grads_all, states):
        results.extend(adam_update(weight, grad * factor, state[0], state[1], count))
    return tuple(results)


MESH = pl.DeviceIdType.MESH
VMEM_LIMIT = 60 * 1024 * 1024
LANES = 128
HALF = 128
TOKENS = 256


class Place:
    def __init__(self):
        self.f = lax.axis_index("fsdp")
        self.t = lax.axis_index("tp")
        self.z = self.f // 2
        self.y = lax.rem(self.f, 2)
        self.core = (self.f, self.t + 1 - 2 * lax.rem(self.t, 2))
        self.across = (self.f, lax.rem(self.t + 2, 4))
        self.diagonal = (self.f, 3 - self.t)
        self.pair = (self.f + 1 - 2 * self.y, self.t)

    def down_z(self, k):
        return (lax.rem(self.z + 4 - k, 4) * 2 + self.y, self.t)

    def up_z(self, k):
        return (lax.rem(self.z + k, 4) * 2 + self.y, self.t)

    def up_f(self, k):
        return (lax.rem(self.f + k, 8), self.t)

    def slot_of(self, owner):
        pair_part = lax.rem(self.y + owner % 2, 2)
        return pair_part * 4 + lax.rem(owner // 2 + 4 - self.z, 4)


class Mail:
    def __init__(self, send_sem, recv_sem, local_sem):
        self.send_sem, self.recv_sem, self.local_sem = (send_sem, recv_sem, local_sem)
        self.sent = []
        self.local = []

    def send(self, source, target, device):
        index = len(self.sent)
        copy = pltpu.make_async_remote_copy(
            src_ref=source,
            dst_ref=target,
            send_sem=self.send_sem.at[index],
            recv_sem=self.recv_sem.at[index],
            device_id=device,
            device_id_type=MESH,
        )
        copy.start()
        self.sent.append(copy)
        return copy

    def move(self, source, target):
        copy = pltpu.make_async_copy(source, target, self.local_sem.at[len(self.local)])
        copy.start()
        self.local.append(copy)
        return copy

    def finish(self, skip=()):
        for copy in self.sent:
            copy.wait_send()
        for copy in self.local:
            if not any(copy is other for other in skip):
                copy.wait()


def greet(place):
    barrier = pltpu.get_barrier_semaphore()
    friends = [place.up_f(k) for k in range(1, 8)]
    friends += [place.core, place.across, place.diagonal]
    for device in friends:
        pl.semaphore_signal(barrier, inc=1, device_id=device, device_id_type=MESH)
    pl.semaphore_wait(barrier, len(friends))


def mm(left, right):
    return lax.dot_general(left, right, (((1,), (0,)), ((), ())), preferred_element_type=jnp.float32)


def mm_nt(left, right):
    return lax.dot_general(left, right, (((1,), (1,)), ((), ())), preferred_element_type=jnp.float32)


def mm_tn(left, right):
    return lax.dot_general(left, right, (((0,), (0,)), ((), ())), preferred_element_type=jnp.float32)


class Gather:
    def __init__(self, place, mail, shard, own, other=None):
        self.place, self.mail, self.shard, self.own, self.other = (place, mail, shard, own, other)
        self.rows = shard.shape[0]

    def at(self, ref, slot):
        return ref.at[pl.ds(slot * self.rows, self.rows)]

    def start(self):
        place, mail = (self.place, self.mail)
        self.kept = mail.move(self.shard, self.at(self.own, 0))
        self.from_z = [
            mail.send(self.shard, self.at(self.own, k), place.down_z(k)) for k in range(1, 4)
        ]
        self.from_y = [mail.send(self.shard, self.at(self.own, 4), place.pair)]
        self.from_x = []
        if self.other is not None:
            self.from_x.append(mail.send(self.shard, self.at(self.other, 0), place.across))

    def pass_z(self):
        for k in range(1, 4):
            self.from_z[k - 1].wait_recv()
            block = self.at(self.own, k)
            self.from_y.append(self.mail.send(block, self.at(self.own, 4 + k), self.place.pair))
            if self.other is not None:
                self.from_x.append(self.mail.send(block, self.at(self.other, k), self.place.across))

    def pass_y(self):
        for k in range(4):
            self.from_y[k].wait_recv()
            if self.other is not None:
                block = self.at(self.own, 4 + k)
                target = self.at(self.other, 4 + k)
                self.from_x.append(self.mail.send(block, target, self.place.across))

    def pass_x(self):
        for copy in self.from_x:
            copy.wait_recv()
        self.kept.wait()


def gelu_parts(value):
    inner = math.sqrt(2.0 / math.pi) * (value + 0.044715 * (value * value * value))
    return 0.5 * (1.0 + jnp.tanh(inner))


def half_mask(rows, upper):
    lanes = lax.broadcasted_iota(jnp.int32, (rows, LANES), 1)
    return lanes >= 64 if upper else lanes < 64


def forward_kernel(shapes, total_entries, *refs):
    names = list(shapes)
    r = dict(zip(names, refs))
    rest = refs[len(names) :]
    outs = dict(zip(FORWARD_OUTS, rest))
    rest = rest[len(FORWARD_OUTS) :]
    s = dict(zip(FORWARD_SCRATCH, rest))
    rest = rest[len(FORWARD_SCRATCH) :]
    mail = Mail(*rest)
    place = Place()
    greet(place)

    def out(name, source, index=None):
        target = outs[name] if index is None else outs[name].at[index]
        mail.move(source, target)

    attn = [
        Gather(place, mail, r["shards"].at[l, 0], s["wattn"].at[l, 0], s["wattn"].at[l, 1])
        for l in range(LAYERS)
    ]
    up = [Gather(place, mail, r["shards"].at[l, 1], s["wmlp"].at[l, 0]) for l in range(LAYERS)]
    down = [Gather(place, mail, r["shards"].at[l, 2], s["wmlp"].at[l, 1]) for l in range(LAYERS)]

    cond_from = [
        mail.send(r["cond_part"], s["cond_in"].at[k - 1], place.up_f(k)) for k in range(1, 8)
    ]
    attn[0].start()
    across_index = place.t // 2
    own_data = r["data"].at[across_index]
    far_data = r["data"].at[1 - across_index]
    data_from = [
        mail.send(far_data, s["data_in"].at[1], place.across),
        mail.send(own_data, s["data_in"].at[2], place.core),
        mail.send(far_data, s["data_in"].at[3], place.diagonal),
    ]
    head_rows = r["head"].shape[0]
    head_kept = mail.move(r["head"], s["head"].at[pl.ds(0, head_rows)])
    data_kept = mail.move(own_data, s["data_in"].at[0])
    head_from = [
        mail.send(r["head"], s["head"].at[pl.ds(k * head_rows, head_rows)], place.down_z(k))
        for k in range(1, 4)
    ]

    rows_id = lax.broadcasted_iota(jnp.int32, (LANES, D), 0)
    offset = lax.broadcasted_iota(jnp.int32, (LANES, D), 1) - rows_id
    for owner in range(8):
        hit = (offset == place.slot_of(owner) * head_rows) & (rows_id < head_rows)
        s["order"][pl.ds(owner * LANES, LANES), :] = jnp.where(hit, 1.0, 0.0).astype(jnp.bfloat16)

    waves = mm(r["waves"][...], s["order"][...])
    s["waves"][...] = waves[0:32] + waves[32:64] + waves[64:96]

    cond = r["cond_part"][...]
    for k in range(7):
        cond_from[k].wait_recv()
        cond = cond + s["cond_in"][k]
    s["cond"][...] = cond
    out("cond", s["cond"])
    cond_act = (cond * jax.nn.sigmoid(cond)).astype(jnp.bfloat16)
    blocks = r["cond_weight"].shape[0]
    all_latents = cond.shape[0]
    for b in range(blocks):
        part = mm_nt(cond_act, r["cond_weight"][b]) + r["cond_bias"][b : b + 1, :]
        part = part.astype(jnp.bfloat16).astype(jnp.float32)
        for i in range(all_latents):
            s["mod_out"][i, b : b + 1, 0:head_rows] = part[i : i + 1, :]
    mod_from = []
    for k in range(1, 8):
        target_f = lax.rem(place.f + k, 8)
        source = s["mod_out"].at[target_f * 2 + across_index]
        mod_from.append(mail.send(source, s["mod_in"].at[k], place.up_f(k)))
    mod_kept = mail.move(s["mod_out"].at[place.f * 2 + across_index], s["mod_in"].at[0])
    attn[1].start()

    for k in range(3):
        head_from[k].wait_recv()
    head_kept.wait()
    lower = s["head"].at[pl.ds(0, 4 * head_rows)]
    upper = s["head"].at[pl.ds(4 * head_rows, 4 * head_rows)]
    head_pair = mail.send(lower, upper, place.pair)
    attn[0].pass_z()

    mod_kept.wait()
    for copy in mod_from:
        copy.wait_recv()
    s["mod_rows"][...] = jnp.zeros_like(s["mod_rows"])
    for g in range(8 * blocks):
        piece, owner = (g // 8, g % 8)
        k = lax.rem(place.f + 8 - g // blocks, 8)
        b = g % blocks
        s["mod_rows"][piece : piece + 1, owner * LANES : owner * LANES + head_rows] = s["mod_in"][
            k, b : b + 1, 0:head_rows
        ]
    s["pieces"][...] = mm(s["mod_rows"][...].astype(jnp.bfloat16), s["order"][...])
    out("pieces", s["pieces"])

    data_kept.wait()
    for copy in data_from:
        copy.wait_recv()
    head_pair.wait_recv()
    out("head", s["head"])
    chunk_rows = s["data_in"].shape[1] // 2
    grid_rows = chunk_rows // GRID
    cols = s["waves"][16:32, :]
    chunk_ids = [place.t, place.across[1], place.core[1], place.diagonal[1]]
    for j in range(4):
        low = pl.ds(j * chunk_rows, chunk_rows)
        s["noisy"][low, :] = s["data_in"][j, 0:chunk_rows, :].astype(jnp.bfloat16)
        s["noise"][low, :] = s["data_in"][j, chunk_rows : 2 * chunk_rows, :]
        for i in range(grid_rows):
            row = s["waves"][pl.ds(chunk_ids[j] * grid_rows + i, 1), :]
            s["resid"][pl.ds(j * chunk_rows + i * GRID, GRID), :] = cols + row
    out("noisy", s["noisy"])
    for n in range(0, D, 256):
        s["resid"][:, n : n + 256] += mm_nt(s["noisy"][...], s["head"][n : n + 256, :])

    def piece(index):
        return s["pieces"][index : index + 1, :]

    def normalize(which, shift, scale, target, low):
        value = s["resid"][low : low + HALF, :]
        centred = value - jnp.mean(value, axis=-1, keepdims=True)
        inverse = lax.rsqrt(jnp.mean(centred * centred, axis=-1, keepdims=True) + norm_eps)
        normed = centred * inverse
        s["normed"][which, low : low + HALF, :] = normed
        s["inverse"][which, low : low + HALF, :] = jnp.broadcast_to(inverse, (HALF, LANES))
        target[low : low + HALF, :] = (normed * (1.0 + scale) + shift).astype(jnp.bfloat16)

    low_mask = half_mask(TOKENS, False)
    high_mask = half_mask(TOKENS, True)
    for l in range(LAYERS):
        base = 6 * l
        hidden = s["hidden"].at[l]
        for low in (0, HALF):
            normalize(2 * l, piece(base), piece(base + 1), hidden, low)
        if l == 0:
            attn[0].pass_y()
            attn[1].pass_z()
            up[0].start()
        attn[l].pass_x()
        for x in range(2):
            weight = s["wattn"].at[l, x]
            qkv = s["qkv"].at[l, x]
            for n in range(0, D, 256):
                qkv[:, n : n + 256] = mm(hidden[...], weight[:, n : n + 256]).astype(jnp.bfloat16)
        if l == 0:
            up[0].pass_z()
            down[0].start()
        for x in range(2):
            qkv = s["qkv"].at[l, x]
            att = s["att"].at[l, x]
            for h, (q, k, v, keep) in enumerate(
                ((0, 1, 2, low_mask), (0, 1, 2, high_mask), (3, 4, 5, low_mask))
            ):
                query = qkv[:, q * LANES : (q + 1) * LANES].astype(jnp.float32)
                query = jnp.where(keep, query, 0.0)
                key = qkv[:, k * LANES : (k + 1) * LANES]
                value = qkv[:, v * LANES : (v + 1) * LANES]
                scores = mm_nt(query.astype(jnp.bfloat16), key) * HEAD_DIM ** (-0.5)
                exped = jnp.exp(scores - jnp.max(scores, axis=-1, keepdims=True))
                probs = exped / jnp.sum(exped, axis=-1, keepdims=True)
                s["probs"][l, x, h] = probs
                mixed = mm(probs.astype(jnp.bfloat16), value)
                if h != 1:
                    mixed = pltpu.roll(mixed, 64, 1)
                att[:, h * LANES : (h + 1) * LANES] = jnp.where(high_mask, mixed, 0.0).astype(
                    jnp.bfloat16
                )
        for n in range(0, D, 256):
            total = mm_nt(s["att"][l, 0], s["wattn"][l, 0, n : n + 256, 384:768])
            total = total + mm_nt(s["att"][l, 1], s["wattn"][l, 1, n : n + 256, 384:768])
            s["core_out"][l, :, n : n + 256] = total.astype(jnp.bfloat16)
        summed = mail.send(s["core_out"].at[l], s["core_in"].at[l], place.core)
        if l == 0:
            attn[1].pass_y()
        gate = piece(base + 2)
        summed.wait_recv()
        for low in (0, HALF):
            output = s["core_out"][l, low : low + HALF, :].astype(jnp.float32)
            output = output + s["core_in"][l, HALF - low : 2 * HALF - low, :].astype(jnp.float32)
            s["attn_out"][l, low : low + HALF, :] = output
            s["resid"][low : low + HALF, :] += gate * output
        rows = s["rows"].at[l]
        normalize(2 * l + 1, piece(base + 3), piece(base + 4), rows, 0)
        far = mail.send(rows.at[pl.ds(0, HALF)], rows.at[pl.ds(2 * HALF, HALF)], place.across)
        normalize(2 * l + 1, piece(base + 3), piece(base + 4), rows, HALF)
        for name in ("hidden", "qkv", "att", "probs", "attn_out", "wattn"):
            out(name, s[name].at[l], l)
        if l == 0:
            down[0].pass_z()
            up[1].start()
        else:
            down[1].pass_z()
        up[l].pass_y()
        up[l].pass_x()
        w_up = s["wmlp"].at[l, 0]
        w_down = s["wmlp"].at[l, 1]

        def rise(low, size):
            for n in range(0, D, 256):
                upward = mm(rows[low : low + size, :], w_up[:, n : n + 256])
                s["upward"][l, low : low + size, n : n + 256] = upward
                s["active"][l, low : low + size, n : n + 256] = (
                    upward * gelu_parts(upward)
                ).astype(jnp.bfloat16)

        rise(0, HALF)
        rise(HALF, HALF)
        far.wait_recv()
        side = mail.send(
            rows.at[pl.ds(2 * HALF, HALF)], rows.at[pl.ds(3 * HALF, HALF)], place.core
        )
        rise(2 * HALF, HALF)
        side.wait_recv()
        rise(3 * HALF, HALF)
        if l == 0:
            up[1].pass_z()
            down[1].start()
        down[l].pass_y()
        down[l].pass_x()

        def fall(low, target):
            for n in range(0, D, 256):
                part = mm_nt(s["active"][l, low : low + HALF, :], w_down[n : n + 256, :])
                target[:, n : n + 256] = part.astype(target.dtype)

        sum_out, sum_in, keep = (s["sum_out"].at[l], s["sum_in"].at[l], s["keep"])
        fall(3 * HALF, sum_out.at[0])
        first = mail.send(sum_out.at[0], sum_in.at[0], place.core)
        fall(2 * HALF, keep.at[0])
        fall(HALF, sum_out.at[1])
        second = mail.send(sum_out.at[1], sum_in.at[1], place.core)
        first.wait_recv()
        s["far_out"][l] = (keep[0] + sum_in[0].astype(jnp.float32)).astype(jnp.bfloat16)
        third = mail.send(s["far_out"].at[l], s["far_in"].at[l], place.across)
        fall(0, keep.at[1])
        second.wait_recv()
        keep[1] = keep[1] + sum_in[1].astype(jnp.float32)
        for name in ("rows", "upward", "active", "wmlp"):
            out(name, s[name].at[l], l)
        third.wait_recv()
        total = (keep[1] + s["far_in"][l].astype(jnp.float32)).astype(jnp.bfloat16)
        s["own_out"][l] = total
        fourth = mail.send(s["own_out"].at[l], s["own_in"].at[l], place.core)
        gate = piece(base + 5)
        output = total.astype(jnp.float32)
        s["mlp_out"][l, 0:HALF, :] = output
        s["resid"][0:HALF, :] += gate * output
        fourth.wait_recv()
        output = s["own_in"][l].astype(jnp.float32)
        s["mlp_out"][l, HALF : 2 * HALF, :] = output
        s["resid"][HALF : 2 * HALF, :] += gate * output
        out("mlp_out", s["mlp_out"].at[l], l)

    for low in (0, HALF):
        normalize(
            2 * LAYERS, piece(6 * LAYERS), piece(6 * LAYERS + 1), s["final_low"], low
        )
    predicted = mm(s["final_low"][...], s["head"][...])
    lanes = lax.broadcasted_iota(jnp.int32, (TOKENS, LANES), 1)
    taken = (lanes >= PATCH_DIM) & (lanes < 2 * PATCH_DIM)
    difference = jnp.where(taken, predicted - s["noise"][...], 0.0)
    square = difference[0:HALF] * difference[0:HALF]
    s["loss"][...] = jnp.sum(square.reshape(HALF // 8, 8, LANES), axis=0)
    s["grad_pred"][...] = (difference * (2.0 / total_entries)).astype(jnp.bfloat16)
    for name in ("normed", "inverse", "final_low", "loss", "grad_pred"):
        out(name, s[name])
    waited = [head_kept, data_kept, mod_kept] + [g.kept for g in attn + up + down]
    mail.finish(waited)


FORWARD_OUTS = {
    "wattn": ((LAYERS, 2, D, D), jnp.bfloat16),
    "wmlp": ((LAYERS, 2, D, D), jnp.bfloat16),
    "head": ((D, LANES), jnp.bfloat16),
    "pieces": ((16, D), jnp.float32),
    "cond": ((16, D), jnp.float32),
    "hidden": ((LAYERS, TOKENS, D), jnp.bfloat16),
    "qkv": ((LAYERS, 2, TOKENS, D), jnp.bfloat16),
    "att": ((LAYERS, 2, TOKENS, D // 2), jnp.bfloat16),
    "probs": ((LAYERS, 2, 3, TOKENS, TOKENS), jnp.float32),
    "attn_out": ((LAYERS, TOKENS, D), jnp.float32),
    "rows": ((LAYERS, 2 * TOKENS, D), jnp.bfloat16),
    "upward": ((LAYERS, 2 * TOKENS, D), jnp.float32),
    "active": ((LAYERS, 2 * TOKENS, D), jnp.bfloat16),
    "mlp_out": ((LAYERS, TOKENS, D), jnp.float32),
    "normed": ((2 * LAYERS + 1, TOKENS, D), jnp.float32),
    "inverse": ((2 * LAYERS + 1, TOKENS, LANES), jnp.float32),
    "final_low": ((TOKENS, D), jnp.bfloat16),
    "noisy": ((TOKENS, LANES), jnp.bfloat16),
    "grad_pred": ((TOKENS, LANES), jnp.bfloat16),
    "loss": ((8, LANES), jnp.float32),
}
FORWARD_OWN = {
    "order": ((8 * LANES, D), jnp.bfloat16),
    "waves": ((32, D), jnp.float32),
    "cond_in": ((7, 16, D), jnp.float32),
    "data_in": ((4, HALF, LANES), jnp.float32),
    "noise": ((TOKENS, LANES), jnp.float32),
    "mod_out": ((16, 16, LANES), jnp.float32),
    "mod_in": ((8, 16, LANES), jnp.float32),
    "mod_rows": ((16, 8 * LANES), jnp.float32),
    "resid": ((TOKENS, D), jnp.float32),
    "core_out": ((LAYERS, TOKENS, D), jnp.bfloat16),
    "core_in": ((LAYERS, TOKENS, D), jnp.bfloat16),
    "sum_out": ((LAYERS, 2, HALF, D), jnp.bfloat16),
    "sum_in": ((LAYERS, 2, HALF, D), jnp.bfloat16),
    "far_out": ((LAYERS, HALF, D), jnp.bfloat16),
    "far_in": ((LAYERS, HALF, D), jnp.bfloat16),
    "own_out": ((LAYERS, HALF, D), jnp.bfloat16),
    "own_in": ((LAYERS, HALF, D), jnp.bfloat16),
    "keep": ((2, HALF, D), jnp.float32),
}
FORWARD_SCRATCH = {**FORWARD_OUTS, **FORWARD_OWN}


def run_forward(inputs, total_entries):
    vmem = pl.BlockSpec(memory_space=pltpu.VMEM)
    outs = pl.pallas_call(
        partial(forward_kernel, {name: value.shape for name, value in inputs.items()}, total_entries),
        out_shape=[jax.ShapeDtypeStruct(*spec) for spec in FORWARD_OUTS.values()],
        in_specs=[vmem] * len(inputs),
        out_specs=[pl.BlockSpec(memory_space=pl.ANY)] * len(FORWARD_OUTS),
        scratch_shapes=[pltpu.VMEM(*spec) for spec in FORWARD_SCRATCH.values()]
        + [
            pltpu.SemaphoreType.DMA((128,)),
            pltpu.SemaphoreType.DMA((128,)),
            pltpu.SemaphoreType.DMA((48,)),
        ],
        compiler_params=pltpu.CompilerParams(
            collective_id=0, has_side_effects=True, vmem_limit_bytes=VMEM_LIMIT
        ),
    )(*inputs.values())
    return dict(zip(FORWARD_OUTS, outs))

def shard_tiles(attn_weight):
    q, k, v, o = (attn_weight[:, j].astype(jnp.bfloat16) for j in range(4))
    return jnp.concatenate(
        [
            q[..., :128],
            k[..., :128],
            v[..., :128],
            q[..., 128:],
            o[..., :64],
            k[..., 128:],
            o[..., 64:128],
            v[..., 128:],
            o[..., 128:],
        ],
        axis=-1,
    )


def tile_grads(grad):
    q = jnp.concatenate([grad[..., 0:128], grad[..., 384:448]], axis=-1)
    k = jnp.concatenate([grad[..., 128:256], grad[..., 512:576]], axis=-1)
    v = jnp.concatenate([grad[..., 256:384], grad[..., 640:704]], axis=-1)
    o = jnp.concatenate([grad[..., 448:512], grad[..., 576:640], grad[..., 704:768]], axis=-1)
    return jnp.stack([q, k, v, o], axis=1)


def wave_table():
    quarter = D // 4
    omegas = 1.0 / np.power(10000.0, np.arange(quarter, dtype=np.float32) / quarter)
    angles = np.arange(GRID, dtype=np.float32)[:, None] * omegas.astype(np.float32)[None, :]
    waves = np.concatenate([np.sin(angles), np.cos(angles)], axis=1).astype(np.float32)
    table = np.zeros((2 * GRID, D), np.float32)
    table[:GRID, : D // 2] = waves
    table[GRID:, D // 2 :] = waves
    padded = np.zeros((2 * GRID, 8, LANES), np.float32)
    padded[:, :, : D // 8] = table.reshape(2 * GRID, 8, D // 8)
    left = padded.reshape(2 * GRID, 8 * LANES)
    parts = []
    for _ in range(3):
        part = left.astype(jnp.bfloat16)
        parts.append(part)
        left = left - part.astype(np.float32)
    return np.concatenate(parts, axis=0)


def body_kernels(
    routes,
    latents,
    noise,
    timesteps,
    labels,
    step_count,
    tables,
    time_weight,
    cond_weight,
    cond_bias,
    attn_weight,
    mlp_weight,
    *states,
):
    fsdp_index = lax.axis_index("fsdp")
    tp_index = lax.axis_index("tp")
    across_index = tp_index // 2
    num_fsdp = routes.num_fsdp
    col_share = tables.shape[1]
    all_latents = timesteps.shape[0]
    total_entries = all_latents * SEQ * PATCH_DIM
    col_start = fsdp_index * col_share
    low_tables = tables.astype(jnp.bfloat16)
    blocks = cond_bias.shape[0] // col_share

    features = timestep_features(timesteps).astype(jnp.bfloat16)
    time_pre = jnp.dot(
        features,
        low_tables[2 * PATCH_DIM : 2 * PATCH_DIM + FREQ],
        preferred_element_type=jnp.float32,
    )
    time_hidden = jax.nn.silu(time_pre).astype(jnp.bfloat16)
    label_hot = (labels[:, None] == jnp.arange(NCLASS, dtype=jnp.int32)[None, :]).astype(
        jnp.bfloat16
    )
    label_part = jnp.dot(
        label_hot, low_tables[2 * PATCH_DIM + FREQ :], preferred_element_type=jnp.float32
    )
    low_time = time_weight.astype(jnp.bfloat16)
    cond_part = jnp.dot(time_hidden, low_time, preferred_element_type=jnp.float32)
    placed = lax.dynamic_update_slice(
        jnp.zeros((all_latents, D), jnp.float32), label_part, (0, col_start)
    )
    low_cond = cond_weight.astype(jnp.bfloat16)
    low_bias = cond_bias.astype(jnp.bfloat16).astype(jnp.float32)

    latent_id = fsdp_index * latents.shape[0]
    share = signal_share(lax.dynamic_slice_in_dim(timesteps, latent_id, latents.shape[0]))
    share = share[:, None, None]
    noisy = (jnp.sqrt(share) * latents + jnp.sqrt(1.0 - share) * noise).astype(jnp.bfloat16)
    data = jnp.concatenate(
        [
            jnp.pad(noisy.astype(jnp.float32), ((0, 0), (0, 0), (0, LANES - PATCH_DIM))),
            jnp.pad(noise, ((0, 0), (0, 0), (PATCH_DIM, LANES - 2 * PATCH_DIM))),
        ],
        axis=1,
    )
    shards = jnp.concatenate(
        [shard_tiles(attn_weight)[:, None], mlp_weight.astype(jnp.bfloat16)], axis=1
    )
    head = jnp.pad(low_tables[: 2 * PATCH_DIM].T, ((0, 0), (0, LANES - 2 * PATCH_DIM)))
    inputs = {
        "cond_part": cond_part + placed,
        "shards": shards,
        "data": data,
        "head": head,
        "waves": jnp.asarray(wave_table()),
        "cond_weight": low_cond.reshape(blocks, col_share, D),
        "cond_bias": low_bias.reshape(blocks, col_share),
    }
    kept = run_forward(inputs, total_entries)

    cond = kept["cond"]
    cond_act = jax.nn.silu(cond).astype(jnp.bfloat16)
    pieces_all = kept["pieces"]
    slots = jnp.arange(num_fsdp, dtype=jnp.int32)
    owners = routes.slot_owner(fsdp_index, slots)
    slot_hot = (owners[:, None] == slots[None, :]).astype(jnp.bfloat16)
    counted = SEQ // 2
    head = kept["head"]
    noisy = kept["noisy"][:, :PATCH_DIM]
    grad_pred = kept["grad_pred"][:, PATCH_DIM : 2 * PATCH_DIM]
    final_low = kept["final_low"]
    loss_part = jnp.sum(kept["loss"])
    def tiles(value, which):
        return jnp.concatenate([value[..., i * 64 : (i + 1) * 64] for i in which], axis=-1)
    qk_cols, vo_cols = ((0, 1, 6, 2, 3, 8), (4, 5, 10, 7, 9, 11))
    gathered, saved = ([], [])
    for l in range(LAYERS):
        w = kept["wattn"][l]
        weights = (
            ((tiles(w[0], qk_cols), tiles(w[1], qk_cols)), (tiles(w[0], vo_cols), tiles(w[1], vo_cols))),
            (kept["wmlp"][l, 0], kept["wmlp"][l, 1]),
        )
        gathered.append(weights)
        qkv = kept["qkv"][l]
        heads = lambda which: tiles(qkv, which).reshape(2, SEQ, 3, HEAD_DIM)
        padded = tiles(jnp.concatenate([jnp.zeros_like(kept["att"][l]), kept["att"][l]], axis=2), vo_cols)
        padded = jnp.concatenate([jnp.zeros_like(padded[..., :192]), padded[..., 192:]], axis=2)
        attn_saved = (
            kept["normed"][2 * l], kept["inverse"][2 * l][:, :1], kept["attn_out"][l],
            (kept["hidden"][l], heads((0, 1, 6)), heads((2, 3, 8)), heads((4, 5, 10)), kept["probs"][l], padded),
        )
        mlp_saved = (
            kept["normed"][2 * l + 1], kept["inverse"][2 * l + 1][:, :1], kept["mlp_out"][l],
            (kept["rows"][l], kept["upward"][l], kept["active"][l]),
        )
        saved.append((attn_saved, mlp_saved))
    final_normed, final_inverse = (kept["normed"][2 * LAYERS], kept["inverse"][2 * LAYERS][:, :1])
    final_scale = pieces_all[6 * LAYERS + 1][None, :]
    output_grad = dot_f32(final_low[:counted], grad_pred[:counted], 0, 0)
    grad_final = dot_f32(grad_pred, head[:, PATCH_DIM : 2 * PATCH_DIM], 1, 1)
    grad_resid, grad_fshift, grad_fscale = norm_backward(
        grad_final, final_normed, final_inverse, final_scale, counted
    )
    layer_mods = [None] * LAYERS
    layer_grads = [None] * LAYERS
    for layer in reversed(range(LAYERS)):
        pieces = [pieces_all[6 * layer + k][None, :] for k in range(6)]
        attn_w, mlp_w = gathered[layer]
        grad_resid, mlp_mods, mlp_grads = branch_backward(
            routes, grad_resid, pieces[3:], saved[layer][1], feed_backward, mlp_w
        )
        grad_resid, attn_mods, attn_grads = branch_backward(
            routes, grad_resid, pieces[:3], saved[layer][0], attend_backward, attn_w
        )
        layer_mods[layer] = attn_mods + mlp_mods
        layer_grads[layer] = attn_grads + mlp_grads
    grad_embed = grad_resid.astype(jnp.bfloat16)
    patch_grad = dot_f32(grad_embed[:counted], noisy[:counted], 0, 0)

    head_grad = jnp.concatenate([patch_grad, output_grad], axis=1)
    head_grad = head_grad + routes.core(head_grad)
    head_grad = head_grad + routes.across(head_grad)
    head_cols = routes.scatter_rows(head_grad, jnp.float32).T

    modul_grad = jnp.stack(layer_mods[0] + layer_mods[1] + [grad_fshift, grad_fscale])
    modul_grad = (modul_grad + routes.core(modul_grad)).astype(jnp.bfloat16)
    modul_grad = jnp.einsum(
        "psr,sf->pfr",
        modul_grad.reshape(-1, num_fsdp, col_share),
        slot_hot,
        preferred_element_type=jnp.float32,
    ).astype(jnp.bfloat16)
    modul_back = lax.all_to_all(
        modul_grad.reshape(num_fsdp, -1), "fsdp", split_axis=0, concat_axis=0, tiled=True
    )
    far_back = routes.across(modul_back)
    is_first = across_index == 0
    modul_back = jnp.stack(
        [jnp.where(is_first, modul_back, far_back), jnp.where(is_first, far_back, modul_back)],
        axis=1,
    ).reshape(all_latents, -1)
    cond_grad_w = dot_f32(modul_back, cond_act, 0, 0)
    bias_grad = jnp.sum(modul_back.astype(jnp.float32), axis=0)
    grad_cond_act = routes.sum_fsdp(dot_f32(modul_back, low_cond, 1, 0))
    silu_slope = jax.vjp(jax.nn.silu, cond)[1]
    grad_cond = silu_slope(grad_cond_act)[0].astype(jnp.bfloat16)
    time_grad = dot_f32(time_hidden, grad_cond, 0, 0)
    grad_hidden = dot_f32(grad_cond, low_time, 1, 1)
    time_slope = jax.vjp(jax.nn.silu, time_pre)[1]
    grad_pre = time_slope(grad_hidden)[0].astype(jnp.bfloat16)
    first_layer_grad = dot_f32(features, grad_pre, 0, 0)
    cond_cols = lax.dynamic_slice_in_dim(grad_cond, col_start, col_share, 1)
    label_grad = dot_f32(label_hot, cond_cols, 0, 0)
    tables_grad = jnp.concatenate([head_cols, first_layer_grad, label_grad], axis=0)

    squares = sum(jnp.sum(part * part) for parts in layer_grads for part in parts)
    owner = (tp_index == 0).astype(jnp.float32)
    squares = squares + owner * sum(
        jnp.sum(part * part) for part in (tables_grad, time_grad, cond_grad_w, bias_grad)
    )
    totals = routes.sum_all(jnp.stack([loss_part, squares]))
    loss = totals[0] / total_entries
    norm = jnp.sqrt(totals[1])
    entries = NTAB * D + D * D + (D + 1) * NCOND + LAYERS * (4 * D * D + 2 * D * FF)
    limit = clip_scale * math.sqrt(entries / (all_latents * SEQ))
    factor = jnp.minimum(1.0, limit / norm)
    count = step_count[0].astype(jnp.float32)
    width = attn_weight.shape[3]
    attn_grad = jnp.stack(
        [
            jnp.stack([qk[:, :width], qk[:, width:], vo[:, :width], vo[:, width:]])
            for qk, vo, _, _ in layer_grads
        ]
    )
    mlp_grad = jnp.stack([jnp.stack([up, down]) for _, _, up, down in layer_grads])
    weights_all = (tables, time_weight, cond_weight, cond_bias, attn_weight, mlp_weight)
    grads_all = (tables_grad, time_grad, cond_grad_w, bias_grad, attn_grad, mlp_grad)
    states = tuple(zip(states[0::2], states[1::2]))
    results = [loss, norm]
    for weight, grad, state in zip(weights_all, grads_all, states):
        results.extend(adam_update(weight, grad * factor, state[0], state[1], count))
    return tuple(results)


def body(routes, *args):
    if routes.num_fsdp == 8 and args[5].shape[1] % 16 == 0:
        return body_kernels(routes, *args)
    return body_steps(routes, *args)


def solution(mesh):
    vectors = P("fsdp")
    columns = P(None, "fsdp")
    rows = P("fsdp", None)
    blocks = P(None, None, "fsdp", "tp")
    data = P("fsdp", "tp", None)
    weights = (columns, rows, rows, vectors, blocks, blocks)
    states = tuple(spec for spec in weights for _ in range(2))
    updated = tuple(spec for spec in weights for _ in range(3))
    return jax.shard_map(
        partial(body, Routes(mesh)),
        mesh=mesh,
        in_specs=(data, data, P(), P(), P()) + weights + states,
        out_specs=(P(), P()) + updated,
        check_vma=False,
    )
```

```python
from functools import partial
import math
from types import SimpleNamespace

import jax
import jax.numpy as jnp
from jax import lax
import numpy as np
from jax.experimental import pallas as pl
from jax.experimental.pallas import tpu as pltpu
from jax.sharding import PartitionSpec as P

D = 768
HEAD_DIM = 64
FF = 3072
NCLASS = 1000
FREQ = 256
PATCH_DIM = 16
GRID = 16
LAYERS = 2
SEQ = 256
NCOND = 10752
NTAB = 1288


norm_eps = 1e-06
beta_first = 0.9
beta_second = 0.999
adam_eps = 1e-08
learn_rate = 0.2
weight_decay = 0.01
clip_scale = 0.002
diffusion_steps = 1000.0


def timestep_features(timesteps):
    half_width = FREQ // 2
    omegas = jnp.exp(-math.log(10000.0) * jnp.arange(half_width, dtype=jnp.float32) / half_width)
    angles = timesteps.astype(jnp.float32)[:, None] * omegas[None, :]
    return jnp.concatenate([jnp.cos(angles), jnp.sin(angles)], axis=1)


def signal_share(timesteps):
    phase = (timesteps.astype(jnp.float32) / diffusion_steps + 0.008) / 1.008 * (math.pi / 2)
    return jnp.cos(phase) ** 2


def butterfly_bits(number):
    bits = []
    bit = 1
    while bit < number:
        bits.append(bit)
        bit *= 2
    return bits


def split_radices(number):
    radices = []
    while number > 1:
        radix = 4 if number % 4 == 0 else 2
        radices.append(radix)
        number //= radix
    return radices


class Routes:
    def __init__(self, mesh):
        self.num_fsdp = mesh.shape["fsdp"]
        self.num_tp = mesh.shape["tp"]
        self.outer = split_radices(self.num_fsdp // 2)

    def core(self, value):
        return lax.ppermute(value, "tp", [(t, t ^ 1) for t in range(self.num_tp)])

    def across(self, value):
        return lax.ppermute(value, "tp", [(t, t ^ 2) for t in range(self.num_tp)])

    def pair(self, value):
        return lax.ppermute(value, "fsdp", [(f, f ^ 1) for f in range(self.num_fsdp)])

    def shift(self, value, stride, radix, amount):
        pairs = []
        for f in range(self.num_fsdp):
            digit = (f // stride) % radix
            pairs.append((f, f + ((digit + amount) % radix - digit) * stride))
        return lax.ppermute(value, "fsdp", pairs)

    def slot_owner(self, fsdp_index, slots):
        per_pair = self.num_fsdp // 2
        pair_part = (slots // per_pair + fsdp_index) % 2
        rest = slots % per_pair
        owner = pair_part
        stride = 2
        for radix in self.outer:
            digit = (rest + fsdp_index // stride) % radix
            owner = owner + digit * stride
            rest = rest // radix
            stride *= radix
        return owner

    def gather_outer(self, block):
        stride = 2
        for radix in self.outer:
            block = jnp.concatenate(
                [block] + [self.shift(block, stride, radix, -k) for k in range(1, radix)], axis=0
            )
            stride *= radix
        return block

    def gather_rows(self, block):
        held = self.gather_outer(block)
        return jnp.concatenate([held, self.pair(held)], axis=0)

    def gather_both(self, block, across_last):
        held = self.gather_outer(block)
        if across_last:
            own = jnp.concatenate([held, self.pair(held)], axis=0)
            return (own, self.across(own))
        other = self.across(held)
        return (
            jnp.concatenate([held, self.pair(held)], axis=0),
            jnp.concatenate([other, self.pair(other)], axis=0),
        )

    def scatter_rows(self, total, dtype=jnp.bfloat16):
        half = total.shape[0] // 2
        received = self.pair(total[half:].astype(dtype))
        held = total[:half] + received.astype(jnp.float32)
        strides = []
        stride = 2
        for radix in self.outer:
            strides.append(stride)
            stride *= radix
        for radix, stride in reversed(list(zip(self.outer, strides))):
            size = held.shape[0] // radix
            parts = [
                self.shift(held[k * size : (k + 1) * size].astype(dtype), stride, radix, k)
                for k in range(1, radix)
            ]
            held = held[:size]
            for part in parts:
                held = held + part.astype(jnp.float32)
        return held

    def scatter_both(self, own, other):
        received = self.across(other.astype(jnp.bfloat16))
        return self.scatter_rows(own + received.astype(jnp.float32))

    def sum_fsdp(self, value):
        for bit in butterfly_bits(self.num_fsdp):
            value = value + lax.ppermute(
                value, "fsdp", [(f, f ^ bit) for f in range(self.num_fsdp)]
            )
        return value

    def sum_all(self, value):
        value = value + self.core(value)
        value = value + self.across(value)
        return self.sum_fsdp(value)


def after(value, *earlier):
    return lax.optimization_barrier((value,) + earlier)[0]


def dot_f32(left, right, left_dim, right_dim):
    return lax.dot_general(
        left, right, (((left_dim,), (right_dim,)), ((), ())), preferred_element_type=jnp.float32
    )


def layer_norm(values):
    centred = values - jnp.mean(values, axis=-1, keepdims=True)
    inverse = lax.rsqrt(jnp.mean(centred * centred, axis=-1, keepdims=True) + norm_eps)
    return (centred * inverse, inverse)


def modulate(values, shift, scale):
    normed, inverse = layer_norm(values)
    return ((normed * (1.0 + scale) + shift).astype(jnp.bfloat16), normed, inverse)


def norm_backward(grad_mixed, normed, inverse, scale, counted):
    grad_shift = jnp.sum(grad_mixed[:counted], axis=0)
    grad_scale = jnp.sum(grad_mixed[:counted] * normed[:counted], axis=0)
    grad_normed = grad_mixed * (1.0 + scale)
    centred = grad_normed - jnp.mean(grad_normed, axis=-1, keepdims=True)
    grad_input = (
        centred - normed * jnp.mean(grad_normed * normed, axis=-1, keepdims=True)
    ) * inverse
    return (grad_input, grad_shift, grad_scale)


def core_sum(routes, partial):
    low = partial.astype(jnp.bfloat16)
    far = routes.core(low)
    half = far.shape[0] // 2
    swapped = jnp.concatenate([far[half:], far[:half]], axis=0)
    return low.astype(jnp.float32) + swapped.astype(jnp.float32)


def attend(routes, hidden, weights):
    seq_len = hidden.shape[0]
    query_key = jnp.stack([dot_f32(hidden, w, 1, 0) for w in weights[0]]).astype(jnp.bfloat16)
    value_out = jnp.stack([dot_f32(hidden, w, 1, 0) for w in weights[1]]).astype(jnp.bfloat16)
    width = query_key.shape[2] // 2
    local_heads = width // HEAD_DIM
    query_key = query_key.reshape(2, seq_len, 2 * local_heads, HEAD_DIM)
    query, key = (query_key[:, :, :local_heads], query_key[:, :, local_heads:])
    value = value_out[:, :, :width].reshape(2, seq_len, local_heads, HEAD_DIM)
    scores = jnp.einsum(
        "xqhe,xkhe->xhqk", query, key, preferred_element_type=jnp.float32
    ) * HEAD_DIM ** (-0.5)
    exped = jnp.exp(scores - jnp.max(scores, axis=-1, keepdims=True))
    probs = exped / jnp.sum(exped, axis=-1, keepdims=True)
    attended = jnp.einsum(
        "xhqk,xkhe->xqhe", probs.astype(jnp.bfloat16), value, preferred_element_type=jnp.float32
    )
    attended = attended.astype(jnp.bfloat16).reshape(2, seq_len, width)
    padded = jnp.concatenate([jnp.zeros_like(attended), attended], axis=2)
    partial_out = dot_f32(padded[0], weights[1][0], 1, 1) + dot_f32(padded[1], weights[1][1], 1, 1)
    return (core_sum(routes, partial_out), (hidden, query, key, value, probs, padded))


def attend_backward(routes, grad_full, kept, weights):
    hidden, query, key, value, probs, padded = kept
    seq_len = hidden.shape[0]
    scale = HEAD_DIM ** (-0.5)
    width = padded.shape[2] // 2
    local_heads = width // HEAD_DIM
    grad_attended = jnp.stack([dot_f32(grad_full, w, 1, 0) for w in weights[1]])
    grad_attended = grad_attended[:, :, width:].astype(jnp.bfloat16)
    grad_attended = grad_attended.reshape(2, seq_len, local_heads, HEAD_DIM)
    grad_probs = jnp.einsum(
        "xqhe,xkhe->xhqk", grad_attended, value, preferred_element_type=jnp.float32
    )
    grad_value = jnp.einsum(
        "xhqk,xqhe->xkhe",
        probs.astype(jnp.bfloat16),
        grad_attended,
        preferred_element_type=jnp.float32,
    )
    inner = jnp.sum(probs * grad_probs, axis=-1, keepdims=True)
    grad_scores = (probs * (grad_probs - inner)).astype(jnp.bfloat16)
    grad_query = (
        jnp.einsum("xhqk,xkhe->xqhe", grad_scores, key, preferred_element_type=jnp.float32) * scale
    )
    grad_key = (
        jnp.einsum("xhqk,xqhe->xkhe", grad_scores, query, preferred_element_type=jnp.float32) * scale
    )
    grad_qk = jnp.concatenate([grad_query, grad_key], axis=2).astype(jnp.bfloat16)
    grad_qk = grad_qk.reshape(2, seq_len, 2 * width)
    grad_v = grad_value.astype(jnp.bfloat16).reshape(2, seq_len, width)
    grad_v = jnp.concatenate([grad_v, jnp.zeros_like(grad_v)], axis=2)
    grad_hidden = jnp.zeros(hidden.shape, jnp.float32)
    for k in range(2):
        grad_hidden = grad_hidden + dot_f32(grad_qk[k], weights[0][k], 1, 1)
        grad_hidden = grad_hidden + dot_f32(grad_v[k], weights[1][k], 1, 1)
    grad_hidden = core_sum(routes, grad_hidden)
    qk_own, qk_other = [dot_f32(hidden, grad_qk[k], 0, 0) for k in range(2)]
    both = jnp.concatenate([hidden, grad_full], axis=0)
    vo_own, vo_other = [
        dot_f32(both, jnp.concatenate([grad_v[k], padded[k]], axis=0), 0, 0) for k in range(2)
    ]
    grads = (routes.scatter_both(qk_own, qk_other), routes.scatter_both(vo_own, vo_other))
    return (grad_hidden, grads)


def share_rows(routes, rows):
    half = rows.shape[0] // 2
    far = routes.across(rows[:half])
    return jnp.concatenate([rows, far, routes.core(far)], axis=0)


def sum_rows(routes, partial):
    half = partial.shape[0] // 4
    low = partial.astype(jnp.bfloat16)
    received = routes.core(jnp.concatenate([low[3 * half :], low[half : 2 * half]], axis=0))
    received = received.astype(jnp.float32)
    far_sum = (partial[2 * half : 3 * half] + received[:half]).astype(jnp.bfloat16)
    own_sum = partial[:half] + received[half:]
    own_total = (own_sum + routes.across(far_sum).astype(jnp.float32)).astype(jnp.bfloat16)
    return jnp.concatenate([own_total, routes.core(own_total)], axis=0).astype(jnp.float32)


def feed_forward(routes, hidden, weights):
    rows = share_rows(routes, hidden)
    upward = dot_f32(rows, weights[0], 1, 0)
    active = jax.nn.gelu(upward, approximate=True).astype(jnp.bfloat16)
    output = sum_rows(routes, dot_f32(active, weights[1], 1, 1))
    return (output, (rows, upward, active))


def feed_backward(routes, grad_full, kept, weights):
    rows, upward, active = kept
    grad_rows = share_rows(routes, grad_full)
    grad_active = dot_f32(grad_rows, weights[1], 1, 0)
    slope = jax.vjp(partial(jax.nn.gelu, approximate=True), upward)[1]
    grad_up = slope(grad_active)[0].astype(jnp.bfloat16)
    grad_hidden = sum_rows(routes, dot_f32(grad_up, weights[0], 1, 1))
    grad_down_w = routes.scatter_rows(dot_f32(grad_rows, active, 0, 0))
    grad_up_w = routes.scatter_rows(dot_f32(rows, grad_up, 0, 0))
    return (grad_hidden, (grad_up_w, grad_down_w))


def branch_forward(routes, resid, pieces, inner_fn, weights):
    shift, scale, gate = pieces
    hidden, normed, inverse = modulate(resid, shift, scale)
    output, kept = inner_fn(routes, hidden, weights)
    return (resid + gate * output, (normed, inverse, output, kept))


def branch_backward(routes, grad_resid, pieces, saved, inner_back, weights):
    shift, scale, gate = pieces
    normed, inverse, output, kept = saved
    counted = grad_resid.shape[0] // 2
    grad_gate = jnp.sum(grad_resid[:counted] * output[:counted], axis=0)
    grad_output = (gate * grad_resid).astype(jnp.bfloat16)
    grad_mixed, grads = inner_back(routes, grad_output, kept, weights)
    grad_input, grad_shift, grad_scale = norm_backward(grad_mixed, normed, inverse, scale, counted)
    return (grad_resid + grad_input, [grad_shift, grad_scale, grad_gate], grads)


def gather_weights(routes, attn_weight, mlp_weight):
    shards = []
    for layer in range(LAYERS):
        attn = attn_weight[layer].astype(jnp.bfloat16)
        mlp = mlp_weight[layer].astype(jnp.bfloat16)
        shards.append(
            (
                jnp.concatenate([attn[0], attn[1]], axis=1),
                jnp.concatenate([attn[2], attn[3]], axis=1),
                mlp[0],
                mlp[1],
            )
        )
    gathered = []
    earlier = []

    def in_turn(block):
        return after(block, earlier[-2]) if len(earlier) >= 2 else block

    for layer in range(LAYERS):
        query_key, value_out, up, down = shards[layer]
        pairs = []
        for block, across_last in ((query_key, True), (value_out, layer > 0)):
            both = routes.gather_both(in_turn(block), across_last)
            pairs.append(both)
            earlier.append(both[0])
        rows = []
        for block in (up, down):
            rows.append(routes.gather_rows(in_turn(block)))
            earlier.append(rows[-1])
        gathered.append((tuple(pairs), tuple(rows)))
    return gathered


def adam_update(weight, grad, first, second, count):
    first_new = beta_first * first + (1.0 - beta_first) * grad
    second_new = beta_second * second + (1.0 - beta_second) * grad * grad
    first_hat = first_new / (1.0 - jnp.power(beta_first, count))
    second_hat = second_new / (1.0 - jnp.power(beta_second, count))
    weight_new = weight - learn_rate * (
        first_hat / (jnp.sqrt(second_hat) + adam_eps) + weight_decay * weight
    )
    return [weight_new, first_new, second_new]


def body_steps(
    routes,
    latents,
    noise,
    timesteps,
    labels,
    step_count,
    tables,
    time_weight,
    cond_weight,
    cond_bias,
    attn_weight,
    mlp_weight,
    tables_first,
    tables_second,
    time_first,
    time_second,
    cond_first,
    cond_second,
    bias_first,
    bias_second,
    attn_first,
    attn_second,
    mlp_first,
    mlp_second,
):
    fsdp_index = lax.axis_index("fsdp")
    tp_index = lax.axis_index("tp")
    across_index = tp_index // 2
    num_fsdp = routes.num_fsdp
    local_seq = latents.shape[1]
    col_share = tables.shape[1]
    all_latents = timesteps.shape[0]
    total_entries = all_latents * SEQ * PATCH_DIM
    col_start = fsdp_index * col_share
    low_tables = tables.astype(jnp.bfloat16)

    gathered = gather_weights(routes, attn_weight, mlp_weight)
    head = routes.gather_rows(low_tables[: 2 * PATCH_DIM].T)

    features = timestep_features(timesteps).astype(jnp.bfloat16)
    time_pre = jnp.dot(
        features,
        low_tables[2 * PATCH_DIM : 2 * PATCH_DIM + FREQ],
        preferred_element_type=jnp.float32,
    )
    time_hidden = jax.nn.silu(time_pre).astype(jnp.bfloat16)
    label_hot = (labels[:, None] == jnp.arange(NCLASS, dtype=jnp.int32)[None, :]).astype(
        jnp.bfloat16
    )
    label_part = jnp.dot(
        label_hot, low_tables[2 * PATCH_DIM + FREQ :], preferred_element_type=jnp.float32
    )
    low_time = time_weight.astype(jnp.bfloat16)
    cond_part = jnp.dot(time_hidden, low_time, preferred_element_type=jnp.float32)
    placed = lax.dynamic_update_slice(
        jnp.zeros((all_latents, D), jnp.float32), label_part, (0, col_start)
    )
    cond = routes.sum_fsdp(cond_part + placed)
    cond_act = jax.nn.silu(cond).astype(jnp.bfloat16)
    low_cond = cond_weight.astype(jnp.bfloat16)
    low_bias = cond_bias.astype(jnp.bfloat16).astype(jnp.float32)
    mod_part = dot_f32(cond_act, low_cond, 1, 1) + low_bias[None, :]
    modul = lax.all_to_all(
        mod_part.astype(jnp.bfloat16), "fsdp", split_axis=0, concat_axis=1, tiled=True
    )
    modul = lax.dynamic_slice_in_dim(modul, across_index, 1, 0)

    slots = jnp.arange(num_fsdp, dtype=jnp.int32)
    owners = routes.slot_owner(fsdp_index, slots)
    slot_hot = (owners[:, None] == slots[None, :]).astype(jnp.bfloat16)
    pieces_all = jnp.einsum(
        "pfr,sf->psr",
        modul.reshape(-1, num_fsdp, col_share),
        slot_hot,
        preferred_element_type=jnp.float32,
    ).reshape(-1, D)

    data = jnp.stack([latents, noise], axis=1)
    own_data = lax.dynamic_index_in_dim(data, across_index, 0, keepdims=False)
    far_data = lax.dynamic_index_in_dim(data, 1 - across_index, 0, keepdims=False)
    first_data = jnp.concatenate([own_data, routes.across(far_data)], axis=1)
    chip_data = jnp.concatenate([first_data, routes.core(first_data)], axis=1)
    clean, noise_part = (chip_data[0], chip_data[1])
    chunks = jnp.stack([tp_index, tp_index ^ 2, tp_index ^ 1, tp_index ^ 3])
    token_ids = (
        chunks[:, None] * local_seq + jnp.arange(local_seq, dtype=jnp.int32)[None, :]
    ).reshape(-1)
    counted = token_ids.shape[0] // 2

    quarter = D // 4
    col_ids = (
        owners[:, None] * col_share + jnp.arange(col_share, dtype=jnp.int32)[None, :]
    ).reshape(-1)
    omegas = 1.0 / jnp.power(10000.0, (col_ids % quarter).astype(jnp.float32) / quarter)
    angles = jnp.arange(GRID, dtype=jnp.float32)[:, None] * omegas[None, :]
    kinds = (col_ids // quarter)[None, :]
    waves = jnp.where(kinds % 2 == 0, jnp.sin(angles), jnp.cos(angles))
    row_waves = jnp.where(kinds < 2, waves, 0.0)
    col_waves = jnp.where(kinds >= 2, waves, 0.0)
    grid_ids = jnp.arange(GRID, dtype=jnp.int32)[None, :]
    row_hot = (token_ids[:, None] // GRID == grid_ids).astype(jnp.float32)
    col_hot = (token_ids[:, None] % GRID == grid_ids).astype(jnp.float32)
    positions = jnp.dot(
        jnp.concatenate([row_hot, col_hot], axis=1),
        jnp.concatenate([row_waves, col_waves], axis=0),
        precision=lax.Precision.HIGHEST,
    )

    latent_id = fsdp_index * latents.shape[0] + across_index
    share = signal_share(lax.dynamic_slice_in_dim(timesteps, latent_id, 1))[:, None]
    noisy = (jnp.sqrt(share) * clean + jnp.sqrt(1.0 - share) * noise_part).astype(jnp.bfloat16)
    resid = dot_f32(noisy, head[:, :PATCH_DIM], 1, 1) + positions

    saved = []
    for layer in range(LAYERS):
        pieces = [pieces_all[6 * layer + k][None, :] for k in range(6)]
        attn_w, mlp_w = gathered[layer]
        resid, attn_saved = branch_forward(routes, resid, pieces[:3], attend, attn_w)
        resid, mlp_saved = branch_forward(routes, resid, pieces[3:], feed_forward, mlp_w)
        saved.append((attn_saved, mlp_saved))
    final_shift = pieces_all[6 * LAYERS][None, :]
    final_scale = pieces_all[6 * LAYERS + 1][None, :]
    final_low, final_normed, final_inverse = modulate(resid, final_shift, final_scale)
    predicted = dot_f32(final_low, head[:, PATCH_DIM:], 1, 0)
    difference = predicted - noise_part
    loss_part = jnp.sum(difference[:counted] * difference[:counted])
    grad_pred = (difference * (2.0 / total_entries)).astype(jnp.bfloat16)
    output_grad = dot_f32(final_low[:counted], grad_pred[:counted], 0, 0)
    grad_final = dot_f32(grad_pred, head[:, PATCH_DIM:], 1, 1)
    grad_resid, grad_fshift, grad_fscale = norm_backward(
        grad_final, final_normed, final_inverse, final_scale, counted
    )
    layer_mods = [None] * LAYERS
    layer_grads = [None] * LAYERS
    for layer in reversed(range(LAYERS)):
        pieces = [pieces_all[6 * layer + k][None, :] for k in range(6)]
        attn_w, mlp_w = gathered[layer]
        grad_resid, mlp_mods, mlp_grads = branch_backward(
            routes, grad_resid, pieces[3:], saved[layer][1], feed_backward, mlp_w
        )
        grad_resid, attn_mods, attn_grads = branch_backward(
            routes, grad_resid, pieces[:3], saved[layer][0], attend_backward, attn_w
        )
        layer_mods[layer] = attn_mods + mlp_mods
        layer_grads[layer] = attn_grads + mlp_grads
    grad_embed = grad_resid.astype(jnp.bfloat16)
    patch_grad = dot_f32(grad_embed[:counted], noisy[:counted], 0, 0)

    head_grad = jnp.concatenate([patch_grad, output_grad], axis=1)
    head_grad = head_grad + routes.core(head_grad)
    head_grad = head_grad + routes.across(head_grad)
    head_cols = routes.scatter_rows(head_grad, jnp.float32).T

    modul_grad = jnp.stack(layer_mods[0] + layer_mods[1] + [grad_fshift, grad_fscale])
    modul_grad = (modul_grad + routes.core(modul_grad)).astype(jnp.bfloat16)
    modul_grad = jnp.einsum(
        "psr,sf->pfr",
        modul_grad.reshape(-1, num_fsdp, col_share),
        slot_hot,
        preferred_element_type=jnp.float32,
    ).astype(jnp.bfloat16)
    modul_back = lax.all_to_all(
        modul_grad.reshape(num_fsdp, -1), "fsdp", split_axis=0, concat_axis=0, tiled=True
    )
    far_back = routes.across(modul_back)
    is_first = across_index == 0
    modul_back = jnp.stack(
        [jnp.where(is_first, modul_back, far_back), jnp.where(is_first, far_back, modul_back)],
        axis=1,
    ).reshape(all_latents, -1)
    cond_grad_w = dot_f32(modul_back, cond_act, 0, 0)
    bias_grad = jnp.sum(modul_back.astype(jnp.float32), axis=0)
    grad_cond_act = routes.sum_fsdp(dot_f32(modul_back, low_cond, 1, 0))
    silu_slope = jax.vjp(jax.nn.silu, cond)[1]
    grad_cond = silu_slope(grad_cond_act)[0].astype(jnp.bfloat16)
    time_grad = dot_f32(time_hidden, grad_cond, 0, 0)
    grad_hidden = dot_f32(grad_cond, low_time, 1, 1)
    time_slope = jax.vjp(jax.nn.silu, time_pre)[1]
    grad_pre = time_slope(grad_hidden)[0].astype(jnp.bfloat16)
    first_layer_grad = dot_f32(features, grad_pre, 0, 0)
    cond_cols = lax.dynamic_slice_in_dim(grad_cond, col_start, col_share, 1)
    label_grad = dot_f32(label_hot, cond_cols, 0, 0)
    tables_grad = jnp.concatenate([head_cols, first_layer_grad, label_grad], axis=0)

    squares = sum(jnp.sum(part * part) for parts in layer_grads for part in parts)
    owner = (tp_index == 0).astype(jnp.float32)
    squares = squares + owner * sum(
        jnp.sum(part * part) for part in (tables_grad, time_grad, cond_grad_w, bias_grad)
    )
    totals = routes.sum_all(jnp.stack([loss_part, squares]))
    loss = totals[0] / total_entries
    norm = jnp.sqrt(totals[1])
    entries = NTAB * D + D * D + (D + 1) * NCOND + LAYERS * (4 * D * D + 2 * D * FF)
    limit = clip_scale * math.sqrt(entries / (all_latents * SEQ))
    factor = jnp.minimum(1.0, limit / norm)
    count = step_count[0].astype(jnp.float32)
    width = attn_weight.shape[3]
    attn_grad = jnp.stack(
        [
            jnp.stack([qk[:, :width], qk[:, width:], vo[:, :width], vo[:, width:]])
            for qk, vo, _, _ in layer_grads
        ]
    )
    mlp_grad = jnp.stack([jnp.stack([up, down]) for _, _, up, down in layer_grads])
    weights_all = (tables, time_weight, cond_weight, cond_bias, attn_weight, mlp_weight)
    grads_all = (tables_grad, time_grad, cond_grad_w, bias_grad, attn_grad, mlp_grad)
    states = (
        (tables_first, tables_second),
        (time_first, time_second),
        (cond_first, cond_second),
        (bias_first, bias_second),
        (attn_first, attn_second),
        (mlp_first, mlp_second),
    )
    results = [loss, norm]
    for weight, grad, state in zip(weights_all, grads_all, states):
        results.extend(adam_update(weight, grad * factor, state[0], state[1], count))
    return tuple(results)


MESH = pl.DeviceIdType.MESH
VMEM_LIMIT = 60 * 1024 * 1024
LANES = 128
HALF = 128
TOKENS = 256


class Place:
    def __init__(self):
        self.f = lax.axis_index("fsdp")
        self.t = lax.axis_index("tp")
        self.z = self.f // 2
        self.y = lax.rem(self.f, 2)
        self.core = (self.f, self.t + 1 - 2 * lax.rem(self.t, 2))
        self.across = (self.f, lax.rem(self.t + 2, 4))
        self.diagonal = (self.f, 3 - self.t)
        self.pair = (self.f + 1 - 2 * self.y, self.t)

    def down_z(self, k):
        return (lax.rem(self.z + 4 - k, 4) * 2 + self.y, self.t)

    def up_z(self, k):
        return (lax.rem(self.z + k, 4) * 2 + self.y, self.t)

    def up_f(self, k):
        return (lax.rem(self.f + k, 8), self.t)

    def slot_of(self, owner):
        pair_part = lax.rem(self.y + owner % 2, 2)
        return pair_part * 4 + lax.rem(owner // 2 + 4 - self.z, 4)


class Mail:
    def __init__(self, send_sem, recv_sem, local_sem):
        self.send_sem, self.recv_sem, self.local_sem = (send_sem, recv_sem, local_sem)
        self.sent = []
        self.local = []

    def send(self, source, target, device):
        index = len(self.sent)
        copy = pltpu.make_async_remote_copy(
            src_ref=source,
            dst_ref=target,
            send_sem=self.send_sem.at[index],
            recv_sem=self.recv_sem.at[index],
            device_id=device,
            device_id_type=MESH,
        )
        copy.start()
        self.sent.append(copy)
        return copy

    def move(self, source, target):
        copy = pltpu.make_async_copy(source, target, self.local_sem.at[len(self.local)])
        copy.start()
        self.local.append(copy)
        return copy

    def finish(self, skip=()):
        for copy in self.sent:
            copy.wait_send()
        for copy in self.local:
            if not any(copy is other for other in skip):
                copy.wait()


def greet(place):
    barrier = pltpu.get_barrier_semaphore()
    friends = [place.up_f(k) for k in range(1, 8)]
    friends += [place.core, place.across, place.diagonal]
    for device in friends:
        pl.semaphore_signal(barrier, inc=1, device_id=device, device_id_type=MESH)
    pl.semaphore_wait(barrier, len(friends))


def mm(left, right):
    return lax.dot_general(left, right, (((1,), (0,)), ((), ())), preferred_element_type=jnp.float32)


def mm_nt(left, right):
    return lax.dot_general(left, right, (((1,), (1,)), ((), ())), preferred_element_type=jnp.float32)


def mm_tn(left, right):
    return lax.dot_general(left, right, (((0,), (0,)), ((), ())), preferred_element_type=jnp.float32)


class Gather:
    def __init__(self, place, mail, shard, own, other=None):
        self.place, self.mail, self.shard, self.own, self.other = (place, mail, shard, own, other)
        self.rows = shard.shape[0]

    def at(self, ref, slot):
        return ref.at[pl.ds(slot * self.rows, self.rows)]

    def start_z(self):
        self.kept = self.mail.move(self.shard, self.at(self.own, 0))
        self.from_z = [
            self.mail.send(self.shard, self.at(self.own, k), self.place.down_z(k))
            for k in range(1, 4)
        ]

    def start_y(self):
        self.from_y = [self.mail.send(self.shard, self.at(self.own, 4), self.place.pair)]

    def start_x(self):
        self.from_x = [self.mail.send(self.shard, self.at(self.other, 0), self.place.across)]

    def pass_z(self):
        for k in range(1, 4):
            self.from_z[k - 1].wait_recv()
            block = self.at(self.own, k)
            self.from_y.append(self.mail.send(block, self.at(self.own, 4 + k), self.place.pair))
            if self.other is not None:
                self.from_x.append(self.mail.send(block, self.at(self.other, k), self.place.across))

    def pass_y(self, slots=(0, 1, 2, 3)):
        for k in slots:
            self.from_y[k].wait_recv()
            if self.other is not None:
                block = self.at(self.own, 4 + k)
                target = self.at(self.other, 4 + k)
                self.from_x.append(self.mail.send(block, target, self.place.across))

    def pass_x(self):
        if self.other is not None:
            for copy in self.from_x:
                copy.wait_recv()
        self.kept.wait()


def gelu_parts(value):
    inner = math.sqrt(2.0 / math.pi) * (value + 0.044715 * (value * value * value))
    return 0.5 * (1.0 + jnp.tanh(inner))


def half_mask(rows, upper):
    lanes = lax.broadcasted_iota(jnp.int32, (rows, LANES), 1)
    return lanes >= 64 if upper else lanes < 64


def forward_kernel(shapes, total_entries, *refs):
    names = list(shapes)
    r = SimpleNamespace(**dict(zip(names, refs)))
    rest = refs[len(names) :]
    outs = SimpleNamespace(**dict(zip(FORWARD_OUTS, rest)))
    rest = rest[len(FORWARD_OUTS) :]
    s = SimpleNamespace(**dict(zip(FORWARD_SCRATCH, rest)))
    rest = rest[len(FORWARD_SCRATCH) :]
    mail = Mail(*rest)
    place = Place()
    greet(place)

    attn = [
        Gather(place, mail, r.shards.at[l, 0], s.wattn.at[l, 0], s.wattn.at[l, 1])
        for l in range(LAYERS)
    ]
    up = [Gather(place, mail, r.shards.at[l, 1], s.wmlp.at[l, 0]) for l in range(LAYERS)]
    down = [Gather(place, mail, r.shards.at[l, 2], s.wmlp.at[l, 1]) for l in range(LAYERS)]

    across_index = place.t // 2
    core_index = lax.rem(place.t, 2)
    cond_own = r.cond_part.at[across_index, core_index]
    cond_from = [mail.send(cond_own, s.cond_in.at[k - 1], place.up_f(k)) for k in range(1, 8)]
    own_data = r.data.at[across_index]
    data_far = mail.send(r.data.at[1 - across_index], s.data_in.at[1], place.across)
    data_side = mail.send(own_data, s.data_in.at[2], place.core)
    attn[0].start_z()
    attn[0].start_y()
    attn[0].start_x()
    head_rows = r.head.shape[0]
    head_kept = mail.move(r.head, s.head.at[pl.ds(0, head_rows)])
    data_kept = mail.move(own_data, s.data_in.at[0])
    head_from = [
        mail.send(r.head, s.head.at[pl.ds(k * head_rows, head_rows)], place.down_z(k))
        for k in range(1, 4)
    ]
    attn[1].start_y()
    up[0].start_y()

    rows_id = lax.broadcasted_iota(jnp.int32, (LANES, D), 0)
    offset = lax.broadcasted_iota(jnp.int32, (LANES, D), 1) - rows_id
    for owner in range(8):
        hit = (offset == place.slot_of(owner) * head_rows) & (rows_id < head_rows)
        s.order[pl.ds(owner * LANES, LANES), :] = jnp.where(hit, 1.0, 0.0).astype(jnp.bfloat16)

    waves = mm(r.waves[...], s.order[...])
    s.waves[...] = waves[0:32] + waves[32:64] + waves[64:96]

    part = r.cond_part[across_index, core_index]
    for k in range(7):
        cond_from[k].wait_recv()
        part = part + s.cond_in[k]
    s.cond[across_index, core_index] = part
    cond_part = s.cond.at[across_index, core_index]
    cond_side = mail.send(cond_part, cond_part, place.core)
    data_far.wait_recv()
    data_diagonal = mail.send(s.data_in.at[1], s.data_in.at[3], place.core)
    attn[0].pass_y((0,))
    cond_side.wait_recv()
    cond_half = s.cond.at[across_index]
    cond_far = mail.send(cond_half, cond_half, place.across)
    cond = jnp.concatenate([s.cond[across_index, 0], s.cond[across_index, 1]], axis=0)
    cond_act = (cond * jax.nn.sigmoid(cond)).astype(jnp.bfloat16)
    blocks = r.cond_weight.shape[0]
    for b in range(blocks):
        part = mm_nt(cond_act, r.cond_weight[b]) + r.cond_bias[b : b + 1, :]
        part = part.astype(jnp.bfloat16).astype(jnp.float32)
        for i in range(8):
            s.mod_out[i, b : b + 1, 0:head_rows] = part[i : i + 1, :]
    mod_from = []
    for k in range(1, 8):
        source = s.mod_out.at[lax.rem(place.f + k, 8)]
        mod_from.append(mail.send(source, s.mod_in.at[k], place.up_f(k)))
    mod_kept = mail.move(s.mod_out.at[place.f], s.mod_in.at[0])
    attn[1].start_z()

    attn[0].pass_z()
    up[0].start_z()
    for k in range(3):
        head_from[k].wait_recv()
    head_kept.wait()
    lower = s.head.at[pl.ds(0, 4 * head_rows)]
    upper = s.head.at[pl.ds(4 * head_rows, 4 * head_rows)]
    head_pair = mail.send(lower, upper, place.pair)
    attn[1].start_x()
    down[0].start_y()
    up[1].start_y()

    mod_kept.wait()
    for copy in mod_from:
        copy.wait_recv()
    s.mod_rows[...] = jnp.zeros_like(s.mod_rows)
    for g in range(8 * blocks):
        piece, owner = (g // 8, g % 8)
        k = lax.rem(place.f + 8 - g // blocks, 8)
        b = g % blocks
        s.mod_rows[piece : piece + 1, owner * LANES : owner * LANES + head_rows] = s.mod_in[
            k, b : b + 1, 0:head_rows
        ]
    s.pieces[...] = mm(s.mod_rows[...].astype(jnp.bfloat16), s.order[...])
    mail.move(s.pieces, outs.pieces)

    data_kept.wait()
    data_side.wait_recv()
    data_diagonal.wait_recv()
    head_pair.wait_recv()
    cond_far.wait_recv()
    mail.move(s.cond, outs.cond)
    mail.move(s.head, outs.head)
    chunk_rows = s.data_in.shape[1] // 2
    grid_rows = chunk_rows // GRID
    cols = s.waves[16:32, :]
    chunk_ids = [place.t, place.across[1], place.core[1], place.diagonal[1]]
    for j in range(4):
        low = pl.ds(j * chunk_rows, chunk_rows)
        s.noisy[low, :] = s.data_in[j, 0:chunk_rows, :].astype(jnp.bfloat16)
        s.noise[low, :] = s.data_in[j, chunk_rows : 2 * chunk_rows, :]
        for i in range(grid_rows):
            row = s.waves[pl.ds(chunk_ids[j] * grid_rows + i, 1), :]
            s.resid[pl.ds(j * chunk_rows + i * GRID, GRID), :] = cols + row
    mail.move(s.noisy, outs.noisy)
    for n in range(0, D, 256):
        s.resid[:, n : n + 256] += mm_nt(s.noisy[...], s.head[n : n + 256, :])

    def piece(index):
        return s.pieces[index : index + 1, :]

    def normalize(which, shift, scale, target, low):
        value = s.resid[low : low + HALF, :]
        centred = value - jnp.mean(value, axis=-1, keepdims=True)
        inverse = lax.rsqrt(jnp.mean(centred * centred, axis=-1, keepdims=True) + norm_eps)
        normed = centred * inverse
        s.normed[which, low : low + HALF, :] = normed
        s.inverse[which, low : low + HALF, :] = jnp.broadcast_to(inverse, (HALF, LANES))
        target[low : low + HALF, :] = (normed * (1.0 + scale) + shift).astype(jnp.bfloat16)

    low_mask = half_mask(TOKENS, False)
    high_mask = half_mask(TOKENS, True)
    for l in range(LAYERS):
        base = 6 * l
        hidden = s.hidden.at[l]
        for low in (0, HALF):
            normalize(2 * l, piece(base), piece(base + 1), hidden, low)
        if l == 0:
            attn[0].pass_y((1, 2, 3))
            attn[1].pass_z()
            down[0].start_z()
        attn[l].pass_x()
        for x in range(2):
            weight = s.wattn.at[l, x]
            qkv = s.qkv.at[l, x]
            for n in range(0, D, 256):
                qkv[:, n : n + 256] = mm(hidden[...], weight[:, n : n + 256]).astype(jnp.bfloat16)
        for x in range(2):
            qkv = s.qkv.at[l, x]
            att = s.att.at[l, x]
            for h, (q, k, v, keep) in enumerate(
                ((0, 1, 2, low_mask), (0, 1, 2, high_mask), (3, 4, 5, low_mask))
            ):
                query = qkv[:, q * LANES : (q + 1) * LANES].astype(jnp.float32)
                query = jnp.where(keep, query, 0.0)
                key = qkv[:, k * LANES : (k + 1) * LANES]
                value = qkv[:, v * LANES : (v + 1) * LANES]
                scores = mm_nt(query.astype(jnp.bfloat16), key) * HEAD_DIM ** (-0.5)
                exped = jnp.exp(scores - jnp.max(scores, axis=-1, keepdims=True))
                probs = exped / jnp.sum(exped, axis=-1, keepdims=True)
                s.probs[l, x, h] = probs
                mixed = mm(probs.astype(jnp.bfloat16), value)
                if h != 1:
                    mixed = pltpu.roll(mixed, 64, 1)
                att[:, h * LANES : (h + 1) * LANES] = jnp.where(high_mask, mixed, 0.0).astype(
                    jnp.bfloat16
                )
        up[l].pass_z()
        if l == 0:
            up[1].start_z()
        for n in range(0, D, 256):
            total = mm_nt(s.att[l, 0], s.wattn[l, 0, n : n + 256, 384:768])
            total = total + mm_nt(s.att[l, 1], s.wattn[l, 1, n : n + 256, 384:768])
            s.core_out[l, :, n : n + 256] = total.astype(jnp.bfloat16)
        summed = mail.send(s.core_out.at[l], s.core_in.at[l], place.core)
        gate = piece(base + 2)
        summed.wait_recv()
        for low in (0, HALF):
            output = s.core_out[l, low : low + HALF, :].astype(jnp.float32)
            output = output + s.core_in[l, HALF - low : 2 * HALF - low, :].astype(jnp.float32)
            s.attn_out[l, low : low + HALF, :] = output
            s.resid[low : low + HALF, :] += gate * output
        rows = s.rows.at[l]
        normalize(2 * l + 1, piece(base + 3), piece(base + 4), rows, 0)
        far = mail.send(rows.at[pl.ds(0, HALF)], rows.at[pl.ds(2 * HALF, HALF)], place.across)
        normalize(2 * l + 1, piece(base + 3), piece(base + 4), rows, HALF)
        for source, target in (
            (s.hidden, outs.hidden),
            (s.qkv, outs.qkv),
            (s.att, outs.att),
            (s.probs, outs.probs),
            (s.attn_out, outs.attn_out),
            (s.wattn, outs.wattn),
        ):
            mail.move(source.at[l], target.at[l])
        if l == 0:
            attn[1].pass_y()
        up[l].pass_y()
        up[l].pass_x()
        w_up = s.wmlp.at[l, 0]
        w_down = s.wmlp.at[l, 1]

        def rise(low, size):
            for n in range(0, D, 256):
                upward = mm(rows[low : low + size, :], w_up[:, n : n + 256])
                s.upward[l, low : low + size, n : n + 256] = upward
                s.active[l, low : low + size, n : n + 256] = (
                    upward * gelu_parts(upward)
                ).astype(jnp.bfloat16)

        rise(0, HALF)
        rise(HALF, HALF)
        far.wait_recv()
        side = mail.send(
            rows.at[pl.ds(2 * HALF, HALF)], rows.at[pl.ds(3 * HALF, HALF)], place.core
        )
        rise(2 * HALF, HALF)
        side.wait_recv()
        rise(3 * HALF, HALF)
        if l == LAYERS - 1:
            down[l].start_y()
        down[l].pass_z()
        if l == 0:
            down[1].start_z()
        down[l].pass_y()
        down[l].pass_x()

        def fall(low, target):
            for n in range(0, D, 256):
                part = mm_nt(s.active[l, low : low + HALF, :], w_down[n : n + 256, :])
                target[:, n : n + 256] = part.astype(target.dtype)

        sum_out, sum_in, keep = (s.sum_out.at[l], s.sum_in.at[l], s.keep)
        fall(3 * HALF, sum_out.at[0])
        first = mail.send(sum_out.at[0], sum_in.at[0], place.core)
        fall(2 * HALF, keep.at[0])
        fall(HALF, sum_out.at[1])
        second = mail.send(sum_out.at[1], sum_in.at[1], place.core)
        first.wait_recv()
        s.far_out[l] = (keep[0] + sum_in[0].astype(jnp.float32)).astype(jnp.bfloat16)
        third = mail.send(s.far_out.at[l], s.far_in.at[l], place.across)
        fall(0, keep.at[1])
        second.wait_recv()
        keep[1] = keep[1] + sum_in[1].astype(jnp.float32)
        for source, target in (
            (s.rows, outs.rows),
            (s.upward, outs.upward),
            (s.active, outs.active),
            (s.wmlp, outs.wmlp),
        ):
            mail.move(source.at[l], target.at[l])
        third.wait_recv()
        total = (keep[1] + s.far_in[l].astype(jnp.float32)).astype(jnp.bfloat16)
        s.own_out[l] = total
        fourth = mail.send(s.own_out.at[l], s.own_in.at[l], place.core)
        gate = piece(base + 5)
        output = total.astype(jnp.float32)
        s.mlp_out[l, 0:HALF, :] = output
        s.resid[0:HALF, :] += gate * output
        fourth.wait_recv()
        output = s.own_in[l].astype(jnp.float32)
        s.mlp_out[l, HALF : 2 * HALF, :] = output
        s.resid[HALF : 2 * HALF, :] += gate * output
        mail.move(s.mlp_out.at[l], outs.mlp_out.at[l])

    for low in (0, HALF):
        normalize(
            2 * LAYERS, piece(6 * LAYERS), piece(6 * LAYERS + 1), s.final_low, low
        )
    predicted = mm(s.final_low[...], s.head[...])
    lanes = lax.broadcasted_iota(jnp.int32, (TOKENS, LANES), 1)
    taken = (lanes >= PATCH_DIM) & (lanes < 2 * PATCH_DIM)
    difference = jnp.where(taken, predicted - s.noise[...], 0.0)
    square = difference[0:HALF] * difference[0:HALF]
    s.loss[...] = jnp.sum(square.reshape(HALF // 8, 8, LANES), axis=0)
    s.grad_pred[...] = (difference * (2.0 / total_entries)).astype(jnp.bfloat16)
    for source, target in (
        (s.normed, outs.normed),
        (s.inverse, outs.inverse),
        (s.final_low, outs.final_low),
        (s.loss, outs.loss),
        (s.grad_pred, outs.grad_pred),
    ):
        mail.move(source, target)
    waited = [head_kept, data_kept, mod_kept] + [g.kept for g in attn + up + down]
    mail.finish(waited)


FORWARD_OUTS = dict(
    wattn=((LAYERS, 2, D, D), jnp.bfloat16),
    wmlp=((LAYERS, 2, D, D), jnp.bfloat16),
    head=((D, LANES), jnp.bfloat16),
    pieces=((16, D), jnp.float32),
    cond=((2, 2, 4, D), jnp.float32),
    hidden=((LAYERS, TOKENS, D), jnp.bfloat16),
    qkv=((LAYERS, 2, TOKENS, D), jnp.bfloat16),
    att=((LAYERS, 2, TOKENS, D // 2), jnp.bfloat16),
    probs=((LAYERS, 2, 3, TOKENS, TOKENS), jnp.float32),
    attn_out=((LAYERS, TOKENS, D), jnp.float32),
    rows=((LAYERS, 2 * TOKENS, D), jnp.bfloat16),
    upward=((LAYERS, 2 * TOKENS, D), jnp.float32),
    active=((LAYERS, 2 * TOKENS, D), jnp.bfloat16),
    mlp_out=((LAYERS, TOKENS, D), jnp.float32),
    normed=((2 * LAYERS + 1, TOKENS, D), jnp.float32),
    inverse=((2 * LAYERS + 1, TOKENS, LANES), jnp.float32),
    final_low=((TOKENS, D), jnp.bfloat16),
    noisy=((TOKENS, LANES), jnp.bfloat16),
    grad_pred=((TOKENS, LANES), jnp.bfloat16),
    loss=((8, LANES), jnp.float32),
)
FORWARD_OWN = dict(
    order=((8 * LANES, D), jnp.bfloat16),
    waves=((32, D), jnp.float32),
    cond_in=((7, 4, D), jnp.float32),
    data_in=((4, HALF, LANES), jnp.float32),
    noise=((TOKENS, LANES), jnp.float32),
    mod_out=((8, 16, LANES), jnp.float32),
    mod_in=((8, 16, LANES), jnp.float32),
    mod_rows=((16, 8 * LANES), jnp.float32),
    resid=((TOKENS, D), jnp.float32),
    core_out=((LAYERS, TOKENS, D), jnp.bfloat16),
    core_in=((LAYERS, TOKENS, D), jnp.bfloat16),
    sum_out=((LAYERS, 2, HALF, D), jnp.bfloat16),
    sum_in=((LAYERS, 2, HALF, D), jnp.bfloat16),
    far_out=((LAYERS, HALF, D), jnp.bfloat16),
    far_in=((LAYERS, HALF, D), jnp.bfloat16),
    own_out=((LAYERS, HALF, D), jnp.bfloat16),
    own_in=((LAYERS, HALF, D), jnp.bfloat16),
    keep=((2, HALF, D), jnp.float32),
)
FORWARD_SCRATCH = {**FORWARD_OUTS, **FORWARD_OWN}


def run_forward(inputs, total_entries):
    vmem = pl.BlockSpec(memory_space=pltpu.VMEM)
    outs = pl.pallas_call(
        partial(forward_kernel, {name: value.shape for name, value in inputs.items()}, total_entries),
        out_shape=[jax.ShapeDtypeStruct(*spec) for spec in FORWARD_OUTS.values()],
        in_specs=[vmem] * len(inputs),
        out_specs=[pl.BlockSpec(memory_space=pl.ANY)] * len(FORWARD_OUTS),
        scratch_shapes=[pltpu.VMEM(*spec) for spec in FORWARD_SCRATCH.values()]
        + [
            pltpu.SemaphoreType.DMA((128,)),
            pltpu.SemaphoreType.DMA((128,)),
            pltpu.SemaphoreType.DMA((48,)),
        ],
        compiler_params=pltpu.CompilerParams(
            collective_id=0, has_side_effects=True, vmem_limit_bytes=VMEM_LIMIT
        ),
    )(*inputs.values())
    return SimpleNamespace(**dict(zip(FORWARD_OUTS, outs)))
class Scatter:
    def __init__(self, place, mail, grad, from_y, from_z, result, other=None, from_x=None):
        self.place, self.mail, self.grad, self.result = (place, mail, grad, result)
        self.from_y, self.from_z, self.other, self.from_x = (from_y, from_z, other, from_x)
        self.rows = result.shape[0]
        self.x_copies, self.y_copies, self.z_copies = ({}, {}, {})

    def at(self, ref, slot):
        return ref.at[pl.ds(slot * self.rows, self.rows)]

    def start(self, slots=(4, 5, 6, 7)):
        for slot in slots:
            if self.other is None:
                self.send_y(slot)
            else:
                self.x_copies[slot] = self.mail.send(
                    self.at(self.other, slot), self.at(self.from_x, slot), self.place.across
                )

    def send_y(self, slot):
        self.y_copies[slot - 4] = self.mail.send(
            self.at(self.grad, slot), self.at(self.from_y, slot - 4), self.place.pair
        )

    def total(self, slot, refs):
        low = slot * self.rows
        value = self.grad[low : low + self.rows, :].astype(jnp.float32)
        for ref in refs:
            value = value + ref[low : low + self.rows, :].astype(jnp.float32)
        return value

    def pass_x(self):
        for slot in (4, 5, 6, 7):
            if self.other is not None:
                self.x_copies[slot].wait_recv()
                low = slot * self.rows
                self.grad[low : low + self.rows, :] = self.total(slot, [self.from_x]).astype(
                    jnp.bfloat16
                )
                self.send_y(slot)

    def pass_y(self):
        refs = [self.from_y] if self.other is None else [self.from_x, self.from_y]
        for slot in (1, 2, 3, 0):
            if self.other is not None:
                self.x_copies[slot].wait_recv()
            self.y_copies[slot].wait_recv()
            value = self.total(slot, refs)
            if slot == 0:
                self.result[...] = value
            else:
                low = slot * self.rows
                self.grad[low : low + self.rows, :] = value.astype(jnp.bfloat16)
                self.z_copies[slot] = self.mail.send(
                    self.at(self.grad, slot), self.from_z.at[slot - 1], self.place.up_z(slot)
                )

    def pass_z(self):
        value = self.result[...]
        for slot in (1, 2, 3):
            self.z_copies[slot].wait_recv()
            value = value + self.from_z[slot - 1].astype(jnp.float32)
        self.result[...] = value


def gelu_slope(value):
    const = math.sqrt(2.0 / math.pi)
    square = value * value
    tanh = jnp.tanh(const * (value + 0.044715 * (square * value)))
    return 0.5 * (1.0 + tanh) + 0.5 * value * (1.0 - tanh * tanh) * (
        const * (1.0 + (3.0 * 0.044715) * square)
    )


def backward_kernel(*refs):
    r = SimpleNamespace(**dict(zip(BACKWARD_INS, refs)))
    rest = refs[len(BACKWARD_INS) :]
    outs = SimpleNamespace(**dict(zip(BACKWARD_OUTS, rest)))
    rest = rest[len(BACKWARD_OUTS) :]
    s = SimpleNamespace(**dict(zip(BACKWARD_SCRATCH, rest)))
    rest = rest[len(BACKWARD_SCRATCH) :]
    mail = Mail(*rest)
    place = Place()
    loaded = {}
    waited = []

    def load(name, index=None):
        source = getattr(r, name)
        source = source if index is None else source.at[index]
        loaded[name] = mail.move(source, getattr(s, name))

    def need(*names):
        for name in names:
            if name in loaded:
                copy = loaded.pop(name)
                copy.wait()
                waited.append(copy)

    for name in FINAL_KEPT:
        load(name)
    for name in list(MLP_KEPT) + list(ATTN_KEPT):
        load(name, LAYERS - 1)
    greet(place)

    head_rows = D // 8
    across_index = place.t // 2
    rows_id = lax.broadcasted_iota(jnp.int32, (LANES, D), 0)
    offset = lax.broadcasted_iota(jnp.int32, (LANES, D), 1) - rows_id
    for owner in range(8):
        hit = (offset == place.slot_of(owner) * head_rows) & (rows_id < head_rows)
        s.order[pl.ds(owner * LANES, LANES), :] = jnp.where(hit, 1.0, 0.0).astype(jnp.bfloat16)
    s.mod_grad[...] = jnp.zeros_like(s.mod_grad)
    s.mod_send[...] = jnp.zeros_like(s.mod_send)

    def piece(index):
        return s.pieces[index : index + 1, :]

    def norm_back(which, mod_row, low, first):
        mixed = s.mixed[low : low + HALF, :]
        normed = s.normed[which, low : low + HALF, :]
        inverse = s.inverse[which, low : low + HALF, 0:1]
        if low == 0:
            s.mod_grad[mod_row : mod_row + 1, :] = jnp.sum(mixed, axis=0, keepdims=True)
            s.mod_grad[mod_row + 1 : mod_row + 2, :] = jnp.sum(
                mixed * normed, axis=0, keepdims=True
            )
        scaled = mixed * (1.0 + piece(mod_row + 1))
        centred = scaled - jnp.mean(scaled, axis=-1, keepdims=True)
        grad = (centred - normed * jnp.mean(scaled * normed, axis=-1, keepdims=True)) * inverse
        if first:
            s.grad[low : low + HALF, :] = grad
        else:
            s.grad[low : low + HALF, :] += grad

    need(*FINAL_KEPT)
    s.head_grad[...] = mm_tn(s.final_low[0:HALF, :], s.grad_pred[0:HALF, :])
    for n in range(0, D, 256):
        s.mixed[:, n : n + 256] = mm_nt(s.grad_pred[...], s.head[n : n + 256, :])
    for low in (0, HALF):
        norm_back(2 * LAYERS, 6 * LAYERS, low, True)

    def scatter(l, kind, index, other=None):
        if other is None:
            return Scatter(
                place, mail, s.mlp_grad.at[l, index], s.from_y.at[l, kind],
                s.from_z.at[l, kind], s.result.at[l, kind],
            )
        return Scatter(
            place, mail, s.attn_grad.at[l, 0], s.from_y.at[l, kind],
            s.from_z.at[l, kind], s.result.at[l, kind],
            s.attn_grad.at[l, 1], s.from_x.at[l],
        )

    attn = [scatter(l, 0, 0, True) for l in range(LAYERS)]
    up = [scatter(l, 1, 0) for l in range(LAYERS)]
    down = [scatter(l, 2, 1) for l in range(LAYERS)]

    low_mask = half_mask(TOKENS, False)
    high_mask = half_mask(TOKENS, True)
    for l in reversed(range(LAYERS)):
        base = 6 * l
        last = l == LAYERS - 1
        gate = piece(base + 5)
        need(*list(MLP_KEPT)[:1])
        grads = s.grad_rows.at[l]
        grads[0:HALF, :] = (gate * s.grad[0:HALF, :]).astype(jnp.bfloat16)
        far = mail.send(grads.at[pl.ds(0, HALF)], grads.at[pl.ds(2 * HALF, HALF)], place.across)
        grads[HALF : 2 * HALF, :] = (gate * s.grad[HALF : 2 * HALF, :]).astype(jnp.bfloat16)
        s.mod_grad[base + 5 : base + 6, :] = jnp.sum(
            s.grad[0:HALF, :] * s.mlp_out[0:HALF, :], axis=0, keepdims=True
        )
        if not last:
            attn[1].start((4, 5, 6))
            down[1].pass_y()
        need(*MLP_KEPT)
        w_up, w_down = (s.wmlp.at[0], s.wmlp.at[1])

        def drop(low):
            for n in range(0, D, 256):
                part = mm(grads[low : low + HALF, :], w_down[:, n : n + 256])
                slope = gelu_slope(s.upward[low : low + HALF, n : n + 256])
                s.grad_up[low : low + HALF, n : n + 256] = (part * slope).astype(jnp.bfloat16)

        drop(0)
        drop(HALF)
        far.wait_recv()
        side = mail.send(
            grads.at[pl.ds(2 * HALF, HALF)], grads.at[pl.ds(3 * HALF, HALF)], place.core
        )
        drop(2 * HALF)
        side.wait_recv()
        drop(3 * HALF)

        def fall(low, target):
            for n in range(0, D, 256):
                part = mm_nt(s.grad_up[low : low + HALF, :], w_up[n : n + 256, :])
                target[:, n : n + 256] = part.astype(target.dtype)

        sum_out, sum_in, keep = (s.sum_out.at[l], s.sum_in.at[l], s.keep)
        fall(3 * HALF, sum_out.at[0])
        first = mail.send(sum_out.at[0], sum_in.at[0], place.core)
        fall(2 * HALF, keep.at[0])
        fall(HALF, sum_out.at[1])
        second = mail.send(sum_out.at[1], sum_in.at[1], place.core)
        first.wait_recv()
        s.far_out[l] = (keep[0] + sum_in[0].astype(jnp.float32)).astype(jnp.bfloat16)
        third = mail.send(s.far_out.at[l], s.far_in.at[l], place.across)
        if not last:
            attn[1].start((7, 1, 2, 3, 0))
            up[1].pass_y()
        fall(0, keep.at[1])
        for n in range(0, D, 256):
            s.mlp_grad[l, 1, :, n : n + 256] = mm_tn(
                grads[...], s.active[:, n : n + 256]
            ).astype(jnp.bfloat16)
        down[l].start()
        second.wait_recv()
        keep[1] = keep[1] + sum_in[1].astype(jnp.float32)
        third.wait_recv()
        total = (keep[1] + s.far_in[l].astype(jnp.float32)).astype(jnp.bfloat16)
        s.own_out[l] = total
        fourth = mail.send(s.own_out.at[l], s.own_in.at[l], place.core)
        s.mixed[0:HALF, :] = total.astype(jnp.float32)
        norm_back(2 * l + 1, base + 3, 0, False)
        fourth.wait_recv()
        s.mixed[HALF : 2 * HALF, :] = s.own_in[l].astype(jnp.float32)
        norm_back(2 * l + 1, base + 3, HALF, False)
        for n in range(0, D, 256):
            s.mlp_grad[l, 0, :, n : n + 256] = mm_tn(
                s.rows[...], s.grad_up[:, n : n + 256]
            ).astype(jnp.bfloat16)
        up[l].start()
        if last:
            for name in MLP_KEPT:
                load(name, 0)

        gate = piece(base + 2)
        need(*ATTN_KEPT)
        both = s.both
        both[0:TOKENS, :] = s.hidden[...]
        both[TOKENS : 2 * TOKENS, :] = (gate * s.grad[...]).astype(jnp.bfloat16)
        s.mod_grad[base + 2 : base + 3, :] = jnp.sum(
            s.grad[0:HALF, :] * s.attn_out[0:HALF, :], axis=0, keepdims=True
        )
        scale = HEAD_DIM ** (-0.5)
        for x in range(2):
            qkv = s.qkv.at[x]
            grad_qkv = s.grad_qkv.at[x]

            def tile(ref, index):
                return ref[:, index * LANES : (index + 1) * LANES]

            def put(index, value):
                grad_qkv[0:TOKENS, index * LANES : (index + 1) * LANES] = value.astype(jnp.bfloat16)

            found = {}
            for h, (q, k, v, keep_mask) in enumerate(
                ((0, 1, 2, low_mask), (0, 1, 2, high_mask), (3, 4, 5, low_mask))
            ):
                weight = s.wattn[x, :, (3 + h) * LANES : (4 + h) * LANES]
                grad_att = mm(both[TOKENS : 2 * TOKENS, :], weight)
                if h != 1:
                    grad_att = pltpu.roll(grad_att, 64, 1)
                grad_att = jnp.where(keep_mask, grad_att, 0.0).astype(jnp.bfloat16)
                probs = s.probs[x, h]
                grad_probs = mm_nt(grad_att, tile(qkv, v))
                inner = jnp.sum(probs * grad_probs, axis=-1, keepdims=True)
                grad_scores = (probs * (grad_probs - inner)).astype(jnp.bfloat16)
                found[h] = (
                    jnp.where(keep_mask, mm(grad_scores, tile(qkv, k)) * scale, 0.0),
                    jnp.where(keep_mask, mm_tn(grad_scores, tile(qkv, q)) * scale, 0.0),
                    mm_tn(probs.astype(jnp.bfloat16), grad_att),
                )
                if h == 1:
                    for index in range(3):
                        put(index, found[0][index] + found[1][index])
                if h == 2:
                    for index in range(3):
                        put(3 + index, found[2][index])
        for n in range(0, D, 256):
            part = mm_nt(s.grad_qkv[0, 0:TOKENS, :], s.wattn[0, n : n + 256, :])
            part = part + mm_nt(s.grad_qkv[1, 0:TOKENS, :], s.wattn[1, n : n + 256, :])
            s.core_out[l, :, n : n + 256] = part.astype(jnp.bfloat16)
        summed = mail.send(s.core_out.at[l], s.core_in.at[l], place.core)
        for x in (1, 0):
            s.grad_qkv[x, TOKENS : 2 * TOKENS, D // 2 : D] = s.att[x]
            half = s.grad_qkv[x, 0:TOKENS, 0 : D // 2]
            s.attn_grad[l, x, :, 0 : D // 2] = mm_tn(both[0:TOKENS, :], half).astype(jnp.bfloat16)
            half = s.grad_qkv[x, :, D // 2 : D]
            s.attn_grad[l, x, :, D // 2 : D] = mm_tn(both[...], half).astype(jnp.bfloat16)
            if x == 1 and not last:
                attn[0].start()
        if not last:
            attn[1].pass_x()
        summed.wait_recv()
        for low in (0, HALF):
            value = s.core_out[l, low : low + HALF, :].astype(jnp.float32)
            s.mixed[low : low + HALF, :] = value + s.core_in[
                l, HALF - low : 2 * HALF - low, :
            ].astype(jnp.float32)
            norm_back(2 * l, base, low, False)
        if last:
            for name in ATTN_KEPT:
                load(name, 0)

    mod_first = mail.send(s.mod_grad, s.mod_other, place.core)
    s.head_grad[...] += mm_tn(
        s.grad[0:HALF, :].astype(jnp.bfloat16), s.noisy[0:HALF, :]
    )
    head_first = mail.send(s.head_grad, s.head_other, place.core)
    down[0].pass_y()
    mod_first.wait_recv()
    summed = (s.mod_grad[...] + s.mod_other[...]).astype(jnp.bfloat16)
    blocks = r.cond_weight.shape[0]
    for owner in range(8):
        part = mm_nt(summed, s.order[owner * LANES : (owner + 1) * LANES, :])
        s.mod_rows[:, owner * LANES : (owner + 1) * LANES] = part
    for g in range(8 * blocks):
        row, owner = (g // 8, g % 8)
        s.mod_send[g // blocks, g % blocks : g % blocks + 1, :] = s.mod_rows[
            row : row + 1, owner * LANES : (owner + 1) * LANES
        ]
    back_from = []
    for k in range(1, 8):
        source = s.mod_send.at[lax.rem(place.f + k, 8)]
        back_from.append(mail.send(source, s.back.at[0, k], place.up_f(k)))
    back_own = mail.move(s.mod_send.at[place.f], s.back.at[0, 0])
    head_first.wait_recv()
    s.head_low[...] = (s.head_grad[...] + s.head_other[...]).astype(jnp.bfloat16)
    head_second = mail.send(s.head_low, s.head_far, place.across)
    back_own.wait()
    for copy in back_from:
        copy.wait_recv()
    back_far = mail.send(s.back.at[0], s.back.at[1], place.across)
    attn[0].start((1, 2, 3, 0))
    head_second.wait_recv()
    half = 4 * head_rows
    head_total = s.head_low[...].astype(jnp.float32) + s.head_far[...].astype(jnp.float32)
    s.head_mid[...] = head_total
    s.head_sum[...] = head_total.astype(jnp.bfloat16)
    head_third = mail.send(s.head_sum.at[pl.ds(half, half)], s.head_y, place.pair)
    back_far.wait_recv()
    for i in range(16):
        x_part = lax.rem(across_index + i % 2, 2)
        k = lax.rem(place.f + 8 - i // 2, 8)
        s.back_rows[i] = s.back[x_part, k]
    partial_cond = jnp.zeros((16, D), jnp.float32)
    for b in range(blocks):
        block = s.back_rows[:, b, 0:head_rows].astype(jnp.bfloat16)
        partial_cond = partial_cond + mm(block, r.cond_weight[b])
    s.cond_out[...] = partial_cond
    cond_from = [
        mail.send(s.cond_out, s.cond_in.at[k - 1], place.up_f(k)) for k in range(1, 8)
    ]
    mail.move(s.back_rows, outs.back_rows)
    up[0].pass_y()
    attn[1].pass_y()
    attn[0].pass_x()
    head_third.wait_recv()
    head_from = []
    for k in range(1, 4):
        low = k * head_rows
        value = s.head_mid[low : low + head_rows, :] + s.head_y[
            low : low + head_rows, :
        ].astype(jnp.float32)
        s.head_sum[low : low + head_rows, :] = value.astype(jnp.bfloat16)
        head_from.append(
            mail.send(
                s.head_sum.at[pl.ds(low, head_rows)], s.head_z.at[k - 1], place.up_z(k)
            )
        )
    head_own = s.head_mid[0:head_rows, :] + s.head_y[0:head_rows, :].astype(jnp.float32)
    value = s.cond_out[...]
    for k in range(7):
        cond_from[k].wait_recv()
        value = value + s.cond_in[k]
    for c in range(16):
        s.cond_rows[c : c + 1, :] = r.cond[c % 2, c // 8, c // 2 % 4 : c // 2 % 4 + 1, :]
    cond = s.cond_rows[...]
    sigmoid = jax.nn.sigmoid(cond)
    cond_act = (cond * sigmoid).astype(jnp.bfloat16)
    cond_grad = (value * (sigmoid * (1.0 + cond * (1.0 - sigmoid)))).astype(jnp.bfloat16)
    s.time_grad[...] = mm_tn(r.time_hidden[...], cond_grad)
    mail.move(s.time_grad, outs.time_grad)
    time_pre = r.time_pre[...]
    sigmoid = jax.nn.sigmoid(time_pre)
    slope = sigmoid * (1.0 + time_pre * (1.0 - sigmoid))
    pre_grad = (mm_nt(cond_grad, r.low_time[...]) * slope).astype(jnp.bfloat16)
    s.first_grad[...] = mm_tn(r.features[...], pre_grad)
    mail.move(s.first_grad, outs.first_grad)
    column = lax.broadcasted_iota(jnp.int32, (D, head_rows), 0)
    column = column - lax.broadcasted_iota(jnp.int32, (D, head_rows), 1)
    picked = jnp.where(column == place.f * head_rows, 1.0, 0.0).astype(jnp.bfloat16)
    own_cols = mm(cond_grad, picked).astype(jnp.bfloat16)
    s.label_grad[...] = mm_tn(r.label_hot[...], own_cols)
    mail.move(s.label_grad, outs.label_grad)
    shared = jnp.sum(s.time_grad[...] * s.time_grad[...])
    shared = shared + jnp.sum(s.first_grad[...] * s.first_grad[...])
    shared = shared + jnp.sum(s.label_grad[...] * s.label_grad[...])
    bias = s.back_rows[0]
    for c in range(1, 16):
        bias = bias + s.back_rows[c]
    shared = shared + jnp.sum(bias * bias)
    weight_squares = jnp.zeros((8, D), jnp.float32)
    for c in range(blocks):
        block = mm_tn(s.back_rows[:, c, 0:head_rows].astype(jnp.bfloat16), cond_act)
        weight_squares = weight_squares + jnp.sum(
            (block * block).reshape(head_rows // 8, 8, D), axis=0
        )
    shared = shared + jnp.sum(weight_squares)
    for k in range(3):
        head_from[k].wait_recv()
        head_own = head_own + s.head_z[k].astype(jnp.float32)
    s.head_result[...] = head_own
    shared = shared + jnp.sum(head_own * head_own)
    mail.move(s.head_result, outs.head_result)
    squares = jnp.zeros((8, D), jnp.float32)
    for item in (down[1], up[1], down[0], up[0], attn[1], attn[0]):
        if item is attn[0]:
            attn[0].pass_y()
        item.pass_z()
        grad = item.result[...]
        squares = squares + jnp.sum((grad * grad).reshape(head_rows // 8, 8, D), axis=0)
    mail.move(s.result, outs.result)

    owned = jnp.where(place.t == 0, 1.0, 0.0)
    total = jnp.sum(squares) + owned * shared
    tile_rows = lax.broadcasted_iota(jnp.int32, (8, LANES), 0)
    s.part[...] = jnp.where(tile_rows == 0, total, jnp.sum(r.loss[...]))
    s.by_fsdp[place.f] = s.part[...]
    copies = [mail.send(s.part, s.by_fsdp.at[place.f], place.up_f(k)) for k in range(1, 8)]
    for copy in copies:
        copy.wait_recv()
    value = s.by_fsdp[0]
    for k in range(1, 8):
        value = value + s.by_fsdp[k]
    s.group[...] = value
    s.by_tp[place.t] = value
    copies = [
        mail.send(s.group, s.by_tp.at[place.t], device)
        for device in (place.core, place.across, place.diagonal)
    ]
    for copy in copies:
        copy.wait_recv()
    s.totals[...] = s.by_tp[0] + s.by_tp[1] + s.by_tp[2] + s.by_tp[3]
    mail.move(s.totals, outs.totals)
    mail.finish(waited + [back_own])


FINAL_KEPT = dict(
    grad_pred=None, head=None, final_low=None, normed=None, inverse=None, pieces=None, noisy=None
)
MLP_KEPT = dict(mlp_out=None, wmlp=None, upward=None, active=None, rows=None)
ATTN_KEPT = dict(attn_out=None, wattn=None, qkv=None, probs=None, hidden=None, att=None)
SMALL_INS = dict(
    cond_weight=None,
    cond=None,
    loss=None,
    time_hidden=None,
    low_time=None,
    features=None,
    time_pre=None,
    label_hot=None,
)
BACKWARD_INS = SMALL_INS | FINAL_KEPT | MLP_KEPT | ATTN_KEPT
BACKWARD_OUTS = dict(
    result=((LAYERS, 3, D // 8, D), jnp.float32),
    head_result=((D // 8, LANES), jnp.float32),
    back_rows=((16, 16, LANES), jnp.float32),
    time_grad=((D // 8, D), jnp.float32),
    first_grad=((FREQ, D // 8), jnp.float32),
    label_grad=((NCLASS, D // 8), jnp.float32),
    totals=((8, LANES), jnp.float32),
)
BACKWARD_OWN = dict(
    cond_rows=((16, D), jnp.float32),
    part=((8, LANES), jnp.float32),
    group=((8, LANES), jnp.float32),
    by_fsdp=((8, 8, LANES), jnp.float32),
    by_tp=((4, 8, LANES), jnp.float32),
    order=((8 * LANES, D), jnp.bfloat16),
    mod_grad=((16, D), jnp.float32),
    mod_other=((16, D), jnp.float32),
    mod_rows=((16, 8 * LANES), jnp.float32),
    mod_send=((8, 16, LANES), jnp.float32),
    back=((2, 8, 16, LANES), jnp.float32),
    cond_out=((16, D), jnp.float32),
    cond_in=((7, 16, D), jnp.float32),
    head_grad=((D, LANES), jnp.float32),
    head_other=((D, LANES), jnp.float32),
    head_mid=((D, LANES), jnp.float32),
    head_low=((D, LANES), jnp.bfloat16),
    head_far=((D, LANES), jnp.bfloat16),
    head_sum=((D, LANES), jnp.bfloat16),
    head_y=((D // 2, LANES), jnp.bfloat16),
    head_z=((3, D // 8, LANES), jnp.bfloat16),
    grad=((TOKENS, D), jnp.float32),
    mixed=((TOKENS, D), jnp.float32),
    grad_rows=((LAYERS, 2 * TOKENS, D), jnp.bfloat16),
    grad_up=((2 * TOKENS, D), jnp.bfloat16),
    both=((2 * TOKENS, D), jnp.bfloat16),
    grad_qkv=((2, 2 * TOKENS, D), jnp.bfloat16),
    sum_out=((LAYERS, 2, HALF, D), jnp.bfloat16),
    sum_in=((LAYERS, 2, HALF, D), jnp.bfloat16),
    far_out=((LAYERS, HALF, D), jnp.bfloat16),
    far_in=((LAYERS, HALF, D), jnp.bfloat16),
    own_out=((LAYERS, HALF, D), jnp.bfloat16),
    own_in=((LAYERS, HALF, D), jnp.bfloat16),
    keep=((2, HALF, D), jnp.float32),
    core_out=((LAYERS, TOKENS, D), jnp.bfloat16),
    core_in=((LAYERS, TOKENS, D), jnp.bfloat16),
    mlp_grad=((LAYERS, 2, D, D), jnp.bfloat16),
    attn_grad=((LAYERS, 2, D, D), jnp.bfloat16),
    from_x=((LAYERS, D, D), jnp.bfloat16),
    from_y=((LAYERS, 3, D // 2, D), jnp.bfloat16),
    from_z=((LAYERS, 3, 3, D // 8, D), jnp.bfloat16),
)


def backward_scratch():
    layered = MLP_KEPT | ATTN_KEPT
    specs = {}
    for name in BACKWARD_INS:
        if name not in SMALL_INS:
            shape, dtype = FORWARD_OUTS[name]
            specs[name] = (shape[1:] if name in layered else shape, dtype)
    for name in BACKWARD_OUTS:
        specs[name] = BACKWARD_OUTS[name]
    specs.update(BACKWARD_OWN)
    return specs


BACKWARD_SCRATCH = backward_scratch()


def run_backward(kept, inputs):
    anywhere = pl.BlockSpec(memory_space=pl.ANY)
    vmem = pl.BlockSpec(memory_space=pltpu.VMEM)
    given = [
        getattr(kept if hasattr(kept, name) else inputs, name) for name in BACKWARD_INS
    ]
    outs = pl.pallas_call(
        backward_kernel,
        out_shape=[jax.ShapeDtypeStruct(*spec) for spec in BACKWARD_OUTS.values()],
        in_specs=[vmem if name in SMALL_INS else anywhere for name in BACKWARD_INS],
        out_specs=[anywhere] * len(BACKWARD_OUTS),
        scratch_shapes=[pltpu.VMEM(*spec) for spec in BACKWARD_SCRATCH.values()]
        + [
            pltpu.SemaphoreType.DMA((128,)),
            pltpu.SemaphoreType.DMA((128,)),
            pltpu.SemaphoreType.DMA((48,)),
        ],
        compiler_params=pltpu.CompilerParams(
            collective_id=1, has_side_effects=True, vmem_limit_bytes=VMEM_LIMIT
        ),
    )(*given)
    return SimpleNamespace(**dict(zip(BACKWARD_OUTS, outs)))


def shard_tiles(attn_weight):
    q, k, v, o = (attn_weight[:, j].astype(jnp.bfloat16) for j in range(4))
    return jnp.concatenate(
        [
            q[..., :128],
            k[..., :128],
            v[..., :128],
            q[..., 128:],
            o[..., :64],
            k[..., 128:],
            o[..., 64:128],
            v[..., 128:],
            o[..., 128:],
        ],
        axis=-1,
    )


def tile_grads(grad):
    q = jnp.concatenate([grad[..., 0:128], grad[..., 384:448]], axis=-1)
    k = jnp.concatenate([grad[..., 128:256], grad[..., 512:576]], axis=-1)
    v = jnp.concatenate([grad[..., 256:384], grad[..., 640:704]], axis=-1)
    o = jnp.concatenate([grad[..., 448:512], grad[..., 576:640], grad[..., 704:768]], axis=-1)
    return jnp.stack([q, k, v, o], axis=1)


def wave_table():
    quarter = D // 4
    omegas = 1.0 / np.power(10000.0, np.arange(quarter, dtype=np.float32) / quarter)
    angles = np.arange(GRID, dtype=np.float32)[:, None] * omegas.astype(np.float32)[None, :]
    waves = np.concatenate([np.sin(angles), np.cos(angles)], axis=1).astype(np.float32)
    table = np.zeros((2 * GRID, D), np.float32)
    table[:GRID, : D // 2] = waves
    table[GRID:, D // 2 :] = waves
    padded = np.zeros((2 * GRID, 8, LANES), np.float32)
    padded[:, :, : D // 8] = table.reshape(2 * GRID, 8, D // 8)
    left = padded.reshape(2 * GRID, 8 * LANES)
    parts = []
    for _ in range(3):
        part = left.astype(jnp.bfloat16)
        parts.append(part)
        left = left - part.astype(np.float32)
    return np.concatenate(parts, axis=0)


def body_kernels(
    routes,
    latents,
    noise,
    timesteps,
    labels,
    step_count,
    tables,
    time_weight,
    cond_weight,
    cond_bias,
    attn_weight,
    mlp_weight,
    *states,
):
    fsdp_index = lax.axis_index("fsdp")
    tp_index = lax.axis_index("tp")
    across_index = tp_index // 2
    num_fsdp = routes.num_fsdp
    col_share = tables.shape[1]
    all_latents = timesteps.shape[0]
    total_entries = all_latents * SEQ * PATCH_DIM
    col_start = fsdp_index * col_share
    low_tables = tables.astype(jnp.bfloat16)
    blocks = cond_bias.shape[0] // col_share

    features = timestep_features(timesteps).astype(jnp.bfloat16)
    time_pre = jnp.dot(
        features,
        low_tables[2 * PATCH_DIM : 2 * PATCH_DIM + FREQ],
        preferred_element_type=jnp.float32,
    )
    time_hidden = jax.nn.silu(time_pre).astype(jnp.bfloat16)
    label_hot = (labels[:, None] == jnp.arange(NCLASS, dtype=jnp.int32)[None, :]).astype(
        jnp.bfloat16
    )
    label_part = jnp.dot(
        label_hot, low_tables[2 * PATCH_DIM + FREQ :], preferred_element_type=jnp.float32
    )
    low_time = time_weight.astype(jnp.bfloat16)
    cond_part = jnp.dot(time_hidden, low_time, preferred_element_type=jnp.float32)
    placed = lax.dynamic_update_slice(
        jnp.zeros((all_latents, D), jnp.float32), label_part, (0, col_start)
    )
    low_cond = cond_weight.astype(jnp.bfloat16)
    low_bias = cond_bias.astype(jnp.bfloat16).astype(jnp.float32)

    latent_id = fsdp_index * latents.shape[0]
    share = signal_share(lax.dynamic_slice_in_dim(timesteps, latent_id, latents.shape[0]))
    share = share[:, None, None]
    noisy = (jnp.sqrt(share) * latents + jnp.sqrt(1.0 - share) * noise).astype(jnp.bfloat16)
    data = jnp.concatenate(
        [
            jnp.pad(noisy.astype(jnp.float32), ((0, 0), (0, 0), (0, LANES - PATCH_DIM))),
            jnp.pad(noise, ((0, 0), (0, 0), (PATCH_DIM, LANES - 2 * PATCH_DIM))),
        ],
        axis=1,
    )
    shards = jnp.concatenate(
        [shard_tiles(attn_weight)[:, None], mlp_weight.astype(jnp.bfloat16)], axis=1
    )
    head = jnp.pad(low_tables[: 2 * PATCH_DIM].T, ((0, 0), (0, LANES - 2 * PATCH_DIM)))
    cond_part = (cond_part + placed).reshape(num_fsdp, 2, D).transpose(1, 0, 2)
    inputs = SimpleNamespace(
        cond_part=cond_part.reshape(2, 2, num_fsdp // 2, D),
        shards=shards,
        data=data,
        head=head,
        waves=jnp.asarray(wave_table()),
        cond_weight=low_cond.reshape(blocks, col_share, D),
        cond_bias=low_bias.reshape(blocks, col_share),
    )
    kept = run_forward(vars(inputs), total_entries)
    inputs.time_hidden = time_hidden
    inputs.low_time = low_time
    inputs.features = features
    inputs.time_pre = time_pre
    inputs.label_hot = label_hot
    back = run_backward(kept, inputs)

    cond = kept.cond.reshape(2, num_fsdp, D).transpose(1, 0, 2).reshape(all_latents, D)
    cond_act = jax.nn.silu(cond).astype(jnp.bfloat16)
    head_cols = back.head_result[:, : 2 * PATCH_DIM].T
    modul_back = back.back_rows[:, :blocks, :col_share].reshape(all_latents, -1)
    modul_back = modul_back.astype(jnp.bfloat16)
    cond_grad_w = dot_f32(modul_back, cond_act, 0, 0)
    bias_grad = jnp.sum(modul_back.astype(jnp.float32), axis=0)
    time_grad = back.time_grad
    tables_grad = jnp.concatenate([head_cols, back.first_grad, back.label_grad], axis=0)
    loss = back.totals[1, 0] / total_entries
    norm = jnp.sqrt(back.totals[0, 0])
    entries = NTAB * D + D * D + (D + 1) * NCOND + LAYERS * (4 * D * D + 2 * D * FF)
    limit = clip_scale * math.sqrt(entries / (all_latents * SEQ))
    factor = jnp.minimum(1.0, limit / norm)
    count = step_count[0].astype(jnp.float32)
    attn_grad = tile_grads(back.result[:, 0])
    mlp_grad = back.result[:, 1:]
    weights_all = (tables, time_weight, cond_weight, cond_bias, attn_weight, mlp_weight)
    grads_all = (tables_grad, time_grad, cond_grad_w, bias_grad, attn_grad, mlp_grad)
    states = tuple(zip(states[0::2], states[1::2]))
    results = [loss, norm]
    for weight, grad, state in zip(weights_all, grads_all, states):
        results.extend(adam_update(weight, grad * factor, state[0], state[1], count))
    return tuple(results)


def body(routes, *args):
    if routes.num_fsdp == 8 and args[5].shape[1] % 16 == 0:
        return body_kernels(routes, *args)
    return body_steps(routes, *args)


def solution(mesh):
    vectors = P("fsdp")
    columns = P(None, "fsdp")
    rows = P("fsdp", None)
    blocks = P(None, None, "fsdp", "tp")
    data = P("fsdp", "tp", None)
    weights = (columns, rows, rows, vectors, blocks, blocks)
    states = tuple(spec for spec in weights for _ in range(2))
    updated = tuple(spec for spec in weights for _ in range(3))
    return jax.shard_map(
        partial(body, Routes(mesh)),
        mesh=mesh,
        in_specs=(data, data, P(), P(), P()) + weights + states,
        out_specs=(P(), P()) + updated,
        check_vma=False,
    )
```

```python
from functools import partial
import math
from types import SimpleNamespace

import jax
import jax.numpy as jnp
from jax import lax
import numpy as np
from jax.experimental import pallas as pl
from jax.experimental.pallas import tpu as pltpu
from jax.sharding import PartitionSpec as P

D = 768
HEAD_DIM = 64
FF = 3072
NCLASS = 1000
FREQ = 256
PATCH_DIM = 16
GRID = 16
LAYERS = 2
SEQ = 256
NCOND = 10752
NTAB = 1288


norm_eps = 1e-06
beta_first = 0.9
beta_second = 0.999
adam_eps = 1e-08
learn_rate = 0.2
weight_decay = 0.01
clip_scale = 0.002
diffusion_steps = 1000.0


def timestep_features(timesteps):
    half_width = FREQ // 2
    omegas = jnp.exp(-math.log(10000.0) * jnp.arange(half_width, dtype=jnp.float32) / half_width)
    angles = timesteps.astype(jnp.float32)[:, None] * omegas[None, :]
    return jnp.concatenate([jnp.cos(angles), jnp.sin(angles)], axis=1)


def signal_share(timesteps):
    phase = (timesteps.astype(jnp.float32) / diffusion_steps + 0.008) / 1.008 * (math.pi / 2)
    return jnp.cos(phase) ** 2


def butterfly_bits(number):
    bits = []
    bit = 1
    while bit < number:
        bits.append(bit)
        bit *= 2
    return bits


def split_radices(number):
    radices = []
    while number > 1:
        radix = 4 if number % 4 == 0 else 2
        radices.append(radix)
        number //= radix
    return radices


class Routes:
    def __init__(self, mesh):
        self.num_fsdp = mesh.shape["fsdp"]
        self.num_tp = mesh.shape["tp"]
        self.outer = split_radices(self.num_fsdp // 2)

    def core(self, value):
        return lax.ppermute(value, "tp", [(t, t ^ 1) for t in range(self.num_tp)])

    def across(self, value):
        return lax.ppermute(value, "tp", [(t, t ^ 2) for t in range(self.num_tp)])

    def pair(self, value):
        return lax.ppermute(value, "fsdp", [(f, f ^ 1) for f in range(self.num_fsdp)])

    def shift(self, value, stride, radix, amount):
        pairs = []
        for f in range(self.num_fsdp):
            digit = (f // stride) % radix
            pairs.append((f, f + ((digit + amount) % radix - digit) * stride))
        return lax.ppermute(value, "fsdp", pairs)

    def slot_owner(self, fsdp_index, slots):
        per_pair = self.num_fsdp // 2
        pair_part = (slots // per_pair + fsdp_index) % 2
        rest = slots % per_pair
        owner = pair_part
        stride = 2
        for radix in self.outer:
            digit = (rest + fsdp_index // stride) % radix
            owner = owner + digit * stride
            rest = rest // radix
            stride *= radix
        return owner

    def gather_outer(self, block):
        stride = 2
        for radix in self.outer:
            block = jnp.concatenate(
                [block] + [self.shift(block, stride, radix, -k) for k in range(1, radix)], axis=0
            )
            stride *= radix
        return block

    def gather_rows(self, block):
        held = self.gather_outer(block)
        return jnp.concatenate([held, self.pair(held)], axis=0)

    def gather_both(self, block, across_last):
        held = self.gather_outer(block)
        if across_last:
            own = jnp.concatenate([held, self.pair(held)], axis=0)
            return (own, self.across(own))
        other = self.across(held)
        return (
            jnp.concatenate([held, self.pair(held)], axis=0),
            jnp.concatenate([other, self.pair(other)], axis=0),
        )

    def scatter_rows(self, total, dtype=jnp.bfloat16):
        half = total.shape[0] // 2
        received = self.pair(total[half:].astype(dtype))
        held = total[:half] + received.astype(jnp.float32)
        strides = []
        stride = 2
        for radix in self.outer:
            strides.append(stride)
            stride *= radix
        for radix, stride in reversed(list(zip(self.outer, strides))):
            size = held.shape[0] // radix
            parts = [
                self.shift(held[k * size : (k + 1) * size].astype(dtype), stride, radix, k)
                for k in range(1, radix)
            ]
            held = held[:size]
            for part in parts:
                held = held + part.astype(jnp.float32)
        return held

    def scatter_both(self, own, other):
        received = self.across(other.astype(jnp.bfloat16))
        return self.scatter_rows(own + received.astype(jnp.float32))

    def sum_fsdp(self, value):
        for bit in butterfly_bits(self.num_fsdp):
            value = value + lax.ppermute(
                value, "fsdp", [(f, f ^ bit) for f in range(self.num_fsdp)]
            )
        return value

    def sum_all(self, value):
        value = value + self.core(value)
        value = value + self.across(value)
        return self.sum_fsdp(value)


def after(value, *earlier):
    return lax.optimization_barrier((value,) + earlier)[0]


def dot_f32(left, right, left_dim, right_dim):
    return lax.dot_general(
        left, right, (((left_dim,), (right_dim,)), ((), ())), preferred_element_type=jnp.float32
    )


def layer_norm(values):
    centred = values - jnp.mean(values, axis=-1, keepdims=True)
    inverse = lax.rsqrt(jnp.mean(centred * centred, axis=-1, keepdims=True) + norm_eps)
    return (centred * inverse, inverse)


def modulate(values, shift, scale):
    normed, inverse = layer_norm(values)
    return ((normed * (1.0 + scale) + shift).astype(jnp.bfloat16), normed, inverse)


def norm_backward(grad_mixed, normed, inverse, scale, counted):
    grad_shift = jnp.sum(grad_mixed[:counted], axis=0)
    grad_scale = jnp.sum(grad_mixed[:counted] * normed[:counted], axis=0)
    grad_normed = grad_mixed * (1.0 + scale)
    centred = grad_normed - jnp.mean(grad_normed, axis=-1, keepdims=True)
    grad_input = (
        centred - normed * jnp.mean(grad_normed * normed, axis=-1, keepdims=True)
    ) * inverse
    return (grad_input, grad_shift, grad_scale)


def core_sum(routes, partial):
    low = partial.astype(jnp.bfloat16)
    far = routes.core(low)
    half = far.shape[0] // 2
    swapped = jnp.concatenate([far[half:], far[:half]], axis=0)
    return low.astype(jnp.float32) + swapped.astype(jnp.float32)


def attend(routes, hidden, weights):
    seq_len = hidden.shape[0]
    query_key = jnp.stack([dot_f32(hidden, w, 1, 0) for w in weights[0]]).astype(jnp.bfloat16)
    value_out = jnp.stack([dot_f32(hidden, w, 1, 0) for w in weights[1]]).astype(jnp.bfloat16)
    width = query_key.shape[2] // 2
    local_heads = width // HEAD_DIM
    query_key = query_key.reshape(2, seq_len, 2 * local_heads, HEAD_DIM)
    query, key = (query_key[:, :, :local_heads], query_key[:, :, local_heads:])
    value = value_out[:, :, :width].reshape(2, seq_len, local_heads, HEAD_DIM)
    scores = jnp.einsum(
        "xqhe,xkhe->xhqk", query, key, preferred_element_type=jnp.float32
    ) * HEAD_DIM ** (-0.5)
    exped = jnp.exp(scores - jnp.max(scores, axis=-1, keepdims=True))
    probs = exped / jnp.sum(exped, axis=-1, keepdims=True)
    attended = jnp.einsum(
        "xhqk,xkhe->xqhe", probs.astype(jnp.bfloat16), value, preferred_element_type=jnp.float32
    )
    attended = attended.astype(jnp.bfloat16).reshape(2, seq_len, width)
    padded = jnp.concatenate([jnp.zeros_like(attended), attended], axis=2)
    partial_out = dot_f32(padded[0], weights[1][0], 1, 1) + dot_f32(padded[1], weights[1][1], 1, 1)
    return (core_sum(routes, partial_out), (hidden, query, key, value, probs, padded))


def attend_backward(routes, grad_full, kept, weights):
    hidden, query, key, value, probs, padded = kept
    seq_len = hidden.shape[0]
    scale = HEAD_DIM ** (-0.5)
    width = padded.shape[2] // 2
    local_heads = width // HEAD_DIM
    grad_attended = jnp.stack([dot_f32(grad_full, w, 1, 0) for w in weights[1]])
    grad_attended = grad_attended[:, :, width:].astype(jnp.bfloat16)
    grad_attended = grad_attended.reshape(2, seq_len, local_heads, HEAD_DIM)
    grad_probs = jnp.einsum(
        "xqhe,xkhe->xhqk", grad_attended, value, preferred_element_type=jnp.float32
    )
    grad_value = jnp.einsum(
        "xhqk,xqhe->xkhe",
        probs.astype(jnp.bfloat16),
        grad_attended,
        preferred_element_type=jnp.float32,
    )
    inner = jnp.sum(probs * grad_probs, axis=-1, keepdims=True)
    grad_scores = (probs * (grad_probs - inner)).astype(jnp.bfloat16)
    grad_query = (
        jnp.einsum("xhqk,xkhe->xqhe", grad_scores, key, preferred_element_type=jnp.float32) * scale
    )
    grad_key = (
        jnp.einsum("xhqk,xqhe->xkhe", grad_scores, query, preferred_element_type=jnp.float32) * scale
    )
    grad_qk = jnp.concatenate([grad_query, grad_key], axis=2).astype(jnp.bfloat16)
    grad_qk = grad_qk.reshape(2, seq_len, 2 * width)
    grad_v = grad_value.astype(jnp.bfloat16).reshape(2, seq_len, width)
    grad_v = jnp.concatenate([grad_v, jnp.zeros_like(grad_v)], axis=2)
    grad_hidden = jnp.zeros(hidden.shape, jnp.float32)
    for k in range(2):
        grad_hidden = grad_hidden + dot_f32(grad_qk[k], weights[0][k], 1, 1)
        grad_hidden = grad_hidden + dot_f32(grad_v[k], weights[1][k], 1, 1)
    grad_hidden = core_sum(routes, grad_hidden)
    qk_own, qk_other = [dot_f32(hidden, grad_qk[k], 0, 0) for k in range(2)]
    both = jnp.concatenate([hidden, grad_full], axis=0)
    vo_own, vo_other = [
        dot_f32(both, jnp.concatenate([grad_v[k], padded[k]], axis=0), 0, 0) for k in range(2)
    ]
    grads = (routes.scatter_both(qk_own, qk_other), routes.scatter_both(vo_own, vo_other))
    return (grad_hidden, grads)


def share_rows(routes, rows):
    half = rows.shape[0] // 2
    far = routes.across(rows[:half])
    return jnp.concatenate([rows, far, routes.core(far)], axis=0)


def sum_rows(routes, partial):
    half = partial.shape[0] // 4
    low = partial.astype(jnp.bfloat16)
    received = routes.core(jnp.concatenate([low[3 * half :], low[half : 2 * half]], axis=0))
    received = received.astype(jnp.float32)
    far_sum = (partial[2 * half : 3 * half] + received[:half]).astype(jnp.bfloat16)
    own_sum = partial[:half] + received[half:]
    own_total = (own_sum + routes.across(far_sum).astype(jnp.float32)).astype(jnp.bfloat16)
    return jnp.concatenate([own_total, routes.core(own_total)], axis=0).astype(jnp.float32)


def feed_forward(routes, hidden, weights):
    rows = share_rows(routes, hidden)
    upward = dot_f32(rows, weights[0], 1, 0)
    active = jax.nn.gelu(upward, approximate=True).astype(jnp.bfloat16)
    output = sum_rows(routes, dot_f32(active, weights[1], 1, 1))
    return (output, (rows, upward, active))


def feed_backward(routes, grad_full, kept, weights):
    rows, upward, active = kept
    grad_rows = share_rows(routes, grad_full)
    grad_active = dot_f32(grad_rows, weights[1], 1, 0)
    slope = jax.vjp(partial(jax.nn.gelu, approximate=True), upward)[1]
    grad_up = slope(grad_active)[0].astype(jnp.bfloat16)
    grad_hidden = sum_rows(routes, dot_f32(grad_up, weights[0], 1, 1))
    grad_down_w = routes.scatter_rows(dot_f32(grad_rows, active, 0, 0))
    grad_up_w = routes.scatter_rows(dot_f32(rows, grad_up, 0, 0))
    return (grad_hidden, (grad_up_w, grad_down_w))


def branch_forward(routes, resid, pieces, inner_fn, weights):
    shift, scale, gate = pieces
    hidden, normed, inverse = modulate(resid, shift, scale)
    output, kept = inner_fn(routes, hidden, weights)
    return (resid + gate * output, (normed, inverse, output, kept))


def branch_backward(routes, grad_resid, pieces, saved, inner_back, weights):
    shift, scale, gate = pieces
    normed, inverse, output, kept = saved
    counted = grad_resid.shape[0] // 2
    grad_gate = jnp.sum(grad_resid[:counted] * output[:counted], axis=0)
    grad_output = (gate * grad_resid).astype(jnp.bfloat16)
    grad_mixed, grads = inner_back(routes, grad_output, kept, weights)
    grad_input, grad_shift, grad_scale = norm_backward(grad_mixed, normed, inverse, scale, counted)
    return (grad_resid + grad_input, [grad_shift, grad_scale, grad_gate], grads)


def gather_weights(routes, attn_weight, mlp_weight):
    shards = []
    for layer in range(LAYERS):
        attn = attn_weight[layer].astype(jnp.bfloat16)
        mlp = mlp_weight[layer].astype(jnp.bfloat16)
        shards.append(
            (
                jnp.concatenate([attn[0], attn[1]], axis=1),
                jnp.concatenate([attn[2], attn[3]], axis=1),
                mlp[0],
                mlp[1],
            )
        )
    gathered = []
    earlier = []

    def in_turn(block):
        return after(block, earlier[-2]) if len(earlier) >= 2 else block

    for layer in range(LAYERS):
        query_key, value_out, up, down = shards[layer]
        pairs = []
        for block, across_last in ((query_key, True), (value_out, layer > 0)):
            both = routes.gather_both(in_turn(block), across_last)
            pairs.append(both)
            earlier.append(both[0])
        rows = []
        for block in (up, down):
            rows.append(routes.gather_rows(in_turn(block)))
            earlier.append(rows[-1])
        gathered.append((tuple(pairs), tuple(rows)))
    return gathered


def adam_update(weight, grad, first, second, count):
    first_new = beta_first * first + (1.0 - beta_first) * grad
    second_new = beta_second * second + (1.0 - beta_second) * grad * grad
    first_hat = first_new / (1.0 - jnp.power(beta_first, count))
    second_hat = second_new / (1.0 - jnp.power(beta_second, count))
    weight_new = weight - learn_rate * (
        first_hat / (jnp.sqrt(second_hat) + adam_eps) + weight_decay * weight
    )
    return [weight_new, first_new, second_new]


def body_steps(
    routes,
    latents,
    noise,
    timesteps,
    labels,
    step_count,
    tables,
    time_weight,
    cond_weight,
    cond_bias,
    attn_weight,
    mlp_weight,
    tables_first,
    tables_second,
    time_first,
    time_second,
    cond_first,
    cond_second,
    bias_first,
    bias_second,
    attn_first,
    attn_second,
    mlp_first,
    mlp_second,
):
    fsdp_index = lax.axis_index("fsdp")
    tp_index = lax.axis_index("tp")
    across_index = tp_index // 2
    num_fsdp = routes.num_fsdp
    local_seq = latents.shape[1]
    col_share = tables.shape[1]
    all_latents = timesteps.shape[0]
    total_entries = all_latents * SEQ * PATCH_DIM
    col_start = fsdp_index * col_share
    low_tables = tables.astype(jnp.bfloat16)

    gathered = gather_weights(routes, attn_weight, mlp_weight)
    head = routes.gather_rows(low_tables[: 2 * PATCH_DIM].T)

    features = timestep_features(timesteps).astype(jnp.bfloat16)
    time_pre = jnp.dot(
        features,
        low_tables[2 * PATCH_DIM : 2 * PATCH_DIM + FREQ],
        preferred_element_type=jnp.float32,
    )
    time_hidden = jax.nn.silu(time_pre).astype(jnp.bfloat16)
    label_hot = (labels[:, None] == jnp.arange(NCLASS, dtype=jnp.int32)[None, :]).astype(
        jnp.bfloat16
    )
    label_part = jnp.dot(
        label_hot, low_tables[2 * PATCH_DIM + FREQ :], preferred_element_type=jnp.float32
    )
    low_time = time_weight.astype(jnp.bfloat16)
    cond_part = jnp.dot(time_hidden, low_time, preferred_element_type=jnp.float32)
    placed = lax.dynamic_update_slice(
        jnp.zeros((all_latents, D), jnp.float32), label_part, (0, col_start)
    )
    cond = routes.sum_fsdp(cond_part + placed)
    cond_act = jax.nn.silu(cond).astype(jnp.bfloat16)
    low_cond = cond_weight.astype(jnp.bfloat16)
    low_bias = cond_bias.astype(jnp.bfloat16).astype(jnp.float32)
    mod_part = dot_f32(cond_act, low_cond, 1, 1) + low_bias[None, :]
    modul = lax.all_to_all(
        mod_part.astype(jnp.bfloat16), "fsdp", split_axis=0, concat_axis=1, tiled=True
    )
    modul = lax.dynamic_slice_in_dim(modul, across_index, 1, 0)

    slots = jnp.arange(num_fsdp, dtype=jnp.int32)
    owners = routes.slot_owner(fsdp_index, slots)
    slot_hot = (owners[:, None] == slots[None, :]).astype(jnp.bfloat16)
    pieces_all = jnp.einsum(
        "pfr,sf->psr",
        modul.reshape(-1, num_fsdp, col_share),
        slot_hot,
        preferred_element_type=jnp.float32,
    ).reshape(-1, D)

    data = jnp.stack([latents, noise], axis=1)
    own_data = lax.dynamic_index_in_dim(data, across_index, 0, keepdims=False)
    far_data = lax.dynamic_index_in_dim(data, 1 - across_index, 0, keepdims=False)
    first_data = jnp.concatenate([own_data, routes.across(far_data)], axis=1)
    chip_data = jnp.concatenate([first_data, routes.core(first_data)], axis=1)
    clean, noise_part = (chip_data[0], chip_data[1])
    chunks = jnp.stack([tp_index, tp_index ^ 2, tp_index ^ 1, tp_index ^ 3])
    token_ids = (
        chunks[:, None] * local_seq + jnp.arange(local_seq, dtype=jnp.int32)[None, :]
    ).reshape(-1)
    counted = token_ids.shape[0] // 2

    quarter = D // 4
    col_ids = (
        owners[:, None] * col_share + jnp.arange(col_share, dtype=jnp.int32)[None, :]
    ).reshape(-1)
    omegas = 1.0 / jnp.power(10000.0, (col_ids % quarter).astype(jnp.float32) / quarter)
    angles = jnp.arange(GRID, dtype=jnp.float32)[:, None] * omegas[None, :]
    kinds = (col_ids // quarter)[None, :]
    waves = jnp.where(kinds % 2 == 0, jnp.sin(angles), jnp.cos(angles))
    row_waves = jnp.where(kinds < 2, waves, 0.0)
    col_waves = jnp.where(kinds >= 2, waves, 0.0)
    grid_ids = jnp.arange(GRID, dtype=jnp.int32)[None, :]
    row_hot = (token_ids[:, None] // GRID == grid_ids).astype(jnp.float32)
    col_hot = (token_ids[:, None] % GRID == grid_ids).astype(jnp.float32)
    positions = jnp.dot(
        jnp.concatenate([row_hot, col_hot], axis=1),
        jnp.concatenate([row_waves, col_waves], axis=0),
        precision=lax.Precision.HIGHEST,
    )

    latent_id = fsdp_index * latents.shape[0] + across_index
    share = signal_share(lax.dynamic_slice_in_dim(timesteps, latent_id, 1))[:, None]
    noisy = (jnp.sqrt(share) * clean + jnp.sqrt(1.0 - share) * noise_part).astype(jnp.bfloat16)
    resid = dot_f32(noisy, head[:, :PATCH_DIM], 1, 1) + positions

    saved = []
    for layer in range(LAYERS):
        pieces = [pieces_all[6 * layer + k][None, :] for k in range(6)]
        attn_w, mlp_w = gathered[layer]
        resid, attn_saved = branch_forward(routes, resid, pieces[:3], attend, attn_w)
        resid, mlp_saved = branch_forward(routes, resid, pieces[3:], feed_forward, mlp_w)
        saved.append((attn_saved, mlp_saved))
    final_shift = pieces_all[6 * LAYERS][None, :]
    final_scale = pieces_all[6 * LAYERS + 1][None, :]
    final_low, final_normed, final_inverse = modulate(resid, final_shift, final_scale)
    predicted = dot_f32(final_low, head[:, PATCH_DIM:], 1, 0)
    difference = predicted - noise_part
    loss_part = jnp.sum(difference[:counted] * difference[:counted])
    grad_pred = (difference * (2.0 / total_entries)).astype(jnp.bfloat16)
    output_grad = dot_f32(final_low[:counted], grad_pred[:counted], 0, 0)
    grad_final = dot_f32(grad_pred, head[:, PATCH_DIM:], 1, 1)
    grad_resid, grad_fshift, grad_fscale = norm_backward(
        grad_final, final_normed, final_inverse, final_scale, counted
    )
    layer_mods = [None] * LAYERS
    layer_grads = [None] * LAYERS
    for layer in reversed(range(LAYERS)):
        pieces = [pieces_all[6 * layer + k][None, :] for k in range(6)]
        attn_w, mlp_w = gathered[layer]
        grad_resid, mlp_mods, mlp_grads = branch_backward(
            routes, grad_resid, pieces[3:], saved[layer][1], feed_backward, mlp_w
        )
        grad_resid, attn_mods, attn_grads = branch_backward(
            routes, grad_resid, pieces[:3], saved[layer][0], attend_backward, attn_w
        )
        layer_mods[layer] = attn_mods + mlp_mods
        layer_grads[layer] = attn_grads + mlp_grads
    grad_embed = grad_resid.astype(jnp.bfloat16)
    patch_grad = dot_f32(grad_embed[:counted], noisy[:counted], 0, 0)

    head_grad = jnp.concatenate([patch_grad, output_grad], axis=1)
    head_grad = head_grad + routes.core(head_grad)
    head_grad = head_grad + routes.across(head_grad)
    head_cols = routes.scatter_rows(head_grad, jnp.float32).T

    modul_grad = jnp.stack(layer_mods[0] + layer_mods[1] + [grad_fshift, grad_fscale])
    modul_grad = (modul_grad + routes.core(modul_grad)).astype(jnp.bfloat16)
    modul_grad = jnp.einsum(
        "psr,sf->pfr",
        modul_grad.reshape(-1, num_fsdp, col_share),
        slot_hot,
        preferred_element_type=jnp.float32,
    ).astype(jnp.bfloat16)
    modul_back = lax.all_to_all(
        modul_grad.reshape(num_fsdp, -1), "fsdp", split_axis=0, concat_axis=0, tiled=True
    )
    far_back = routes.across(modul_back)
    is_first = across_index == 0
    modul_back = jnp.stack(
        [jnp.where(is_first, modul_back, far_back), jnp.where(is_first, far_back, modul_back)],
        axis=1,
    ).reshape(all_latents, -1)
    cond_grad_w = dot_f32(modul_back, cond_act, 0, 0)
    bias_grad = jnp.sum(modul_back.astype(jnp.float32), axis=0)
    grad_cond_act = routes.sum_fsdp(dot_f32(modul_back, low_cond, 1, 0))
    silu_slope = jax.vjp(jax.nn.silu, cond)[1]
    grad_cond = silu_slope(grad_cond_act)[0].astype(jnp.bfloat16)
    time_grad = dot_f32(time_hidden, grad_cond, 0, 0)
    grad_hidden = dot_f32(grad_cond, low_time, 1, 1)
    time_slope = jax.vjp(jax.nn.silu, time_pre)[1]
    grad_pre = time_slope(grad_hidden)[0].astype(jnp.bfloat16)
    first_layer_grad = dot_f32(features, grad_pre, 0, 0)
    cond_cols = lax.dynamic_slice_in_dim(grad_cond, col_start, col_share, 1)
    label_grad = dot_f32(label_hot, cond_cols, 0, 0)
    tables_grad = jnp.concatenate([head_cols, first_layer_grad, label_grad], axis=0)

    squares = sum(jnp.sum(part * part) for parts in layer_grads for part in parts)
    owner = (tp_index == 0).astype(jnp.float32)
    squares = squares + owner * sum(
        jnp.sum(part * part) for part in (tables_grad, time_grad, cond_grad_w, bias_grad)
    )
    totals = routes.sum_all(jnp.stack([loss_part, squares]))
    loss = totals[0] / total_entries
    norm = jnp.sqrt(totals[1])
    entries = NTAB * D + D * D + (D + 1) * NCOND + LAYERS * (4 * D * D + 2 * D * FF)
    limit = clip_scale * math.sqrt(entries / (all_latents * SEQ))
    factor = jnp.minimum(1.0, limit / norm)
    count = step_count[0].astype(jnp.float32)
    width = attn_weight.shape[3]
    attn_grad = jnp.stack(
        [
            jnp.stack([qk[:, :width], qk[:, width:], vo[:, :width], vo[:, width:]])
            for qk, vo, _, _ in layer_grads
        ]
    )
    mlp_grad = jnp.stack([jnp.stack([up, down]) for _, _, up, down in layer_grads])
    weights_all = (tables, time_weight, cond_weight, cond_bias, attn_weight, mlp_weight)
    grads_all = (tables_grad, time_grad, cond_grad_w, bias_grad, attn_grad, mlp_grad)
    states = (
        (tables_first, tables_second),
        (time_first, time_second),
        (cond_first, cond_second),
        (bias_first, bias_second),
        (attn_first, attn_second),
        (mlp_first, mlp_second),
    )
    results = [loss, norm]
    for weight, grad, state in zip(weights_all, grads_all, states):
        results.extend(adam_update(weight, grad * factor, state[0], state[1], count))
    return tuple(results)


MESH = pl.DeviceIdType.MESH
VMEM_LIMIT = 60 * 1024 * 1024
LANES = 128
HALF = 128
TOKENS = 256


class Place:
    def __init__(self):
        self.f = lax.axis_index("fsdp")
        self.t = lax.axis_index("tp")
        self.z = self.f // 2
        self.y = lax.rem(self.f, 2)
        self.core = (self.f, self.t + 1 - 2 * lax.rem(self.t, 2))
        self.across = (self.f, lax.rem(self.t + 2, 4))
        self.diagonal = (self.f, 3 - self.t)
        self.pair = (self.f + 1 - 2 * self.y, self.t)

    def down_z(self, k):
        return (lax.rem(self.z + 4 - k, 4) * 2 + self.y, self.t)

    def up_z(self, k):
        return (lax.rem(self.z + k, 4) * 2 + self.y, self.t)

    def up_f(self, k):
        return (lax.rem(self.f + k, 8), self.t)

    def slot_of(self, owner):
        pair_part = lax.rem(self.y + owner % 2, 2)
        return pair_part * 4 + lax.rem(owner // 2 + 4 - self.z, 4)


class Mail:
    def __init__(self, send_sem, recv_sem, local_sem):
        self.send_sem, self.recv_sem, self.local_sem = (send_sem, recv_sem, local_sem)
        self.sent = []
        self.local = []

    def send(self, source, target, device):
        index = len(self.sent)
        copy = pltpu.make_async_remote_copy(
            src_ref=source,
            dst_ref=target,
            send_sem=self.send_sem.at[index],
            recv_sem=self.recv_sem.at[index],
            device_id=device,
            device_id_type=MESH,
        )
        copy.start()
        self.sent.append(copy)
        return copy

    def move(self, source, target):
        copy = pltpu.make_async_copy(source, target, self.local_sem.at[len(self.local)])
        copy.start()
        self.local.append(copy)
        return copy

    def finish(self, skip=()):
        for copy in self.sent:
            copy.wait_send()
        for copy in self.local:
            if not any(copy is other for other in skip):
                copy.wait()


def greet(place):
    barrier = pltpu.get_barrier_semaphore()
    friends = [place.up_f(k) for k in range(1, 8)]
    friends += [place.core, place.across, place.diagonal]
    for device in friends:
        pl.semaphore_signal(barrier, inc=1, device_id=device, device_id_type=MESH)
    pl.semaphore_wait(barrier, len(friends))


def mm(left, right):
    return lax.dot_general(left, right, (((1,), (0,)), ((), ())), preferred_element_type=jnp.float32)


def mm_nt(left, right):
    return lax.dot_general(left, right, (((1,), (1,)), ((), ())), preferred_element_type=jnp.float32)


def mm_tn(left, right):
    return lax.dot_general(left, right, (((0,), (0,)), ((), ())), preferred_element_type=jnp.float32)


class Gather:
    def __init__(self, place, mail, shard, own, other=None):
        self.place, self.mail, self.shard, self.own, self.other = (place, mail, shard, own, other)
        self.rows = shard.shape[0]

    def at(self, ref, slot):
        return ref.at[pl.ds(slot * self.rows, self.rows)]

    def start_z(self):
        self.kept = self.mail.move(self.shard, self.at(self.own, 0))
        self.from_z = [
            self.mail.send(self.shard, self.at(self.own, k), self.place.down_z(k))
            for k in range(1, 4)
        ]

    def start_y(self):
        self.from_y = [self.mail.send(self.shard, self.at(self.own, 4), self.place.pair)]

    def start_x(self):
        self.from_x = [self.mail.send(self.shard, self.at(self.other, 0), self.place.across)]

    def pass_z(self):
        for k in range(1, 4):
            self.from_z[k - 1].wait_recv()
            block = self.at(self.own, k)
            self.from_y.append(self.mail.send(block, self.at(self.own, 4 + k), self.place.pair))
            if self.other is not None:
                self.from_x.append(self.mail.send(block, self.at(self.other, k), self.place.across))

    def pass_y(self, slots=(0, 1, 2, 3)):
        for k in slots:
            self.from_y[k].wait_recv()
            if self.other is not None:
                block = self.at(self.own, 4 + k)
                target = self.at(self.other, 4 + k)
                self.from_x.append(self.mail.send(block, target, self.place.across))

    def pass_x(self):
        if self.other is not None:
            for copy in self.from_x:
                copy.wait_recv()
        self.kept.wait()


def gelu_parts(value):
    inner = math.sqrt(2.0 / math.pi) * (value + 0.044715 * (value * value * value))
    return 0.5 * (1.0 + jnp.tanh(inner))


def half_mask(rows, upper):
    lanes = lax.broadcasted_iota(jnp.int32, (rows, LANES), 1)
    return lanes >= 64 if upper else lanes < 64


def forward_kernel(shapes, total_entries, *refs):
    names = list(shapes)
    r = SimpleNamespace(**dict(zip(names, refs)))
    rest = refs[len(names) :]
    outs = SimpleNamespace(**dict(zip(FORWARD_OUTS, rest)))
    rest = rest[len(FORWARD_OUTS) :]
    s = SimpleNamespace(**dict(zip(FORWARD_SCRATCH, rest)))
    rest = rest[len(FORWARD_SCRATCH) :]
    mail = Mail(*rest)
    place = Place()
    greet(place)

    attn = [
        Gather(place, mail, r.shards.at[l, 0], s.wattn.at[l, 0], s.wattn.at[l, 1])
        for l in range(LAYERS)
    ]
    up = [Gather(place, mail, r.shards.at[l, 1], s.wmlp.at[l, 0]) for l in range(LAYERS)]
    down = [Gather(place, mail, r.shards.at[l, 2], s.wmlp.at[l, 1]) for l in range(LAYERS)]

    across_index = place.t // 2
    core_index = lax.rem(place.t, 2)
    cond_loaded = mail.move(r.cond_weight, s.cond_weight)
    cond_own = r.cond_part.at[across_index, core_index]
    cond_from = [mail.send(cond_own, s.cond_in.at[k - 1], place.up_f(k)) for k in range(1, 8)]
    own_data = r.data.at[across_index]
    data_far = mail.send(r.data.at[1 - across_index], s.data_in.at[1], place.across)
    data_side = mail.send(own_data, s.data_in.at[2], place.core)
    attn[0].start_z()
    attn[0].start_y()
    attn[0].start_x()
    head_rows = r.head.shape[0]
    head_kept = mail.move(r.head, s.head.at[pl.ds(0, head_rows)])
    data_kept = mail.move(own_data, s.data_in.at[0])
    head_from = [
        mail.send(r.head, s.head.at[pl.ds(k * head_rows, head_rows)], place.down_z(k))
        for k in range(1, 4)
    ]
    attn[1].start_y()
    up[0].start_y()

    rows_id = lax.broadcasted_iota(jnp.int32, (LANES, D), 0)
    offset = lax.broadcasted_iota(jnp.int32, (LANES, D), 1) - rows_id
    for owner in range(8):
        hit = (offset == place.slot_of(owner) * head_rows) & (rows_id < head_rows)
        s.order[pl.ds(owner * LANES, LANES), :] = jnp.where(hit, 1.0, 0.0).astype(jnp.bfloat16)

    waves = mm(r.waves[...], s.order[...])
    s.waves[...] = waves[0:32] + waves[32:64] + waves[64:96]

    part = r.cond_part[across_index, core_index]
    for k in range(7):
        cond_from[k].wait_recv()
        part = part + s.cond_in[k]
    s.cond[across_index, core_index] = part
    cond_part = s.cond.at[across_index, core_index]
    cond_side = mail.send(cond_part, cond_part, place.core)
    data_far.wait_recv()
    data_diagonal = mail.send(s.data_in.at[1], s.data_in.at[3], place.core)
    attn[0].pass_y((0,))
    cond_side.wait_recv()
    cond_half = s.cond.at[across_index]
    cond_far = mail.send(cond_half, cond_half, place.across)
    cond = jnp.concatenate([s.cond[across_index, 0], s.cond[across_index, 1]], axis=0)
    cond_act = (cond * jax.nn.sigmoid(cond)).astype(jnp.bfloat16)
    blocks = r.cond_weight.shape[0]
    cond_loaded.wait()
    for b in range(blocks):
        part = mm_nt(cond_act, s.cond_weight[b].astype(jnp.bfloat16)) + r.cond_bias[b : b + 1, :]
        part = part.astype(jnp.bfloat16).astype(jnp.float32)
        for i in range(8):
            s.mod_out[i, b : b + 1, 0:head_rows] = part[i : i + 1, :]
    mod_from = []
    for k in range(1, 8):
        source = s.mod_out.at[lax.rem(place.f + k, 8)]
        mod_from.append(mail.send(source, s.mod_in.at[k], place.up_f(k)))
    mod_kept = mail.move(s.mod_out.at[place.f], s.mod_in.at[0])
    attn[1].start_z()

    attn[0].pass_z()
    up[0].start_z()
    for k in range(3):
        head_from[k].wait_recv()
    head_kept.wait()
    lower = s.head.at[pl.ds(0, 4 * head_rows)]
    upper = s.head.at[pl.ds(4 * head_rows, 4 * head_rows)]
    head_pair = mail.send(lower, upper, place.pair)
    attn[1].start_x()
    down[0].start_y()
    up[1].start_y()

    mod_kept.wait()
    for copy in mod_from:
        copy.wait_recv()
    s.mod_rows[...] = jnp.zeros_like(s.mod_rows)
    for g in range(8 * blocks):
        piece, owner = (g // 8, g % 8)
        k = lax.rem(place.f + 8 - g // blocks, 8)
        b = g % blocks
        s.mod_rows[piece : piece + 1, owner * LANES : owner * LANES + head_rows] = s.mod_in[
            k, b : b + 1, 0:head_rows
        ]
    s.pieces[...] = mm(s.mod_rows[...].astype(jnp.bfloat16), s.order[...])
    mail.move(s.pieces, outs.pieces)

    data_kept.wait()
    data_side.wait_recv()
    data_diagonal.wait_recv()
    head_pair.wait_recv()
    cond_far.wait_recv()
    mail.move(s.cond, outs.cond)
    mail.move(s.head, outs.head)
    chunk_rows = s.data_in.shape[1] // 2
    grid_rows = chunk_rows // GRID
    cols = s.waves[16:32, :]
    chunk_ids = [place.t, place.across[1], place.core[1], place.diagonal[1]]
    for j in range(4):
        low = pl.ds(j * chunk_rows, chunk_rows)
        s.noisy[low, :] = s.data_in[j, 0:chunk_rows, :].astype(jnp.bfloat16)
        s.noise[low, :] = s.data_in[j, chunk_rows : 2 * chunk_rows, :]
        for i in range(grid_rows):
            row = s.waves[pl.ds(chunk_ids[j] * grid_rows + i, 1), :]
            s.resid[pl.ds(j * chunk_rows + i * GRID, GRID), :] = cols + row
    mail.move(s.noisy, outs.noisy)
    for n in range(0, D, 256):
        s.resid[:, n : n + 256] += mm_nt(s.noisy[...], s.head[n : n + 256, :])

    def piece(index):
        return s.pieces[index : index + 1, :]

    def normalize(which, shift, scale, target, low):
        value = s.resid[low : low + HALF, :]
        centred = value - jnp.mean(value, axis=-1, keepdims=True)
        inverse = lax.rsqrt(jnp.mean(centred * centred, axis=-1, keepdims=True) + norm_eps)
        normed = centred * inverse
        s.normed[which, low : low + HALF, :] = normed
        s.inverse[which, low : low + HALF, :] = jnp.broadcast_to(inverse, (HALF, LANES))
        target[low : low + HALF, :] = (normed * (1.0 + scale) + shift).astype(jnp.bfloat16)
        if low:
            mail.move(s.normed.at[which], outs.normed.at[which])
            mail.move(s.inverse.at[which], outs.inverse.at[which])

    low_mask = half_mask(TOKENS, False)
    high_mask = half_mask(TOKENS, True)
    for l in range(LAYERS):
        base = 6 * l
        hidden = s.hidden.at[l]
        for low in (0, HALF):
            normalize(2 * l, piece(base), piece(base + 1), hidden, low)
        if l == 0:
            attn[0].pass_y((1, 2, 3))
            attn[1].pass_z()
            down[0].start_z()
        attn[l].pass_x()
        for x in range(2):
            weight = s.wattn.at[l, x]
            qkv = s.qkv.at[l, x]
            for n in range(0, D, 256):
                qkv[:, n : n + 256] = mm(hidden[...], weight[:, n : n + 256]).astype(jnp.bfloat16)
        for x in range(2):
            qkv = s.qkv.at[l, x]
            att = s.att.at[l, x]
            for h, (q, k, v, keep) in enumerate(
                ((0, 1, 2, low_mask), (0, 1, 2, high_mask), (3, 4, 5, low_mask))
            ):
                query = qkv[:, q * LANES : (q + 1) * LANES].astype(jnp.float32)
                query = jnp.where(keep, query, 0.0)
                key = qkv[:, k * LANES : (k + 1) * LANES]
                value = qkv[:, v * LANES : (v + 1) * LANES]
                scores = mm_nt(query.astype(jnp.bfloat16), key) * HEAD_DIM ** (-0.5)
                exped = jnp.exp(scores - jnp.max(scores, axis=-1, keepdims=True))
                probs = exped / jnp.sum(exped, axis=-1, keepdims=True)
                s.probs[l, x, h] = probs
                mixed = mm(probs.astype(jnp.bfloat16), value)
                if h != 1:
                    mixed = pltpu.roll(mixed, 64, 1)
                att[:, h * LANES : (h + 1) * LANES] = jnp.where(high_mask, mixed, 0.0).astype(
                    jnp.bfloat16
                )
            if x == 0 and l == 0:
                up[0].pass_z()
                up[1].start_z()
            elif x == 0:
                down[1].start_y()
                down[1].pass_z()
        for n in range(0, D, 256):
            total = mm_nt(s.att[l, 0], s.wattn[l, 0, n : n + 256, 384:768])
            total = total + mm_nt(s.att[l, 1], s.wattn[l, 1, n : n + 256, 384:768])
            s.core_out[l, :, n : n + 256] = total.astype(jnp.bfloat16)
        summed = mail.send(s.core_out.at[l], s.core_in.at[l], place.core)
        gate = piece(base + 2)
        summed.wait_recv()
        for low in (0, HALF):
            output = s.core_out[l, low : low + HALF, :].astype(jnp.float32)
            output = output + s.core_in[l, HALF - low : 2 * HALF - low, :].astype(jnp.float32)
            s.attn_out[l, low : low + HALF, :] = output
            s.resid[low : low + HALF, :] += gate * output
        rows = s.rows.at[l]
        normalize(2 * l + 1, piece(base + 3), piece(base + 4), rows, 0)
        far = mail.send(rows.at[pl.ds(0, HALF)], rows.at[pl.ds(2 * HALF, HALF)], place.across)
        normalize(2 * l + 1, piece(base + 3), piece(base + 4), rows, HALF)
        for source, target in (
            (s.hidden, outs.hidden),
            (s.qkv, outs.qkv),
            (s.att, outs.att),
            (s.probs, outs.probs),
            (s.attn_out, outs.attn_out),
            (s.wattn, outs.wattn),
        ):
            mail.move(source.at[l], target.at[l])
        if l == 0:
            attn[1].pass_y()
            down[0].pass_z()
            down[1].start_z()
        up[l].pass_y()
        up[l].pass_x()
        w_up = s.wmlp.at[l, 0]
        w_down = s.wmlp.at[l, 1]

        def rise(low, size):
            for n in range(0, D, 256):
                upward = mm(rows[low : low + size, :], w_up[:, n : n + 256])
                s.upward[l, low : low + size, n : n + 256] = upward
                s.active[l, low : low + size, n : n + 256] = (
                    upward * gelu_parts(upward)
                ).astype(jnp.bfloat16)

        rise(0, HALF)
        rise(HALF, HALF)
        far.wait_recv()
        side = mail.send(
            rows.at[pl.ds(2 * HALF, HALF)], rows.at[pl.ds(3 * HALF, HALF)], place.core
        )
        rise(2 * HALF, HALF)
        side.wait_recv()
        rise(3 * HALF, HALF)
        down[l].pass_y()
        down[l].pass_x()

        def fall(low, target):
            for n in range(0, D, 256):
                part = mm_nt(s.active[l, low : low + HALF, :], w_down[n : n + 256, :])
                target[:, n : n + 256] = part.astype(target.dtype)

        sum_out, sum_in, keep = (s.sum_out.at[l], s.sum_in.at[l], s.keep)
        fall(3 * HALF, sum_out.at[0])
        first = mail.send(sum_out.at[0], sum_in.at[0], place.core)
        fall(2 * HALF, keep.at[0])
        fall(HALF, sum_out.at[1])
        second = mail.send(sum_out.at[1], sum_in.at[1], place.core)
        first.wait_recv()
        s.far_out[l] = (keep[0] + sum_in[0].astype(jnp.float32)).astype(jnp.bfloat16)
        third = mail.send(s.far_out.at[l], s.far_in.at[l], place.across)
        if l == 0:
            up[1].pass_z()
        fall(0, keep.at[1])
        second.wait_recv()
        keep[1] = keep[1] + sum_in[1].astype(jnp.float32)
        for source, target in (
            (s.rows, outs.rows),
            (s.upward, outs.upward),
            (s.active, outs.active),
            (s.wmlp, outs.wmlp),
        ):
            mail.move(source.at[l], target.at[l])
        third.wait_recv()
        total = (keep[1] + s.far_in[l].astype(jnp.float32)).astype(jnp.bfloat16)
        s.own_out[l] = total
        fourth = mail.send(s.own_out.at[l], s.own_in.at[l], place.core)
        gate = piece(base + 5)
        output = total.astype(jnp.float32)
        s.mlp_out[l, 0:HALF, :] = output
        s.resid[0:HALF, :] += gate * output
        fourth.wait_recv()
        output = s.own_in[l].astype(jnp.float32)
        s.mlp_out[l, HALF : 2 * HALF, :] = output
        s.resid[HALF : 2 * HALF, :] += gate * output
        mail.move(s.mlp_out.at[l], outs.mlp_out.at[l])

    for low in (0, HALF):
        normalize(
            2 * LAYERS, piece(6 * LAYERS), piece(6 * LAYERS + 1), s.final_low, low
        )
    predicted = mm(s.final_low[...], s.head[...])
    lanes = lax.broadcasted_iota(jnp.int32, (TOKENS, LANES), 1)
    taken = (lanes >= PATCH_DIM) & (lanes < 2 * PATCH_DIM)
    difference = jnp.where(taken, predicted - s.noise[...], 0.0)
    square = difference[0:HALF] * difference[0:HALF]
    s.loss[...] = jnp.sum(square.reshape(HALF // 8, 8, LANES), axis=0)
    s.grad_pred[...] = (difference * (2.0 / total_entries)).astype(jnp.bfloat16)
    for source, target in (
        (s.final_low, outs.final_low),
        (s.loss, outs.loss),
        (s.grad_pred, outs.grad_pred),
    ):
        mail.move(source, target)
    waited = [cond_loaded, head_kept, data_kept, mod_kept] + [g.kept for g in attn + up + down]
    mail.finish(waited)


FORWARD_OUTS = dict(
    wattn=((LAYERS, 2, D, D), jnp.bfloat16),
    wmlp=((LAYERS, 2, D, D), jnp.bfloat16),
    head=((D, LANES), jnp.bfloat16),
    pieces=((16, D), jnp.float32),
    cond=((2, 2, 4, D), jnp.float32),
    hidden=((LAYERS, TOKENS, D), jnp.bfloat16),
    qkv=((LAYERS, 2, TOKENS, D), jnp.bfloat16),
    att=((LAYERS, 2, TOKENS, D // 2), jnp.bfloat16),
    probs=((LAYERS, 2, 3, TOKENS, TOKENS), jnp.float32),
    attn_out=((LAYERS, TOKENS, D), jnp.float32),
    rows=((LAYERS, 2 * TOKENS, D), jnp.bfloat16),
    upward=((LAYERS, 2 * TOKENS, D), jnp.float32),
    active=((LAYERS, 2 * TOKENS, D), jnp.bfloat16),
    mlp_out=((LAYERS, TOKENS, D), jnp.float32),
    normed=((2 * LAYERS + 1, TOKENS, D), jnp.float32),
    inverse=((2 * LAYERS + 1, TOKENS, LANES), jnp.float32),
    final_low=((TOKENS, D), jnp.bfloat16),
    noisy=((TOKENS, LANES), jnp.bfloat16),
    grad_pred=((TOKENS, LANES), jnp.bfloat16),
    loss=((8, LANES), jnp.float32),
)
FORWARD_OWN = dict(
    cond_weight=((NCOND // D, D // 8, D), jnp.float32),
    order=((8 * LANES, D), jnp.bfloat16),
    waves=((32, D), jnp.float32),
    cond_in=((7, 4, D), jnp.float32),
    data_in=((4, HALF, LANES), jnp.float32),
    noise=((TOKENS, LANES), jnp.float32),
    mod_out=((8, 16, LANES), jnp.float32),
    mod_in=((8, 16, LANES), jnp.float32),
    mod_rows=((16, 8 * LANES), jnp.float32),
    resid=((TOKENS, D), jnp.float32),
    core_out=((LAYERS, TOKENS, D), jnp.bfloat16),
    core_in=((LAYERS, TOKENS, D), jnp.bfloat16),
    sum_out=((LAYERS, 2, HALF, D), jnp.bfloat16),
    sum_in=((LAYERS, 2, HALF, D), jnp.bfloat16),
    far_out=((LAYERS, HALF, D), jnp.bfloat16),
    far_in=((LAYERS, HALF, D), jnp.bfloat16),
    own_out=((LAYERS, HALF, D), jnp.bfloat16),
    own_in=((LAYERS, HALF, D), jnp.bfloat16),
    keep=((2, HALF, D), jnp.float32),
)
FORWARD_SCRATCH = {**FORWARD_OUTS, **FORWARD_OWN}


def run_forward(inputs, total_entries):
    vmem = pl.BlockSpec(memory_space=pltpu.VMEM)
    outs = pl.pallas_call(
        partial(forward_kernel, {name: value.shape for name, value in inputs.items()}, total_entries),
        out_shape=[jax.ShapeDtypeStruct(*spec) for spec in FORWARD_OUTS.values()],
        in_specs=[
            pl.BlockSpec(memory_space=pl.ANY) if value.size > D * D * 2 and value.dtype == jnp.float32 else vmem
            for value in inputs.values()
        ],
        out_specs=[pl.BlockSpec(memory_space=pl.ANY)] * len(FORWARD_OUTS),
        scratch_shapes=[pltpu.VMEM(*spec) for spec in FORWARD_SCRATCH.values()]
        + [
            pltpu.SemaphoreType.DMA((128,)),
            pltpu.SemaphoreType.DMA((128,)),
            pltpu.SemaphoreType.DMA((64,)),
        ],
        compiler_params=pltpu.CompilerParams(
            collective_id=0, has_side_effects=True, vmem_limit_bytes=VMEM_LIMIT
        ),
    )(*inputs.values())
    return SimpleNamespace(**dict(zip(FORWARD_OUTS, outs)))
class Scatter:
    def __init__(self, place, mail, grad, from_y, from_z, result, other=None, from_x=None):
        self.place, self.mail, self.grad, self.result = (place, mail, grad, result)
        self.from_y, self.from_z, self.other, self.from_x = (from_y, from_z, other, from_x)
        self.rows = result.shape[0]
        self.x_copies, self.y_copies, self.z_copies = ({}, {}, {})

    def at(self, ref, slot):
        return ref.at[pl.ds(slot * self.rows, self.rows)]

    def start(self, slots=(4, 5, 6, 7)):
        for slot in slots:
            if self.other is None:
                self.send_y(slot)
            else:
                self.x_copies[slot] = self.mail.send(
                    self.at(self.other, slot), self.at(self.from_x, slot), self.place.across
                )

    def send_y(self, slot):
        self.y_copies[slot - 4] = self.mail.send(
            self.at(self.grad, slot), self.at(self.from_y, slot - 4), self.place.pair
        )

    def total(self, slot, refs):
        low = slot * self.rows
        value = self.grad[low : low + self.rows, :].astype(jnp.float32)
        for ref in refs:
            value = value + ref[low : low + self.rows, :].astype(jnp.float32)
        return value

    def pass_x(self):
        for slot in (4, 5, 6, 7):
            if self.other is not None:
                self.x_copies[slot].wait_recv()
                low = slot * self.rows
                self.grad[low : low + self.rows, :] = self.total(slot, [self.from_x]).astype(
                    jnp.bfloat16
                )
                self.send_y(slot)

    def pass_y(self):
        refs = [self.from_y] if self.other is None else [self.from_x, self.from_y]
        for slot in (1, 2, 3, 0):
            if self.other is not None:
                self.x_copies[slot].wait_recv()
            self.y_copies[slot].wait_recv()
            value = self.total(slot, refs)
            if slot == 0:
                self.result[...] = value
            else:
                low = slot * self.rows
                self.grad[low : low + self.rows, :] = value.astype(jnp.bfloat16)
                self.z_copies[slot] = self.mail.send(
                    self.at(self.grad, slot), self.from_z.at[slot - 1], self.place.up_z(slot)
                )

    def pass_z(self):
        value = self.result[...]
        for slot in (1, 2, 3):
            self.z_copies[slot].wait_recv()
            value = value + self.from_z[slot - 1].astype(jnp.float32)
        self.result[...] = value


def gelu_slope(value):
    const = math.sqrt(2.0 / math.pi)
    square = value * value
    tanh = jnp.tanh(const * (value + 0.044715 * (square * value)))
    return 0.5 * (1.0 + tanh) + 0.5 * value * (1.0 - tanh * tanh) * (
        const * (1.0 + (3.0 * 0.044715) * square)
    )


def backward_kernel(*refs):
    r = SimpleNamespace(**dict(zip(BACKWARD_INS, refs)))
    rest = refs[len(BACKWARD_INS) :]
    outs = SimpleNamespace(**dict(zip(BACKWARD_OUTS, rest)))
    rest = rest[len(BACKWARD_OUTS) :]
    s = SimpleNamespace(**dict(zip(BACKWARD_SCRATCH, rest)))
    rest = rest[len(BACKWARD_SCRATCH) :]
    mail = Mail(*rest)
    place = Place()
    loaded = {}
    waited = []

    def load(name, index=None):
        source = getattr(r, name)
        source = source if index is None else source.at[index]
        loaded[name] = mail.move(source, getattr(s, name))

    def need(*names):
        for name in names:
            if name in loaded:
                copy = loaded.pop(name)
                copy.wait()
                waited.append(copy)

    for name in FINAL_KEPT:
        load(name)
    normed_from = {}

    def load_normed(which):
        normed_from[which] = [
            mail.move(r.normed.at[which], s.normed.at[which]),
            mail.move(r.inverse.at[which], s.inverse.at[which]),
        ]

    load_normed(2 * LAYERS)
    for name in list(MLP_KEPT) + list(ATTN_KEPT):
        load(name, LAYERS - 1)
    for which in reversed(range(2 * LAYERS)):
        load_normed(which)
    load(*LATE_KEPT)
    greet(place)

    head_rows = D // 8
    across_index = place.t // 2
    rows_id = lax.broadcasted_iota(jnp.int32, (LANES, D), 0)
    offset = lax.broadcasted_iota(jnp.int32, (LANES, D), 1) - rows_id
    for owner in range(8):
        hit = (offset == place.slot_of(owner) * head_rows) & (rows_id < head_rows)
        s.order[pl.ds(owner * LANES, LANES), :] = jnp.where(hit, 1.0, 0.0).astype(jnp.bfloat16)
    s.mod_grad[...] = jnp.zeros_like(s.mod_grad)
    s.mod_send[...] = jnp.zeros_like(s.mod_send)

    def piece(index):
        return s.pieces[index : index + 1, :]

    def norm_back(which, mod_row, low, first):
        if low == 0:
            for copy in normed_from[which]:
                copy.wait()
                waited.append(copy)
        mixed = s.mixed[low : low + HALF, :]
        normed = s.normed[which, low : low + HALF, :]
        inverse = s.inverse[which, low : low + HALF, 0:1]
        if low == 0:
            s.mod_grad[mod_row : mod_row + 1, :] = jnp.sum(mixed, axis=0, keepdims=True)
            s.mod_grad[mod_row + 1 : mod_row + 2, :] = jnp.sum(
                mixed * normed, axis=0, keepdims=True
            )
        scaled = mixed * (1.0 + piece(mod_row + 1))
        centred = scaled - jnp.mean(scaled, axis=-1, keepdims=True)
        grad = (centred - normed * jnp.mean(scaled * normed, axis=-1, keepdims=True)) * inverse
        if first:
            s.grad[low : low + HALF, :] = grad
        else:
            s.grad[low : low + HALF, :] += grad

    need(*FINAL_KEPT)
    s.head_grad[...] = mm_tn(s.final_low[0:HALF, :], s.grad_pred[0:HALF, :])
    for n in range(0, D, 256):
        s.mixed[:, n : n + 256] = mm_nt(s.grad_pred[...], s.head[n : n + 256, :])
    for low in (0, HALF):
        norm_back(2 * LAYERS, 6 * LAYERS, low, True)

    def scatter(l, kind, index, other=None):
        if other is None:
            return Scatter(
                place, mail, s.mlp_grad.at[l, index], s.from_y.at[l, kind],
                s.from_z.at[l, kind], s.result.at[l, kind],
            )
        return Scatter(
            place, mail, s.attn_grad.at[l, 0], s.from_y.at[l, kind],
            s.from_z.at[l, kind], s.result.at[l, kind],
            s.attn_grad.at[l, 1], s.from_x.at[l],
        )

    attn = [scatter(l, 0, 0, True) for l in range(LAYERS)]
    up = [scatter(l, 1, 0) for l in range(LAYERS)]
    down = [scatter(l, 2, 1) for l in range(LAYERS)]

    low_mask = half_mask(TOKENS, False)
    high_mask = half_mask(TOKENS, True)
    for l in reversed(range(LAYERS)):
        base = 6 * l
        last = l == LAYERS - 1
        gate = piece(base + 5)
        need(*list(MLP_KEPT)[:1])
        grads = s.grad_rows.at[l]
        grads[0:HALF, :] = (gate * s.grad[0:HALF, :]).astype(jnp.bfloat16)
        far = mail.send(grads.at[pl.ds(0, HALF)], grads.at[pl.ds(2 * HALF, HALF)], place.across)
        grads[HALF : 2 * HALF, :] = (gate * s.grad[HALF : 2 * HALF, :]).astype(jnp.bfloat16)
        s.mod_grad[base + 5 : base + 6, :] = jnp.sum(
            s.grad[0:HALF, :] * s.mlp_out[0:HALF, :], axis=0, keepdims=True
        )
        if not last:
            attn[1].start((5, 6))
            up[1].pass_y()
        need(*MLP_KEPT)
        w_up, w_down = (s.wmlp.at[0], s.wmlp.at[1])

        def drop(low):
            for n in range(0, D, 256):
                part = mm(grads[low : low + HALF, :], w_down[:, n : n + 256])
                slope = gelu_slope(s.upward[low : low + HALF, n : n + 256])
                s.grad_up[low : low + HALF, n : n + 256] = (part * slope).astype(jnp.bfloat16)

        drop(0)
        drop(HALF)
        far.wait_recv()
        side = mail.send(
            grads.at[pl.ds(2 * HALF, HALF)], grads.at[pl.ds(3 * HALF, HALF)], place.core
        )
        drop(2 * HALF)
        side.wait_recv()
        drop(3 * HALF)

        def fall(low, target):
            for n in range(0, D, 256):
                part = mm_nt(s.grad_up[low : low + HALF, :], w_up[n : n + 256, :])
                target[:, n : n + 256] = part.astype(target.dtype)

        sum_out, sum_in, keep = (s.sum_out.at[l], s.sum_in.at[l], s.keep)
        fall(3 * HALF, sum_out.at[0])
        first = mail.send(sum_out.at[0], sum_in.at[0], place.core)
        fall(2 * HALF, keep.at[0])
        fall(HALF, sum_out.at[1])
        second = mail.send(sum_out.at[1], sum_in.at[1], place.core)
        first.wait_recv()
        s.far_out[l] = (keep[0] + sum_in[0].astype(jnp.float32)).astype(jnp.bfloat16)
        third = mail.send(s.far_out.at[l], s.far_in.at[l], place.across)
        if not last:
            attn[1].start((7, 1, 2, 3, 0))
        fall(0, keep.at[1])
        for n in range(0, D, 256):
            s.mlp_grad[l, 1, :, n : n + 256] = mm_tn(
                grads[...], s.active[:, n : n + 256]
            ).astype(jnp.bfloat16)
        down[l].start()
        second.wait_recv()
        keep[1] = keep[1] + sum_in[1].astype(jnp.float32)
        third.wait_recv()
        total = (keep[1] + s.far_in[l].astype(jnp.float32)).astype(jnp.bfloat16)
        s.own_out[l] = total
        fourth = mail.send(s.own_out.at[l], s.own_in.at[l], place.core)
        s.mixed[0:HALF, :] = total.astype(jnp.float32)
        norm_back(2 * l + 1, base + 3, 0, False)
        fourth.wait_recv()
        s.mixed[HALF : 2 * HALF, :] = s.own_in[l].astype(jnp.float32)
        norm_back(2 * l + 1, base + 3, HALF, False)
        for n in range(0, D, 256):
            s.mlp_grad[l, 0, :, n : n + 256] = mm_tn(
                s.rows[...], s.grad_up[:, n : n + 256]
            ).astype(jnp.bfloat16)
        up[l].start()
        if last:
            for name in MLP_KEPT:
                load(name, 0)

        gate = piece(base + 2)
        need(*ATTN_KEPT)
        both = s.both
        both[0:TOKENS, :] = s.hidden[...]
        both[TOKENS : 2 * TOKENS, :] = (gate * s.grad[...]).astype(jnp.bfloat16)
        s.mod_grad[base + 2 : base + 3, :] = jnp.sum(
            s.grad[0:HALF, :] * s.attn_out[0:HALF, :], axis=0, keepdims=True
        )
        scale = HEAD_DIM ** (-0.5)
        for x in range(2):
            qkv = s.qkv.at[x]
            grad_qkv = s.grad_qkv.at[x]

            def tile(ref, index):
                return ref[:, index * LANES : (index + 1) * LANES]

            def put(index, value):
                grad_qkv[0:TOKENS, index * LANES : (index + 1) * LANES] = value.astype(jnp.bfloat16)

            found = {}
            for h, (q, k, v, keep_mask) in enumerate(
                ((0, 1, 2, low_mask), (0, 1, 2, high_mask), (3, 4, 5, low_mask))
            ):
                weight = s.wattn[x, :, (3 + h) * LANES : (4 + h) * LANES]
                grad_att = mm(both[TOKENS : 2 * TOKENS, :], weight)
                if h != 1:
                    grad_att = pltpu.roll(grad_att, 64, 1)
                grad_att = jnp.where(keep_mask, grad_att, 0.0).astype(jnp.bfloat16)
                probs = s.probs[x, h]
                grad_probs = mm_nt(grad_att, tile(qkv, v))
                inner = jnp.sum(probs * grad_probs, axis=-1, keepdims=True)
                grad_scores = (probs * (grad_probs - inner)).astype(jnp.bfloat16)
                found[h] = (
                    jnp.where(keep_mask, mm(grad_scores, tile(qkv, k)) * scale, 0.0),
                    jnp.where(keep_mask, mm_tn(grad_scores, tile(qkv, q)) * scale, 0.0),
                    mm_tn(probs.astype(jnp.bfloat16), grad_att),
                )
                if h == 1:
                    for index in range(3):
                        put(index, found[0][index] + found[1][index])
                if h == 2:
                    for index in range(3):
                        put(3 + index, found[2][index])
            if last and x == 0:
                down[1].pass_y()
            elif not last and x == 0:
                attn[1].pass_x()
            elif not last:
                down[0].pass_y()
        for n in range(0, D, 256):
            part = mm_nt(s.grad_qkv[0, 0:TOKENS, :], s.wattn[0, n : n + 256, :])
            part = part + mm_nt(s.grad_qkv[1, 0:TOKENS, :], s.wattn[1, n : n + 256, :])
            s.core_out[l, :, n : n + 256] = part.astype(jnp.bfloat16)
        summed = mail.send(s.core_out.at[l], s.core_in.at[l], place.core)
        for x in (1, 0):
            s.grad_qkv[x, TOKENS : 2 * TOKENS, D // 2 : D] = s.att[x]
            half = s.grad_qkv[x, 0:TOKENS, 0 : D // 2]
            s.attn_grad[l, x, :, 0 : D // 2] = mm_tn(both[0:TOKENS, :], half).astype(jnp.bfloat16)
            half = s.grad_qkv[x, :, D // 2 : D]
            s.attn_grad[l, x, :, D // 2 : D] = mm_tn(both[...], half).astype(jnp.bfloat16)
            if x == 1 and last:
                attn[1].start((4,))
            elif x == 1:
                attn[0].start((4, 5, 6, 7, 1, 2, 3, 0))
        summed.wait_recv()
        for low in (0, HALF):
            value = s.core_out[l, low : low + HALF, :].astype(jnp.float32)
            s.mixed[low : low + HALF, :] = value + s.core_in[
                l, HALF - low : 2 * HALF - low, :
            ].astype(jnp.float32)
            norm_back(2 * l, base, low, False)
        if last:
            for name in ATTN_KEPT:
                load(name, 0)

    mod_first = mail.send(s.mod_grad, s.mod_other, place.core)
    s.head_grad[...] += mm_tn(
        s.grad[0:HALF, :].astype(jnp.bfloat16), s.noisy[0:HALF, :]
    )
    head_first = mail.send(s.head_grad, s.head_other, place.core)
    mod_first.wait_recv()
    summed = (s.mod_grad[...] + s.mod_other[...]).astype(jnp.bfloat16)
    blocks = s.cond_weight.shape[0]
    for owner in range(8):
        part = mm_nt(summed, s.order[owner * LANES : (owner + 1) * LANES, :])
        s.mod_rows[:, owner * LANES : (owner + 1) * LANES] = part
    for g in range(8 * blocks):
        row, owner = (g // 8, g % 8)
        s.mod_send[g // blocks, g % blocks : g % blocks + 1, :] = s.mod_rows[
            row : row + 1, owner * LANES : (owner + 1) * LANES
        ]
    back_from = []
    for k in range(1, 8):
        source = s.mod_send.at[lax.rem(place.f + k, 8)]
        back_from.append(mail.send(source, s.back.at[0, k], place.up_f(k)))
    back_own = mail.move(s.mod_send.at[place.f], s.back.at[0, 0])
    up[0].pass_y()
    head_first.wait_recv()
    s.head_low[...] = (s.head_grad[...] + s.head_other[...]).astype(jnp.bfloat16)
    head_second = mail.send(s.head_low, s.head_far, place.across)
    attn[0].pass_x()
    attn[1].pass_y()
    back_own.wait()
    for copy in back_from:
        copy.wait_recv()
    back_far = mail.send(s.back.at[0], s.back.at[1], place.across)
    head_second.wait_recv()
    half = 4 * head_rows
    head_total = s.head_low[...].astype(jnp.float32) + s.head_far[...].astype(jnp.float32)
    s.head_mid[...] = head_total
    s.head_sum[...] = head_total.astype(jnp.bfloat16)
    head_third = mail.send(s.head_sum.at[pl.ds(half, half)], s.head_y, place.pair)
    back_far.wait_recv()
    for i in range(16):
        x_part = lax.rem(across_index + i % 2, 2)
        k = lax.rem(place.f + 8 - i // 2, 8)
        s.back_rows[i] = s.back[x_part, k]
    need(*LATE_KEPT)
    partial_cond = jnp.zeros((16, D), jnp.float32)
    for b in range(blocks):
        block = s.back_rows[:, b, 0:head_rows].astype(jnp.bfloat16)
        partial_cond = partial_cond + mm(block, s.cond_weight[b].astype(jnp.bfloat16))
    s.cond_out[...] = partial_cond
    cond_from = [
        mail.send(s.cond_out, s.cond_in.at[k - 1], place.up_f(k)) for k in range(1, 8)
    ]
    mail.move(s.back_rows, outs.back_rows)
    attn[0].pass_y()
    head_third.wait_recv()
    head_from = []
    for k in range(1, 4):
        low = k * head_rows
        value = s.head_mid[low : low + head_rows, :] + s.head_y[
            low : low + head_rows, :
        ].astype(jnp.float32)
        s.head_sum[low : low + head_rows, :] = value.astype(jnp.bfloat16)
        head_from.append(
            mail.send(
                s.head_sum.at[pl.ds(low, head_rows)], s.head_z.at[k - 1], place.up_z(k)
            )
        )
    head_own = s.head_mid[0:head_rows, :] + s.head_y[0:head_rows, :].astype(jnp.float32)
    value = s.cond_out[...]
    for k in range(7):
        cond_from[k].wait_recv()
        value = value + s.cond_in[k]
    for c in range(16):
        s.cond_rows[c : c + 1, :] = r.cond[c % 2, c // 8, c // 2 % 4 : c // 2 % 4 + 1, :]
    cond = s.cond_rows[...]
    sigmoid = jax.nn.sigmoid(cond)
    cond_act = (cond * sigmoid).astype(jnp.bfloat16)
    cond_grad = (value * (sigmoid * (1.0 + cond * (1.0 - sigmoid)))).astype(jnp.bfloat16)
    s.time_grad[...] = mm_tn(r.time_hidden[...], cond_grad)
    mail.move(s.time_grad, outs.time_grad)
    time_pre = r.time_pre[...]
    sigmoid = jax.nn.sigmoid(time_pre)
    slope = sigmoid * (1.0 + time_pre * (1.0 - sigmoid))
    pre_grad = (mm_nt(cond_grad, r.low_time[...]) * slope).astype(jnp.bfloat16)
    s.first_grad[...] = mm_tn(pre_grad, r.features[...])
    mail.move(s.first_grad, outs.first_grad)
    column = lax.broadcasted_iota(jnp.int32, (D, head_rows), 0)
    column = column - lax.broadcasted_iota(jnp.int32, (D, head_rows), 1)
    picked = jnp.where(column == place.f * head_rows, 1.0, 0.0).astype(jnp.bfloat16)
    own_cols = mm(cond_grad, picked).astype(jnp.bfloat16)
    s.label_grad[...] = mm_tn(own_cols, r.label_hot[...])
    mail.move(s.label_grad, outs.label_grad)
    shared = jnp.sum(s.time_grad[...] * s.time_grad[...])
    shared = shared + jnp.sum(s.first_grad[...] * s.first_grad[...])
    shared = shared + jnp.sum(s.label_grad[...] * s.label_grad[...])
    bias = s.back_rows[0]
    for c in range(1, 16):
        bias = bias + s.back_rows[c]
    shared = shared + jnp.sum(bias * bias)
    weight_squares = jnp.zeros((8, D), jnp.float32)
    for c in range(blocks):
        block = mm_tn(s.back_rows[:, c, 0:head_rows].astype(jnp.bfloat16), cond_act)
        weight_squares = weight_squares + jnp.sum(
            (block * block).reshape(head_rows // 8, 8, D), axis=0
        )
    shared = shared + jnp.sum(weight_squares)
    for k in range(3):
        head_from[k].wait_recv()
        head_own = head_own + s.head_z[k].astype(jnp.float32)
    s.head_result[...] = head_own
    shared = shared + jnp.sum(head_own * head_own)
    mail.move(s.head_result, outs.head_result)
    squares = jnp.zeros((8, D), jnp.float32)
    for item in (down[1], up[1], down[0], up[0], attn[1], attn[0]):
        item.pass_z()
        grad = item.result[...]
        squares = squares + jnp.sum((grad * grad).reshape(head_rows // 8, 8, D), axis=0)
    mail.move(s.result.at[:, pl.ds(1, 2)], outs.mlp_result)
    upper = half_mask(head_rows, True)
    for l in range(LAYERS):
        tiles = [s.result[l, 0, :, k * LANES : (k + 1) * LANES] for k in range(6)]
        for k in range(3):
            s.attn_result[l, k, :, 0:LANES] = tiles[k]
            s.attn_result[l, k, :, LANES : LANES + 64] = tiles[3 + k][:, 0:64]
        s.attn_result[l, 3, :, 0:LANES] = jnp.where(upper, tiles[4], pltpu.roll(tiles[3], 64, 1))
        s.attn_result[l, 3, :, LANES : LANES + 64] = pltpu.roll(tiles[5], 64, 1)[:, 0:64]
    mail.move(s.attn_result, outs.attn_result)

    owned = jnp.where(place.t == 0, 1.0, 0.0)
    total = jnp.sum(squares) + owned * shared
    tile_rows = lax.broadcasted_iota(jnp.int32, (8, LANES), 0)
    s.part[...] = jnp.where(tile_rows == 0, total, jnp.sum(r.loss[...]))
    s.by_fsdp[place.f] = s.part[...]
    copies = [mail.send(s.part, s.by_fsdp.at[place.f], place.up_f(k)) for k in range(1, 8)]
    for copy in copies:
        copy.wait_recv()
    value = s.by_fsdp[0]
    for k in range(1, 8):
        value = value + s.by_fsdp[k]
    s.group[...] = value
    s.by_tp[place.t] = value
    copies = [
        mail.send(s.group, s.by_tp.at[place.t], device)
        for device in (place.core, place.across, place.diagonal)
    ]
    for copy in copies:
        copy.wait_recv()
    s.totals[...] = s.by_tp[0] + s.by_tp[1] + s.by_tp[2] + s.by_tp[3]
    mail.move(s.totals, outs.totals)
    mail.finish(waited + [back_own])


FINAL_KEPT = dict(
    grad_pred=None, head=None, final_low=None, pieces=None, noisy=None
)
LATE_KEPT = dict(cond_weight=None)
NORM_KEPT = dict(normed=None, inverse=None)
MLP_KEPT = dict(mlp_out=None, wmlp=None, upward=None, active=None, rows=None)
ATTN_KEPT = dict(attn_out=None, wattn=None, qkv=None, probs=None, hidden=None, att=None)
SMALL_INS = dict(
    cond=None,
    loss=None,
    time_hidden=None,
    low_time=None,
    features=None,
    time_pre=None,
    label_hot=None,
)
BACKWARD_INS = SMALL_INS | LATE_KEPT | NORM_KEPT | FINAL_KEPT | MLP_KEPT | ATTN_KEPT
BACKWARD_OUTS = dict(
    mlp_result=((LAYERS, 2, D // 8, D), jnp.float32),
    attn_result=((LAYERS, 4, D // 8, D // 4), jnp.float32),
    head_result=((D // 8, LANES), jnp.float32),
    back_rows=((16, 16, LANES), jnp.float32),
    time_grad=((D // 8, D), jnp.float32),
    first_grad=((D // 8, FREQ), jnp.float32),
    label_grad=((D // 8, NCLASS), jnp.float32),
    totals=((8, LANES), jnp.float32),
)
MLP_RESULT = dict(mlp_result=None)
BACKWARD_OWN = dict(
    result=((LAYERS, 3, D // 8, D), jnp.float32),
    cond_rows=((16, D), jnp.float32),
    part=((8, LANES), jnp.float32),
    group=((8, LANES), jnp.float32),
    by_fsdp=((8, 8, LANES), jnp.float32),
    by_tp=((4, 8, LANES), jnp.float32),
    order=((8 * LANES, D), jnp.bfloat16),
    mod_grad=((16, D), jnp.float32),
    mod_other=((16, D), jnp.float32),
    mod_rows=((16, 8 * LANES), jnp.float32),
    mod_send=((8, 16, LANES), jnp.float32),
    back=((2, 8, 16, LANES), jnp.float32),
    cond_out=((16, D), jnp.float32),
    cond_in=((7, 16, D), jnp.float32),
    head_grad=((D, LANES), jnp.float32),
    head_other=((D, LANES), jnp.float32),
    head_mid=((D, LANES), jnp.float32),
    head_low=((D, LANES), jnp.bfloat16),
    head_far=((D, LANES), jnp.bfloat16),
    head_sum=((D, LANES), jnp.bfloat16),
    head_y=((D // 2, LANES), jnp.bfloat16),
    head_z=((3, D // 8, LANES), jnp.bfloat16),
    grad=((TOKENS, D), jnp.float32),
    mixed=((TOKENS, D), jnp.float32),
    grad_rows=((LAYERS, 2 * TOKENS, D), jnp.bfloat16),
    grad_up=((2 * TOKENS, D), jnp.bfloat16),
    both=((2 * TOKENS, D), jnp.bfloat16),
    grad_qkv=((2, 2 * TOKENS, D), jnp.bfloat16),
    sum_out=((LAYERS, 2, HALF, D), jnp.bfloat16),
    sum_in=((LAYERS, 2, HALF, D), jnp.bfloat16),
    far_out=((LAYERS, HALF, D), jnp.bfloat16),
    far_in=((LAYERS, HALF, D), jnp.bfloat16),
    own_out=((LAYERS, HALF, D), jnp.bfloat16),
    own_in=((LAYERS, HALF, D), jnp.bfloat16),
    keep=((2, HALF, D), jnp.float32),
    core_out=((LAYERS, TOKENS, D), jnp.bfloat16),
    core_in=((LAYERS, TOKENS, D), jnp.bfloat16),
    mlp_grad=((LAYERS, 2, D, D), jnp.bfloat16),
    attn_grad=((LAYERS, 2, D, D), jnp.bfloat16),
    from_x=((LAYERS, D, D), jnp.bfloat16),
    from_y=((LAYERS, 3, D // 2, D), jnp.bfloat16),
    from_z=((LAYERS, 3, 3, D // 8, D), jnp.bfloat16),
)


def backward_scratch():
    layered = MLP_KEPT | ATTN_KEPT
    specs = {}
    for name in BACKWARD_INS:
        if name in LATE_KEPT:
            specs[name] = FORWARD_OWN[name]
        elif name not in SMALL_INS:
            shape, dtype = FORWARD_OUTS[name]
            specs[name] = (shape[1:] if name in layered else shape, dtype)
    for name in BACKWARD_OUTS:
        if name not in MLP_RESULT:
            specs[name] = BACKWARD_OUTS[name]
    specs.update(BACKWARD_OWN)
    return specs


BACKWARD_SCRATCH = backward_scratch()


def run_backward(kept, inputs):
    anywhere = pl.BlockSpec(memory_space=pl.ANY)
    vmem = pl.BlockSpec(memory_space=pltpu.VMEM)
    given = [
        getattr(kept if hasattr(kept, name) else inputs, name) for name in BACKWARD_INS
    ]
    outs = pl.pallas_call(
        backward_kernel,
        out_shape=[jax.ShapeDtypeStruct(*spec) for spec in BACKWARD_OUTS.values()],
        in_specs=[vmem if name in SMALL_INS else anywhere for name in BACKWARD_INS],
        out_specs=[anywhere] * len(BACKWARD_OUTS),
        scratch_shapes=[pltpu.VMEM(*spec) for spec in BACKWARD_SCRATCH.values()]
        + [
            pltpu.SemaphoreType.DMA((128,)),
            pltpu.SemaphoreType.DMA((128,)),
            pltpu.SemaphoreType.DMA((64,)),
        ],
        compiler_params=pltpu.CompilerParams(
            collective_id=1, has_side_effects=True, vmem_limit_bytes=VMEM_LIMIT
        ),
    )(*given)
    return SimpleNamespace(**dict(zip(BACKWARD_OUTS, outs)))


def shard_tiles(attn_weight):
    q, k, v, o = (attn_weight[:, j].astype(jnp.bfloat16) for j in range(4))
    return jnp.concatenate(
        [
            q[..., :128],
            k[..., :128],
            v[..., :128],
            q[..., 128:],
            o[..., :64],
            k[..., 128:],
            o[..., 64:128],
            v[..., 128:],
            o[..., 128:],
        ],
        axis=-1,
    )


def wave_table():
    quarter = D // 4
    omegas = 1.0 / np.power(10000.0, np.arange(quarter, dtype=np.float32) / quarter)
    angles = np.arange(GRID, dtype=np.float32)[:, None] * omegas.astype(np.float32)[None, :]
    waves = np.concatenate([np.sin(angles), np.cos(angles)], axis=1).astype(np.float32)
    table = np.zeros((2 * GRID, D), np.float32)
    table[:GRID, : D // 2] = waves
    table[GRID:, D // 2 :] = waves
    padded = np.zeros((2 * GRID, 8, LANES), np.float32)
    padded[:, :, : D // 8] = table.reshape(2 * GRID, 8, D // 8)
    left = padded.reshape(2 * GRID, 8 * LANES)
    parts = []
    for _ in range(3):
        part = left.astype(jnp.bfloat16)
        parts.append(part)
        left = left - part.astype(np.float32)
    return np.concatenate(parts, axis=0)


def body_kernels(
    routes,
    latents,
    noise,
    timesteps,
    labels,
    step_count,
    tables,
    time_weight,
    cond_weight,
    cond_bias,
    attn_weight,
    mlp_weight,
    *states,
):
    fsdp_index = lax.axis_index("fsdp")
    tp_index = lax.axis_index("tp")
    across_index = tp_index // 2
    num_fsdp = routes.num_fsdp
    col_share = tables.shape[1]
    all_latents = timesteps.shape[0]
    total_entries = all_latents * SEQ * PATCH_DIM
    col_start = fsdp_index * col_share
    low_tables = tables.astype(jnp.bfloat16)
    blocks = cond_bias.shape[0] // col_share

    features = timestep_features(timesteps).astype(jnp.bfloat16)
    time_pre = jnp.dot(
        features,
        low_tables[2 * PATCH_DIM : 2 * PATCH_DIM + FREQ],
        preferred_element_type=jnp.float32,
    )
    time_hidden = jax.nn.silu(time_pre).astype(jnp.bfloat16)
    label_hot = (labels[:, None] == jnp.arange(NCLASS, dtype=jnp.int32)[None, :]).astype(
        jnp.bfloat16
    )
    label_part = jnp.dot(
        label_hot, low_tables[2 * PATCH_DIM + FREQ :], preferred_element_type=jnp.float32
    )
    low_time = time_weight.astype(jnp.bfloat16)
    cond_part = jnp.dot(time_hidden, low_time, preferred_element_type=jnp.float32)
    placed = lax.dynamic_update_slice(
        jnp.zeros((all_latents, D), jnp.float32), label_part, (0, col_start)
    )
    low_bias = cond_bias.astype(jnp.bfloat16).astype(jnp.float32)

    latent_id = fsdp_index * latents.shape[0]
    share = signal_share(lax.dynamic_slice_in_dim(timesteps, latent_id, latents.shape[0]))
    share = share[:, None, None]
    noisy = (jnp.sqrt(share) * latents + jnp.sqrt(1.0 - share) * noise).astype(jnp.bfloat16)
    data = jnp.concatenate(
        [
            jnp.pad(noisy.astype(jnp.float32), ((0, 0), (0, 0), (0, LANES - PATCH_DIM))),
            jnp.pad(noise, ((0, 0), (0, 0), (PATCH_DIM, LANES - 2 * PATCH_DIM))),
        ],
        axis=1,
    )
    shards = jnp.concatenate(
        [shard_tiles(attn_weight)[:, None], mlp_weight.astype(jnp.bfloat16)], axis=1
    )
    head = jnp.pad(low_tables[: 2 * PATCH_DIM].T, ((0, 0), (0, LANES - 2 * PATCH_DIM)))
    cond_part = (cond_part + placed).reshape(num_fsdp, 2, D).transpose(1, 0, 2)
    inputs = SimpleNamespace(
        cond_part=cond_part.reshape(2, 2, num_fsdp // 2, D),
        shards=shards,
        data=data,
        head=head,
        waves=jnp.asarray(wave_table()),
        cond_weight=cond_weight.reshape(blocks, col_share, D),
        cond_bias=low_bias.reshape(blocks, col_share),
    )
    kept = run_forward(vars(inputs), total_entries)
    inputs.time_hidden = time_hidden
    inputs.low_time = low_time
    inputs.features = features
    inputs.time_pre = time_pre
    inputs.label_hot = label_hot
    back = run_backward(kept, inputs)

    cond = kept.cond.reshape(2, num_fsdp, D).transpose(1, 0, 2).reshape(all_latents, D)
    cond_act = jax.nn.silu(cond).astype(jnp.bfloat16)
    modul_back = back.back_rows[:, :blocks, :col_share].reshape(all_latents, -1)
    modul_back = modul_back.astype(jnp.bfloat16)
    cond_grad_w = dot_f32(modul_back, cond_act, 0, 0)
    bias_grad = jnp.sum(modul_back.astype(jnp.float32), axis=0)
    time_grad = back.time_grad
    tables_grad = jnp.concatenate(
        [back.head_result[:, : 2 * PATCH_DIM], back.first_grad, back.label_grad], axis=1
    ).T
    loss = back.totals[1, 0] / total_entries
    norm = jnp.sqrt(back.totals[0, 0])
    entries = NTAB * D + D * D + (D + 1) * NCOND + LAYERS * (4 * D * D + 2 * D * FF)
    limit = clip_scale * math.sqrt(entries / (all_latents * SEQ))
    factor = jnp.minimum(1.0, limit / norm)
    count = step_count[0].astype(jnp.float32)
    attn_grad = back.attn_result
    mlp_grad = back.mlp_result
    weights_all = (tables, time_weight, cond_weight, cond_bias, attn_weight, mlp_weight)
    grads_all = (tables_grad, time_grad, cond_grad_w, bias_grad, attn_grad, mlp_grad)
    states = tuple(zip(states[0::2], states[1::2]))
    results = [loss, norm]
    for weight, grad, state in zip(weights_all, grads_all, states):
        results.extend(adam_update(weight, grad * factor, state[0], state[1], count))
    return tuple(results)


def body(routes, *args):
    if routes.num_fsdp == 8 and args[5].shape[1] % 16 == 0:
        return body_kernels(routes, *args)
    return body_steps(routes, *args)


def solution(mesh):
    vectors = P("fsdp")
    columns = P(None, "fsdp")
    rows = P("fsdp", None)
    blocks = P(None, None, "fsdp", "tp")
    data = P("fsdp", "tp", None)
    weights = (columns, rows, rows, vectors, blocks, blocks)
    states = tuple(spec for spec in weights for _ in range(2))
    updated = tuple(spec for spec in weights for _ in range(3))
    return jax.shard_map(
        partial(body, Routes(mesh)),
        mesh=mesh,
        in_specs=(data, data, P(), P(), P()) + weights + states,
        out_specs=(P(), P()) + updated,
        check_vma=False,
    )
```

```python
from functools import partial
import math
from types import SimpleNamespace

import jax
import jax.numpy as jnp
from jax import lax
import numpy as np
from jax.experimental import pallas as pl
from jax.experimental.pallas import tpu as pltpu
from jax.sharding import PartitionSpec as P

D = 768
HEAD_DIM = 64
FF = 3072
NCLASS = 1000
FREQ = 256
PATCH_DIM = 16
GRID = 16
LAYERS = 2
SEQ = 256
NCOND = 10752
NTAB = 1288


norm_eps = 1e-06
beta_first = 0.9
beta_second = 0.999
adam_eps = 1e-08
learn_rate = 0.2
weight_decay = 0.01
clip_scale = 0.002
diffusion_steps = 1000.0


def timestep_features(timesteps):
    half_width = FREQ // 2
    omegas = jnp.exp(-math.log(10000.0) * jnp.arange(half_width, dtype=jnp.float32) / half_width)
    angles = timesteps.astype(jnp.float32)[:, None] * omegas[None, :]
    return jnp.concatenate([jnp.cos(angles), jnp.sin(angles)], axis=1)


def signal_share(timesteps):
    phase = (timesteps.astype(jnp.float32) / diffusion_steps + 0.008) / 1.008 * (math.pi / 2)
    return jnp.cos(phase) ** 2


def butterfly_bits(number):
    bits = []
    bit = 1
    while bit < number:
        bits.append(bit)
        bit *= 2
    return bits


def split_radices(number):
    radices = []
    while number > 1:
        radix = 4 if number % 4 == 0 else 2
        radices.append(radix)
        number //= radix
    return radices


class Routes:
    def __init__(self, mesh):
        self.num_fsdp = mesh.shape["fsdp"]
        self.num_tp = mesh.shape["tp"]
        self.outer = split_radices(self.num_fsdp // 2)

    def core(self, value):
        return lax.ppermute(value, "tp", [(t, t ^ 1) for t in range(self.num_tp)])

    def across(self, value):
        return lax.ppermute(value, "tp", [(t, t ^ 2) for t in range(self.num_tp)])

    def pair(self, value):
        return lax.ppermute(value, "fsdp", [(f, f ^ 1) for f in range(self.num_fsdp)])

    def shift(self, value, stride, radix, amount):
        pairs = []
        for f in range(self.num_fsdp):
            digit = (f // stride) % radix
            pairs.append((f, f + ((digit + amount) % radix - digit) * stride))
        return lax.ppermute(value, "fsdp", pairs)

    def slot_owner(self, fsdp_index, slots):
        per_pair = self.num_fsdp // 2
        pair_part = (slots // per_pair + fsdp_index) % 2
        rest = slots % per_pair
        owner = pair_part
        stride = 2
        for radix in self.outer:
            digit = (rest + fsdp_index // stride) % radix
            owner = owner + digit * stride
            rest = rest // radix
            stride *= radix
        return owner

    def gather_outer(self, block):
        stride = 2
        for radix in self.outer:
            block = jnp.concatenate(
                [block] + [self.shift(block, stride, radix, -k) for k in range(1, radix)], axis=0
            )
            stride *= radix
        return block

    def gather_rows(self, block):
        held = self.gather_outer(block)
        return jnp.concatenate([held, self.pair(held)], axis=0)

    def gather_both(self, block, across_last):
        held = self.gather_outer(block)
        if across_last:
            own = jnp.concatenate([held, self.pair(held)], axis=0)
            return (own, self.across(own))
        other = self.across(held)
        return (
            jnp.concatenate([held, self.pair(held)], axis=0),
            jnp.concatenate([other, self.pair(other)], axis=0),
        )

    def scatter_rows(self, total, dtype=jnp.bfloat16):
        half = total.shape[0] // 2
        received = self.pair(total[half:].astype(dtype))
        held = total[:half] + received.astype(jnp.float32)
        strides = []
        stride = 2
        for radix in self.outer:
            strides.append(stride)
            stride *= radix
        for radix, stride in reversed(list(zip(self.outer, strides))):
            size = held.shape[0] // radix
            parts = [
                self.shift(held[k * size : (k + 1) * size].astype(dtype), stride, radix, k)
                for k in range(1, radix)
            ]
            held = held[:size]
            for part in parts:
                held = held + part.astype(jnp.float32)
        return held

    def scatter_both(self, own, other):
        received = self.across(other.astype(jnp.bfloat16))
        return self.scatter_rows(own + received.astype(jnp.float32))

    def sum_fsdp(self, value):
        for bit in butterfly_bits(self.num_fsdp):
            value = value + lax.ppermute(
                value, "fsdp", [(f, f ^ bit) for f in range(self.num_fsdp)]
            )
        return value

    def sum_all(self, value):
        value = value + self.core(value)
        value = value + self.across(value)
        return self.sum_fsdp(value)


def after(value, *earlier):
    return lax.optimization_barrier((value,) + earlier)[0]


def dot_f32(left, right, left_dim, right_dim):
    return lax.dot_general(
        left, right, (((left_dim,), (right_dim,)), ((), ())), preferred_element_type=jnp.float32
    )


def layer_norm(values):
    centred = values - jnp.mean(values, axis=-1, keepdims=True)
    inverse = lax.rsqrt(jnp.mean(centred * centred, axis=-1, keepdims=True) + norm_eps)
    return (centred * inverse, inverse)


def modulate(values, shift, scale):
    normed, inverse = layer_norm(values)
    return ((normed * (1.0 + scale) + shift).astype(jnp.bfloat16), normed, inverse)


def norm_backward(grad_mixed, normed, inverse, scale, counted):
    grad_shift = jnp.sum(grad_mixed[:counted], axis=0)
    grad_scale = jnp.sum(grad_mixed[:counted] * normed[:counted], axis=0)
    grad_normed = grad_mixed * (1.0 + scale)
    centred = grad_normed - jnp.mean(grad_normed, axis=-1, keepdims=True)
    grad_input = (
        centred - normed * jnp.mean(grad_normed * normed, axis=-1, keepdims=True)
    ) * inverse
    return (grad_input, grad_shift, grad_scale)


def core_sum(routes, partial):
    low = partial.astype(jnp.bfloat16)
    far = routes.core(low)
    half = far.shape[0] // 2
    swapped = jnp.concatenate([far[half:], far[:half]], axis=0)
    return low.astype(jnp.float32) + swapped.astype(jnp.float32)


def attend(routes, hidden, weights):
    seq_len = hidden.shape[0]
    query_key = jnp.stack([dot_f32(hidden, w, 1, 0) for w in weights[0]]).astype(jnp.bfloat16)
    value_out = jnp.stack([dot_f32(hidden, w, 1, 0) for w in weights[1]]).astype(jnp.bfloat16)
    width = query_key.shape[2] // 2
    local_heads = width // HEAD_DIM
    query_key = query_key.reshape(2, seq_len, 2 * local_heads, HEAD_DIM)
    query, key = (query_key[:, :, :local_heads], query_key[:, :, local_heads:])
    value = value_out[:, :, :width].reshape(2, seq_len, local_heads, HEAD_DIM)
    scores = jnp.einsum(
        "xqhe,xkhe->xhqk", query, key, preferred_element_type=jnp.float32
    ) * HEAD_DIM ** (-0.5)
    exped = jnp.exp(scores - jnp.max(scores, axis=-1, keepdims=True))
    probs = exped / jnp.sum(exped, axis=-1, keepdims=True)
    attended = jnp.einsum(
        "xhqk,xkhe->xqhe", probs.astype(jnp.bfloat16), value, preferred_element_type=jnp.float32
    )
    attended = attended.astype(jnp.bfloat16).reshape(2, seq_len, width)
    padded = jnp.concatenate([jnp.zeros_like(attended), attended], axis=2)
    partial_out = dot_f32(padded[0], weights[1][0], 1, 1) + dot_f32(padded[1], weights[1][1], 1, 1)
    return (core_sum(routes, partial_out), (hidden, query, key, value, probs, padded))


def attend_backward(routes, grad_full, kept, weights):
    hidden, query, key, value, probs, padded = kept
    seq_len = hidden.shape[0]
    scale = HEAD_DIM ** (-0.5)
    width = padded.shape[2] // 2
    local_heads = width // HEAD_DIM
    grad_attended = jnp.stack([dot_f32(grad_full, w, 1, 0) for w in weights[1]])
    grad_attended = grad_attended[:, :, width:].astype(jnp.bfloat16)
    grad_attended = grad_attended.reshape(2, seq_len, local_heads, HEAD_DIM)
    grad_probs = jnp.einsum(
        "xqhe,xkhe->xhqk", grad_attended, value, preferred_element_type=jnp.float32
    )
    grad_value = jnp.einsum(
        "xhqk,xqhe->xkhe",
        probs.astype(jnp.bfloat16),
        grad_attended,
        preferred_element_type=jnp.float32,
    )
    inner = jnp.sum(probs * grad_probs, axis=-1, keepdims=True)
    grad_scores = (probs * (grad_probs - inner)).astype(jnp.bfloat16)
    grad_query = (
        jnp.einsum("xhqk,xkhe->xqhe", grad_scores, key, preferred_element_type=jnp.float32) * scale
    )
    grad_key = (
        jnp.einsum("xhqk,xqhe->xkhe", grad_scores, query, preferred_element_type=jnp.float32) * scale
    )
    grad_qk = jnp.concatenate([grad_query, grad_key], axis=2).astype(jnp.bfloat16)
    grad_qk = grad_qk.reshape(2, seq_len, 2 * width)
    grad_v = grad_value.astype(jnp.bfloat16).reshape(2, seq_len, width)
    grad_v = jnp.concatenate([grad_v, jnp.zeros_like(grad_v)], axis=2)
    grad_hidden = jnp.zeros(hidden.shape, jnp.float32)
    for k in range(2):
        grad_hidden = grad_hidden + dot_f32(grad_qk[k], weights[0][k], 1, 1)
        grad_hidden = grad_hidden + dot_f32(grad_v[k], weights[1][k], 1, 1)
    grad_hidden = core_sum(routes, grad_hidden)
    qk_own, qk_other = [dot_f32(hidden, grad_qk[k], 0, 0) for k in range(2)]
    both = jnp.concatenate([hidden, grad_full], axis=0)
    vo_own, vo_other = [
        dot_f32(both, jnp.concatenate([grad_v[k], padded[k]], axis=0), 0, 0) for k in range(2)
    ]
    grads = (routes.scatter_both(qk_own, qk_other), routes.scatter_both(vo_own, vo_other))
    return (grad_hidden, grads)


def share_rows(routes, rows):
    half = rows.shape[0] // 2
    far = routes.across(rows[:half])
    return jnp.concatenate([rows, far, routes.core(far)], axis=0)


def sum_rows(routes, partial):
    half = partial.shape[0] // 4
    low = partial.astype(jnp.bfloat16)
    received = routes.core(jnp.concatenate([low[3 * half :], low[half : 2 * half]], axis=0))
    received = received.astype(jnp.float32)
    far_sum = (partial[2 * half : 3 * half] + received[:half]).astype(jnp.bfloat16)
    own_sum = partial[:half] + received[half:]
    own_total = (own_sum + routes.across(far_sum).astype(jnp.float32)).astype(jnp.bfloat16)
    return jnp.concatenate([own_total, routes.core(own_total)], axis=0).astype(jnp.float32)


def feed_forward(routes, hidden, weights):
    rows = share_rows(routes, hidden)
    upward = dot_f32(rows, weights[0], 1, 0)
    active = jax.nn.gelu(upward, approximate=True).astype(jnp.bfloat16)
    output = sum_rows(routes, dot_f32(active, weights[1], 1, 1))
    return (output, (rows, upward, active))


def feed_backward(routes, grad_full, kept, weights):
    rows, upward, active = kept
    grad_rows = share_rows(routes, grad_full)
    grad_active = dot_f32(grad_rows, weights[1], 1, 0)
    slope = jax.vjp(partial(jax.nn.gelu, approximate=True), upward)[1]
    grad_up = slope(grad_active)[0].astype(jnp.bfloat16)
    grad_hidden = sum_rows(routes, dot_f32(grad_up, weights[0], 1, 1))
    grad_down_w = routes.scatter_rows(dot_f32(grad_rows, active, 0, 0))
    grad_up_w = routes.scatter_rows(dot_f32(rows, grad_up, 0, 0))
    return (grad_hidden, (grad_up_w, grad_down_w))


def branch_forward(routes, resid, pieces, inner_fn, weights):
    shift, scale, gate = pieces
    hidden, normed, inverse = modulate(resid, shift, scale)
    output, kept = inner_fn(routes, hidden, weights)
    return (resid + gate * output, (normed, inverse, output, kept))


def branch_backward(routes, grad_resid, pieces, saved, inner_back, weights):
    shift, scale, gate = pieces
    normed, inverse, output, kept = saved
    counted = grad_resid.shape[0] // 2
    grad_gate = jnp.sum(grad_resid[:counted] * output[:counted], axis=0)
    grad_output = (gate * grad_resid).astype(jnp.bfloat16)
    grad_mixed, grads = inner_back(routes, grad_output, kept, weights)
    grad_input, grad_shift, grad_scale = norm_backward(grad_mixed, normed, inverse, scale, counted)
    return (grad_resid + grad_input, [grad_shift, grad_scale, grad_gate], grads)


def gather_weights(routes, attn_weight, mlp_weight):
    shards = []
    for layer in range(LAYERS):
        attn = attn_weight[layer].astype(jnp.bfloat16)
        mlp = mlp_weight[layer].astype(jnp.bfloat16)
        shards.append(
            (
                jnp.concatenate([attn[0], attn[1]], axis=1),
                jnp.concatenate([attn[2], attn[3]], axis=1),
                mlp[0],
                mlp[1],
            )
        )
    gathered = []
    earlier = []

    def in_turn(block):
        return after(block, earlier[-2]) if len(earlier) >= 2 else block

    for layer in range(LAYERS):
        query_key, value_out, up, down = shards[layer]
        pairs = []
        for block, across_last in ((query_key, True), (value_out, layer > 0)):
            both = routes.gather_both(in_turn(block), across_last)
            pairs.append(both)
            earlier.append(both[0])
        rows = []
        for block in (up, down):
            rows.append(routes.gather_rows(in_turn(block)))
            earlier.append(rows[-1])
        gathered.append((tuple(pairs), tuple(rows)))
    return gathered


def adam_update(weight, grad, first, second, count):
    first_new = beta_first * first + (1.0 - beta_first) * grad
    second_new = beta_second * second + (1.0 - beta_second) * grad * grad
    first_hat = first_new / (1.0 - jnp.power(beta_first, count))
    second_hat = second_new / (1.0 - jnp.power(beta_second, count))
    weight_new = weight - learn_rate * (
        first_hat / (jnp.sqrt(second_hat) + adam_eps) + weight_decay * weight
    )
    return [weight_new, first_new, second_new]


def body_steps(
    routes,
    latents,
    noise,
    timesteps,
    labels,
    step_count,
    tables,
    time_weight,
    cond_weight,
    cond_bias,
    attn_weight,
    mlp_weight,
    tables_first,
    tables_second,
    time_first,
    time_second,
    cond_first,
    cond_second,
    bias_first,
    bias_second,
    attn_first,
    attn_second,
    mlp_first,
    mlp_second,
):
    fsdp_index = lax.axis_index("fsdp")
    tp_index = lax.axis_index("tp")
    across_index = tp_index // 2
    num_fsdp = routes.num_fsdp
    local_seq = latents.shape[1]
    col_share = tables.shape[1]
    all_latents = timesteps.shape[0]
    total_entries = all_latents * SEQ * PATCH_DIM
    col_start = fsdp_index * col_share
    low_tables = tables.astype(jnp.bfloat16)

    gathered = gather_weights(routes, attn_weight, mlp_weight)
    head = routes.gather_rows(low_tables[: 2 * PATCH_DIM].T)

    features = timestep_features(timesteps).astype(jnp.bfloat16)
    time_pre = jnp.dot(
        features,
        low_tables[2 * PATCH_DIM : 2 * PATCH_DIM + FREQ],
        preferred_element_type=jnp.float32,
    )
    time_hidden = jax.nn.silu(time_pre).astype(jnp.bfloat16)
    label_hot = (labels[:, None] == jnp.arange(NCLASS, dtype=jnp.int32)[None, :]).astype(
        jnp.bfloat16
    )
    label_part = jnp.dot(
        label_hot, low_tables[2 * PATCH_DIM + FREQ :], preferred_element_type=jnp.float32
    )
    low_time = time_weight.astype(jnp.bfloat16)
    cond_part = jnp.dot(time_hidden, low_time, preferred_element_type=jnp.float32)
    placed = lax.dynamic_update_slice(
        jnp.zeros((all_latents, D), jnp.float32), label_part, (0, col_start)
    )
    cond = routes.sum_fsdp(cond_part + placed)
    cond_act = jax.nn.silu(cond).astype(jnp.bfloat16)
    low_cond = cond_weight.astype(jnp.bfloat16)
    low_bias = cond_bias.astype(jnp.bfloat16).astype(jnp.float32)
    mod_part = dot_f32(cond_act, low_cond, 1, 1) + low_bias[None, :]
    modul = lax.all_to_all(
        mod_part.astype(jnp.bfloat16), "fsdp", split_axis=0, concat_axis=1, tiled=True
    )
    modul = lax.dynamic_slice_in_dim(modul, across_index, 1, 0)

    slots = jnp.arange(num_fsdp, dtype=jnp.int32)
    owners = routes.slot_owner(fsdp_index, slots)
    slot_hot = (owners[:, None] == slots[None, :]).astype(jnp.bfloat16)
    pieces_all = jnp.einsum(
        "pfr,sf->psr",
        modul.reshape(-1, num_fsdp, col_share),
        slot_hot,
        preferred_element_type=jnp.float32,
    ).reshape(-1, D)

    data = jnp.stack([latents, noise], axis=1)
    own_data = lax.dynamic_index_in_dim(data, across_index, 0, keepdims=False)
    far_data = lax.dynamic_index_in_dim(data, 1 - across_index, 0, keepdims=False)
    first_data = jnp.concatenate([own_data, routes.across(far_data)], axis=1)
    chip_data = jnp.concatenate([first_data, routes.core(first_data)], axis=1)
    clean, noise_part = (chip_data[0], chip_data[1])
    chunks = jnp.stack([tp_index, tp_index ^ 2, tp_index ^ 1, tp_index ^ 3])
    token_ids = (
        chunks[:, None] * local_seq + jnp.arange(local_seq, dtype=jnp.int32)[None, :]
    ).reshape(-1)
    counted = token_ids.shape[0] // 2

    quarter = D // 4
    col_ids = (
        owners[:, None] * col_share + jnp.arange(col_share, dtype=jnp.int32)[None, :]
    ).reshape(-1)
    omegas = 1.0 / jnp.power(10000.0, (col_ids % quarter).astype(jnp.float32) / quarter)
    angles = jnp.arange(GRID, dtype=jnp.float32)[:, None] * omegas[None, :]
    kinds = (col_ids // quarter)[None, :]
    waves = jnp.where(kinds % 2 == 0, jnp.sin(angles), jnp.cos(angles))
    row_waves = jnp.where(kinds < 2, waves, 0.0)
    col_waves = jnp.where(kinds >= 2, waves, 0.0)
    grid_ids = jnp.arange(GRID, dtype=jnp.int32)[None, :]
    row_hot = (token_ids[:, None] // GRID == grid_ids).astype(jnp.float32)
    col_hot = (token_ids[:, None] % GRID == grid_ids).astype(jnp.float32)
    positions = jnp.dot(
        jnp.concatenate([row_hot, col_hot], axis=1),
        jnp.concatenate([row_waves, col_waves], axis=0),
        precision=lax.Precision.HIGHEST,
    )

    latent_id = fsdp_index * latents.shape[0] + across_index
    share = signal_share(lax.dynamic_slice_in_dim(timesteps, latent_id, 1))[:, None]
    noisy = (jnp.sqrt(share) * clean + jnp.sqrt(1.0 - share) * noise_part).astype(jnp.bfloat16)
    resid = dot_f32(noisy, head[:, :PATCH_DIM], 1, 1) + positions

    saved = []
    for layer in range(LAYERS):
        pieces = [pieces_all[6 * layer + k][None, :] for k in range(6)]
        attn_w, mlp_w = gathered[layer]
        resid, attn_saved = branch_forward(routes, resid, pieces[:3], attend, attn_w)
        resid, mlp_saved = branch_forward(routes, resid, pieces[3:], feed_forward, mlp_w)
        saved.append((attn_saved, mlp_saved))
    final_shift = pieces_all[6 * LAYERS][None, :]
    final_scale = pieces_all[6 * LAYERS + 1][None, :]
    final_low, final_normed, final_inverse = modulate(resid, final_shift, final_scale)
    predicted = dot_f32(final_low, head[:, PATCH_DIM:], 1, 0)
    difference = predicted - noise_part
    loss_part = jnp.sum(difference[:counted] * difference[:counted])
    grad_pred = (difference * (2.0 / total_entries)).astype(jnp.bfloat16)
    output_grad = dot_f32(final_low[:counted], grad_pred[:counted], 0, 0)
    grad_final = dot_f32(grad_pred, head[:, PATCH_DIM:], 1, 1)
    grad_resid, grad_fshift, grad_fscale = norm_backward(
        grad_final, final_normed, final_inverse, final_scale, counted
    )
    layer_mods = [None] * LAYERS
    layer_grads = [None] * LAYERS
    for layer in reversed(range(LAYERS)):
        pieces = [pieces_all[6 * layer + k][None, :] for k in range(6)]
        attn_w, mlp_w = gathered[layer]
        grad_resid, mlp_mods, mlp_grads = branch_backward(
            routes, grad_resid, pieces[3:], saved[layer][1], feed_backward, mlp_w
        )
        grad_resid, attn_mods, attn_grads = branch_backward(
            routes, grad_resid, pieces[:3], saved[layer][0], attend_backward, attn_w
        )
        layer_mods[layer] = attn_mods + mlp_mods
        layer_grads[layer] = attn_grads + mlp_grads
    grad_embed = grad_resid.astype(jnp.bfloat16)
    patch_grad = dot_f32(grad_embed[:counted], noisy[:counted], 0, 0)

    head_grad = jnp.concatenate([patch_grad, output_grad], axis=1)
    head_grad = head_grad + routes.core(head_grad)
    head_grad = head_grad + routes.across(head_grad)
    head_cols = routes.scatter_rows(head_grad, jnp.float32).T

    modul_grad = jnp.stack(layer_mods[0] + layer_mods[1] + [grad_fshift, grad_fscale])
    modul_grad = (modul_grad + routes.core(modul_grad)).astype(jnp.bfloat16)
    modul_grad = jnp.einsum(
        "psr,sf->pfr",
        modul_grad.reshape(-1, num_fsdp, col_share),
        slot_hot,
        preferred_element_type=jnp.float32,
    ).astype(jnp.bfloat16)
    modul_back = lax.all_to_all(
        modul_grad.reshape(num_fsdp, -1), "fsdp", split_axis=0, concat_axis=0, tiled=True
    )
    far_back = routes.across(modul_back)
    is_first = across_index == 0
    modul_back = jnp.stack(
        [jnp.where(is_first, modul_back, far_back), jnp.where(is_first, far_back, modul_back)],
        axis=1,
    ).reshape(all_latents, -1)
    cond_grad_w = dot_f32(modul_back, cond_act, 0, 0)
    bias_grad = jnp.sum(modul_back.astype(jnp.float32), axis=0)
    grad_cond_act = routes.sum_fsdp(dot_f32(modul_back, low_cond, 1, 0))
    silu_slope = jax.vjp(jax.nn.silu, cond)[1]
    grad_cond = silu_slope(grad_cond_act)[0].astype(jnp.bfloat16)
    time_grad = dot_f32(time_hidden, grad_cond, 0, 0)
    grad_hidden = dot_f32(grad_cond, low_time, 1, 1)
    time_slope = jax.vjp(jax.nn.silu, time_pre)[1]
    grad_pre = time_slope(grad_hidden)[0].astype(jnp.bfloat16)
    first_layer_grad = dot_f32(features, grad_pre, 0, 0)
    cond_cols = lax.dynamic_slice_in_dim(grad_cond, col_start, col_share, 1)
    label_grad = dot_f32(label_hot, cond_cols, 0, 0)
    tables_grad = jnp.concatenate([head_cols, first_layer_grad, label_grad], axis=0)

    squares = sum(jnp.sum(part * part) for parts in layer_grads for part in parts)
    owner = (tp_index == 0).astype(jnp.float32)
    squares = squares + owner * sum(
        jnp.sum(part * part) for part in (tables_grad, time_grad, cond_grad_w, bias_grad)
    )
    totals = routes.sum_all(jnp.stack([loss_part, squares]))
    loss = totals[0] / total_entries
    norm = jnp.sqrt(totals[1])
    entries = NTAB * D + D * D + (D + 1) * NCOND + LAYERS * (4 * D * D + 2 * D * FF)
    limit = clip_scale * math.sqrt(entries / (all_latents * SEQ))
    factor = jnp.minimum(1.0, limit / norm)
    count = step_count[0].astype(jnp.float32)
    width = attn_weight.shape[3]
    attn_grad = jnp.stack(
        [
            jnp.stack([qk[:, :width], qk[:, width:], vo[:, :width], vo[:, width:]])
            for qk, vo, _, _ in layer_grads
        ]
    )
    mlp_grad = jnp.stack([jnp.stack([up, down]) for _, _, up, down in layer_grads])
    weights_all = (tables, time_weight, cond_weight, cond_bias, attn_weight, mlp_weight)
    grads_all = (tables_grad, time_grad, cond_grad_w, bias_grad, attn_grad, mlp_grad)
    states = (
        (tables_first, tables_second),
        (time_first, time_second),
        (cond_first, cond_second),
        (bias_first, bias_second),
        (attn_first, attn_second),
        (mlp_first, mlp_second),
    )
    results = [loss, norm]
    for weight, grad, state in zip(weights_all, grads_all, states):
        results.extend(adam_update(weight, grad * factor, state[0], state[1], count))
    return tuple(results)


MESH = pl.DeviceIdType.MESH
VMEM_LIMIT = 60 * 1024 * 1024
LANES = 128
HALF = 128
TOKENS = 256


class Place:
    def __init__(self):
        self.f = lax.axis_index("fsdp")
        self.t = lax.axis_index("tp")
        self.z = self.f // 2
        self.y = lax.rem(self.f, 2)
        self.core = (self.f, self.t + 1 - 2 * lax.rem(self.t, 2))
        self.across = (self.f, lax.rem(self.t + 2, 4))
        self.diagonal = (self.f, 3 - self.t)
        self.pair = (self.f + 1 - 2 * self.y, self.t)

    def down_z(self, k):
        return (lax.rem(self.z + 4 - k, 4) * 2 + self.y, self.t)

    def up_z(self, k):
        return (lax.rem(self.z + k, 4) * 2 + self.y, self.t)

    def up_f(self, k):
        return (lax.rem(self.f + k, 8), self.t)

    def slot_of(self, owner):
        pair_part = lax.rem(self.y + owner % 2, 2)
        return pair_part * 4 + lax.rem(owner // 2 + 4 - self.z, 4)


class Mail:
    def __init__(self, send_sem, recv_sem, local_sem):
        self.send_sem, self.recv_sem, self.local_sem = (send_sem, recv_sem, local_sem)
        self.sent = []
        self.local = []

    def send(self, source, target, device):
        index = len(self.sent)
        copy = pltpu.make_async_remote_copy(
            src_ref=source,
            dst_ref=target,
            send_sem=self.send_sem.at[index],
            recv_sem=self.recv_sem.at[index],
            device_id=device,
            device_id_type=MESH,
        )
        copy.start()
        self.sent.append(copy)
        return copy

    def move(self, source, target):
        copy = pltpu.make_async_copy(source, target, self.local_sem.at[len(self.local)])
        copy.start()
        self.local.append(copy)
        return copy

    def finish(self, skip=()):
        for copy in self.sent:
            copy.wait_send()
        for copy in self.local:
            if not any(copy is other for other in skip):
                copy.wait()


def greet(place):
    barrier = pltpu.get_barrier_semaphore()
    friends = [place.up_f(k) for k in range(1, 8)]
    friends += [place.core, place.across, place.diagonal]
    for device in friends:
        pl.semaphore_signal(barrier, inc=1, device_id=device, device_id_type=MESH)
    pl.semaphore_wait(barrier, len(friends))


def mm(left, right):
    return lax.dot_general(left, right, (((1,), (0,)), ((), ())), preferred_element_type=jnp.float32)


def mm_nt(left, right):
    return lax.dot_general(left, right, (((1,), (1,)), ((), ())), preferred_element_type=jnp.float32)


def mm_tn(left, right):
    return lax.dot_general(left, right, (((0,), (0,)), ((), ())), preferred_element_type=jnp.float32)


class Gather:
    def __init__(self, place, mail, shard, own, other=None):
        self.place, self.mail, self.shard, self.own, self.other = (place, mail, shard, own, other)
        self.rows = shard.shape[0]

    def at(self, ref, slot):
        return ref.at[pl.ds(slot * self.rows, self.rows)]

    def start_z(self):
        self.kept = self.mail.move(self.shard, self.at(self.own, 0))
        self.from_z = [
            self.mail.send(self.shard, self.at(self.own, k), self.place.down_z(k))
            for k in range(1, 4)
        ]

    def start_y(self):
        self.from_y = [self.mail.send(self.shard, self.at(self.own, 4), self.place.pair)]

    def start_x(self):
        self.from_x = [self.mail.send(self.shard, self.at(self.other, 0), self.place.across)]

    def pass_z(self):
        for k in range(1, 4):
            self.from_z[k - 1].wait_recv()
            block = self.at(self.own, k)
            self.from_y.append(self.mail.send(block, self.at(self.own, 4 + k), self.place.pair))
            if self.other is not None:
                self.from_x.append(self.mail.send(block, self.at(self.other, k), self.place.across))

    def pass_y(self, slots=(0, 1, 2, 3)):
        for k in slots:
            self.from_y[k].wait_recv()
            if self.other is not None:
                block = self.at(self.own, 4 + k)
                target = self.at(self.other, 4 + k)
                self.from_x.append(self.mail.send(block, target, self.place.across))

    def pass_x(self):
        if self.other is not None:
            for copy in self.from_x:
                copy.wait_recv()
        self.kept.wait()


def gelu_parts(value):
    inner = math.sqrt(2.0 / math.pi) * (value + 0.044715 * (value * value * value))
    return 0.5 * (1.0 + jnp.tanh(inner))


def half_mask(rows, upper):
    lanes = lax.broadcasted_iota(jnp.int32, (rows, LANES), 1)
    return lanes >= 64 if upper else lanes < 64


def forward_kernel(shapes, total_entries, *refs):
    names = list(shapes)
    r = SimpleNamespace(**dict(zip(names, refs)))
    rest = refs[len(names) :]
    outs = SimpleNamespace(**dict(zip(FORWARD_OUTS, rest)))
    rest = rest[len(FORWARD_OUTS) :]
    s = SimpleNamespace(**dict(zip(FORWARD_SCRATCH, rest)))
    rest = rest[len(FORWARD_SCRATCH) :]
    mail = Mail(*rest)
    place = Place()
    greet(place)

    attn = [
        Gather(place, mail, r.shards.at[l, 0], s.wattn.at[l, 0], s.wattn.at[l, 1])
        for l in range(LAYERS)
    ]
    up = [Gather(place, mail, r.shards.at[l, 1], s.wmlp.at[l, 0]) for l in range(LAYERS)]
    down = [Gather(place, mail, r.shards.at[l, 2], s.wmlp.at[l, 1]) for l in range(LAYERS)]

    across_index = place.t // 2
    core_index = lax.rem(place.t, 2)
    cond_loaded = mail.move(r.cond_weight, s.cond_weight)
    cond_own = r.cond_part.at[across_index, core_index]
    cond_from = [mail.send(cond_own, s.cond_in.at[k - 1], place.up_f(k)) for k in range(1, 8)]
    own_data = r.data.at[across_index]
    data_far = mail.send(r.data.at[1 - across_index], s.data_in.at[1], place.across)
    data_side = mail.send(own_data, s.data_in.at[2], place.core)
    attn[0].start_z()
    attn[0].start_y()
    attn[0].start_x()
    head_rows = r.head.shape[0]
    head_kept = mail.move(r.head, s.head.at[pl.ds(0, head_rows)])
    data_kept = mail.move(own_data, s.data_in.at[0])
    head_from = [
        mail.send(r.head, s.head.at[pl.ds(k * head_rows, head_rows)], place.down_z(k))
        for k in range(1, 4)
    ]
    attn[1].start_y()
    up[0].start_y()

    rows_id = lax.broadcasted_iota(jnp.int32, (LANES, D), 0)
    offset = lax.broadcasted_iota(jnp.int32, (LANES, D), 1) - rows_id
    for owner in range(8):
        hit = (offset == place.slot_of(owner) * head_rows) & (rows_id < head_rows)
        s.order[pl.ds(owner * LANES, LANES), :] = jnp.where(hit, 1.0, 0.0).astype(jnp.bfloat16)

    waves = mm(r.waves[...], s.order[...])
    s.waves[...] = waves[0:32] + waves[32:64] + waves[64:96]

    part = r.cond_part[across_index, core_index]
    for k in range(7):
        cond_from[k].wait_recv()
        part = part + s.cond_in[k]
    s.cond[across_index, core_index] = part
    cond_part = s.cond.at[across_index, core_index]
    cond_side = mail.send(cond_part, cond_part, place.core)
    data_far.wait_recv()
    data_diagonal = mail.send(s.data_in.at[1], s.data_in.at[3], place.core)
    attn[0].pass_y((0,))
    cond_side.wait_recv()
    cond_half = s.cond.at[across_index]
    cond_far = mail.send(cond_half, cond_half, place.across)
    cond = jnp.concatenate([s.cond[across_index, 0], s.cond[across_index, 1]], axis=0)
    cond_act = (cond * jax.nn.sigmoid(cond)).astype(jnp.bfloat16)
    blocks = r.cond_weight.shape[0]
    cond_loaded.wait()
    for b in range(blocks):
        part = mm_nt(cond_act, s.cond_weight[b].astype(jnp.bfloat16)) + r.cond_bias[b : b + 1, :]
        part = part.astype(jnp.bfloat16).astype(jnp.float32)
        for i in range(8):
            s.mod_out[i, b : b + 1, 0:head_rows] = part[i : i + 1, :]
    mod_from = []
    for k in range(1, 8):
        source = s.mod_out.at[lax.rem(place.f + k, 8)]
        mod_from.append(mail.send(source, s.mod_in.at[k], place.up_f(k)))
    mod_kept = mail.move(s.mod_out.at[place.f], s.mod_in.at[0])
    attn[1].start_z()

    attn[0].pass_z()
    up[0].start_z()
    for k in range(3):
        head_from[k].wait_recv()
    head_kept.wait()
    lower = s.head.at[pl.ds(0, 4 * head_rows)]
    upper = s.head.at[pl.ds(4 * head_rows, 4 * head_rows)]
    head_pair = mail.send(lower, upper, place.pair)
    attn[1].start_x()
    down[0].start_y()
    up[1].start_y()
    down[1].start_y()

    mod_kept.wait()
    for copy in mod_from:
        copy.wait_recv()
    s.mod_rows[...] = jnp.zeros_like(s.mod_rows)
    for g in range(8 * blocks):
        piece, owner = (g // 8, g % 8)
        k = lax.rem(place.f + 8 - g // blocks, 8)
        b = g % blocks
        s.mod_rows[piece : piece + 1, owner * LANES : owner * LANES + head_rows] = s.mod_in[
            k, b : b + 1, 0:head_rows
        ]
    s.pieces[...] = mm(s.mod_rows[...].astype(jnp.bfloat16), s.order[...])
    mail.move(s.pieces, outs.pieces)

    data_kept.wait()
    data_side.wait_recv()
    data_diagonal.wait_recv()
    head_pair.wait_recv()
    cond_far.wait_recv()
    mail.move(s.cond, outs.cond)
    mail.move(s.head, outs.head)
    chunk_rows = s.data_in.shape[1] // 2
    grid_rows = chunk_rows // GRID
    cols = s.waves[16:32, :]
    chunk_ids = [place.t, place.across[1], place.core[1], place.diagonal[1]]
    for j in range(4):
        low = pl.ds(j * chunk_rows, chunk_rows)
        s.noisy[low, :] = s.data_in[j, 0:chunk_rows, :].astype(jnp.bfloat16)
        s.noise[low, :] = s.data_in[j, chunk_rows : 2 * chunk_rows, :]
        for i in range(grid_rows):
            row = s.waves[pl.ds(chunk_ids[j] * grid_rows + i, 1), :]
            s.resid[pl.ds(j * chunk_rows + i * GRID, GRID), :] = cols + row
    mail.move(s.noisy, outs.noisy)
    for n in range(0, D, 256):
        s.resid[:, n : n + 256] += mm_nt(s.noisy[...], s.head[n : n + 256, :])

    def piece(index):
        return s.pieces[index : index + 1, :]

    def normalize(which, shift, scale, target, low):
        value = s.resid[low : low + HALF, :]
        centred = value - jnp.mean(value, axis=-1, keepdims=True)
        inverse = lax.rsqrt(jnp.mean(centred * centred, axis=-1, keepdims=True) + norm_eps)
        normed = centred * inverse
        s.normed[which, low : low + HALF, :] = normed
        s.inverse[which, low : low + HALF, :] = jnp.broadcast_to(inverse, (HALF, LANES))
        target[low : low + HALF, :] = (normed * (1.0 + scale) + shift).astype(jnp.bfloat16)
        if low:
            mail.move(s.normed.at[which], outs.normed.at[which])
            mail.move(s.inverse.at[which], outs.inverse.at[which])

    low_mask = half_mask(TOKENS, False)
    high_mask = half_mask(TOKENS, True)
    for l in range(LAYERS):
        base = 6 * l
        hidden = s.hidden.at[l]
        for low in (0, HALF):
            normalize(2 * l, piece(base), piece(base + 1), hidden, low)
        if l == 0:
            attn[0].pass_y((1, 2, 3))
            attn[1].pass_z()
            down[0].start_z()
        attn[l].pass_x()
        for x in range(2):
            weight = s.wattn.at[l, x]
            qkv = s.qkv.at[l, x]
            for n in range(0, D, 256):
                qkv[:, n : n + 256] = mm(hidden[...], weight[:, n : n + 256]).astype(jnp.bfloat16)
        for x in range(2):
            qkv = s.qkv.at[l, x]
            att = s.att.at[l, x]
            for h, (q, k, v, keep) in enumerate(
                ((0, 1, 2, low_mask), (0, 1, 2, high_mask), (3, 4, 5, low_mask))
            ):
                query = qkv[:, q * LANES : (q + 1) * LANES].astype(jnp.float32)
                query = jnp.where(keep, query, 0.0)
                key = qkv[:, k * LANES : (k + 1) * LANES]
                value = qkv[:, v * LANES : (v + 1) * LANES]
                scores = mm_nt(query.astype(jnp.bfloat16), key) * HEAD_DIM ** (-0.5)
                exped = jnp.exp(scores - jnp.max(scores, axis=-1, keepdims=True))
                probs = exped / jnp.sum(exped, axis=-1, keepdims=True)
                s.probs[l, x, h] = probs
                mixed = mm(probs.astype(jnp.bfloat16), value)
                if h != 1:
                    mixed = pltpu.roll(mixed, 64, 1)
                att[:, h * LANES : (h + 1) * LANES] = jnp.where(high_mask, mixed, 0.0).astype(
                    jnp.bfloat16
                )
            if x == 0 and l == 0:
                up[0].pass_z()
                up[1].start_z()
            elif x == 0:
                down[1].pass_z()
        for n in range(0, D, 256):
            total = mm_nt(s.att[l, 0], s.wattn[l, 0, n : n + 256, 384:768])
            total = total + mm_nt(s.att[l, 1], s.wattn[l, 1, n : n + 256, 384:768])
            s.core_out[l, :, n : n + 256] = total.astype(jnp.bfloat16)
        summed = mail.send(s.core_out.at[l], s.core_in.at[l], place.core)
        gate = piece(base + 2)
        summed.wait_recv()
        for low in (0, HALF):
            output = s.core_out[l, low : low + HALF, :].astype(jnp.float32)
            output = output + s.core_in[l, HALF - low : 2 * HALF - low, :].astype(jnp.float32)
            s.attn_out[l, low : low + HALF, :] = output
            s.resid[low : low + HALF, :] += gate * output
        rows = s.rows.at[l]
        normalize(2 * l + 1, piece(base + 3), piece(base + 4), rows, 0)
        far = mail.send(rows.at[pl.ds(0, HALF)], rows.at[pl.ds(2 * HALF, HALF)], place.across)
        normalize(2 * l + 1, piece(base + 3), piece(base + 4), rows, HALF)
        for source, target in (
            (s.hidden, outs.hidden),
            (s.qkv, outs.qkv),
            (s.att, outs.att),
            (s.probs, outs.probs),
            (s.attn_out, outs.attn_out),
            (s.wattn, outs.wattn),
        ):
            mail.move(source.at[l], target.at[l])
        if l == 0:
            attn[1].pass_y()
            down[0].pass_z()
            down[1].start_z()
        up[l].pass_y()
        up[l].pass_x()
        w_up = s.wmlp.at[l, 0]
        w_down = s.wmlp.at[l, 1]

        def rise(low, size):
            for n in range(0, D, 256):
                upward = mm(rows[low : low + size, :], w_up[:, n : n + 256])
                s.upward[l, low : low + size, n : n + 256] = upward
                s.active[l, low : low + size, n : n + 256] = (
                    upward * gelu_parts(upward)
                ).astype(jnp.bfloat16)

        rise(0, HALF)
        rise(HALF, HALF)
        far.wait_recv()
        side = mail.send(
            rows.at[pl.ds(2 * HALF, HALF)], rows.at[pl.ds(3 * HALF, HALF)], place.core
        )
        rise(2 * HALF, HALF)
        side.wait_recv()
        rise(3 * HALF, HALF)
        down[l].pass_y()
        down[l].pass_x()

        def fall(low, target):
            for n in range(0, D, 256):
                part = mm_nt(s.active[l, low : low + HALF, :], w_down[n : n + 256, :])
                target[:, n : n + 256] = part.astype(target.dtype)

        sum_out, sum_in, keep = (s.sum_out.at[l], s.sum_in.at[l], s.keep)
        fall(3 * HALF, sum_out.at[0])
        first = mail.send(sum_out.at[0], sum_in.at[0], place.core)
        fall(2 * HALF, keep.at[0])
        fall(HALF, sum_out.at[1])
        second = mail.send(sum_out.at[1], sum_in.at[1], place.core)
        first.wait_recv()
        s.far_out[l] = (keep[0] + sum_in[0].astype(jnp.float32)).astype(jnp.bfloat16)
        third = mail.send(s.far_out.at[l], s.far_in.at[l], place.across)
        if l == 0:
            up[1].pass_z()
        fall(0, keep.at[1])
        second.wait_recv()
        keep[1] = keep[1] + sum_in[1].astype(jnp.float32)
        for source, target in (
            (s.rows, outs.rows),
            (s.upward, outs.upward),
            (s.active, outs.active),
            (s.wmlp, outs.wmlp),
        ):
            mail.move(source.at[l], target.at[l])
        third.wait_recv()
        total = (keep[1] + s.far_in[l].astype(jnp.float32)).astype(jnp.bfloat16)
        s.own_out[l] = total
        fourth = mail.send(s.own_out.at[l], s.own_in.at[l], place.core)
        gate = piece(base + 5)
        output = total.astype(jnp.float32)
        s.mlp_out[l, 0:HALF, :] = output
        s.resid[0:HALF, :] += gate * output
        fourth.wait_recv()
        output = s.own_in[l].astype(jnp.float32)
        s.mlp_out[l, HALF : 2 * HALF, :] = output
        s.resid[HALF : 2 * HALF, :] += gate * output
        mail.move(s.mlp_out.at[l], outs.mlp_out.at[l])

    for low in (0, HALF):
        normalize(
            2 * LAYERS, piece(6 * LAYERS), piece(6 * LAYERS + 1), s.final_low, low
        )
    predicted = mm(s.final_low[...], s.head[...])
    lanes = lax.broadcasted_iota(jnp.int32, (TOKENS, LANES), 1)
    taken = (lanes >= PATCH_DIM) & (lanes < 2 * PATCH_DIM)
    difference = jnp.where(taken, predicted - s.noise[...], 0.0)
    square = difference[0:HALF] * difference[0:HALF]
    s.loss[...] = jnp.sum(square.reshape(HALF // 8, 8, LANES), axis=0)
    s.grad_pred[...] = (difference * (2.0 / total_entries)).astype(jnp.bfloat16)
    for source, target in (
        (s.final_low, outs.final_low),
        (s.loss, outs.loss),
        (s.grad_pred, outs.grad_pred),
    ):
        mail.move(source, target)
    waited = [cond_loaded, head_kept, data_kept, mod_kept] + [g.kept for g in attn + up + down]
    mail.finish(waited)


FORWARD_OUTS = dict(
    wattn=((LAYERS, 2, D, D), jnp.bfloat16),
    wmlp=((LAYERS, 2, D, D), jnp.bfloat16),
    head=((D, LANES), jnp.bfloat16),
    pieces=((16, D), jnp.float32),
    cond=((2, 2, 4, D), jnp.float32),
    hidden=((LAYERS, TOKENS, D), jnp.bfloat16),
    qkv=((LAYERS, 2, TOKENS, D), jnp.bfloat16),
    att=((LAYERS, 2, TOKENS, D // 2), jnp.bfloat16),
    probs=((LAYERS, 2, 3, TOKENS, TOKENS), jnp.float32),
    attn_out=((LAYERS, TOKENS, D), jnp.float32),
    rows=((LAYERS, 2 * TOKENS, D), jnp.bfloat16),
    upward=((LAYERS, 2 * TOKENS, D), jnp.float32),
    active=((LAYERS, 2 * TOKENS, D), jnp.bfloat16),
    mlp_out=((LAYERS, TOKENS, D), jnp.float32),
    normed=((2 * LAYERS + 1, TOKENS, D), jnp.float32),
    inverse=((2 * LAYERS + 1, TOKENS, LANES), jnp.float32),
    final_low=((TOKENS, D), jnp.bfloat16),
    noisy=((TOKENS, LANES), jnp.bfloat16),
    grad_pred=((TOKENS, LANES), jnp.bfloat16),
    loss=((8, LANES), jnp.float32),
)
FORWARD_OWN = dict(
    cond_weight=((NCOND // D, D // 8, D), jnp.float32),
    order=((8 * LANES, D), jnp.bfloat16),
    waves=((32, D), jnp.float32),
    cond_in=((7, 4, D), jnp.float32),
    data_in=((4, HALF, LANES), jnp.float32),
    noise=((TOKENS, LANES), jnp.float32),
    mod_out=((8, 16, LANES), jnp.float32),
    mod_in=((8, 16, LANES), jnp.float32),
    mod_rows=((16, 8 * LANES), jnp.float32),
    resid=((TOKENS, D), jnp.float32),
    core_out=((LAYERS, TOKENS, D), jnp.bfloat16),
    core_in=((LAYERS, TOKENS, D), jnp.bfloat16),
    sum_out=((LAYERS, 2, HALF, D), jnp.bfloat16),
    sum_in=((LAYERS, 2, HALF, D), jnp.bfloat16),
    far_out=((LAYERS, HALF, D), jnp.bfloat16),
    far_in=((LAYERS, HALF, D), jnp.bfloat16),
    own_out=((LAYERS, HALF, D), jnp.bfloat16),
    own_in=((LAYERS, HALF, D), jnp.bfloat16),
    keep=((2, HALF, D), jnp.float32),
)
FORWARD_SCRATCH = {**FORWARD_OUTS, **FORWARD_OWN}


def run_forward(inputs, total_entries):
    vmem = pl.BlockSpec(memory_space=pltpu.VMEM)
    outs = pl.pallas_call(
        partial(forward_kernel, {name: value.shape for name, value in inputs.items()}, total_entries),
        out_shape=[jax.ShapeDtypeStruct(*spec) for spec in FORWARD_OUTS.values()],
        in_specs=[
            pl.BlockSpec(memory_space=pl.ANY) if value.size > D * D * 2 and value.dtype == jnp.float32 else vmem
            for value in inputs.values()
        ],
        out_specs=[pl.BlockSpec(memory_space=pl.ANY)] * len(FORWARD_OUTS),
        scratch_shapes=[pltpu.VMEM(*spec) for spec in FORWARD_SCRATCH.values()]
        + [
            pltpu.SemaphoreType.DMA((128,)),
            pltpu.SemaphoreType.DMA((128,)),
            pltpu.SemaphoreType.DMA((64,)),
        ],
        compiler_params=pltpu.CompilerParams(
            collective_id=0, has_side_effects=True, vmem_limit_bytes=VMEM_LIMIT
        ),
    )(*inputs.values())
    return SimpleNamespace(**dict(zip(FORWARD_OUTS, outs)))
class Scatter:
    def __init__(self, place, mail, grad, from_y, from_z, result, other=None, from_x=None):
        self.place, self.mail, self.grad, self.result = (place, mail, grad, result)
        self.from_y, self.from_z, self.other, self.from_x = (from_y, from_z, other, from_x)
        self.rows = result.shape[0]
        self.x_copies, self.y_copies, self.z_copies = ({}, {}, {})

    def at(self, ref, slot):
        return ref.at[pl.ds(slot * self.rows, self.rows)]

    def start(self, slots=(4, 5, 6, 7)):
        for slot in slots:
            if self.other is None:
                self.send_y(slot)
            else:
                self.x_copies[slot] = self.mail.send(
                    self.at(self.other, slot), self.at(self.from_x, slot), self.place.across
                )

    def send_y(self, slot):
        self.y_copies[slot - 4] = self.mail.send(
            self.at(self.grad, slot), self.at(self.from_y, slot - 4), self.place.pair
        )

    def total(self, slot, refs):
        low = slot * self.rows
        value = self.grad[low : low + self.rows, :].astype(jnp.float32)
        for ref in refs:
            value = value + ref[low : low + self.rows, :].astype(jnp.float32)
        return value

    def pass_x(self):
        for slot in (4, 5, 6, 7):
            if self.other is not None:
                self.x_copies[slot].wait_recv()
                low = slot * self.rows
                self.grad[low : low + self.rows, :] = self.total(slot, [self.from_x]).astype(
                    jnp.bfloat16
                )
                self.send_y(slot)

    def pass_y(self):
        refs = [self.from_y] if self.other is None else [self.from_x, self.from_y]
        for slot in (1, 2, 3, 0):
            if self.other is not None:
                self.x_copies[slot].wait_recv()
            self.y_copies[slot].wait_recv()
            value = self.total(slot, refs)
            if slot == 0:
                self.result[...] = value
            else:
                low = slot * self.rows
                self.grad[low : low + self.rows, :] = value.astype(jnp.bfloat16)
                self.z_copies[slot] = self.mail.send(
                    self.at(self.grad, slot), self.from_z.at[slot - 1], self.place.up_z(slot)
                )

    def pass_z(self):
        value = self.result[...]
        for slot in (1, 2, 3):
            self.z_copies[slot].wait_recv()
            value = value + self.from_z[slot - 1].astype(jnp.float32)
        self.result[...] = value


def gelu_slope(value):
    const = math.sqrt(2.0 / math.pi)
    square = value * value
    tanh = jnp.tanh(const * (value + 0.044715 * (square * value)))
    return 0.5 * (1.0 + tanh) + 0.5 * value * (1.0 - tanh * tanh) * (
        const * (1.0 + (3.0 * 0.044715) * square)
    )


def backward_kernel(*refs):
    r = SimpleNamespace(**dict(zip(BACKWARD_INS, refs)))
    rest = refs[len(BACKWARD_INS) :]
    outs = SimpleNamespace(**dict(zip(BACKWARD_OUTS, rest)))
    rest = rest[len(BACKWARD_OUTS) :]
    s = SimpleNamespace(**dict(zip(BACKWARD_SCRATCH, rest)))
    rest = rest[len(BACKWARD_SCRATCH) :]
    mail = Mail(*rest)
    place = Place()
    loaded = {}
    waited = []

    def load(name, index=None):
        source = getattr(r, name)
        source = source if index is None else source.at[index]
        loaded[name] = mail.move(source, getattr(s, name))

    def need(*names):
        for name in names:
            if name in loaded:
                copy = loaded.pop(name)
                copy.wait()
                waited.append(copy)

    for name in FINAL_KEPT:
        load(name)
    normed_from = {}

    def load_normed(which):
        normed_from[which] = [
            mail.move(r.normed.at[which], s.normed.at[which]),
            mail.move(r.inverse.at[which], s.inverse.at[which]),
        ]

    load_normed(2 * LAYERS)
    for name in list(MLP_KEPT) + list(ATTN_KEPT):
        load(name, LAYERS - 1)
    for which in reversed(range(2 * LAYERS)):
        load_normed(which)
    load(*LATE_KEPT)
    greet(place)

    head_rows = D // 8
    across_index = place.t // 2
    core_index = lax.rem(place.t, 2)
    rows_id = lax.broadcasted_iota(jnp.int32, (LANES, D), 0)
    offset = lax.broadcasted_iota(jnp.int32, (LANES, D), 1) - rows_id
    for owner in range(8):
        hit = (offset == place.slot_of(owner) * head_rows) & (rows_id < head_rows)
        s.order[pl.ds(owner * LANES, LANES), :] = jnp.where(hit, 1.0, 0.0).astype(jnp.bfloat16)
    s.mod_grad[...] = jnp.zeros_like(s.mod_grad)
    s.mod_send[...] = jnp.zeros_like(s.mod_send)

    def piece(index):
        return s.pieces[index : index + 1, :]

    def norm_back(which, mod_row, low, first):
        if low == 0:
            for copy in normed_from[which]:
                copy.wait()
                waited.append(copy)
        mixed = s.mixed[low : low + HALF, :]
        normed = s.normed[which, low : low + HALF, :]
        inverse = s.inverse[which, low : low + HALF, 0:1]
        if low == 0:
            s.mod_grad[mod_row : mod_row + 1, :] = jnp.sum(mixed, axis=0, keepdims=True)
            s.mod_grad[mod_row + 1 : mod_row + 2, :] = jnp.sum(
                mixed * normed, axis=0, keepdims=True
            )
        scaled = mixed * (1.0 + piece(mod_row + 1))
        centred = scaled - jnp.mean(scaled, axis=-1, keepdims=True)
        grad = (centred - normed * jnp.mean(scaled * normed, axis=-1, keepdims=True)) * inverse
        if first:
            s.grad[low : low + HALF, :] = grad
        else:
            s.grad[low : low + HALF, :] += grad

    need(*FINAL_KEPT)
    s.head_grad[...] = mm_tn(s.final_low[0:HALF, :], s.grad_pred[0:HALF, :])
    for n in range(0, D, 256):
        s.mixed[:, n : n + 256] = mm_nt(s.grad_pred[...], s.head[n : n + 256, :])
    for low in (0, HALF):
        norm_back(2 * LAYERS, 6 * LAYERS, low, True)

    def scatter(l, kind, index, other=None):
        if other is None:
            return Scatter(
                place, mail, s.mlp_grad.at[l, index], s.from_y.at[l, kind],
                s.from_z.at[l, kind], s.result.at[l, kind],
            )
        return Scatter(
            place, mail, s.attn_grad.at[l, 0], s.from_y.at[l, kind],
            s.from_z.at[l, kind], s.result.at[l, kind],
            s.attn_grad.at[l, 1], s.from_x.at[l],
        )

    attn = [scatter(l, 0, 0, True) for l in range(LAYERS)]
    up = [scatter(l, 1, 0) for l in range(LAYERS)]
    down = [scatter(l, 2, 1) for l in range(LAYERS)]

    low_mask = half_mask(TOKENS, False)
    high_mask = half_mask(TOKENS, True)
    for l in reversed(range(LAYERS)):
        base = 6 * l
        last = l == LAYERS - 1
        gate = piece(base + 5)
        need(*list(MLP_KEPT)[:1])
        grads = s.grad_rows.at[l]
        grads[0:HALF, :] = (gate * s.grad[0:HALF, :]).astype(jnp.bfloat16)
        far = mail.send(grads.at[pl.ds(0, HALF)], grads.at[pl.ds(2 * HALF, HALF)], place.across)
        grads[HALF : 2 * HALF, :] = (gate * s.grad[HALF : 2 * HALF, :]).astype(jnp.bfloat16)
        s.mod_grad[base + 5 : base + 6, :] = jnp.sum(
            s.grad[0:HALF, :] * s.mlp_out[0:HALF, :], axis=0, keepdims=True
        )
        if not last:
            attn[1].start((5, 6))
            up[1].pass_y()
        need(*MLP_KEPT)
        w_up, w_down = (s.wmlp.at[0], s.wmlp.at[1])

        def drop(low):
            for n in range(0, D, 256):
                part = mm(grads[low : low + HALF, :], w_down[:, n : n + 256])
                slope = gelu_slope(s.upward[low : low + HALF, n : n + 256])
                s.grad_up[low : low + HALF, n : n + 256] = (part * slope).astype(jnp.bfloat16)

        drop(0)
        drop(HALF)
        far.wait_recv()
        side = mail.send(
            grads.at[pl.ds(2 * HALF, HALF)], grads.at[pl.ds(3 * HALF, HALF)], place.core
        )
        drop(2 * HALF)
        side.wait_recv()
        drop(3 * HALF)

        def fall(low, target):
            for n in range(0, D, 256):
                part = mm_nt(s.grad_up[low : low + HALF, :], w_up[n : n + 256, :])
                target[:, n : n + 256] = part.astype(target.dtype)

        sum_out, sum_in, keep = (s.sum_out.at[l], s.sum_in.at[l], s.keep)
        fall(3 * HALF, sum_out.at[0])
        first = mail.send(sum_out.at[0], sum_in.at[0], place.core)
        fall(2 * HALF, keep.at[0])
        fall(HALF, sum_out.at[1])
        second = mail.send(sum_out.at[1], sum_in.at[1], place.core)
        first.wait_recv()
        s.far_out[l] = (keep[0] + sum_in[0].astype(jnp.float32)).astype(jnp.bfloat16)
        third = mail.send(s.far_out.at[l], s.far_in.at[l], place.across)
        if not last:
            attn[1].start((7, 1, 2, 3, 0))
        fall(0, keep.at[1])
        for n in range(0, D, 256):
            s.mlp_grad[l, 1, :, n : n + 256] = mm_tn(
                grads[...], s.active[:, n : n + 256]
            ).astype(jnp.bfloat16)
        down[l].start()
        second.wait_recv()
        keep[1] = keep[1] + sum_in[1].astype(jnp.float32)
        third.wait_recv()
        total = (keep[1] + s.far_in[l].astype(jnp.float32)).astype(jnp.bfloat16)
        s.own_out[l] = total
        fourth = mail.send(s.own_out.at[l], s.own_in.at[l], place.core)
        s.mixed[0:HALF, :] = total.astype(jnp.float32)
        norm_back(2 * l + 1, base + 3, 0, False)
        fourth.wait_recv()
        s.mixed[HALF : 2 * HALF, :] = s.own_in[l].astype(jnp.float32)
        norm_back(2 * l + 1, base + 3, HALF, False)
        for n in range(0, D, 256):
            s.mlp_grad[l, 0, :, n : n + 256] = mm_tn(
                s.rows[...], s.grad_up[:, n : n + 256]
            ).astype(jnp.bfloat16)
        up[l].start()
        if last:
            for name in MLP_KEPT:
                load(name, 0)

        gate = piece(base + 2)
        need(*ATTN_KEPT)
        both = s.both
        both[0:TOKENS, :] = s.hidden[...]
        both[TOKENS : 2 * TOKENS, :] = (gate * s.grad[...]).astype(jnp.bfloat16)
        s.mod_grad[base + 2 : base + 3, :] = jnp.sum(
            s.grad[0:HALF, :] * s.attn_out[0:HALF, :], axis=0, keepdims=True
        )
        scale = HEAD_DIM ** (-0.5)
        for x in range(2):
            qkv = s.qkv.at[x]
            grad_qkv = s.grad_qkv.at[x]

            def tile(ref, index):
                return ref[:, index * LANES : (index + 1) * LANES]

            def put(index, value):
                grad_qkv[0:TOKENS, index * LANES : (index + 1) * LANES] = value.astype(jnp.bfloat16)

            found = {}
            for h, (q, k, v, keep_mask) in enumerate(
                ((0, 1, 2, low_mask), (0, 1, 2, high_mask), (3, 4, 5, low_mask))
            ):
                weight = s.wattn[x, :, (3 + h) * LANES : (4 + h) * LANES]
                grad_att = mm(both[TOKENS : 2 * TOKENS, :], weight)
                if h != 1:
                    grad_att = pltpu.roll(grad_att, 64, 1)
                grad_att = jnp.where(keep_mask, grad_att, 0.0).astype(jnp.bfloat16)
                probs = s.probs[x, h]
                grad_probs = mm_nt(grad_att, tile(qkv, v))
                inner = jnp.sum(probs * grad_probs, axis=-1, keepdims=True)
                grad_scores = (probs * (grad_probs - inner)).astype(jnp.bfloat16)
                found[h] = (
                    jnp.where(keep_mask, mm(grad_scores, tile(qkv, k)) * scale, 0.0),
                    jnp.where(keep_mask, mm_tn(grad_scores, tile(qkv, q)) * scale, 0.0),
                    mm_tn(probs.astype(jnp.bfloat16), grad_att),
                )
                if h == 1:
                    for index in range(3):
                        put(index, found[0][index] + found[1][index])
                if h == 2:
                    for index in range(3):
                        put(3 + index, found[2][index])
            if last and x == 0:
                down[1].pass_y()
            elif not last and x == 0:
                attn[1].pass_x()
            elif not last:
                down[0].pass_y()
        for n in range(0, D, 256):
            part = mm_nt(s.grad_qkv[0, 0:TOKENS, :], s.wattn[0, n : n + 256, :])
            part = part + mm_nt(s.grad_qkv[1, 0:TOKENS, :], s.wattn[1, n : n + 256, :])
            s.core_out[l, :, n : n + 256] = part.astype(jnp.bfloat16)
        summed = mail.send(s.core_out.at[l], s.core_in.at[l], place.core)
        for x in (1, 0):
            s.grad_qkv[x, TOKENS : 2 * TOKENS, D // 2 : D] = s.att[x]
            half = s.grad_qkv[x, 0:TOKENS, 0 : D // 2]
            s.attn_grad[l, x, :, 0 : D // 2] = mm_tn(both[0:TOKENS, :], half).astype(jnp.bfloat16)
            half = s.grad_qkv[x, :, D // 2 : D]
            s.attn_grad[l, x, :, D // 2 : D] = mm_tn(both[...], half).astype(jnp.bfloat16)
            if x == 1 and last:
                attn[1].start((4,))
        summed.wait_recv()
        for low in (0, HALF):
            value = s.core_out[l, low : low + HALF, :].astype(jnp.float32)
            s.mixed[low : low + HALF, :] = value + s.core_in[
                l, HALF - low : 2 * HALF - low, :
            ].astype(jnp.float32)
            norm_back(2 * l, base, low, False)
        if last:
            for name in ATTN_KEPT:
                load(name, 0)

    mod_first = mail.send(s.mod_grad, s.mod_other, place.core)
    s.head_grad[...] += mm_tn(
        s.grad[0:HALF, :].astype(jnp.bfloat16), s.noisy[0:HALF, :]
    )
    head_first = mail.send(s.head_grad, s.head_other, place.core)
    mod_first.wait_recv()
    s.mod_low[0] = (s.mod_grad[...] + s.mod_other[...]).astype(jnp.bfloat16)
    mod_second = mail.send(s.mod_low.at[0], s.mod_low.at[1], place.across)
    attn[0].start((4, 5, 6, 7, 1, 2, 3, 0))
    blocks = s.cond_weight.shape[0]
    mod_second.wait_recv()
    both_mods = jnp.concatenate([s.mod_low[0], s.mod_low[1]], axis=0)
    for owner in range(8):
        part = mm_nt(both_mods, s.order[owner * LANES : (owner + 1) * LANES, :])
        s.mod_rows[:, owner * LANES : (owner + 1) * LANES] = part
    for g in range(8 * blocks):
        row, owner = (g // 8, g % 8)
        for far in range(2):
            s.mod_send[g // blocks, far, g % blocks : g % blocks + 1, :] = s.mod_rows[
                16 * far + row : 16 * far + row + 1, owner * LANES : (owner + 1) * LANES
            ]
    back_from = []
    for k in range(1, 8):
        source = s.mod_send.at[lax.rem(place.f + k, 8)]
        back_from.append(mail.send(source, s.back.at[k], place.up_f(k)))
    back_own = mail.move(s.mod_send.at[place.f], s.back.at[0])
    head_first.wait_recv()
    s.head_low[...] = (s.head_grad[...] + s.head_other[...]).astype(jnp.bfloat16)
    head_second = mail.send(s.head_low, s.head_far, place.across)
    up[0].pass_y()
    attn[0].pass_x()
    attn[1].pass_y()
    need(*LATE_KEPT)
    back_own.wait()
    for copy in back_from:
        copy.wait_recv()
    for i in range(16):
        x_part = lax.rem(across_index + i // 8, 2)
        k = lax.rem(place.f + 8 - i % 8, 8)
        s.back_rows[i] = s.back[k, x_part]
    partial_cond = jnp.zeros((16, D), jnp.float32)
    for b in range(blocks):
        block = s.back_rows[:, b, 0:head_rows].astype(jnp.bfloat16)
        partial_cond = partial_cond + mm(block, s.cond_weight[b].astype(jnp.bfloat16))
    quarters = [(a, b) for a in range(2) for b in range(2)]
    for a, b in quarters:
        s.cond_out[a, b] = partial_cond[8 * a + 4 * b : 8 * a + 4 * b + 4]
    cond_mine = s.cond_out.at[across_index, core_index]
    cond_from = [mail.send(cond_mine, s.cond_in.at[k - 1], place.up_f(k)) for k in range(1, 8)]
    mail.move(s.back_rows, outs.back_rows)
    for item in (down[1], up[1]):
        item.pass_z()
    value = s.cond_out[across_index, core_index]
    for k in range(7):
        cond_from[k].wait_recv()
        value = value + s.cond_in[k]
    s.cond_sum[across_index, core_index] = value
    cond_mine = s.cond_sum.at[across_index, core_index]
    cond_side = mail.send(cond_mine, cond_mine, place.core)
    attn[0].pass_y()
    cond_side.wait_recv()
    cond_half = s.cond_sum.at[across_index]
    cond_far = mail.send(cond_half, cond_half, place.across)
    head_second.wait_recv()
    half = 4 * head_rows
    head_total = s.head_low[...].astype(jnp.float32) + s.head_far[...].astype(jnp.float32)
    s.head_mid[...] = head_total
    s.head_sum[...] = head_total.astype(jnp.bfloat16)
    head_third = mail.send(s.head_sum.at[pl.ds(half, half)], s.head_y, place.pair)
    head_third.wait_recv()
    head_from = []
    for k in range(1, 4):
        low = k * head_rows
        part = s.head_mid[low : low + head_rows, :] + s.head_y[
            low : low + head_rows, :
        ].astype(jnp.float32)
        s.head_sum[low : low + head_rows, :] = part.astype(jnp.bfloat16)
        head_from.append(
            mail.send(
                s.head_sum.at[pl.ds(low, head_rows)], s.head_z.at[k - 1], place.up_z(k)
            )
        )
    head_own = s.head_mid[0:head_rows, :] + s.head_y[0:head_rows, :].astype(jnp.float32)
    cond_far.wait_recv()
    value = jnp.concatenate([s.cond_sum[a, b] for a, b in quarters], axis=0)
    cond = jnp.concatenate([r.cond[a, b] for a, b in quarters], axis=0)
    sigmoid = jax.nn.sigmoid(cond)
    cond_act = (cond * sigmoid).astype(jnp.bfloat16)
    cond_grad = (value * (sigmoid * (1.0 + cond * (1.0 - sigmoid)))).astype(jnp.bfloat16)
    s.time_grad[...] = mm_tn(r.time_hidden[...], cond_grad)
    mail.move(s.time_grad, outs.time_grad)
    time_pre = r.time_pre[...]
    sigmoid = jax.nn.sigmoid(time_pre)
    slope = sigmoid * (1.0 + time_pre * (1.0 - sigmoid))
    pre_grad = (mm_nt(cond_grad, r.low_time[...]) * slope).astype(jnp.bfloat16)
    s.first_grad[...] = mm_tn(pre_grad, r.features[...])
    mail.move(s.first_grad, outs.first_grad)
    column = lax.broadcasted_iota(jnp.int32, (D, head_rows), 0)
    column = column - lax.broadcasted_iota(jnp.int32, (D, head_rows), 1)
    picked = jnp.where(column == place.f * head_rows, 1.0, 0.0).astype(jnp.bfloat16)
    own_cols = mm(cond_grad, picked).astype(jnp.bfloat16)
    s.label_grad[...] = mm_tn(own_cols, r.label_hot[...])
    mail.move(s.label_grad, outs.label_grad)
    shared = jnp.sum(s.time_grad[...] * s.time_grad[...])
    shared = shared + jnp.sum(s.first_grad[...] * s.first_grad[...])
    shared = shared + jnp.sum(s.label_grad[...] * s.label_grad[...])
    bias = s.back_rows[0]
    for c in range(1, 16):
        bias = bias + s.back_rows[c]
    shared = shared + jnp.sum(bias * bias)
    weight_squares = jnp.zeros((8, D), jnp.float32)
    for c in range(blocks):
        block = mm_tn(s.back_rows[:, c, 0:head_rows].astype(jnp.bfloat16), cond_act)
        weight_squares = weight_squares + jnp.sum(
            (block * block).reshape(head_rows // 8, 8, D), axis=0
        )
    shared = shared + jnp.sum(weight_squares)
    squares = jnp.zeros((8, D), jnp.float32)
    upper = half_mask(head_rows, True)
    for item in (down[1], up[1], down[0], up[0], attn[1], attn[0]):
        if item is attn[0]:
            mail.move(s.result.at[:, pl.ds(1, 2)], outs.mlp_result)
            for k in range(3):
                head_from[k].wait_recv()
                head_own = head_own + s.head_z[k].astype(jnp.float32)
            s.head_result[...] = head_own
            shared = shared + jnp.sum(head_own * head_own)
            mail.move(s.head_result, outs.head_result)
        if item not in (down[1], up[1]):
            item.pass_z()
        grad = item.result[...]
        squares = squares + jnp.sum((grad * grad).reshape(head_rows // 8, 8, D), axis=0)
        if item in attn:
            l = attn.index(item)
            tiles = [grad[:, k * LANES : (k + 1) * LANES] for k in range(6)]
            target = s.attn_result.at[l]
            for k in range(3):
                target[k, :, 0:LANES] = tiles[k]
                target[k, :, LANES : LANES + 64] = tiles[3 + k][:, 0:64]
            target[3, :, 0:LANES] = jnp.where(upper, tiles[4], pltpu.roll(tiles[3], 64, 1))
            target[3, :, LANES : LANES + 64] = pltpu.roll(tiles[5], 64, 1)[:, 0:64]
            mail.move(target, outs.attn_result.at[l])

    owned = jnp.where(place.t == 0, 1.0, 0.0)
    total = jnp.sum(squares) + owned * shared
    tile_rows = lax.broadcasted_iota(jnp.int32, (8, LANES), 0)
    s.part[...] = jnp.where(tile_rows == 0, total, jnp.sum(r.loss[...]))
    s.by_fsdp[place.f] = s.part[...]
    copies = [mail.send(s.part, s.by_fsdp.at[place.f], place.up_f(k)) for k in range(1, 8)]
    for copy in copies:
        copy.wait_recv()
    value = s.by_fsdp[0]
    for k in range(1, 8):
        value = value + s.by_fsdp[k]
    s.group[...] = value
    s.by_tp[place.t] = value
    copies = [
        mail.send(s.group, s.by_tp.at[place.t], device)
        for device in (place.core, place.across, place.diagonal)
    ]
    for copy in copies:
        copy.wait_recv()
    s.totals[...] = s.by_tp[0] + s.by_tp[1] + s.by_tp[2] + s.by_tp[3]
    mail.move(s.totals, outs.totals)
    mail.finish(waited + [back_own])


FINAL_KEPT = dict(
    grad_pred=None, head=None, final_low=None, pieces=None, noisy=None
)
LATE_KEPT = dict(cond_weight=None)
NORM_KEPT = dict(normed=None, inverse=None)
MLP_KEPT = dict(mlp_out=None, wmlp=None, upward=None, active=None, rows=None)
ATTN_KEPT = dict(attn_out=None, wattn=None, qkv=None, probs=None, hidden=None, att=None)
SMALL_INS = dict(
    cond=None,
    loss=None,
    time_hidden=None,
    low_time=None,
    features=None,
    time_pre=None,
    label_hot=None,
)
BACKWARD_INS = SMALL_INS | LATE_KEPT | NORM_KEPT | FINAL_KEPT | MLP_KEPT | ATTN_KEPT
BACKWARD_OUTS = dict(
    mlp_result=((LAYERS, 2, D // 8, D), jnp.float32),
    attn_result=((LAYERS, 4, D // 8, D // 4), jnp.float32),
    head_result=((D // 8, LANES), jnp.float32),
    back_rows=((16, 16, LANES), jnp.float32),
    time_grad=((D // 8, D), jnp.float32),
    first_grad=((D // 8, FREQ), jnp.float32),
    label_grad=((D // 8, NCLASS), jnp.float32),
    totals=((8, LANES), jnp.float32),
)
MLP_RESULT = dict(mlp_result=None)
BACKWARD_OWN = dict(
    result=((LAYERS, 3, D // 8, D), jnp.float32),
    part=((8, LANES), jnp.float32),
    group=((8, LANES), jnp.float32),
    by_fsdp=((8, 8, LANES), jnp.float32),
    by_tp=((4, 8, LANES), jnp.float32),
    order=((8 * LANES, D), jnp.bfloat16),
    mod_grad=((16, D), jnp.float32),
    mod_other=((16, D), jnp.float32),
    mod_low=((2, 16, D), jnp.bfloat16),
    mod_rows=((32, 8 * LANES), jnp.float32),
    mod_send=((8, 2, 16, LANES), jnp.float32),
    back=((8, 2, 16, LANES), jnp.float32),
    cond_out=((2, 2, 4, D), jnp.float32),
    cond_sum=((2, 2, 4, D), jnp.float32),
    cond_in=((7, 4, D), jnp.float32),
    head_grad=((D, LANES), jnp.float32),
    head_other=((D, LANES), jnp.float32),
    head_mid=((D, LANES), jnp.float32),
    head_low=((D, LANES), jnp.bfloat16),
    head_far=((D, LANES), jnp.bfloat16),
    head_sum=((D, LANES), jnp.bfloat16),
    head_y=((D // 2, LANES), jnp.bfloat16),
    head_z=((3, D // 8, LANES), jnp.bfloat16),
    grad=((TOKENS, D), jnp.float32),
    mixed=((TOKENS, D), jnp.float32),
    grad_rows=((LAYERS, 2 * TOKENS, D), jnp.bfloat16),
    grad_up=((2 * TOKENS, D), jnp.bfloat16),
    both=((2 * TOKENS, D), jnp.bfloat16),
    grad_qkv=((2, 2 * TOKENS, D), jnp.bfloat16),
    sum_out=((LAYERS, 2, HALF, D), jnp.bfloat16),
    sum_in=((LAYERS, 2, HALF, D), jnp.bfloat16),
    far_out=((LAYERS, HALF, D), jnp.bfloat16),
    far_in=((LAYERS, HALF, D), jnp.bfloat16),
    own_out=((LAYERS, HALF, D), jnp.bfloat16),
    own_in=((LAYERS, HALF, D), jnp.bfloat16),
    keep=((2, HALF, D), jnp.float32),
    core_out=((LAYERS, TOKENS, D), jnp.bfloat16),
    core_in=((LAYERS, TOKENS, D), jnp.bfloat16),
    mlp_grad=((LAYERS, 2, D, D), jnp.bfloat16),
    attn_grad=((LAYERS, 2, D, D), jnp.bfloat16),
    from_x=((LAYERS, D, D), jnp.bfloat16),
    from_y=((LAYERS, 3, D // 2, D), jnp.bfloat16),
    from_z=((LAYERS, 3, 3, D // 8, D), jnp.bfloat16),
)


def backward_scratch():
    layered = MLP_KEPT | ATTN_KEPT
    specs = {}
    for name in BACKWARD_INS:
        if name in LATE_KEPT:
            specs[name] = FORWARD_OWN[name]
        elif name not in SMALL_INS:
            shape, dtype = FORWARD_OUTS[name]
            specs[name] = (shape[1:] if name in layered else shape, dtype)
    for name in BACKWARD_OUTS:
        if name not in MLP_RESULT:
            specs[name] = BACKWARD_OUTS[name]
    specs.update(BACKWARD_OWN)
    return specs


BACKWARD_SCRATCH = backward_scratch()


def run_backward(kept, inputs):
    anywhere = pl.BlockSpec(memory_space=pl.ANY)
    vmem = pl.BlockSpec(memory_space=pltpu.VMEM)
    given = [
        getattr(kept if hasattr(kept, name) else inputs, name) for name in BACKWARD_INS
    ]
    outs = pl.pallas_call(
        backward_kernel,
        out_shape=[jax.ShapeDtypeStruct(*spec) for spec in BACKWARD_OUTS.values()],
        in_specs=[vmem if name in SMALL_INS else anywhere for name in BACKWARD_INS],
        out_specs=[anywhere] * len(BACKWARD_OUTS),
        scratch_shapes=[pltpu.VMEM(*spec) for spec in BACKWARD_SCRATCH.values()]
        + [
            pltpu.SemaphoreType.DMA((128,)),
            pltpu.SemaphoreType.DMA((128,)),
            pltpu.SemaphoreType.DMA((64,)),
        ],
        compiler_params=pltpu.CompilerParams(
            collective_id=1, has_side_effects=True, vmem_limit_bytes=VMEM_LIMIT
        ),
    )(*given)
    return SimpleNamespace(**dict(zip(BACKWARD_OUTS, outs)))


def shard_tiles(attn_weight):
    q, k, v, o = (attn_weight[:, j].astype(jnp.bfloat16) for j in range(4))
    return jnp.concatenate(
        [
            q[..., :128],
            k[..., :128],
            v[..., :128],
            q[..., 128:],
            o[..., :64],
            k[..., 128:],
            o[..., 64:128],
            v[..., 128:],
            o[..., 128:],
        ],
        axis=-1,
    )


def wave_table():
    quarter = D // 4
    omegas = 1.0 / np.power(10000.0, np.arange(quarter, dtype=np.float32) / quarter)
    angles = np.arange(GRID, dtype=np.float32)[:, None] * omegas.astype(np.float32)[None, :]
    waves = np.concatenate([np.sin(angles), np.cos(angles)], axis=1).astype(np.float32)
    table = np.zeros((2 * GRID, D), np.float32)
    table[:GRID, : D // 2] = waves
    table[GRID:, D // 2 :] = waves
    padded = np.zeros((2 * GRID, 8, LANES), np.float32)
    padded[:, :, : D // 8] = table.reshape(2 * GRID, 8, D // 8)
    left = padded.reshape(2 * GRID, 8 * LANES)
    parts = []
    for _ in range(3):
        part = left.astype(jnp.bfloat16)
        parts.append(part)
        left = left - part.astype(np.float32)
    return np.concatenate(parts, axis=0)


def body_kernels(
    routes,
    latents,
    noise,
    timesteps,
    labels,
    step_count,
    tables,
    time_weight,
    cond_weight,
    cond_bias,
    attn_weight,
    mlp_weight,
    *states,
):
    fsdp_index = lax.axis_index("fsdp")
    tp_index = lax.axis_index("tp")
    across_index = tp_index // 2
    num_fsdp = routes.num_fsdp
    col_share = tables.shape[1]
    all_latents = timesteps.shape[0]
    total_entries = all_latents * SEQ * PATCH_DIM
    col_start = fsdp_index * col_share
    low_tables = tables.astype(jnp.bfloat16)
    blocks = cond_bias.shape[0] // col_share

    ordered = timesteps.reshape(num_fsdp, 2).T.reshape(-1)
    labels = labels.reshape(num_fsdp, 2).T.reshape(-1)
    features = timestep_features(ordered).astype(jnp.bfloat16)
    time_pre = jnp.dot(
        features,
        low_tables[2 * PATCH_DIM : 2 * PATCH_DIM + FREQ],
        preferred_element_type=jnp.float32,
    )
    time_hidden = jax.nn.silu(time_pre).astype(jnp.bfloat16)
    label_hot = (labels[:, None] == jnp.arange(NCLASS, dtype=jnp.int32)[None, :]).astype(
        jnp.bfloat16
    )
    label_part = jnp.dot(
        label_hot, low_tables[2 * PATCH_DIM + FREQ :], preferred_element_type=jnp.float32
    )
    low_time = time_weight.astype(jnp.bfloat16)
    cond_part = jnp.dot(time_hidden, low_time, preferred_element_type=jnp.float32)
    placed = lax.dynamic_update_slice(
        jnp.zeros((all_latents, D), jnp.float32), label_part, (0, col_start)
    )
    low_bias = cond_bias.astype(jnp.bfloat16).astype(jnp.float32)

    latent_id = fsdp_index * latents.shape[0]
    share = signal_share(lax.dynamic_slice_in_dim(timesteps, latent_id, latents.shape[0]))
    share = share[:, None, None]
    noisy = (jnp.sqrt(share) * latents + jnp.sqrt(1.0 - share) * noise).astype(jnp.bfloat16)
    data = jnp.concatenate(
        [
            jnp.pad(noisy.astype(jnp.float32), ((0, 0), (0, 0), (0, LANES - PATCH_DIM))),
            jnp.pad(noise, ((0, 0), (0, 0), (PATCH_DIM, LANES - 2 * PATCH_DIM))),
        ],
        axis=1,
    )
    shards = jnp.concatenate(
        [shard_tiles(attn_weight)[:, None], mlp_weight.astype(jnp.bfloat16)], axis=1
    )
    head = jnp.pad(low_tables[: 2 * PATCH_DIM].T, ((0, 0), (0, LANES - 2 * PATCH_DIM)))
    cond_part = cond_part + placed
    inputs = SimpleNamespace(
        cond_part=cond_part.reshape(2, 2, num_fsdp // 2, D),
        shards=shards,
        data=data,
        head=head,
        waves=jnp.asarray(wave_table()),
        cond_weight=cond_weight.reshape(blocks, col_share, D),
        cond_bias=low_bias.reshape(blocks, col_share),
    )
    kept = run_forward(vars(inputs), total_entries)
    inputs.time_hidden = time_hidden
    inputs.low_time = low_time
    inputs.features = features
    inputs.time_pre = time_pre
    inputs.label_hot = label_hot
    back = run_backward(kept, inputs)

    cond = kept.cond.reshape(all_latents, D)
    cond_act = jax.nn.silu(cond).astype(jnp.bfloat16)
    modul_back = back.back_rows[:, :blocks, :col_share].reshape(all_latents, -1)
    modul_back = modul_back.astype(jnp.bfloat16)
    cond_grad_w = dot_f32(modul_back, cond_act, 0, 0)
    bias_grad = jnp.sum(modul_back.astype(jnp.float32), axis=0)
    time_grad = back.time_grad
    tables_grad = jnp.concatenate(
        [back.head_result[:, : 2 * PATCH_DIM], back.first_grad, back.label_grad], axis=1
    ).T
    loss = back.totals[1, 0] / total_entries
    norm = jnp.sqrt(back.totals[0, 0])
    entries = NTAB * D + D * D + (D + 1) * NCOND + LAYERS * (4 * D * D + 2 * D * FF)
    limit = clip_scale * math.sqrt(entries / (all_latents * SEQ))
    factor = jnp.minimum(1.0, limit / norm)
    count = step_count[0].astype(jnp.float32)
    attn_grad = back.attn_result
    mlp_grad = back.mlp_result
    weights_all = (tables, time_weight, cond_weight, cond_bias, attn_weight, mlp_weight)
    grads_all = (tables_grad, time_grad, cond_grad_w, bias_grad, attn_grad, mlp_grad)
    states = tuple(zip(states[0::2], states[1::2]))
    results = [loss, norm]
    for weight, grad, state in zip(weights_all, grads_all, states):
        results.extend(adam_update(weight, grad * factor, state[0], state[1], count))
    return tuple(results)


def body(routes, *args):
    if routes.num_fsdp == 8 and args[5].shape[1] % 16 == 0:
        return body_kernels(routes, *args)
    return body_steps(routes, *args)


def solution(mesh):
    vectors = P("fsdp")
    columns = P(None, "fsdp")
    rows = P("fsdp", None)
    blocks = P(None, None, "fsdp", "tp")
    data = P("fsdp", "tp", None)
    weights = (columns, rows, rows, vectors, blocks, blocks)
    states = tuple(spec for spec in weights for _ in range(2))
    updated = tuple(spec for spec in weights for _ in range(3))
    return jax.shard_map(
        partial(body, Routes(mesh)),
        mesh=mesh,
        in_specs=(data, data, P(), P(), P()) + weights + states,
        out_specs=(P(), P()) + updated,
        check_vma=False,
    )
```

```python
from functools import partial
import math
from types import SimpleNamespace

import jax
import jax.numpy as jnp
from jax import lax
import numpy as np
from jax.experimental import pallas as pl
from jax.experimental.pallas import tpu as pltpu
from jax.sharding import PartitionSpec as P

D = 768
HEAD_DIM = 64
FF = 3072
NCLASS = 1000
FREQ = 256
PATCH_DIM = 16
GRID = 16
LAYERS = 2
SEQ = 256
NCOND = 10752
NTAB = 1288


norm_eps = 1e-06
beta_first = 0.9
beta_second = 0.999
adam_eps = 1e-08
learn_rate = 0.2
weight_decay = 0.01
clip_scale = 0.002
diffusion_steps = 1000.0


def timestep_features(timesteps):
    half_width = FREQ // 2
    omegas = jnp.exp(-math.log(10000.0) * jnp.arange(half_width, dtype=jnp.float32) / half_width)
    angles = timesteps.astype(jnp.float32)[:, None] * omegas[None, :]
    return jnp.concatenate([jnp.cos(angles), jnp.sin(angles)], axis=1)


def signal_share(timesteps):
    phase = (timesteps.astype(jnp.float32) / diffusion_steps + 0.008) / 1.008 * (math.pi / 2)
    return jnp.cos(phase) ** 2


def butterfly_bits(number):
    bits = []
    bit = 1
    while bit < number:
        bits.append(bit)
        bit *= 2
    return bits


def split_radices(number):
    radices = []
    while number > 1:
        radix = 4 if number % 4 == 0 else 2
        radices.append(radix)
        number //= radix
    return radices


class Routes:
    def __init__(self, mesh):
        self.num_fsdp = mesh.shape["fsdp"]
        self.num_tp = mesh.shape["tp"]
        self.outer = split_radices(self.num_fsdp // 2)

    def core(self, value):
        return lax.ppermute(value, "tp", [(t, t ^ 1) for t in range(self.num_tp)])

    def across(self, value):
        return lax.ppermute(value, "tp", [(t, t ^ 2) for t in range(self.num_tp)])

    def pair(self, value):
        return lax.ppermute(value, "fsdp", [(f, f ^ 1) for f in range(self.num_fsdp)])

    def shift(self, value, stride, radix, amount):
        pairs = []
        for f in range(self.num_fsdp):
            digit = (f // stride) % radix
            pairs.append((f, f + ((digit + amount) % radix - digit) * stride))
        return lax.ppermute(value, "fsdp", pairs)

    def slot_owner(self, fsdp_index, slots):
        per_pair = self.num_fsdp // 2
        pair_part = (slots // per_pair + fsdp_index) % 2
        rest = slots % per_pair
        owner = pair_part
        stride = 2
        for radix in self.outer:
            digit = (rest + fsdp_index // stride) % radix
            owner = owner + digit * stride
            rest = rest // radix
            stride *= radix
        return owner

    def gather_outer(self, block):
        stride = 2
        for radix in self.outer:
            block = jnp.concatenate(
                [block] + [self.shift(block, stride, radix, -k) for k in range(1, radix)], axis=0
            )
            stride *= radix
        return block

    def gather_rows(self, block):
        held = self.gather_outer(block)
        return jnp.concatenate([held, self.pair(held)], axis=0)

    def gather_both(self, block, across_last):
        held = self.gather_outer(block)
        if across_last:
            own = jnp.concatenate([held, self.pair(held)], axis=0)
            return (own, self.across(own))
        other = self.across(held)
        return (
            jnp.concatenate([held, self.pair(held)], axis=0),
            jnp.concatenate([other, self.pair(other)], axis=0),
        )

    def scatter_rows(self, total, dtype=jnp.bfloat16):
        half = total.shape[0] // 2
        received = self.pair(total[half:].astype(dtype))
        held = total[:half] + received.astype(jnp.float32)
        strides = []
        stride = 2
        for radix in self.outer:
            strides.append(stride)
            stride *= radix
        for radix, stride in reversed(list(zip(self.outer, strides))):
            size = held.shape[0] // radix
            parts = [
                self.shift(held[k * size : (k + 1) * size].astype(dtype), stride, radix, k)
                for k in range(1, radix)
            ]
            held = held[:size]
            for part in parts:
                held = held + part.astype(jnp.float32)
        return held

    def scatter_both(self, own, other):
        received = self.across(other.astype(jnp.bfloat16))
        return self.scatter_rows(own + received.astype(jnp.float32))

    def sum_fsdp(self, value):
        for bit in butterfly_bits(self.num_fsdp):
            value = value + lax.ppermute(
                value, "fsdp", [(f, f ^ bit) for f in range(self.num_fsdp)]
            )
        return value

    def sum_all(self, value):
        value = value + self.core(value)
        value = value + self.across(value)
        return self.sum_fsdp(value)


def after(value, *earlier):
    return lax.optimization_barrier((value,) + earlier)[0]


def dot_f32(left, right, left_dim, right_dim):
    return lax.dot_general(
        left, right, (((left_dim,), (right_dim,)), ((), ())), preferred_element_type=jnp.float32
    )


def layer_norm(values):
    centred = values - jnp.mean(values, axis=-1, keepdims=True)
    inverse = lax.rsqrt(jnp.mean(centred * centred, axis=-1, keepdims=True) + norm_eps)
    return (centred * inverse, inverse)


def modulate(values, shift, scale):
    normed, inverse = layer_norm(values)
    return ((normed * (1.0 + scale) + shift).astype(jnp.bfloat16), normed, inverse)


def norm_backward(grad_mixed, normed, inverse, scale, counted):
    grad_shift = jnp.sum(grad_mixed[:counted], axis=0)
    grad_scale = jnp.sum(grad_mixed[:counted] * normed[:counted], axis=0)
    grad_normed = grad_mixed * (1.0 + scale)
    centred = grad_normed - jnp.mean(grad_normed, axis=-1, keepdims=True)
    grad_input = (
        centred - normed * jnp.mean(grad_normed * normed, axis=-1, keepdims=True)
    ) * inverse
    return (grad_input, grad_shift, grad_scale)


def core_sum(routes, partial):
    low = partial.astype(jnp.bfloat16)
    far = routes.core(low)
    half = far.shape[0] // 2
    swapped = jnp.concatenate([far[half:], far[:half]], axis=0)
    return low.astype(jnp.float32) + swapped.astype(jnp.float32)


def attend(routes, hidden, weights):
    seq_len = hidden.shape[0]
    query_key = jnp.stack([dot_f32(hidden, w, 1, 0) for w in weights[0]]).astype(jnp.bfloat16)
    value_out = jnp.stack([dot_f32(hidden, w, 1, 0) for w in weights[1]]).astype(jnp.bfloat16)
    width = query_key.shape[2] // 2
    local_heads = width // HEAD_DIM
    query_key = query_key.reshape(2, seq_len, 2 * local_heads, HEAD_DIM)
    query, key = (query_key[:, :, :local_heads], query_key[:, :, local_heads:])
    value = value_out[:, :, :width].reshape(2, seq_len, local_heads, HEAD_DIM)
    scores = jnp.einsum(
        "xqhe,xkhe->xhqk", query, key, preferred_element_type=jnp.float32
    ) * HEAD_DIM ** (-0.5)
    exped = jnp.exp(scores - jnp.max(scores, axis=-1, keepdims=True))
    probs = exped / jnp.sum(exped, axis=-1, keepdims=True)
    attended = jnp.einsum(
        "xhqk,xkhe->xqhe", probs.astype(jnp.bfloat16), value, preferred_element_type=jnp.float32
    )
    attended = attended.astype(jnp.bfloat16).reshape(2, seq_len, width)
    padded = jnp.concatenate([jnp.zeros_like(attended), attended], axis=2)
    partial_out = dot_f32(padded[0], weights[1][0], 1, 1) + dot_f32(padded[1], weights[1][1], 1, 1)
    return (core_sum(routes, partial_out), (hidden, query, key, value, probs, padded))


def attend_backward(routes, grad_full, kept, weights):
    hidden, query, key, value, probs, padded = kept
    seq_len = hidden.shape[0]
    scale = HEAD_DIM ** (-0.5)
    width = padded.shape[2] // 2
    local_heads = width // HEAD_DIM
    grad_attended = jnp.stack([dot_f32(grad_full, w, 1, 0) for w in weights[1]])
    grad_attended = grad_attended[:, :, width:].astype(jnp.bfloat16)
    grad_attended = grad_attended.reshape(2, seq_len, local_heads, HEAD_DIM)
    grad_probs = jnp.einsum(
        "xqhe,xkhe->xhqk", grad_attended, value, preferred_element_type=jnp.float32
    )
    grad_value = jnp.einsum(
        "xhqk,xqhe->xkhe",
        probs.astype(jnp.bfloat16),
        grad_attended,
        preferred_element_type=jnp.float32,
    )
    inner = jnp.sum(probs * grad_probs, axis=-1, keepdims=True)
    grad_scores = (probs * (grad_probs - inner)).astype(jnp.bfloat16)
    grad_query = (
        jnp.einsum("xhqk,xkhe->xqhe", grad_scores, key, preferred_element_type=jnp.float32) * scale
    )
    grad_key = (
        jnp.einsum("xhqk,xqhe->xkhe", grad_scores, query, preferred_element_type=jnp.float32) * scale
    )
    grad_qk = jnp.concatenate([grad_query, grad_key], axis=2).astype(jnp.bfloat16)
    grad_qk = grad_qk.reshape(2, seq_len, 2 * width)
    grad_v = grad_value.astype(jnp.bfloat16).reshape(2, seq_len, width)
    grad_v = jnp.concatenate([grad_v, jnp.zeros_like(grad_v)], axis=2)
    grad_hidden = jnp.zeros(hidden.shape, jnp.float32)
    for k in range(2):
        grad_hidden = grad_hidden + dot_f32(grad_qk[k], weights[0][k], 1, 1)
        grad_hidden = grad_hidden + dot_f32(grad_v[k], weights[1][k], 1, 1)
    grad_hidden = core_sum(routes, grad_hidden)
    qk_own, qk_other = [dot_f32(hidden, grad_qk[k], 0, 0) for k in range(2)]
    both = jnp.concatenate([hidden, grad_full], axis=0)
    vo_own, vo_other = [
        dot_f32(both, jnp.concatenate([grad_v[k], padded[k]], axis=0), 0, 0) for k in range(2)
    ]
    grads = (routes.scatter_both(qk_own, qk_other), routes.scatter_both(vo_own, vo_other))
    return (grad_hidden, grads)


def share_rows(routes, rows):
    half = rows.shape[0] // 2
    far = routes.across(rows[:half])
    return jnp.concatenate([rows, far, routes.core(far)], axis=0)


def sum_rows(routes, partial):
    half = partial.shape[0] // 4
    low = partial.astype(jnp.bfloat16)
    received = routes.core(jnp.concatenate([low[3 * half :], low[half : 2 * half]], axis=0))
    received = received.astype(jnp.float32)
    far_sum = (partial[2 * half : 3 * half] + received[:half]).astype(jnp.bfloat16)
    own_sum = partial[:half] + received[half:]
    own_total = (own_sum + routes.across(far_sum).astype(jnp.float32)).astype(jnp.bfloat16)
    return jnp.concatenate([own_total, routes.core(own_total)], axis=0).astype(jnp.float32)


def feed_forward(routes, hidden, weights):
    rows = share_rows(routes, hidden)
    upward = dot_f32(rows, weights[0], 1, 0)
    active = jax.nn.gelu(upward, approximate=True).astype(jnp.bfloat16)
    output = sum_rows(routes, dot_f32(active, weights[1], 1, 1))
    return (output, (rows, upward, active))


def feed_backward(routes, grad_full, kept, weights):
    rows, upward, active = kept
    grad_rows = share_rows(routes, grad_full)
    grad_active = dot_f32(grad_rows, weights[1], 1, 0)
    slope = jax.vjp(partial(jax.nn.gelu, approximate=True), upward)[1]
    grad_up = slope(grad_active)[0].astype(jnp.bfloat16)
    grad_hidden = sum_rows(routes, dot_f32(grad_up, weights[0], 1, 1))
    grad_down_w = routes.scatter_rows(dot_f32(grad_rows, active, 0, 0))
    grad_up_w = routes.scatter_rows(dot_f32(rows, grad_up, 0, 0))
    return (grad_hidden, (grad_up_w, grad_down_w))


def branch_forward(routes, resid, pieces, inner_fn, weights):
    shift, scale, gate = pieces
    hidden, normed, inverse = modulate(resid, shift, scale)
    output, kept = inner_fn(routes, hidden, weights)
    return (resid + gate * output, (normed, inverse, output, kept))


def branch_backward(routes, grad_resid, pieces, saved, inner_back, weights):
    shift, scale, gate = pieces
    normed, inverse, output, kept = saved
    counted = grad_resid.shape[0] // 2
    grad_gate = jnp.sum(grad_resid[:counted] * output[:counted], axis=0)
    grad_output = (gate * grad_resid).astype(jnp.bfloat16)
    grad_mixed, grads = inner_back(routes, grad_output, kept, weights)
    grad_input, grad_shift, grad_scale = norm_backward(grad_mixed, normed, inverse, scale, counted)
    return (grad_resid + grad_input, [grad_shift, grad_scale, grad_gate], grads)


def gather_weights(routes, attn_weight, mlp_weight):
    shards = []
    for layer in range(LAYERS):
        attn = attn_weight[layer].astype(jnp.bfloat16)
        mlp = mlp_weight[layer].astype(jnp.bfloat16)
        shards.append(
            (
                jnp.concatenate([attn[0], attn[1]], axis=1),
                jnp.concatenate([attn[2], attn[3]], axis=1),
                mlp[0],
                mlp[1],
            )
        )
    gathered = []
    earlier = []

    def in_turn(block):
        return after(block, earlier[-2]) if len(earlier) >= 2 else block

    for layer in range(LAYERS):
        query_key, value_out, up, down = shards[layer]
        pairs = []
        for block, across_last in ((query_key, True), (value_out, layer > 0)):
            both = routes.gather_both(in_turn(block), across_last)
            pairs.append(both)
            earlier.append(both[0])
        rows = []
        for block in (up, down):
            rows.append(routes.gather_rows(in_turn(block)))
            earlier.append(rows[-1])
        gathered.append((tuple(pairs), tuple(rows)))
    return gathered


def adam_update(weight, grad, first, second, count):
    first_new = beta_first * first + (1.0 - beta_first) * grad
    second_new = beta_second * second + (1.0 - beta_second) * grad * grad
    first_hat = first_new / (1.0 - jnp.power(beta_first, count))
    second_hat = second_new / (1.0 - jnp.power(beta_second, count))
    weight_new = weight - learn_rate * (
        first_hat / (jnp.sqrt(second_hat) + adam_eps) + weight_decay * weight
    )
    return [weight_new, first_new, second_new]


def body_steps(
    routes,
    latents,
    noise,
    timesteps,
    labels,
    step_count,
    tables,
    time_weight,
    cond_weight,
    cond_bias,
    attn_weight,
    mlp_weight,
    tables_first,
    tables_second,
    time_first,
    time_second,
    cond_first,
    cond_second,
    bias_first,
    bias_second,
    attn_first,
    attn_second,
    mlp_first,
    mlp_second,
):
    fsdp_index = lax.axis_index("fsdp")
    tp_index = lax.axis_index("tp")
    across_index = tp_index // 2
    num_fsdp = routes.num_fsdp
    local_seq = latents.shape[1]
    col_share = tables.shape[1]
    all_latents = timesteps.shape[0]
    total_entries = all_latents * SEQ * PATCH_DIM
    col_start = fsdp_index * col_share
    low_tables = tables.astype(jnp.bfloat16)

    gathered = gather_weights(routes, attn_weight, mlp_weight)
    head = routes.gather_rows(low_tables[: 2 * PATCH_DIM].T)

    features = timestep_features(timesteps).astype(jnp.bfloat16)
    time_pre = jnp.dot(
        features,
        low_tables[2 * PATCH_DIM : 2 * PATCH_DIM + FREQ],
        preferred_element_type=jnp.float32,
    )
    time_hidden = jax.nn.silu(time_pre).astype(jnp.bfloat16)
    label_hot = (labels[:, None] == jnp.arange(NCLASS, dtype=jnp.int32)[None, :]).astype(
        jnp.bfloat16
    )
    label_part = jnp.dot(
        label_hot, low_tables[2 * PATCH_DIM + FREQ :], preferred_element_type=jnp.float32
    )
    low_time = time_weight.astype(jnp.bfloat16)
    cond_part = jnp.dot(time_hidden, low_time, preferred_element_type=jnp.float32)
    placed = lax.dynamic_update_slice(
        jnp.zeros((all_latents, D), jnp.float32), label_part, (0, col_start)
    )
    cond = routes.sum_fsdp(cond_part + placed)
    cond_act = jax.nn.silu(cond).astype(jnp.bfloat16)
    low_cond = cond_weight.astype(jnp.bfloat16)
    low_bias = cond_bias.astype(jnp.bfloat16).astype(jnp.float32)
    mod_part = dot_f32(cond_act, low_cond, 1, 1) + low_bias[None, :]
    modul = lax.all_to_all(
        mod_part.astype(jnp.bfloat16), "fsdp", split_axis=0, concat_axis=1, tiled=True
    )
    modul = lax.dynamic_slice_in_dim(modul, across_index, 1, 0)

    slots = jnp.arange(num_fsdp, dtype=jnp.int32)
    owners = routes.slot_owner(fsdp_index, slots)
    slot_hot = (owners[:, None] == slots[None, :]).astype(jnp.bfloat16)
    pieces_all = jnp.einsum(
        "pfr,sf->psr",
        modul.reshape(-1, num_fsdp, col_share),
        slot_hot,
        preferred_element_type=jnp.float32,
    ).reshape(-1, D)

    data = jnp.stack([latents, noise], axis=1)
    own_data = lax.dynamic_index_in_dim(data, across_index, 0, keepdims=False)
    far_data = lax.dynamic_index_in_dim(data, 1 - across_index, 0, keepdims=False)
    first_data = jnp.concatenate([own_data, routes.across(far_data)], axis=1)
    chip_data = jnp.concatenate([first_data, routes.core(first_data)], axis=1)
    clean, noise_part = (chip_data[0], chip_data[1])
    chunks = jnp.stack([tp_index, tp_index ^ 2, tp_index ^ 1, tp_index ^ 3])
    token_ids = (
        chunks[:, None] * local_seq + jnp.arange(local_seq, dtype=jnp.int32)[None, :]
    ).reshape(-1)
    counted = token_ids.shape[0] // 2

    quarter = D // 4
    col_ids = (
        owners[:, None] * col_share + jnp.arange(col_share, dtype=jnp.int32)[None, :]
    ).reshape(-1)
    omegas = 1.0 / jnp.power(10000.0, (col_ids % quarter).astype(jnp.float32) / quarter)
    angles = jnp.arange(GRID, dtype=jnp.float32)[:, None] * omegas[None, :]
    kinds = (col_ids // quarter)[None, :]
    waves = jnp.where(kinds % 2 == 0, jnp.sin(angles), jnp.cos(angles))
    row_waves = jnp.where(kinds < 2, waves, 0.0)
    col_waves = jnp.where(kinds >= 2, waves, 0.0)
    grid_ids = jnp.arange(GRID, dtype=jnp.int32)[None, :]
    row_hot = (token_ids[:, None] // GRID == grid_ids).astype(jnp.float32)
    col_hot = (token_ids[:, None] % GRID == grid_ids).astype(jnp.float32)
    positions = jnp.dot(
        jnp.concatenate([row_hot, col_hot], axis=1),
        jnp.concatenate([row_waves, col_waves], axis=0),
        precision=lax.Precision.HIGHEST,
    )

    latent_id = fsdp_index * latents.shape[0] + across_index
    share = signal_share(lax.dynamic_slice_in_dim(timesteps, latent_id, 1))[:, None]
    noisy = (jnp.sqrt(share) * clean + jnp.sqrt(1.0 - share) * noise_part).astype(jnp.bfloat16)
    resid = dot_f32(noisy, head[:, :PATCH_DIM], 1, 1) + positions

    saved = []
    for layer in range(LAYERS):
        pieces = [pieces_all[6 * layer + k][None, :] for k in range(6)]
        attn_w, mlp_w = gathered[layer]
        resid, attn_saved = branch_forward(routes, resid, pieces[:3], attend, attn_w)
        resid, mlp_saved = branch_forward(routes, resid, pieces[3:], feed_forward, mlp_w)
        saved.append((attn_saved, mlp_saved))
    final_shift = pieces_all[6 * LAYERS][None, :]
    final_scale = pieces_all[6 * LAYERS + 1][None, :]
    final_low, final_normed, final_inverse = modulate(resid, final_shift, final_scale)
    predicted = dot_f32(final_low, head[:, PATCH_DIM:], 1, 0)
    difference = predicted - noise_part
    loss_part = jnp.sum(difference[:counted] * difference[:counted])
    grad_pred = (difference * (2.0 / total_entries)).astype(jnp.bfloat16)
    output_grad = dot_f32(final_low[:counted], grad_pred[:counted], 0, 0)
    grad_final = dot_f32(grad_pred, head[:, PATCH_DIM:], 1, 1)
    grad_resid, grad_fshift, grad_fscale = norm_backward(
        grad_final, final_normed, final_inverse, final_scale, counted
    )
    layer_mods = [None] * LAYERS
    layer_grads = [None] * LAYERS
    for layer in reversed(range(LAYERS)):
        pieces = [pieces_all[6 * layer + k][None, :] for k in range(6)]
        attn_w, mlp_w = gathered[layer]
        grad_resid, mlp_mods, mlp_grads = branch_backward(
            routes, grad_resid, pieces[3:], saved[layer][1], feed_backward, mlp_w
        )
        grad_resid, attn_mods, attn_grads = branch_backward(
            routes, grad_resid, pieces[:3], saved[layer][0], attend_backward, attn_w
        )
        layer_mods[layer] = attn_mods + mlp_mods
        layer_grads[layer] = attn_grads + mlp_grads
    grad_embed = grad_resid.astype(jnp.bfloat16)
    patch_grad = dot_f32(grad_embed[:counted], noisy[:counted], 0, 0)

    head_grad = jnp.concatenate([patch_grad, output_grad], axis=1)
    head_grad = head_grad + routes.core(head_grad)
    head_grad = head_grad + routes.across(head_grad)
    head_cols = routes.scatter_rows(head_grad, jnp.float32).T

    modul_grad = jnp.stack(layer_mods[0] + layer_mods[1] + [grad_fshift, grad_fscale])
    modul_grad = (modul_grad + routes.core(modul_grad)).astype(jnp.bfloat16)
    modul_grad = jnp.einsum(
        "psr,sf->pfr",
        modul_grad.reshape(-1, num_fsdp, col_share),
        slot_hot,
        preferred_element_type=jnp.float32,
    ).astype(jnp.bfloat16)
    modul_back = lax.all_to_all(
        modul_grad.reshape(num_fsdp, -1), "fsdp", split_axis=0, concat_axis=0, tiled=True
    )
    far_back = routes.across(modul_back)
    is_first = across_index == 0
    modul_back = jnp.stack(
        [jnp.where(is_first, modul_back, far_back), jnp.where(is_first, far_back, modul_back)],
        axis=1,
    ).reshape(all_latents, -1)
    cond_grad_w = dot_f32(modul_back, cond_act, 0, 0)
    bias_grad = jnp.sum(modul_back.astype(jnp.float32), axis=0)
    grad_cond_act = routes.sum_fsdp(dot_f32(modul_back, low_cond, 1, 0))
    silu_slope = jax.vjp(jax.nn.silu, cond)[1]
    grad_cond = silu_slope(grad_cond_act)[0].astype(jnp.bfloat16)
    time_grad = dot_f32(time_hidden, grad_cond, 0, 0)
    grad_hidden = dot_f32(grad_cond, low_time, 1, 1)
    time_slope = jax.vjp(jax.nn.silu, time_pre)[1]
    grad_pre = time_slope(grad_hidden)[0].astype(jnp.bfloat16)
    first_layer_grad = dot_f32(features, grad_pre, 0, 0)
    cond_cols = lax.dynamic_slice_in_dim(grad_cond, col_start, col_share, 1)
    label_grad = dot_f32(label_hot, cond_cols, 0, 0)
    tables_grad = jnp.concatenate([head_cols, first_layer_grad, label_grad], axis=0)

    squares = sum(jnp.sum(part * part) for parts in layer_grads for part in parts)
    owner = (tp_index == 0).astype(jnp.float32)
    squares = squares + owner * sum(
        jnp.sum(part * part) for part in (tables_grad, time_grad, cond_grad_w, bias_grad)
    )
    totals = routes.sum_all(jnp.stack([loss_part, squares]))
    loss = totals[0] / total_entries
    norm = jnp.sqrt(totals[1])
    entries = NTAB * D + D * D + (D + 1) * NCOND + LAYERS * (4 * D * D + 2 * D * FF)
    limit = clip_scale * math.sqrt(entries / (all_latents * SEQ))
    factor = jnp.minimum(1.0, limit / norm)
    count = step_count[0].astype(jnp.float32)
    width = attn_weight.shape[3]
    attn_grad = jnp.stack(
        [
            jnp.stack([qk[:, :width], qk[:, width:], vo[:, :width], vo[:, width:]])
            for qk, vo, _, _ in layer_grads
        ]
    )
    mlp_grad = jnp.stack([jnp.stack([up, down]) for _, _, up, down in layer_grads])
    weights_all = (tables, time_weight, cond_weight, cond_bias, attn_weight, mlp_weight)
    grads_all = (tables_grad, time_grad, cond_grad_w, bias_grad, attn_grad, mlp_grad)
    states = (
        (tables_first, tables_second),
        (time_first, time_second),
        (cond_first, cond_second),
        (bias_first, bias_second),
        (attn_first, attn_second),
        (mlp_first, mlp_second),
    )
    results = [loss, norm]
    for weight, grad, state in zip(weights_all, grads_all, states):
        results.extend(adam_update(weight, grad * factor, state[0], state[1], count))
    return tuple(results)


MESH = pl.DeviceIdType.MESH
VMEM_LIMIT = 60 * 1024 * 1024
LANES = 128
HALF = 128
TOKENS = 256


class Place:
    def __init__(self):
        self.f = lax.axis_index("fsdp")
        self.t = lax.axis_index("tp")
        self.z = self.f // 2
        self.y = lax.rem(self.f, 2)
        self.core = (self.f, self.t + 1 - 2 * lax.rem(self.t, 2))
        self.across = (self.f, lax.rem(self.t + 2, 4))
        self.diagonal = (self.f, 3 - self.t)
        self.pair = (self.f + 1 - 2 * self.y, self.t)

    def down_z(self, k):
        return (lax.rem(self.z + 4 - k, 4) * 2 + self.y, self.t)

    def up_z(self, k):
        return (lax.rem(self.z + k, 4) * 2 + self.y, self.t)

    def up_f(self, k):
        return (lax.rem(self.f + k, 8), self.t)

    def slot_of(self, owner):
        pair_part = lax.rem(self.y + owner % 2, 2)
        return pair_part * 4 + lax.rem(owner // 2 + 4 - self.z, 4)


class Mail:
    def __init__(self, send_sem, recv_sem, local_sem):
        self.send_sem, self.recv_sem, self.local_sem = (send_sem, recv_sem, local_sem)
        self.sent = []
        self.local = []

    def send(self, source, target, device):
        index = len(self.sent)
        copy = pltpu.make_async_remote_copy(
            src_ref=source,
            dst_ref=target,
            send_sem=self.send_sem.at[index],
            recv_sem=self.recv_sem.at[index],
            device_id=device,
            device_id_type=MESH,
        )
        copy.start()
        self.sent.append(copy)
        return copy

    def move(self, source, target):
        copy = pltpu.make_async_copy(source, target, self.local_sem.at[len(self.local)])
        copy.start()
        self.local.append(copy)
        return copy

    def finish(self, skip=()):
        for copy in self.sent:
            copy.wait_send()
        for copy in self.local:
            if not any(copy is other for other in skip):
                copy.wait()


def greet(place):
    barrier = pltpu.get_barrier_semaphore()
    friends = [place.up_f(k) for k in range(1, 8)]
    friends += [place.core, place.across, place.diagonal]
    for device in friends:
        pl.semaphore_signal(barrier, inc=1, device_id=device, device_id_type=MESH)
    pl.semaphore_wait(barrier, len(friends))


def mm(left, right):
    return lax.dot_general(left, right, (((1,), (0,)), ((), ())), preferred_element_type=jnp.float32)


def mm_nt(left, right):
    return lax.dot_general(left, right, (((1,), (1,)), ((), ())), preferred_element_type=jnp.float32)


def mm_tn(left, right):
    return lax.dot_general(left, right, (((0,), (0,)), ((), ())), preferred_element_type=jnp.float32)


class Gather:
    def __init__(self, place, mail, shard, own, other=None):
        self.place, self.mail, self.shard, self.own, self.other = (place, mail, shard, own, other)
        self.rows = shard.shape[0]

    def at(self, ref, slot):
        return ref.at[pl.ds(slot * self.rows, self.rows)]

    def start_z(self):
        self.kept = self.mail.move(self.shard, self.at(self.own, 0))
        self.from_z = [
            self.mail.send(self.shard, self.at(self.own, k), self.place.down_z(k))
            for k in range(1, 4)
        ]

    def start_y(self):
        self.from_y = [self.mail.send(self.shard, self.at(self.own, 4), self.place.pair)]

    def start_x(self):
        self.from_x = [self.mail.send(self.shard, self.at(self.other, 0), self.place.across)]

    def pass_z(self):
        for k in range(1, 4):
            self.from_z[k - 1].wait_recv()
            block = self.at(self.own, k)
            self.from_y.append(self.mail.send(block, self.at(self.own, 4 + k), self.place.pair))
            if self.other is not None:
                self.from_x.append(self.mail.send(block, self.at(self.other, k), self.place.across))

    def pass_y(self, slots=(0, 1, 2, 3)):
        for k in slots:
            self.from_y[k].wait_recv()
            if self.other is not None:
                block = self.at(self.own, 4 + k)
                target = self.at(self.other, 4 + k)
                self.from_x.append(self.mail.send(block, target, self.place.across))

    def pass_x(self):
        if self.other is not None:
            for copy in self.from_x:
                copy.wait_recv()
        self.kept.wait()


def gelu_parts(value):
    inner = math.sqrt(2.0 / math.pi) * (value + 0.044715 * (value * value * value))
    return 0.5 * (1.0 + jnp.tanh(inner))


def half_mask(rows, upper):
    lanes = lax.broadcasted_iota(jnp.int32, (rows, LANES), 1)
    return lanes >= 64 if upper else lanes < 64


def forward_kernel(shapes, total_entries, *refs):
    names = list(shapes)
    r = SimpleNamespace(**dict(zip(names, refs)))
    rest = refs[len(names) :]
    outs = SimpleNamespace(**dict(zip(FORWARD_OUTS, rest)))
    rest = rest[len(FORWARD_OUTS) :]
    s = SimpleNamespace(**dict(zip(FORWARD_SCRATCH, rest)))
    rest = rest[len(FORWARD_SCRATCH) :]
    mail = Mail(*rest)
    place = Place()
    greet(place)

    attn = [
        Gather(place, mail, r.shards.at[l, 0], s.wattn.at[l, 0], s.wattn.at[l, 1])
        for l in range(LAYERS)
    ]
    up = [Gather(place, mail, r.shards.at[l, 1], s.wmlp.at[l, 0]) for l in range(LAYERS)]
    down = [Gather(place, mail, r.shards.at[l, 2], s.wmlp.at[l, 1]) for l in range(LAYERS)]

    across_index = place.t // 2
    core_index = lax.rem(place.t, 2)
    cond_loaded = mail.move(r.cond_weight, s.cond_weight)
    cond_own = r.cond_part.at[across_index, core_index]
    cond_from = [mail.send(cond_own, s.cond_in.at[k - 1], place.up_f(k)) for k in range(1, 8)]
    own_data = r.data.at[across_index]
    data_far = mail.send(r.data.at[1 - across_index], s.data_in.at[1], place.across)
    data_side = mail.send(own_data, s.data_in.at[2], place.core)
    attn[0].start_z()
    attn[0].start_y()
    attn[0].start_x()
    head_rows = r.head.shape[0]
    head_kept = mail.move(r.head, s.head.at[pl.ds(0, head_rows)])
    data_kept = mail.move(own_data, s.data_in.at[0])
    head_from = [
        mail.send(r.head, s.head.at[pl.ds(k * head_rows, head_rows)], place.down_z(k))
        for k in range(1, 4)
    ]
    attn[1].start_y()
    up[0].start_y()

    rows_id = lax.broadcasted_iota(jnp.int32, (LANES, D), 0)
    offset = lax.broadcasted_iota(jnp.int32, (LANES, D), 1) - rows_id
    for owner in range(8):
        hit = (offset == place.slot_of(owner) * head_rows) & (rows_id < head_rows)
        s.order[pl.ds(owner * LANES, LANES), :] = jnp.where(hit, 1.0, 0.0).astype(jnp.bfloat16)

    waves = mm(r.waves[...], s.order[...])
    s.waves[...] = waves[0:32] + waves[32:64] + waves[64:96]

    part = r.cond_part[across_index, core_index]
    for k in range(7):
        cond_from[k].wait_recv()
        part = part + s.cond_in[k]
    s.cond[across_index, core_index] = part
    cond_part = s.cond.at[across_index, core_index]
    cond_side = mail.send(cond_part, cond_part, place.core)
    data_far.wait_recv()
    data_diagonal = mail.send(s.data_in.at[1], s.data_in.at[3], place.core)
    attn[0].pass_y((0,))
    cond_side.wait_recv()
    cond_half = s.cond.at[across_index]
    cond_far = mail.send(cond_half, cond_half, place.across)
    cond = jnp.concatenate([s.cond[across_index, 0], s.cond[across_index, 1]], axis=0)
    cond_act = (cond * jax.nn.sigmoid(cond)).astype(jnp.bfloat16)
    blocks = r.cond_weight.shape[0]
    cond_loaded.wait()
    for b in range(blocks):
        part = mm_nt(cond_act, s.cond_weight[b].astype(jnp.bfloat16)) + r.cond_bias[b : b + 1, :]
        part = part.astype(jnp.bfloat16).astype(jnp.float32)
        for i in range(8):
            s.mod_out[i, b : b + 1, 0:head_rows] = part[i : i + 1, :]
    mod_from = []
    for k in range(1, 8):
        source = s.mod_out.at[lax.rem(place.f + k, 8)]
        mod_from.append(mail.send(source, s.mod_in.at[k], place.up_f(k)))
    mod_kept = mail.move(s.mod_out.at[place.f], s.mod_in.at[0])
    attn[1].start_z()

    attn[0].pass_z()
    up[0].start_z()
    for k in range(3):
        head_from[k].wait_recv()
    head_kept.wait()
    lower = s.head.at[pl.ds(0, 4 * head_rows)]
    upper = s.head.at[pl.ds(4 * head_rows, 4 * head_rows)]
    head_pair = mail.send(lower, upper, place.pair)
    attn[1].start_x()
    down[0].start_y()
    up[1].start_y()
    down[1].start_y()

    mod_kept.wait()
    for copy in mod_from:
        copy.wait_recv()
    s.mod_rows[...] = jnp.zeros_like(s.mod_rows)
    for g in range(8 * blocks):
        piece, owner = (g // 8, g % 8)
        k = lax.rem(place.f + 8 - g // blocks, 8)
        b = g % blocks
        s.mod_rows[piece : piece + 1, owner * LANES : owner * LANES + head_rows] = s.mod_in[
            k, b : b + 1, 0:head_rows
        ]
    s.pieces[...] = mm(s.mod_rows[...].astype(jnp.bfloat16), s.order[...])
    mail.move(s.pieces, outs.pieces)

    data_kept.wait()
    data_side.wait_recv()
    data_diagonal.wait_recv()
    head_pair.wait_recv()
    cond_far.wait_recv()
    mail.move(s.cond, outs.cond)
    mail.move(s.head, outs.head)
    chunk_rows = s.data_in.shape[1] // 2
    grid_rows = chunk_rows // GRID
    cols = s.waves[16:32, :]
    chunk_ids = [place.t, place.across[1], place.core[1], place.diagonal[1]]
    for j in range(4):
        low = pl.ds(j * chunk_rows, chunk_rows)
        s.noisy[low, :] = s.data_in[j, 0:chunk_rows, :].astype(jnp.bfloat16)
        s.noise[low, :] = s.data_in[j, chunk_rows : 2 * chunk_rows, :]
        for i in range(grid_rows):
            row = s.waves[pl.ds(chunk_ids[j] * grid_rows + i, 1), :]
            s.resid[pl.ds(j * chunk_rows + i * GRID, GRID), :] = cols + row
    mail.move(s.noisy, outs.noisy)
    for n in range(0, D, 256):
        s.resid[:, n : n + 256] += mm_nt(s.noisy[...], s.head[n : n + 256, :])

    def piece(index):
        return s.pieces[index : index + 1, :]

    def normalize(which, shift, scale, target, low):
        value = s.resid[low : low + HALF, :]
        centred = value - jnp.mean(value, axis=-1, keepdims=True)
        inverse = lax.rsqrt(jnp.mean(centred * centred, axis=-1, keepdims=True) + norm_eps)
        normed = centred * inverse
        s.normed[which, low : low + HALF, :] = normed
        s.inverse[which, low : low + HALF, :] = jnp.broadcast_to(inverse, (HALF, LANES))
        target[low : low + HALF, :] = (normed * (1.0 + scale) + shift).astype(jnp.bfloat16)
        if low:
            mail.move(s.normed.at[which], outs.normed.at[which])
            mail.move(s.inverse.at[which], outs.inverse.at[which])

    low_mask = half_mask(TOKENS, False)
    high_mask = half_mask(TOKENS, True)
    for l in range(LAYERS):
        base = 6 * l
        hidden = s.hidden.at[l]
        for low in (0, HALF):
            normalize(2 * l, piece(base), piece(base + 1), hidden, low)
        if l == 0:
            attn[0].pass_y((1, 2, 3))
            attn[1].pass_z()
            down[0].start_z()
        attn[l].pass_x()
        for x in range(2):
            weight = s.wattn.at[l, x]
            qkv = s.qkv.at[l, x]
            for n in range(0, D, 256):
                qkv[:, n : n + 256] = mm(hidden[...], weight[:, n : n + 256]).astype(jnp.bfloat16)
        for x in range(2):
            qkv = s.qkv.at[l, x]
            att = s.att.at[l, x]
            for h, (q, k, v, keep) in enumerate(
                ((0, 1, 2, low_mask), (0, 1, 2, high_mask), (3, 4, 5, low_mask))
            ):
                query = qkv[:, q * LANES : (q + 1) * LANES].astype(jnp.float32)
                query = jnp.where(keep, query, 0.0)
                key = qkv[:, k * LANES : (k + 1) * LANES]
                value = qkv[:, v * LANES : (v + 1) * LANES]
                scores = mm_nt(query.astype(jnp.bfloat16), key) * HEAD_DIM ** (-0.5)
                exped = jnp.exp(scores - jnp.max(scores, axis=-1, keepdims=True))
                probs = exped / jnp.sum(exped, axis=-1, keepdims=True)
                s.probs[l, x, h] = probs
                mixed = mm(probs.astype(jnp.bfloat16), value)
                if h != 1:
                    mixed = pltpu.roll(mixed, 64, 1)
                att[:, h * LANES : (h + 1) * LANES] = jnp.where(high_mask, mixed, 0.0).astype(
                    jnp.bfloat16
                )
            if x == 0 and l == 0:
                up[0].pass_z()
                up[1].start_z()
            elif x == 0:
                down[1].pass_z()
        for n in range(0, D, 256):
            total = mm_nt(s.att[l, 0], s.wattn[l, 0, n : n + 256, 384:768])
            total = total + mm_nt(s.att[l, 1], s.wattn[l, 1, n : n + 256, 384:768])
            s.core_out[l, :, n : n + 256] = total.astype(jnp.bfloat16)
        summed = mail.send(s.core_out.at[l], s.core_in.at[l], place.core)
        gate = piece(base + 2)
        summed.wait_recv()
        for low in (0, HALF):
            output = s.core_out[l, low : low + HALF, :].astype(jnp.float32)
            output = output + s.core_in[l, HALF - low : 2 * HALF - low, :].astype(jnp.float32)
            s.attn_out[l, low : low + HALF, :] = output
            s.resid[low : low + HALF, :] += gate * output
        rows = s.rows.at[l]
        normalize(2 * l + 1, piece(base + 3), piece(base + 4), rows, 0)
        far = mail.send(rows.at[pl.ds(0, HALF)], rows.at[pl.ds(2 * HALF, HALF)], place.across)
        normalize(2 * l + 1, piece(base + 3), piece(base + 4), rows, HALF)
        for source, target in (
            (s.hidden, outs.hidden),
            (s.qkv, outs.qkv),
            (s.att, outs.att),
            (s.probs, outs.probs),
            (s.attn_out, outs.attn_out),
            (s.wattn, outs.wattn),
        ):
            mail.move(source.at[l], target.at[l])
        if l == 0:
            attn[1].pass_y()
            down[0].pass_z()
            down[1].start_z()
        up[l].pass_y()
        up[l].pass_x()
        w_up = s.wmlp.at[l, 0]
        w_down = s.wmlp.at[l, 1]

        def rise(low, size):
            for n in range(0, D, 256):
                upward = mm(rows[low : low + size, :], w_up[:, n : n + 256])
                s.upward[l, low : low + size, n : n + 256] = upward
                s.active[l, low : low + size, n : n + 256] = (
                    upward * gelu_parts(upward)
                ).astype(jnp.bfloat16)

        rise(0, HALF)
        rise(HALF, HALF)
        far.wait_recv()
        side = mail.send(
            rows.at[pl.ds(2 * HALF, HALF)], rows.at[pl.ds(3 * HALF, HALF)], place.core
        )
        rise(2 * HALF, HALF)
        side.wait_recv()
        rise(3 * HALF, HALF)
        down[l].pass_y()
        down[l].pass_x()

        def fall(low, target):
            for n in range(0, D, 256):
                part = mm_nt(s.active[l, low : low + HALF, :], w_down[n : n + 256, :])
                target[:, n : n + 256] = part.astype(target.dtype)

        sum_out, sum_in, keep = (s.sum_out.at[l], s.sum_in.at[l], s.keep)
        fall(3 * HALF, sum_out.at[0])
        first = mail.send(sum_out.at[0], sum_in.at[0], place.core)
        fall(2 * HALF, keep.at[0])
        fall(HALF, sum_out.at[1])
        second = mail.send(sum_out.at[1], sum_in.at[1], place.core)
        first.wait_recv()
        s.far_out[l] = (keep[0] + sum_in[0].astype(jnp.float32)).astype(jnp.bfloat16)
        third = mail.send(s.far_out.at[l], s.far_in.at[l], place.across)
        if l == 0:
            up[1].pass_z()
        fall(0, keep.at[1])
        second.wait_recv()
        keep[1] = keep[1] + sum_in[1].astype(jnp.float32)
        for source, target in (
            (s.rows, outs.rows),
            (s.upward, outs.upward),
            (s.active, outs.active),
            (s.wmlp, outs.wmlp),
        ):
            mail.move(source.at[l], target.at[l])
        third.wait_recv()
        total = (keep[1] + s.far_in[l].astype(jnp.float32)).astype(jnp.bfloat16)
        s.own_out[l] = total
        fourth = mail.send(s.own_out.at[l], s.own_in.at[l], place.core)
        gate = piece(base + 5)
        output = total.astype(jnp.float32)
        s.mlp_out[l, 0:HALF, :] = output
        s.resid[0:HALF, :] += gate * output
        fourth.wait_recv()
        output = s.own_in[l].astype(jnp.float32)
        s.mlp_out[l, HALF : 2 * HALF, :] = output
        s.resid[HALF : 2 * HALF, :] += gate * output
        mail.move(s.mlp_out.at[l], outs.mlp_out.at[l])

    for low in (0, HALF):
        normalize(
            2 * LAYERS, piece(6 * LAYERS), piece(6 * LAYERS + 1), s.final_low, low
        )
    predicted = mm(s.final_low[...], s.head[...])
    lanes = lax.broadcasted_iota(jnp.int32, (TOKENS, LANES), 1)
    taken = (lanes >= PATCH_DIM) & (lanes < 2 * PATCH_DIM)
    difference = jnp.where(taken, predicted - s.noise[...], 0.0)
    square = difference[0:HALF] * difference[0:HALF]
    s.loss[...] = jnp.sum(square.reshape(HALF // 8, 8, LANES), axis=0)
    s.grad_pred[...] = (difference * (2.0 / total_entries)).astype(jnp.bfloat16)
    for source, target in (
        (s.final_low, outs.final_low),
        (s.loss, outs.loss),
        (s.grad_pred, outs.grad_pred),
    ):
        mail.move(source, target)
    waited = [cond_loaded, head_kept, data_kept, mod_kept] + [g.kept for g in attn + up + down]
    mail.finish(waited)


FORWARD_OUTS = dict(
    wattn=((LAYERS, 2, D, D), jnp.bfloat16),
    wmlp=((LAYERS, 2, D, D), jnp.bfloat16),
    head=((D, LANES), jnp.bfloat16),
    pieces=((16, D), jnp.float32),
    cond=((2, 2, 4, D), jnp.float32),
    hidden=((LAYERS, TOKENS, D), jnp.bfloat16),
    qkv=((LAYERS, 2, TOKENS, D), jnp.bfloat16),
    att=((LAYERS, 2, TOKENS, D // 2), jnp.bfloat16),
    probs=((LAYERS, 2, 3, TOKENS, TOKENS), jnp.float32),
    attn_out=((LAYERS, TOKENS, D), jnp.float32),
    rows=((LAYERS, 2 * TOKENS, D), jnp.bfloat16),
    upward=((LAYERS, 2 * TOKENS, D), jnp.float32),
    active=((LAYERS, 2 * TOKENS, D), jnp.bfloat16),
    mlp_out=((LAYERS, TOKENS, D), jnp.float32),
    normed=((2 * LAYERS + 1, TOKENS, D), jnp.float32),
    inverse=((2 * LAYERS + 1, TOKENS, LANES), jnp.float32),
    final_low=((TOKENS, D), jnp.bfloat16),
    noisy=((TOKENS, LANES), jnp.bfloat16),
    grad_pred=((TOKENS, LANES), jnp.bfloat16),
    loss=((8, LANES), jnp.float32),
)
FORWARD_OWN = dict(
    cond_weight=((NCOND // D, D // 8, D), jnp.float32),
    order=((8 * LANES, D), jnp.bfloat16),
    waves=((32, D), jnp.float32),
    cond_in=((7, 4, D), jnp.float32),
    data_in=((4, HALF, LANES), jnp.float32),
    noise=((TOKENS, LANES), jnp.float32),
    mod_out=((8, 16, LANES), jnp.float32),
    mod_in=((8, 16, LANES), jnp.float32),
    mod_rows=((16, 8 * LANES), jnp.float32),
    resid=((TOKENS, D), jnp.float32),
    core_out=((LAYERS, TOKENS, D), jnp.bfloat16),
    core_in=((LAYERS, TOKENS, D), jnp.bfloat16),
    sum_out=((LAYERS, 2, HALF, D), jnp.bfloat16),
    sum_in=((LAYERS, 2, HALF, D), jnp.bfloat16),
    far_out=((LAYERS, HALF, D), jnp.bfloat16),
    far_in=((LAYERS, HALF, D), jnp.bfloat16),
    own_out=((LAYERS, HALF, D), jnp.bfloat16),
    own_in=((LAYERS, HALF, D), jnp.bfloat16),
    keep=((2, HALF, D), jnp.float32),
)
FORWARD_SCRATCH = {**FORWARD_OUTS, **FORWARD_OWN}


def run_forward(inputs, total_entries):
    vmem = pl.BlockSpec(memory_space=pltpu.VMEM)
    outs = pl.pallas_call(
        partial(forward_kernel, {name: value.shape for name, value in inputs.items()}, total_entries),
        out_shape=[jax.ShapeDtypeStruct(*spec) for spec in FORWARD_OUTS.values()],
        in_specs=[
            pl.BlockSpec(memory_space=pl.ANY) if value.size > D * D * 2 and value.dtype == jnp.float32 else vmem
            for value in inputs.values()
        ],
        out_specs=[pl.BlockSpec(memory_space=pl.ANY)] * len(FORWARD_OUTS),
        scratch_shapes=[pltpu.VMEM(*spec) for spec in FORWARD_SCRATCH.values()]
        + [
            pltpu.SemaphoreType.DMA((128,)),
            pltpu.SemaphoreType.DMA((128,)),
            pltpu.SemaphoreType.DMA((64,)),
        ],
        compiler_params=pltpu.CompilerParams(
            collective_id=0, has_side_effects=True, vmem_limit_bytes=VMEM_LIMIT
        ),
    )(*inputs.values())
    return SimpleNamespace(**dict(zip(FORWARD_OUTS, outs)))
class Scatter:
    def __init__(self, place, mail, grad, from_y, from_z, result, other=None, from_x=None):
        self.place, self.mail, self.grad, self.result = (place, mail, grad, result)
        self.from_y, self.from_z, self.other, self.from_x = (from_y, from_z, other, from_x)
        self.rows = result.shape[0]
        self.x_copies, self.y_copies, self.z_copies = ({}, {}, {})

    def at(self, ref, slot):
        return ref.at[pl.ds(slot * self.rows, self.rows)]

    def start(self, slots=(5, 6, 7, 4)):
        for slot in slots:
            if self.other is None:
                self.send_y(slot)
            else:
                self.x_copies[slot] = self.mail.send(
                    self.at(self.other, slot), self.at(self.from_x, slot), self.place.across
                )

    def send_y(self, slot):
        self.y_copies[slot - 4] = self.mail.send(
            self.at(self.grad, slot), self.at(self.from_y, slot - 4), self.place.pair
        )

    def total(self, slot, refs):
        low = slot * self.rows
        value = self.grad[low : low + self.rows, :].astype(jnp.float32)
        for ref in refs:
            value = value + ref[low : low + self.rows, :].astype(jnp.float32)
        return value

    def pass_x(self):
        for slot in (5, 6, 7, 4):
            if self.other is not None:
                self.x_copies[slot].wait_recv()
                low = slot * self.rows
                self.grad[low : low + self.rows, :] = self.total(slot, [self.from_x]).astype(
                    jnp.bfloat16
                )
                self.send_y(slot)

    def pass_y(self, slots=(1, 2, 3, 0)):
        refs = [self.from_y] if self.other is None else [self.from_x, self.from_y]
        for slot in slots:
            if self.other is not None:
                self.x_copies[slot].wait_recv()
            self.y_copies[slot].wait_recv()
            value = self.total(slot, refs)
            if slot == 0:
                self.result[...] = value
            else:
                low = slot * self.rows
                self.grad[low : low + self.rows, :] = value.astype(jnp.bfloat16)
                self.z_copies[slot] = self.mail.send(
                    self.at(self.grad, slot), self.from_z.at[slot - 1], self.place.up_z(slot)
                )

    def pass_z(self):
        value = self.result[...]
        for slot in (1, 2, 3):
            self.z_copies[slot].wait_recv()
            value = value + self.from_z[slot - 1].astype(jnp.float32)
        self.result[...] = value


def gelu_slope(value):
    const = math.sqrt(2.0 / math.pi)
    square = value * value
    tanh = jnp.tanh(const * (value + 0.044715 * (square * value)))
    return 0.5 * (1.0 + tanh) + 0.5 * value * (1.0 - tanh * tanh) * (
        const * (1.0 + (3.0 * 0.044715) * square)
    )


def backward_kernel(*refs):
    r = SimpleNamespace(**dict(zip(BACKWARD_INS, refs)))
    rest = refs[len(BACKWARD_INS) :]
    outs = SimpleNamespace(**dict(zip(BACKWARD_OUTS, rest)))
    rest = rest[len(BACKWARD_OUTS) :]
    s = SimpleNamespace(**dict(zip(BACKWARD_SCRATCH, rest)))
    rest = rest[len(BACKWARD_SCRATCH) :]
    mail = Mail(*rest)
    place = Place()
    loaded = {}
    waited = []

    def load(name, index=None):
        source = getattr(r, name)
        source = source if index is None else source.at[index]
        loaded[name] = mail.move(source, getattr(s, name))

    def need(*names):
        for name in names:
            if name in loaded:
                copy = loaded.pop(name)
                copy.wait()
                waited.append(copy)

    for name in FINAL_KEPT:
        load(name)
    normed_from = {}

    def load_normed(which):
        normed_from[which] = [
            mail.move(r.normed.at[which], s.normed.at[which]),
            mail.move(r.inverse.at[which], s.inverse.at[which]),
        ]

    load_normed(2 * LAYERS)
    for name in list(MLP_KEPT) + list(ATTN_KEPT):
        load(name, LAYERS - 1)
    for which in reversed(range(2 * LAYERS)):
        load_normed(which)
    load(*LATE_KEPT)
    greet(place)

    head_rows = D // 8
    across_index = place.t // 2
    core_index = lax.rem(place.t, 2)
    rows_id = lax.broadcasted_iota(jnp.int32, (LANES, D), 0)
    offset = lax.broadcasted_iota(jnp.int32, (LANES, D), 1) - rows_id
    for owner in range(8):
        hit = (offset == place.slot_of(owner) * head_rows) & (rows_id < head_rows)
        s.order[pl.ds(owner * LANES, LANES), :] = jnp.where(hit, 1.0, 0.0).astype(jnp.bfloat16)
    s.mod_grad[...] = jnp.zeros_like(s.mod_grad)
    s.mod_send[...] = jnp.zeros_like(s.mod_send)

    def piece(index):
        return s.pieces[index : index + 1, :]

    def norm_back(which, mod_row, low, first):
        if low == 0:
            for copy in normed_from[which]:
                copy.wait()
                waited.append(copy)
        mixed = s.mixed[low : low + HALF, :]
        normed = s.normed[which, low : low + HALF, :]
        inverse = s.inverse[which, low : low + HALF, 0:1]
        if low == 0:
            s.mod_grad[mod_row : mod_row + 1, :] = jnp.sum(mixed, axis=0, keepdims=True)
            s.mod_grad[mod_row + 1 : mod_row + 2, :] = jnp.sum(
                mixed * normed, axis=0, keepdims=True
            )
        scaled = mixed * (1.0 + piece(mod_row + 1))
        centred = scaled - jnp.mean(scaled, axis=-1, keepdims=True)
        grad = (centred - normed * jnp.mean(scaled * normed, axis=-1, keepdims=True)) * inverse
        if first:
            s.grad[low : low + HALF, :] = grad
        else:
            s.grad[low : low + HALF, :] += grad

    need(*FINAL_KEPT)
    s.head_grad[...] = mm_tn(s.final_low[0:HALF, :], s.grad_pred[0:HALF, :])
    for n in range(0, D, 256):
        s.mixed[:, n : n + 256] = mm_nt(s.grad_pred[...], s.head[n : n + 256, :])
    for low in (0, HALF):
        norm_back(2 * LAYERS, 6 * LAYERS, low, True)

    def scatter(l, kind, index, other=None):
        if other is None:
            return Scatter(
                place, mail, s.mlp_grad.at[l, index], s.from_y.at[l, kind],
                s.from_z.at[l, kind], s.result.at[l, kind],
            )
        return Scatter(
            place, mail, s.attn_grad.at[l, 0], s.from_y.at[l, kind],
            s.from_z.at[l, kind], s.result.at[l, kind],
            s.attn_grad.at[l, 1], s.from_x.at[l],
        )

    attn = [scatter(l, 0, 0, True) for l in range(LAYERS)]
    up = [scatter(l, 1, 0) for l in range(LAYERS)]
    down = [scatter(l, 2, 1) for l in range(LAYERS)]

    low_mask = half_mask(TOKENS, False)
    high_mask = half_mask(TOKENS, True)
    for l in reversed(range(LAYERS)):
        base = 6 * l
        last = l == LAYERS - 1
        gate = piece(base + 5)
        need(*list(MLP_KEPT)[:1])
        grads = s.grad_rows.at[l]
        grads[0:HALF, :] = (gate * s.grad[0:HALF, :]).astype(jnp.bfloat16)
        far = mail.send(grads.at[pl.ds(0, HALF)], grads.at[pl.ds(2 * HALF, HALF)], place.across)
        grads[HALF : 2 * HALF, :] = (gate * s.grad[HALF : 2 * HALF, :]).astype(jnp.bfloat16)
        s.mod_grad[base + 5 : base + 6, :] = jnp.sum(
            s.grad[0:HALF, :] * s.mlp_out[0:HALF, :], axis=0, keepdims=True
        )
        if not last:
            attn[1].start((6, 7, 4))
            up[1].pass_y()
        need(*MLP_KEPT)
        w_up, w_down = (s.wmlp.at[0], s.wmlp.at[1])

        def drop(low):
            for n in range(0, D, 256):
                part = mm(grads[low : low + HALF, :], w_down[:, n : n + 256])
                slope = gelu_slope(s.upward[low : low + HALF, n : n + 256])
                s.grad_up[low : low + HALF, n : n + 256] = (part * slope).astype(jnp.bfloat16)

        drop(0)
        drop(HALF)
        far.wait_recv()
        side = mail.send(
            grads.at[pl.ds(2 * HALF, HALF)], grads.at[pl.ds(3 * HALF, HALF)], place.core
        )
        drop(2 * HALF)
        side.wait_recv()
        drop(3 * HALF)

        def fall(low, target):
            for n in range(0, D, 256):
                part = mm_nt(s.grad_up[low : low + HALF, :], w_up[n : n + 256, :])
                target[:, n : n + 256] = part.astype(target.dtype)

        sum_out, sum_in, keep = (s.sum_out.at[l], s.sum_in.at[l], s.keep)
        fall(3 * HALF, sum_out.at[0])
        first = mail.send(sum_out.at[0], sum_in.at[0], place.core)
        fall(2 * HALF, keep.at[0])
        fall(HALF, sum_out.at[1])
        second = mail.send(sum_out.at[1], sum_in.at[1], place.core)
        first.wait_recv()
        s.far_out[l] = (keep[0] + sum_in[0].astype(jnp.float32)).astype(jnp.bfloat16)
        third = mail.send(s.far_out.at[l], s.far_in.at[l], place.across)
        if not last:
            attn[1].start((1, 2, 3, 0))
        fall(0, keep.at[1])
        for n in range(0, D, 256):
            s.mlp_grad[l, 1, :, n : n + 256] = mm_tn(
                grads[...], s.active[:, n : n + 256]
            ).astype(jnp.bfloat16)
        down[l].start()
        second.wait_recv()
        keep[1] = keep[1] + sum_in[1].astype(jnp.float32)
        third.wait_recv()
        total = (keep[1] + s.far_in[l].astype(jnp.float32)).astype(jnp.bfloat16)
        s.own_out[l] = total
        fourth = mail.send(s.own_out.at[l], s.own_in.at[l], place.core)
        s.mixed[0:HALF, :] = total.astype(jnp.float32)
        norm_back(2 * l + 1, base + 3, 0, False)
        fourth.wait_recv()
        s.mixed[HALF : 2 * HALF, :] = s.own_in[l].astype(jnp.float32)
        norm_back(2 * l + 1, base + 3, HALF, False)
        if not last:
            down[0].pass_y((1, 2))
        for n in range(0, D, 256):
            s.mlp_grad[l, 0, :, n : n + 256] = mm_tn(
                s.rows[...], s.grad_up[:, n : n + 256]
            ).astype(jnp.bfloat16)
        up[l].start()
        if last:
            for name in MLP_KEPT:
                load(name, 0)

        gate = piece(base + 2)
        need(*ATTN_KEPT)
        both = s.both
        both[0:TOKENS, :] = s.hidden[...]
        both[TOKENS : 2 * TOKENS, :] = (gate * s.grad[...]).astype(jnp.bfloat16)
        s.mod_grad[base + 2 : base + 3, :] = jnp.sum(
            s.grad[0:HALF, :] * s.attn_out[0:HALF, :], axis=0, keepdims=True
        )
        scale = HEAD_DIM ** (-0.5)
        for x in range(2):
            qkv = s.qkv.at[x]
            grad_qkv = s.grad_qkv.at[x]

            def tile(ref, index):
                return ref[:, index * LANES : (index + 1) * LANES]

            def put(index, value):
                grad_qkv[0:TOKENS, index * LANES : (index + 1) * LANES] = value.astype(jnp.bfloat16)

            found = {}
            for h, (q, k, v, keep_mask) in enumerate(
                ((0, 1, 2, low_mask), (0, 1, 2, high_mask), (3, 4, 5, low_mask))
            ):
                weight = s.wattn[x, :, (3 + h) * LANES : (4 + h) * LANES]
                grad_att = mm(both[TOKENS : 2 * TOKENS, :], weight)
                if h != 1:
                    grad_att = pltpu.roll(grad_att, 64, 1)
                grad_att = jnp.where(keep_mask, grad_att, 0.0).astype(jnp.bfloat16)
                probs = s.probs[x, h]
                grad_probs = mm_nt(grad_att, tile(qkv, v))
                inner = jnp.sum(probs * grad_probs, axis=-1, keepdims=True)
                grad_scores = (probs * (grad_probs - inner)).astype(jnp.bfloat16)
                found[h] = (
                    jnp.where(keep_mask, mm(grad_scores, tile(qkv, k)) * scale, 0.0),
                    jnp.where(keep_mask, mm_tn(grad_scores, tile(qkv, q)) * scale, 0.0),
                    mm_tn(probs.astype(jnp.bfloat16), grad_att),
                )
                if h == 1:
                    for index in range(3):
                        put(index, found[0][index] + found[1][index])
                if h == 2:
                    for index in range(3):
                        put(3 + index, found[2][index])
            if last and x == 0:
                down[1].pass_y()
            elif not last and x == 0:
                attn[1].pass_x()
            elif not last:
                down[0].pass_y((3, 0))
        for n in range(0, D, 256):
            part = mm_nt(s.grad_qkv[0, 0:TOKENS, :], s.wattn[0, n : n + 256, :])
            part = part + mm_nt(s.grad_qkv[1, 0:TOKENS, :], s.wattn[1, n : n + 256, :])
            s.core_out[l, :, n : n + 256] = part.astype(jnp.bfloat16)
        summed = mail.send(s.core_out.at[l], s.core_in.at[l], place.core)
        for x in (1, 0):
            s.grad_qkv[x, TOKENS : 2 * TOKENS, D // 2 : D] = s.att[x]
            half = s.grad_qkv[x, 0:TOKENS, 0 : D // 2]
            s.attn_grad[l, x, :, 0 : D // 2] = mm_tn(both[0:TOKENS, :], half).astype(jnp.bfloat16)
            half = s.grad_qkv[x, :, D // 2 : D]
            s.attn_grad[l, x, :, D // 2 : D] = mm_tn(both[...], half).astype(jnp.bfloat16)
            if x == 1 and last:
                attn[1].start((5,))
        summed.wait_recv()
        for low in (0, HALF):
            value = s.core_out[l, low : low + HALF, :].astype(jnp.float32)
            s.mixed[low : low + HALF, :] = value + s.core_in[
                l, HALF - low : 2 * HALF - low, :
            ].astype(jnp.float32)
            norm_back(2 * l, base, low, False)
        if last:
            for name in ATTN_KEPT:
                load(name, 0)

    mod_first = mail.send(s.mod_grad, s.mod_other, place.core)
    s.head_grad[...] += mm_tn(
        s.grad[0:HALF, :].astype(jnp.bfloat16), s.noisy[0:HALF, :]
    )
    head_first = mail.send(s.head_grad, s.head_other, place.core)
    mod_first.wait_recv()
    s.mod_low[0] = (s.mod_grad[...] + s.mod_other[...]).astype(jnp.bfloat16)
    mod_second = mail.send(s.mod_low.at[0], s.mod_low.at[1], place.across)
    attn[0].start((5, 6, 7, 4, 1, 2, 3, 0))
    blocks = s.cond_weight.shape[0]
    mod_second.wait_recv()
    both_mods = jnp.concatenate([s.mod_low[0], s.mod_low[1]], axis=0)
    for owner in range(8):
        part = mm_nt(both_mods, s.order[owner * LANES : (owner + 1) * LANES, :])
        s.mod_rows[:, owner * LANES : (owner + 1) * LANES] = part
    for g in range(8 * blocks):
        row, owner = (g // 8, g % 8)
        for far in range(2):
            s.mod_send[g // blocks, far, g % blocks : g % blocks + 1, :] = s.mod_rows[
                16 * far + row : 16 * far + row + 1, owner * LANES : (owner + 1) * LANES
            ]
    back_from = []
    for k in range(1, 8):
        source = s.mod_send.at[lax.rem(place.f + k, 8)]
        back_from.append(mail.send(source, s.back.at[k], place.up_f(k)))
    back_own = mail.move(s.mod_send.at[place.f], s.back.at[0])
    head_first.wait_recv()
    s.head_low[...] = (s.head_grad[...] + s.head_other[...]).astype(jnp.bfloat16)
    head_second = mail.send(s.head_low, s.head_far, place.across)
    up[0].pass_y()
    attn[0].pass_x()
    attn[1].pass_y()
    need(*LATE_KEPT)
    back_own.wait()
    for copy in back_from:
        copy.wait_recv()
    for i in range(16):
        x_part = lax.rem(across_index + i // 8, 2)
        k = lax.rem(place.f + 8 - i % 8, 8)
        s.back_rows[i] = s.back[k, x_part]
    partial_cond = jnp.zeros((16, D), jnp.float32)
    for b in range(blocks):
        block = s.back_rows[:, b, 0:head_rows].astype(jnp.bfloat16)
        partial_cond = partial_cond + mm(block, s.cond_weight[b].astype(jnp.bfloat16))
    quarters = [(a, b) for a in range(2) for b in range(2)]
    for a, b in quarters:
        s.cond_out[a, b] = partial_cond[8 * a + 4 * b : 8 * a + 4 * b + 4]
    cond_mine = s.cond_out.at[across_index, core_index]
    cond_from = [mail.send(cond_mine, s.cond_in.at[k - 1], place.up_f(k)) for k in range(1, 8)]
    mail.move(s.back_rows, outs.back_rows)
    for item in (down[1], up[1]):
        item.pass_z()
    value = s.cond_out[across_index, core_index]
    for k in range(7):
        cond_from[k].wait_recv()
        value = value + s.cond_in[k]
    s.cond_sum[across_index, core_index] = value
    cond_mine = s.cond_sum.at[across_index, core_index]
    cond_side = mail.send(cond_mine, cond_mine, place.core)
    attn[0].pass_y()
    cond_side.wait_recv()
    cond_half = s.cond_sum.at[across_index]
    cond_far = mail.send(cond_half, cond_half, place.across)
    head_second.wait_recv()
    half = 4 * head_rows
    head_total = s.head_low[...].astype(jnp.float32) + s.head_far[...].astype(jnp.float32)
    s.head_mid[...] = head_total
    s.head_sum[...] = head_total.astype(jnp.bfloat16)
    head_third = mail.send(s.head_sum.at[pl.ds(half, half)], s.head_y, place.pair)
    head_third.wait_recv()
    head_from = []
    for k in range(1, 4):
        low = k * head_rows
        part = s.head_mid[low : low + head_rows, :] + s.head_y[
            low : low + head_rows, :
        ].astype(jnp.float32)
        s.head_sum[low : low + head_rows, :] = part.astype(jnp.bfloat16)
        head_from.append(
            mail.send(
                s.head_sum.at[pl.ds(low, head_rows)], s.head_z.at[k - 1], place.up_z(k)
            )
        )
    head_own = s.head_mid[0:head_rows, :] + s.head_y[0:head_rows, :].astype(jnp.float32)
    cond_far.wait_recv()
    value = jnp.concatenate([s.cond_sum[a, b] for a, b in quarters], axis=0)
    cond = jnp.concatenate([r.cond[a, b] for a, b in quarters], axis=0)
    sigmoid = jax.nn.sigmoid(cond)
    cond_act = (cond * sigmoid).astype(jnp.bfloat16)
    cond_grad = (value * (sigmoid * (1.0 + cond * (1.0 - sigmoid)))).astype(jnp.bfloat16)
    s.time_grad[...] = mm_tn(r.time_hidden[...], cond_grad)
    mail.move(s.time_grad, outs.time_grad)
    time_pre = r.time_pre[...]
    sigmoid = jax.nn.sigmoid(time_pre)
    slope = sigmoid * (1.0 + time_pre * (1.0 - sigmoid))
    pre_grad = (mm_nt(cond_grad, r.low_time[...]) * slope).astype(jnp.bfloat16)
    s.first_grad[...] = mm_tn(pre_grad, r.features[...])
    mail.move(s.first_grad, outs.first_grad)
    column = lax.broadcasted_iota(jnp.int32, (D, head_rows), 0)
    column = column - lax.broadcasted_iota(jnp.int32, (D, head_rows), 1)
    picked = jnp.where(column == place.f * head_rows, 1.0, 0.0).astype(jnp.bfloat16)
    own_cols = mm(cond_grad, picked).astype(jnp.bfloat16)
    s.label_grad[...] = mm_tn(own_cols, r.label_hot[...])
    mail.move(s.label_grad, outs.label_grad)
    shared = jnp.sum(s.time_grad[...] * s.time_grad[...])
    shared = shared + jnp.sum(s.first_grad[...] * s.first_grad[...])
    shared = shared + jnp.sum(s.label_grad[...] * s.label_grad[...])
    bias = s.back_rows[0]
    for c in range(1, 16):
        bias = bias + s.back_rows[c]
    shared = shared + jnp.sum(bias * bias)
    weight_squares = jnp.zeros((8, D), jnp.float32)
    for c in range(blocks):
        block = mm_tn(s.back_rows[:, c, 0:head_rows].astype(jnp.bfloat16), cond_act)
        weight_squares = weight_squares + jnp.sum(
            (block * block).reshape(head_rows // 8, 8, D), axis=0
        )
    shared = shared + jnp.sum(weight_squares)
    squares = jnp.zeros((8, D), jnp.float32)
    upper = half_mask(head_rows, True)
    for item in (down[1], up[1], down[0], up[0], attn[1], attn[0]):
        if item is attn[0]:
            mail.move(s.result.at[:, pl.ds(1, 2)], outs.mlp_result)
            for k in range(3):
                head_from[k].wait_recv()
                head_own = head_own + s.head_z[k].astype(jnp.float32)
            s.head_result[...] = head_own
            shared = shared + jnp.sum(head_own * head_own)
            mail.move(s.head_result, outs.head_result)
        if item not in (down[1], up[1]):
            item.pass_z()
        grad = item.result[...]
        squares = squares + jnp.sum((grad * grad).reshape(head_rows // 8, 8, D), axis=0)
        if item in attn:
            l = attn.index(item)
            tiles = [grad[:, k * LANES : (k + 1) * LANES] for k in range(6)]
            target = s.attn_result.at[l]
            for k in range(3):
                target[k, :, 0:LANES] = tiles[k]
                target[k, :, LANES : LANES + 64] = tiles[3 + k][:, 0:64]
            target[3, :, 0:LANES] = jnp.where(upper, tiles[4], pltpu.roll(tiles[3], 64, 1))
            target[3, :, LANES : LANES + 64] = pltpu.roll(tiles[5], 64, 1)[:, 0:64]
            mail.move(target, outs.attn_result.at[l])

    owned = jnp.where(place.t == 0, 1.0, 0.0)
    total = jnp.sum(squares) + owned * shared
    tile_rows = lax.broadcasted_iota(jnp.int32, (8, LANES), 0)
    s.part[...] = jnp.where(tile_rows == 0, total, jnp.sum(r.loss[...]))
    s.by_fsdp[place.f] = s.part[...]
    copies = [mail.send(s.part, s.by_fsdp.at[place.f], place.up_f(k)) for k in range(1, 8)]
    for copy in copies:
        copy.wait_recv()
    value = s.by_fsdp[0]
    for k in range(1, 8):
        value = value + s.by_fsdp[k]
    s.group[...] = value
    s.by_tp[place.t] = value
    copies = [
        mail.send(s.group, s.by_tp.at[place.t], device)
        for device in (place.core, place.across, place.diagonal)
    ]
    for copy in copies:
        copy.wait_recv()
    s.totals[...] = s.by_tp[0] + s.by_tp[1] + s.by_tp[2] + s.by_tp[3]
    mail.move(s.totals, outs.totals)
    mail.finish(waited + [back_own])


FINAL_KEPT = dict(
    grad_pred=None, head=None, final_low=None, pieces=None, noisy=None
)
LATE_KEPT = dict(cond_weight=None)
NORM_KEPT = dict(normed=None, inverse=None)
MLP_KEPT = dict(mlp_out=None, wmlp=None, upward=None, active=None, rows=None)
ATTN_KEPT = dict(attn_out=None, wattn=None, qkv=None, probs=None, hidden=None, att=None)
SMALL_INS = dict(
    cond=None,
    loss=None,
    time_hidden=None,
    low_time=None,
    features=None,
    time_pre=None,
    label_hot=None,
)
BACKWARD_INS = SMALL_INS | LATE_KEPT | NORM_KEPT | FINAL_KEPT | MLP_KEPT | ATTN_KEPT
BACKWARD_OUTS = dict(
    mlp_result=((LAYERS, 2, D // 8, D), jnp.float32),
    attn_result=((LAYERS, 4, D // 8, D // 4), jnp.float32),
    head_result=((D // 8, LANES), jnp.float32),
    back_rows=((16, 16, LANES), jnp.float32),
    time_grad=((D // 8, D), jnp.float32),
    first_grad=((D // 8, FREQ), jnp.float32),
    label_grad=((D // 8, NCLASS), jnp.float32),
    totals=((8, LANES), jnp.float32),
)
MLP_RESULT = dict(mlp_result=None)
BACKWARD_OWN = dict(
    result=((LAYERS, 3, D // 8, D), jnp.float32),
    part=((8, LANES), jnp.float32),
    group=((8, LANES), jnp.float32),
    by_fsdp=((8, 8, LANES), jnp.float32),
    by_tp=((4, 8, LANES), jnp.float32),
    order=((8 * LANES, D), jnp.bfloat16),
    mod_grad=((16, D), jnp.float32),
    mod_other=((16, D), jnp.float32),
    mod_low=((2, 16, D), jnp.bfloat16),
    mod_rows=((32, 8 * LANES), jnp.float32),
    mod_send=((8, 2, 16, LANES), jnp.float32),
    back=((8, 2, 16, LANES), jnp.float32),
    cond_out=((2, 2, 4, D), jnp.float32),
    cond_sum=((2, 2, 4, D), jnp.float32),
    cond_in=((7, 4, D), jnp.float32),
    head_grad=((D, LANES), jnp.float32),
    head_other=((D, LANES), jnp.float32),
    head_mid=((D, LANES), jnp.float32),
    head_low=((D, LANES), jnp.bfloat16),
    head_far=((D, LANES), jnp.bfloat16),
    head_sum=((D, LANES), jnp.bfloat16),
    head_y=((D // 2, LANES), jnp.bfloat16),
    head_z=((3, D // 8, LANES), jnp.bfloat16),
    grad=((TOKENS, D), jnp.float32),
    mixed=((TOKENS, D), jnp.float32),
    grad_rows=((LAYERS, 2 * TOKENS, D), jnp.bfloat16),
    grad_up=((2 * TOKENS, D), jnp.bfloat16),
    both=((2 * TOKENS, D), jnp.bfloat16),
    grad_qkv=((2, 2 * TOKENS, D), jnp.bfloat16),
    sum_out=((LAYERS, 2, HALF, D), jnp.bfloat16),
    sum_in=((LAYERS, 2, HALF, D), jnp.bfloat16),
    far_out=((LAYERS, HALF, D), jnp.bfloat16),
    far_in=((LAYERS, HALF, D), jnp.bfloat16),
    own_out=((LAYERS, HALF, D), jnp.bfloat16),
    own_in=((LAYERS, HALF, D), jnp.bfloat16),
    keep=((2, HALF, D), jnp.float32),
    core_out=((LAYERS, TOKENS, D), jnp.bfloat16),
    core_in=((LAYERS, TOKENS, D), jnp.bfloat16),
    mlp_grad=((LAYERS, 2, D, D), jnp.bfloat16),
    attn_grad=((LAYERS, 2, D, D), jnp.bfloat16),
    from_x=((LAYERS, D, D), jnp.bfloat16),
    from_y=((LAYERS, 3, D // 2, D), jnp.bfloat16),
    from_z=((LAYERS, 3, 3, D // 8, D), jnp.bfloat16),
)


def backward_scratch():
    layered = MLP_KEPT | ATTN_KEPT
    specs = {}
    for name in BACKWARD_INS:
        if name in LATE_KEPT:
            specs[name] = FORWARD_OWN[name]
        elif name not in SMALL_INS:
            shape, dtype = FORWARD_OUTS[name]
            specs[name] = (shape[1:] if name in layered else shape, dtype)
    for name in BACKWARD_OUTS:
        if name not in MLP_RESULT:
            specs[name] = BACKWARD_OUTS[name]
    specs.update(BACKWARD_OWN)
    return specs


BACKWARD_SCRATCH = backward_scratch()


def run_backward(kept, inputs):
    anywhere = pl.BlockSpec(memory_space=pl.ANY)
    vmem = pl.BlockSpec(memory_space=pltpu.VMEM)
    given = [
        getattr(kept if hasattr(kept, name) else inputs, name) for name in BACKWARD_INS
    ]
    outs = pl.pallas_call(
        backward_kernel,
        out_shape=[jax.ShapeDtypeStruct(*spec) for spec in BACKWARD_OUTS.values()],
        in_specs=[vmem if name in SMALL_INS else anywhere for name in BACKWARD_INS],
        out_specs=[anywhere] * len(BACKWARD_OUTS),
        scratch_shapes=[pltpu.VMEM(*spec) for spec in BACKWARD_SCRATCH.values()]
        + [
            pltpu.SemaphoreType.DMA((128,)),
            pltpu.SemaphoreType.DMA((128,)),
            pltpu.SemaphoreType.DMA((64,)),
        ],
        compiler_params=pltpu.CompilerParams(
            collective_id=1, has_side_effects=True, vmem_limit_bytes=VMEM_LIMIT
        ),
    )(*given)
    return SimpleNamespace(**dict(zip(BACKWARD_OUTS, outs)))


def shard_tiles(attn_weight):
    q, k, v, o = (attn_weight[:, j].astype(jnp.bfloat16) for j in range(4))
    return jnp.concatenate(
        [
            q[..., :128],
            k[..., :128],
            v[..., :128],
            q[..., 128:],
            o[..., :64],
            k[..., 128:],
            o[..., 64:128],
            v[..., 128:],
            o[..., 128:],
        ],
        axis=-1,
    )


def wave_table():
    quarter = D // 4
    omegas = 1.0 / np.power(10000.0, np.arange(quarter, dtype=np.float32) / quarter)
    angles = np.arange(GRID, dtype=np.float32)[:, None] * omegas.astype(np.float32)[None, :]
    waves = np.concatenate([np.sin(angles), np.cos(angles)], axis=1).astype(np.float32)
    table = np.zeros((2 * GRID, D), np.float32)
    table[:GRID, : D // 2] = waves
    table[GRID:, D // 2 :] = waves
    padded = np.zeros((2 * GRID, 8, LANES), np.float32)
    padded[:, :, : D // 8] = table.reshape(2 * GRID, 8, D // 8)
    left = padded.reshape(2 * GRID, 8 * LANES)
    parts = []
    for _ in range(3):
        part = left.astype(jnp.bfloat16)
        parts.append(part)
        left = left - part.astype(np.float32)
    return np.concatenate(parts, axis=0)


def body_kernels(
    routes,
    latents,
    noise,
    timesteps,
    labels,
    step_count,
    tables,
    time_weight,
    cond_weight,
    cond_bias,
    attn_weight,
    mlp_weight,
    *states,
):
    fsdp_index = lax.axis_index("fsdp")
    tp_index = lax.axis_index("tp")
    across_index = tp_index // 2
    num_fsdp = routes.num_fsdp
    col_share = tables.shape[1]
    all_latents = timesteps.shape[0]
    total_entries = all_latents * SEQ * PATCH_DIM
    col_start = fsdp_index * col_share
    low_tables = tables.astype(jnp.bfloat16)
    blocks = cond_bias.shape[0] // col_share

    ordered = timesteps.reshape(num_fsdp, 2).T.reshape(-1)
    labels = labels.reshape(num_fsdp, 2).T.reshape(-1)
    features = timestep_features(ordered).astype(jnp.bfloat16)
    time_pre = jnp.dot(
        features,
        low_tables[2 * PATCH_DIM : 2 * PATCH_DIM + FREQ],
        preferred_element_type=jnp.float32,
    )
    time_hidden = jax.nn.silu(time_pre).astype(jnp.bfloat16)
    label_hot = (labels[:, None] == jnp.arange(NCLASS, dtype=jnp.int32)[None, :]).astype(
        jnp.bfloat16
    )
    label_part = jnp.dot(
        label_hot, low_tables[2 * PATCH_DIM + FREQ :], preferred_element_type=jnp.float32
    )
    low_time = time_weight.astype(jnp.bfloat16)
    cond_part = jnp.dot(time_hidden, low_time, preferred_element_type=jnp.float32)
    placed = lax.dynamic_update_slice(
        jnp.zeros((all_latents, D), jnp.float32), label_part, (0, col_start)
    )
    low_bias = cond_bias.astype(jnp.bfloat16).astype(jnp.float32)

    latent_id = fsdp_index * latents.shape[0]
    share = signal_share(lax.dynamic_slice_in_dim(timesteps, latent_id, latents.shape[0]))
    share = share[:, None, None]
    noisy = (jnp.sqrt(share) * latents + jnp.sqrt(1.0 - share) * noise).astype(jnp.bfloat16)
    data = jnp.concatenate(
        [
            jnp.pad(noisy.astype(jnp.float32), ((0, 0), (0, 0), (0, LANES - PATCH_DIM))),
            jnp.pad(noise, ((0, 0), (0, 0), (PATCH_DIM, LANES - 2 * PATCH_DIM))),
        ],
        axis=1,
    )
    shards = jnp.concatenate(
        [shard_tiles(attn_weight)[:, None], mlp_weight.astype(jnp.bfloat16)], axis=1
    )
    head = jnp.pad(low_tables[: 2 * PATCH_DIM].T, ((0, 0), (0, LANES - 2 * PATCH_DIM)))
    cond_part = cond_part + placed
    inputs = SimpleNamespace(
        cond_part=cond_part.reshape(2, 2, num_fsdp // 2, D),
        shards=shards,
        data=data,
        head=head,
        waves=jnp.asarray(wave_table()),
        cond_weight=cond_weight.reshape(blocks, col_share, D),
        cond_bias=low_bias.reshape(blocks, col_share),
    )
    kept = run_forward(vars(inputs), total_entries)
    inputs.time_hidden = time_hidden
    inputs.low_time = low_time
    inputs.features = features
    inputs.time_pre = time_pre
    inputs.label_hot = label_hot
    back = run_backward(kept, inputs)

    cond = kept.cond.reshape(all_latents, D)
    cond_act = jax.nn.silu(cond).astype(jnp.bfloat16)
    modul_back = back.back_rows[:, :blocks, :col_share].reshape(all_latents, -1)
    modul_back = modul_back.astype(jnp.bfloat16)
    cond_grad_w = dot_f32(modul_back, cond_act, 0, 0)
    bias_grad = jnp.sum(modul_back.astype(jnp.float32), axis=0)
    time_grad = back.time_grad
    tables_grad = jnp.concatenate(
        [back.head_result[:, : 2 * PATCH_DIM], back.first_grad, back.label_grad], axis=1
    ).T
    loss = back.totals[1, 0] / total_entries
    norm = jnp.sqrt(back.totals[0, 0])
    entries = NTAB * D + D * D + (D + 1) * NCOND + LAYERS * (4 * D * D + 2 * D * FF)
    limit = clip_scale * math.sqrt(entries / (all_latents * SEQ))
    factor = jnp.minimum(1.0, limit / norm)
    count = step_count[0].astype(jnp.float32)
    attn_grad = back.attn_result
    mlp_grad = back.mlp_result
    weights_all = (tables, time_weight, cond_weight, cond_bias, attn_weight, mlp_weight)
    grads_all = (tables_grad, time_grad, cond_grad_w, bias_grad, attn_grad, mlp_grad)
    states = tuple(zip(states[0::2], states[1::2]))
    results = [loss, norm]
    for weight, grad, state in zip(weights_all, grads_all, states):
        results.extend(adam_update(weight, grad * factor, state[0], state[1], count))
    return tuple(results)


def body(routes, *args):
    if routes.num_fsdp == 8 and args[5].shape[1] % 16 == 0:
        return body_kernels(routes, *args)
    return body_steps(routes, *args)


def solution(mesh):
    vectors = P("fsdp")
    columns = P(None, "fsdp")
    rows = P("fsdp", None)
    blocks = P(None, None, "fsdp", "tp")
    data = P("fsdp", "tp", None)
    weights = (columns, rows, rows, vectors, blocks, blocks)
    states = tuple(spec for spec in weights for _ in range(2))
    updated = tuple(spec for spec in weights for _ in range(3))
    return jax.shard_map(
        partial(body, Routes(mesh)),
        mesh=mesh,
        in_specs=(data, data, P(), P(), P()) + weights + states,
        out_specs=(P(), P()) + updated,
        check_vma=False,
    )
```
